32 devices in a mesh: dp: 8 (over z, x), shard: 4 (over y, core).
Axes of the slice: x: 2, y: 2, z: 4, core: 2. Of those that a mesh axis runs over, the one named last changes fastest.
Arguments:
- layer_input: bfloat16 [16384, 960], P(('dp', 'shard')), may hold values from -6 to 6
- cotangent: bfloat16 [16384, 960], P(('dp', 'shard')), may hold values from -6 to 6
- master_attention: float32 [2457600], P(('dp', 'shard'))
- master_feedforward: float32 [7372800], P(('dp', 'shard'))
- master_gains: float32 [1920], P(('dp', 'shard')), may hold values from 0.5 to 1.5
- first_attention: float32 [2457600], P(('dp', 'shard')), may hold values from -20 to 20
- second_attention: float32 [2457600], P(('dp', 'shard')), may hold values from 0.16384 to 4.9152
- first_feedforward: float32 [7372800], P(('dp', 'shard')), may hold values from -20 to 20
- second_feedforward: float32 [7372800], P(('dp', 'shard')), may hold values from 0.16384 to 4.9152
- first_gains: float32 [1920], P(('dp', 'shard')), may hold values from -20 to 20
- second_gains: float32 [1920], P(('dp', 'shard')), may hold values from 0.16384 to 4.9152
- block_start: int32 [128], P('dp'), may hold values from 0 to 15, as said below
- block_fill: int32 [128], P('dp'), may hold values from 0 to 128
Outputs:
- layer_output: float32 [16384, 960], P(('dp', 'shard'))
- input_gradient: float32 [16384, 960], P(('dp', 'shard'))
- attention_gradient: float32 [2457600], P(('dp', 'shard'))
- feedforward_gradient: float32 [7372800], P(('dp', 'shard'))
- gains_gradient: float32 [1920], P(('dp', 'shard'))
- attention_first: float32 [2457600], P(('dp', 'shard'))
- attention_second: float32 [2457600], P(('dp', 'shard'))
- feedforward_first: float32 [7372800], P(('dp', 'shard'))
- feedforward_second: float32 [7372800], P(('dp', 'shard'))
- gains_first: float32 [1920], P(('dp', 'shard'))
- gains_second: float32 [1920], P(('dp', 'shard'))
- attention_update: float32 [2457600], P(('dp', 'shard'))
- feedforward_update: float32 [7372800], P(('dp', 'shard'))
- gains_update: float32 [1920], P(('dp', 'shard'))
The draws below stay inside these ranges and needn't reach their ends.
Inputs may be any that keep to these rules, and one draw needn't show every extreme that they name: Within each group of 16 blocks, block_start of a block is never above the block's own index and at most 15 below it; a sequence takes consecutive blocks that share block_start, all full but its last; padding blocks (fill 0, their own start) come after all live blocks of a group, of which there are 4 or more; some sequence has exactly 2048 tokens.
All inputs are finite; a program needn't handle non-finite values.
Results may differ from the reference program's by a relative error of at most 0.033.
Values may be sent and summed in bfloat16 or wider, within the bound.
No kernel may reach another device: no remote copies, remote signals or barrier semaphores. Data moves between devices by JAX's collectives and lax.ppermute only.
A program may use at most 448 MiB of HBM per device.

```python
import math
import jax
import jax.numpy as jnp
from jax import lax

MODEL_WIDTH = 960
QUERY_HEADS = 15
KEY_VALUE_HEADS = 5
HEAD_SIZE = 64
FF = 2560
BLK = 128
ADAM_STEP = 10
GROUP_SLOTS = 2048
GROUP_BLOCKS = 16
SEQ_MAX = 2048
TOKENS = 16384
BLOCKS = 128
ATT_P = 2457600
MLP_P = 7372800
GAIN_P = 1920


def block_layout(key):
    base = jax.random.fold_in(key, 4242)
    key_rows = jax.random.split(base, 4)
    groups = BLOCKS // GROUP_BLOCKS
    longest = SEQ_MAX // BLK
    index = jnp.arange(GROUP_BLOCKS, dtype=jnp.int32)[None, :]
    group_index = jnp.arange(groups, dtype=jnp.int32)[:, None]
    fresh = jax.random.randint(key_rows[0], (groups, GROUP_BLOCKS), 0, 4) == 0
    starts = fresh | (index % longest == 0)
    used = jax.random.randint(key_rows[1], (groups, 1), GROUP_BLOCKS // 4, GROUP_BLOCKS + 1)
    chosen = jax.random.randint(key_rows[2], (), 0, groups)
    picked = group_index == chosen
    used = jnp.where(picked, GROUP_BLOCKS, used)
    starts = starts & jnp.logical_not(picked & (index > 0) & (index < longest))
    live = index < used
    starts = starts | jnp.logical_not(live)
    first = lax.cummax(jnp.where(starts, index, 0), axis=1)
    closing = jnp.concatenate([starts[:, 1:], jnp.ones((groups, 1), dtype=jnp.bool_)], axis=1)
    partial_fill = jax.random.randint(key_rows[3], (groups, GROUP_BLOCKS), 1, BLK + 1)
    fill = jnp.where(closing, partial_fill, BLK)
    fill = jnp.where(picked & (index == longest - 1), BLK, fill)
    fill = jnp.where(live, fill, 0)
    return (first.reshape(-1).astype(jnp.int32), fill.reshape(-1).astype(jnp.int32))


def draw_block_start(key, part):
    return block_layout(key)[0]


def draw_block_fill(key, part):
    return block_layout(key)[1]


def draw_master_attention(key, part):
    token_count = MODEL_WIDTH * (2 * QUERY_HEADS * HEAD_SIZE + 2 * KEY_VALUE_HEADS * HEAD_SIZE)
    boundary_edge = MODEL_WIDTH * (QUERY_HEADS * HEAD_SIZE + 2 * KEY_VALUE_HEADS * HEAD_SIZE)
    value_rows = jnp.clip(jax.random.normal(key, (token_count,), jnp.float32), -6.0, 6.0)
    index = jnp.arange(token_count)
    return value_rows * jnp.where(index < boundary_edge, MODEL_WIDTH ** (-0.5), (MODEL_WIDTH // 16) ** (-0.5))


def draw_master_feedforward(key, part):
    token_count = 3 * MODEL_WIDTH * FF
    boundary_edge = 2 * MODEL_WIDTH * FF
    value_rows = jnp.clip(jax.random.normal(key, (token_count,), jnp.float32), -6.0, 6.0)
    index = jnp.arange(token_count)
    return value_rows * jnp.where(index < boundary_edge, MODEL_WIDTH ** (-0.5), (FF // 4) ** (-0.5))


def levels(own_key, extent, shards, least, high):
    level = 1.0
    for dim, shards_of in shards:
        draws = jax.random.uniform(jax.random.fold_in(jax.random.fold_in(own_key, 6), dim), (shards_of,), jnp.float32, least / len(shards), high / len(shards))
        level = level * jnp.repeat(jnp.exp(draws), extent[dim] // shards_of).reshape((-1,) + (1,) * (len(extent) - 1 - dim))
    return level


def normal_values(stream_key, dims, width, most, cuts=(), held_as=jnp.bfloat16):
    drawn = width * jax.random.normal(stream_key, dims, jnp.float32)
    if cuts:
        drawn = drawn * levels(stream_key, dims, cuts, -0.22, 0.18)
    return jnp.clip(drawn, -most, most).astype(held_as)


def setup_inputs(seed: int = 0) -> dict:
    key_list = jax.random.split(jax.random.key(seed), 14)
    layer_input = normal_values(key_list[0], (TOKENS, MODEL_WIDTH), 1.0, 6.0, ((0, 32),))
    cotangent = normal_values(key_list[1], (TOKENS, MODEL_WIDTH), 1.0, 6.0, ((0, 32),))
    master_attention = draw_master_attention(jax.random.fold_in(key_list[13], 71), 0)
    master_feedforward = draw_master_feedforward(jax.random.fold_in(key_list[13], 71), 0)
    master_gains = jnp.clip(1.0 + 0.1 * jax.random.normal(key_list[4], (GAIN_P,), jnp.float32), 0.5, 1.5)
    first_attention = normal_values(key_list[5], (ATT_P,), (0.025 * TOKENS ** 0.5), 20.0, ((0, 32),), jnp.float32)
    second_attention = jnp.clip(jnp.exp(math.log(4.9152) - 3.4011975 * jax.random.uniform(key_list[6], (ATT_P,), jnp.float32) ** levels(key_list[6], (ATT_P,), ((0, 32),), -0.2, 0.2)), 0.16384, 4.9152)
    first_feedforward = normal_values(key_list[7], (MLP_P,), (0.025 * TOKENS ** 0.5), 20.0, ((0, 32),), jnp.float32)
    second_feedforward = jnp.clip(jnp.exp(math.log(4.9152) - 3.4011975 * jax.random.uniform(key_list[8], (MLP_P,), jnp.float32) ** levels(key_list[8], (MLP_P,), ((0, 32),), -0.2, 0.2)), 0.16384, 4.9152)
    first_gains = normal_values(key_list[9], (GAIN_P,), (0.025 * TOKENS ** 0.5), 20.0, ((0, 32),), jnp.float32)
    second_gains = jnp.clip(jnp.exp(math.log(4.9152) - 3.4011975 * jax.random.uniform(key_list[10], (GAIN_P,), jnp.float32) ** levels(key_list[10], (GAIN_P,), ((0, 32),), -0.2, 0.2)), 0.16384, 4.9152)
    block_start = draw_block_start(jax.random.fold_in(key_list[13], 71), 0)
    block_fill = draw_block_fill(jax.random.fold_in(key_list[13], 71), 0)
    return {"layer_input": layer_input, "cotangent": cotangent, "master_attention": master_attention, "master_feedforward": master_feedforward, "master_gains": master_gains, "first_attention": first_attention, "second_attention": second_attention, "first_feedforward": first_feedforward, "second_feedforward": second_feedforward, "first_gains": first_gains, "second_gains": second_gains, "block_start": block_start, "block_fill": block_fill}


highest = lax.Precision.HIGHEST
epsilon = 1e-05
masked_value = -1e+30
learning_rate = 0.03
weight_decay = 0.1

@jax.custom_vjp
def reduced_precision(v):
    return lax.optimization_barrier(v.astype(jnp.bfloat16)).astype(jnp.float32)

@jax.custom_vjp
def reduced_backward(v):
    return v

def low_keep(v):
    return (reduced_precision(v), None)

def low_pass(kept, grad):
    return (grad,)

def back_keep(v):
    return (v, None)

def back_low(kept, grad):
    return (reduced_precision(grad),)
reduced_precision.defvjp(low_keep, low_pass)
reduced_backward.defvjp(back_keep, back_low)

def inner_product(left, right):
    return jnp.dot(left, right, precision=highest, preferred_element_type=jnp.float32)

def rope_tables(positions):
    steps = jnp.arange(HEAD_SIZE // 2, dtype=jnp.float32) * (2.0 / HEAD_SIZE)
    inverse = jnp.exp(-math.log(10000.0) * steps)
    angles = positions.astype(jnp.float32)[:, None] * inverse[None, :]
    return (jnp.cos(angles), jnp.sin(angles))

def apply_rotation(field, cosine_table, sine_table, heads):
    rows = field.shape[0]
    shaped = field.reshape(rows, heads, HEAD_SIZE)
    front = shaped[:, :, :HEAD_SIZE // 2]
    back = shaped[:, :, HEAD_SIZE // 2:]
    cosine_wide = cosine_table[:, None, :]
    sine_wide = sine_table[:, None, :]
    turned = jnp.concatenate([front * cosine_wide - back * sine_wide, back * cosine_wide + front * sine_wide], axis=2)
    return turned.reshape(rows, heads * HEAD_SIZE)

def norm_rows(field, gain):
    scale = lax.rsqrt(lax.optimization_barrier(jnp.mean(field * field, axis=1, keepdims=True)) + epsilon)
    return field * scale * gain[None, :]

def adam_step(grad, moment, second, master):
    moment_new = 0.9 * moment + 0.1 * grad
    second_new = 0.999 * second + 0.001 * grad * grad
    corrected = moment_new / (1.0 - 0.9 ** ADAM_STEP)
    scaled = second_new / (1.0 - 0.999 ** ADAM_STEP)
    update = -learning_rate * (corrected / (jnp.sqrt(scaled) + 1e-08) + weight_decay * master)
    return (moment_new, second_new, update)

def widen(master):
    return lax.optimization_barrier(master.astype(jnp.bfloat16)).astype(jnp.float32)

def reference(layer_input, cotangent, master_attention, master_feedforward, master_gains, first_attention, second_attention, first_feedforward, second_feedforward, first_gains, second_gains, block_start, block_fill):
    query_width = QUERY_HEADS * HEAD_SIZE
    key_head_width = KEY_VALUE_HEADS * HEAD_SIZE
    grouped_rows = QUERY_HEADS // KEY_VALUE_HEADS
    sequence_span = grouped_rows * HEAD_SIZE
    score_scale = 1.0 / math.sqrt(HEAD_SIZE)
    attention_all = widen(master_attention)
    feedforward_all = widen(master_feedforward)
    gains_all = widen(master_gains)
    edge_one = MODEL_WIDTH * query_width
    edge_two = edge_one + MODEL_WIDTH * key_head_width
    edge_three = edge_two + MODEL_WIDTH * key_head_width
    weights = (attention_all[:edge_one].reshape(MODEL_WIDTH, query_width), attention_all[edge_one:edge_two].reshape(MODEL_WIDTH, key_head_width), attention_all[edge_two:edge_three].reshape(MODEL_WIDTH, key_head_width), attention_all[edge_three:].reshape(query_width, MODEL_WIDTH), feedforward_all[:MODEL_WIDTH * FF].reshape(MODEL_WIDTH, FF), feedforward_all[MODEL_WIDTH * FF:2 * MODEL_WIDTH * FF].reshape(MODEL_WIDTH, FF), feedforward_all[2 * MODEL_WIDTH * FF:].reshape(FF, MODEL_WIDTH), gains_all[:MODEL_WIDTH], gains_all[MODEL_WIDTH:])
    groups = TOKENS // GROUP_SLOTS

    def group_step(carry, slices):
        rows, cotangent_rows, starts, fills = slices
        slots = jnp.arange(GROUP_SLOTS, dtype=jnp.int32)
        tags = jnp.repeat(starts, BLK)
        live = slots % BLK < jnp.repeat(fills, BLK)
        positions = slots - tags * BLK
        allowed = (tags[:, None] == tags[None, :]) & (slots[None, :] <= slots[:, None]) & (live[None, :] | (slots[None, :] == slots[:, None]))
        cosine_table, sine_table = rope_tables(positions)

        def head_block(operands):
            query_head, key_head, value_head = operands
            shaped = query_head.reshape(GROUP_SLOTS, grouped_rows, HEAD_SIZE)
            scores = reduced_backward(jnp.einsum('tgd,sd->gts', shaped, key_head, precision=highest) * score_scale)
            masked = jnp.where(allowed[None, :, :], scores, masked_value)
            top = lax.optimization_barrier(jnp.max(masked, axis=2, keepdims=True))
            exponent = jnp.exp(masked - top)
            probs = reduced_precision(exponent / lax.optimization_barrier(jnp.sum(exponent, axis=2, keepdims=True)))
            return jnp.einsum('gts,sd->tgd', probs, value_head, precision=highest).reshape(GROUP_SLOTS, sequence_span)

        def forward(inputs, query_weight, key_matrix, value_weight, out_weight, gate_weight, up_weight, down_weight, gain_one, gain_two):
            first_hidden = reduced_precision(norm_rows(inputs, gain_one))
            query_rows = reduced_precision(apply_rotation(reduced_backward(inner_product(first_hidden, query_weight)), cosine_table, sine_table, QUERY_HEADS))
            key_rows = reduced_precision(apply_rotation(reduced_backward(inner_product(first_hidden, key_matrix)), cosine_table, sine_table, KEY_VALUE_HEADS))
            value_rows = reduced_precision(reduced_backward(inner_product(first_hidden, value_weight)))
            query_head_rows = query_rows.reshape(GROUP_SLOTS, KEY_VALUE_HEADS, sequence_span).transpose(1, 0, 2)
            key_head_rows = key_rows.reshape(GROUP_SLOTS, KEY_VALUE_HEADS, HEAD_SIZE).transpose(1, 0, 2)
            value_head_rows = value_rows.reshape(GROUP_SLOTS, KEY_VALUE_HEADS, HEAD_SIZE).transpose(1, 0, 2)
            attended = lax.map(jax.checkpoint(head_block), (query_head_rows, key_head_rows, value_head_rows))
            attended = attended.transpose(1, 0, 2).reshape(GROUP_SLOTS, query_width)
            mixed = reduced_precision(reduced_backward(attended))
            middle = inputs + reduced_backward(inner_product(mixed, out_weight))
            hidden_two = reduced_precision(norm_rows(middle, gain_two))
            gate = reduced_backward(inner_product(hidden_two, gate_weight))
            upper = reduced_backward(inner_product(hidden_two, up_weight))
            inner = reduced_precision(gate * jax.nn.sigmoid(gate) * upper)
            return middle + reduced_backward(inner_product(inner, down_weight))
        output, pull = jax.vjp(forward, rows.astype(jnp.float32), *weights)
        grads = pull(cotangent_rows.astype(jnp.float32) * live[:, None].astype(jnp.float32))
        carry = tuple((total + term for total, term in zip(carry, grads[1:])))
        return (carry, (output, grads[0]))
    initial = tuple((jnp.zeros(weight.shape, jnp.float32) for weight in weights))
    slices = (layer_input.reshape(groups, GROUP_SLOTS, MODEL_WIDTH), cotangent.reshape(groups, GROUP_SLOTS, MODEL_WIDTH), block_start.reshape(groups, GROUP_BLOCKS), block_fill.reshape(groups, GROUP_BLOCKS))
    totals, stacked = lax.scan(group_step, initial, slices)
    outputs, input_grads = stacked
    attention_gradient = jnp.concatenate([totals[0].reshape(-1), totals[1].reshape(-1), totals[2].reshape(-1), totals[3].reshape(-1)])
    feedforward_gradient = jnp.concatenate([totals[4].reshape(-1), totals[5].reshape(-1), totals[6].reshape(-1)])
    gains_gradient = jnp.concatenate([totals[7], totals[8]])
    attention_first, attention_second, attention_update = adam_step(attention_gradient, first_attention, second_attention, master_attention)
    feedforward_first, feedforward_second, feedforward_update = adam_step(feedforward_gradient, first_feedforward, second_feedforward, master_feedforward)
    gains_first, gains_second, gains_update = adam_step(gains_gradient, first_gains, second_gains, master_gains)
    return (outputs.reshape(TOKENS, MODEL_WIDTH), input_grads.reshape(TOKENS, MODEL_WIDTH), attention_gradient, feedforward_gradient, gains_gradient, attention_first, attention_second, feedforward_first, feedforward_second, gains_first, gains_second, attention_update, feedforward_update, gains_update)
```

```python
import functools
import math

import jax
import jax.numpy as jnp
from jax import lax
from jax.experimental import pallas as pl
from jax.experimental.pallas import tpu as pltpu
from jax.sharding import PartitionSpec as P

MODEL_WIDTH = 960
QUERY_HEADS = 15
KEY_VALUE_HEADS = 5
GROUPED = QUERY_HEADS // KEY_VALUE_HEADS
HEAD_SIZE = 64
FF = 2560
BLK = 128
ADAM_STEP = 10
TOK_DEV = 512
KV_WIDTH = KEY_VALUE_HEADS * HEAD_SIZE
TILE = 256
WIDE = GROUPED * BLK
UNITS = 32
LINES = 600
GAIN_LINES = 8
ALL_AXES = ("dp", "shard")

epsilon = 1e-05
masked_value = -1e30
learning_rate = 0.03
weight_decay = 0.1
score_scale = 1.0 / math.sqrt(HEAD_SIZE)
f32 = jnp.float32
bf16 = jnp.bfloat16


def lines_to_rows_2560(scratch, base, rows, store):
    for c in range(20):
        store(c, scratch[pl.ds(base + c, rows, stride=20), :])


def rows_to_lines_2560(load, scratch, base, rows):
    for c in range(20):
        scratch[pl.ds(base + c, rows, stride=20), :] = load(c)


def lane_low(rows):
    return lax.broadcasted_iota(jnp.int32, (rows, 128), 1) < 64


def lines_to_rows_960(scratch, base, rows, mid, store):
    half = rows // 2
    low = lane_low(half)
    line = [scratch[pl.ds(base + k, half, stride=15), :] for k in range(15)]
    turned = [None] * 7 + [pltpu.roll(line[k], 64, 1) for k in range(7, 15)]
    for c in range(8):
        mid[pl.ds(0, half, stride=2), :] = line[c]
        odd = jnp.where(low, turned[7 + c], turned[8 + c]) if c < 7 else turned[14]
        mid[pl.ds(1, half, stride=2), :] = odd
        store(c, mid[pl.ds(0, rows), :])


def rows_to_lines_960(load, scratch, base, rows, mid):
    half = rows // 2
    low = lane_low(half)
    odds = []
    for c in range(8):
        mid[pl.ds(0, rows), :] = load(c)
        even = mid[pl.ds(0, half, stride=2), :]
        odd = pltpu.roll(mid[pl.ds(1, half, stride=2), :], 64, 1)
        odds.append(odd)
        if c < 7:
            scratch[pl.ds(base + c, half, stride=15), :] = even
        else:
            scratch[pl.ds(base + 7, half, stride=15), :] = jnp.where(low, even, odds[0])
        if c > 0:
            scratch[pl.ds(base + 7 + c, half, stride=15), :] = jnp.where(low, odds[c - 1], odd)


def half_chunks(lines):
    even = [(lines[0], 0), (lines[0], 1), (lines[1], 0), (lines[1], 1), (lines[2], 0)]
    odd = [(lines[2], 1), (lines[3], 0), (lines[3], 1), (lines[4], 0), (lines[4], 1)]
    return even, odd


def placed(chunk, upper):
    line, side = chunk
    return line if side == upper else pltpu.roll(line, 64, 1)


def unpack_ff_kernel(lines_ref, gate_ref, up_ref, down_ref, scratch, mid):
    phase = pl.program_id(0)
    scratch[...] = lines_ref[...].astype(f32)
    for number, out in ((0, gate_ref), (1, up_ref)):

        @pl.when(phase == number)
        def _():
            def store(c, value):
                out[:, 128 * c : 128 * c + 128] = value.astype(bf16)

            lines_to_rows_2560(scratch, 0, 96, store)

    @pl.when(phase == 2)
    def _():
        def store(c, value):
            if c < 7:
                down_ref[:, 128 * c : 128 * c + 128] = value.astype(bf16)
            else:
                down_ref[:, 896:960] = value[:, :64].astype(bf16)

        lines_to_rows_960(scratch, 0, 256, mid, store)


def pinned(phase):
    def index(p, j):
        return (jnp.where(p == phase, j, jnp.where(p < phase, 0, 9)), 0)

    return index


def unpack_ff(lines):
    return pl.pallas_call(
        unpack_ff_kernel,
        grid=(3, 10),
        in_specs=[pl.BlockSpec((1920, 128), lambda p, j: (p * 10 + j, 0))],
        out_specs=[
            pl.BlockSpec((96, FF), pinned(0)),
            pl.BlockSpec((96, FF), pinned(1)),
            pl.BlockSpec((256, MODEL_WIDTH), pinned(2)),
        ],
        out_shape=[
            jax.ShapeDtypeStruct((MODEL_WIDTH, FF), bf16),
            jax.ShapeDtypeStruct((MODEL_WIDTH, FF), bf16),
            jax.ShapeDtypeStruct((FF, MODEL_WIDTH), bf16),
        ],
        scratch_shapes=[pltpu.VMEM((1920, 128), f32), pltpu.VMEM((256, 128), f32)],
        name="unpack_feedforward",
    )(lines)


def pack_ff_kernel(gate_ref, up_ref, down_ref, lines_ref, scratch, mid):
    phase = pl.program_id(0)
    for number, source in ((0, gate_ref), (1, up_ref)):

        @pl.when(phase == number)
        def _():
            rows_to_lines_2560(
                lambda c: source[:, 128 * c : 128 * c + 128].astype(f32), scratch, 0, 96
            )

    @pl.when(phase == 2)
    def _():
        def load(c):
            if c < 7:
                return down_ref[:, 128 * c : 128 * c + 128].astype(f32)
            tail = down_ref[:, 896:960].astype(f32)
            return jnp.concatenate([tail, tail], axis=1)

        rows_to_lines_960(load, scratch, 0, 256, mid)

    lines_ref[...] = scratch[...].astype(bf16)


def pack_ff(gate, up, down):
    return pl.pallas_call(
        pack_ff_kernel,
        grid=(3, 10),
        in_specs=[
            pl.BlockSpec((96, FF), pinned(0)),
            pl.BlockSpec((96, FF), pinned(1)),
            pl.BlockSpec((256, MODEL_WIDTH), pinned(2)),
        ],
        out_specs=pl.BlockSpec((1920, 128), lambda p, j: (p * 10 + j, 0)),
        out_shape=jax.ShapeDtypeStruct((3 * 19200, 128), bf16),
        scratch_shapes=[pltpu.VMEM((1920, 128), f32), pltpu.VMEM((256, 128), f32)],
        name="pack_feedforward",
    )(gate, up, down)


def unpack_wide_kernel(lines_ref, out_ref, scratch, mid):
    for u in range(4):
        scratch[...] = lines_ref[u].astype(f32)
        base = u * 80

        def store(c, value):
            if c < 7:
                out_ref[base : base + 80, 128 * c : 128 * c + 128] = value.astype(bf16)
            else:
                out_ref[base : base + 80, 896:960] = value[:, :64].astype(bf16)

        lines_to_rows_960(scratch, 0, 80, mid, store)


def unpack_wide(lines, first):
    depth = lines.shape[1]
    return pl.pallas_call(
        unpack_wide_kernel,
        grid=(3,),
        in_specs=[pl.BlockSpec((4, depth, 128), lambda j: (first // 4 + j, 0, 0))],
        out_specs=pl.BlockSpec((320, MODEL_WIDTH), lambda j: (j, 0)),
        out_shape=jax.ShapeDtypeStruct((MODEL_WIDTH, MODEL_WIDTH), bf16),
        scratch_shapes=[pltpu.VMEM((depth, 128), f32), pltpu.VMEM((80, 128), f32)],
        name="unpack_attention",
    )(lines)


def unpack_kv_kernel(key_ref, value_ref, out_ref, key_lines, value_lines, mid):
    low = lane_low(120)
    key_lines[...] = key_ref[0].astype(f32)
    value_lines[...] = value_ref[0].astype(f32)
    keys = half_chunks([key_lines[pl.ds(k, 120, stride=5), :] for k in range(5)])
    values = half_chunks([value_lines[pl.ds(k, 120, stride=5), :] for k in range(5)])
    for h in range(KEY_VALUE_HEADS):
        for parity in range(2):
            mid[pl.ds(parity, 120, stride=2), :] = jnp.where(
                low, placed(keys[parity][h], 0), placed(values[parity][h], 1)
            )
        out_ref[:, 128 * h : 128 * h + 128] = mid[...].astype(bf16)


def unpack_kv(lines):
    depth = lines.shape[1]
    return pl.pallas_call(
        unpack_kv_kernel,
        grid=(4,),
        in_specs=[
            pl.BlockSpec((1, depth, 128), lambda j: (12 + j, 0, 0)),
            pl.BlockSpec((1, depth, 128), lambda j: (16 + j, 0, 0)),
        ],
        out_specs=pl.BlockSpec((240, 2 * KV_WIDTH), lambda j: (j, 0)),
        out_shape=jax.ShapeDtypeStruct((MODEL_WIDTH, 2 * KV_WIDTH), bf16),
        scratch_shapes=[
            pltpu.VMEM((depth, 128), f32),
            pltpu.VMEM((depth, 128), f32),
            pltpu.VMEM((240, 128), f32),
        ],
        name="unpack_key_value",
    )(lines, lines)


def pack_attention_kernel(query_ref, kv_ref, out_weight_ref, gains_ref, lines_ref, scratch, mid):
    step = pl.program_id(0)

    def wide(source):
        for u in range(4):
            base = u * 80

            def load(c):
                if c < 7:
                    return source[base : base + 80, 128 * c : 128 * c + 128].astype(f32)
                tail = source[base : base + 80, 896:960].astype(f32)
                return jnp.concatenate([tail, tail], axis=1)

            rows_to_lines_960(load, scratch, 0, 80, mid)
            lines_ref[u, :LINES, :] = scratch[...].astype(bf16)

    @pl.when(step < 3)
    def _():
        wide(query_ref)

    @pl.when(step >= 5)
    def _():
        wide(out_weight_ref)

    for number, upper in ((3, 0), (4, 1)):

        @pl.when(step == number)
        def _():
            low = lane_low(120)
            for u in range(4):
                evens, odds = [], []
                for h in range(KEY_VALUE_HEADS):
                    mid[...] = kv_ref[
                        240 * u : 240 * u + 240, 128 * h : 128 * h + 128
                    ].astype(f32)
                    evens.append((mid[pl.ds(0, 120, stride=2), :], upper))
                    odds.append((mid[pl.ds(1, 120, stride=2), :], upper))
                run = evens + odds
                for k in range(5):
                    scratch[pl.ds(k, 120, stride=5), :] = jnp.where(
                        low, placed(run[2 * k], 0), placed(run[2 * k + 1], 1)
                    )
                lines_ref[u, :LINES, :] = scratch[...].astype(bf16)

    for u in range(4):
        lines_ref[u, LINES:, :] = gains_ref[u]


def pack_attention(d_query, d_kv, d_out, gains):
    return pl.pallas_call(
        pack_attention_kernel,
        grid=(8,),
        in_specs=[
            pl.BlockSpec((320, MODEL_WIDTH), lambda s: (jnp.minimum(s, 2), 0)),
            pl.BlockSpec((MODEL_WIDTH, 2 * KV_WIDTH), lambda s: (0, 0)),
            pl.BlockSpec((320, MODEL_WIDTH), lambda s: (jnp.maximum(s - 5, 0), 0)),
            pl.BlockSpec((4, GAIN_LINES, 128), lambda s: (s, 0, 0)),
        ],
        out_specs=pl.BlockSpec((4, LINES + GAIN_LINES, 128), lambda s: (s, 0, 0)),
        out_shape=jax.ShapeDtypeStruct((UNITS, LINES + GAIN_LINES, 128), bf16),
        scratch_shapes=[pltpu.VMEM((LINES, 128), f32), pltpu.VMEM((240, 128), f32)],
        name="pack_attention",
    )(d_query, d_kv, d_out, gains)


def tile_range(starts_ref, fills_ref, block):
    first_slot = starts_ref[block] * BLK
    last_slot = block * BLK + fills_ref[block]
    tile_first = first_slot // TILE
    tile_last = (block * BLK) // TILE
    ragged_first = jnp.logical_and(first_slot % TILE != 0, tile_first < tile_last)
    return first_slot, last_slot, tile_first, tile_last, ragged_first.astype(jnp.int32)


def allowed_pairs(tile, block, first_slot, last_slot):
    key_slot = tile * TILE + lax.broadcasted_iota(jnp.int32, (TILE, WIDE), 0)
    lane = lax.broadcasted_iota(jnp.int32, (TILE, WIDE), 1)
    query_slot = block * BLK + lax.rem(lane, BLK)
    return jnp.logical_and(
        jnp.logical_and(key_slot >= first_slot, key_slot <= query_slot),
        jnp.logical_or(key_slot < last_slot, key_slot == query_slot),
    )


def over_tiles(span, block, step):
    first_slot, last_slot, tile_first, tile_last, ragged = span

    def masked(tile):
        step(tile, allowed_pairs(tile, block, first_slot, last_slot))

    def edge(k, carry):
        masked(jnp.where(k == ragged, tile_last, tile_first))
        return carry

    lax.fori_loop(0, 1 + ragged, edge, 0)

    def inner(tile, carry):
        step(tile, None)
        return carry

    lax.fori_loop(tile_first + ragged, tile_last, inner, 0)


def transpose_kv(kv_ref, turned, tiles):
    def body(t, carry):
        rows = pl.ds(pl.multiple_of(t * TILE, TILE), TILE)
        for h in range(KEY_VALUE_HEADS):
            turned[t, 128 * h : 128 * h + 128, :] = kv_ref[rows, 128 * h : 128 * h + 128].T
        return carry

    lax.fori_loop(0, tiles, body, 0)


def heads_beside(ref, h):
    return jnp.concatenate(
        [
            ref[HEAD_SIZE * (GROUPED * h + g) : HEAD_SIZE * (GROUPED * h + g + 1), :]
            for g in range(GROUPED)
        ],
        axis=1,
    )


def attention_forward_kernel(
    starts_ref, fills_ref, place_ref, query_ref, kv_ref, mixed_ref, log_ref, turned, pairs, tops, totals, sums
):
    i = pl.program_id(0)
    block = place_ref[0] * (TOK_DEV // BLK) + i

    @pl.when(i == 0)
    def _():
        transpose_kv(kv_ref, turned, kv_ref.shape[0] // TILE)

    for h in range(KEY_VALUE_HEADS):
        pairs[h, :HEAD_SIZE, :] = heads_beside(query_ref, h)
        pairs[h, HEAD_SIZE:, :] = jnp.zeros((HEAD_SIZE, WIDE), bf16)
    tops[...] = jnp.full(tops.shape, masked_value, f32)
    totals[...] = jnp.zeros(totals.shape, f32)
    sums[...] = jnp.zeros(sums.shape, f32)

    def step(tile, allowed):
        rows = pl.ds(pl.multiple_of(tile * TILE, TILE), TILE)
        for h in range(KEY_VALUE_HEADS):
            scores = jnp.dot(
                kv_ref[rows, 128 * h : 128 * h + 128], pairs[h], preferred_element_type=f32
            )
            if allowed is not None:
                scores = jnp.where(allowed, scores, masked_value)
            top_old = tops[h]
            top = jnp.maximum(top_old, jnp.max(scores, axis=0, keepdims=True))
            weights = jnp.exp(scores - top)
            shrink = jnp.exp(top_old - top)
            tops[h] = top
            totals[h] = totals[h] * shrink + jnp.sum(weights, axis=0, keepdims=True)
            sums[h] = sums[h] * shrink + jnp.dot(
                turned[tile, 128 * h + HEAD_SIZE : 128 * h + 128, :],
                weights.astype(bf16),
                preferred_element_type=f32,
            )

    over_tiles(tile_range(starts_ref, fills_ref, block), block, step)
    for h in range(KEY_VALUE_HEADS):
        outcome = (sums[h] / totals[h]).astype(bf16)
        log_total = tops[h] + jnp.log(totals[h])
        for g in range(GROUPED):
            head = GROUPED * h + g
            mixed_ref[HEAD_SIZE * head : HEAD_SIZE * (head + 1), :] = outcome[:, BLK * g : BLK * (g + 1)]
            log_ref[head : head + 1, :] = log_total[:, BLK * g : BLK * (g + 1)]
    log_ref[QUERY_HEADS:, :] = jnp.zeros((1, BLK), f32)


def token_block(rows):
    return pl.BlockSpec((rows, BLK), lambda i, *_: (0, i))


def whole(shape):
    return pl.BlockSpec(shape, lambda i, *_: (0,) * len(shape))


def attention_forward(starts, fills, place, query, kv):
    group = kv.shape[0]
    return pl.pallas_call(
        attention_forward_kernel,
        grid_spec=pltpu.PrefetchScalarGridSpec(
            num_scalar_prefetch=3,
            grid=(TOK_DEV // BLK,),
            in_specs=[token_block(MODEL_WIDTH), whole((group, 2 * KV_WIDTH))],
            out_specs=[token_block(MODEL_WIDTH), token_block(16)],
            scratch_shapes=[
                pltpu.VMEM((group // TILE, 2 * KV_WIDTH, TILE), bf16),
                pltpu.VMEM((KEY_VALUE_HEADS, 2 * HEAD_SIZE, WIDE), bf16),
                pltpu.VMEM((KEY_VALUE_HEADS, 1, WIDE), f32),
                pltpu.VMEM((KEY_VALUE_HEADS, 1, WIDE), f32),
                pltpu.VMEM((KEY_VALUE_HEADS, HEAD_SIZE, WIDE), f32),
            ],
        ),
        out_shape=[
            jax.ShapeDtypeStruct((MODEL_WIDTH, TOK_DEV), bf16),
            jax.ShapeDtypeStruct((16, TOK_DEV), f32),
        ],
        name="attention_forward",
    )(starts, fills, place, query, kv)


def attention_backward_kernel(
    starts_ref,
    fills_ref,
    place_ref,
    query_ref,
    upstream_ref,
    mixed_ref,
    log_ref,
    cosine_ref,
    sine_ref,
    kv_ref,
    d_query_ref,
    d_kv_ref,
    turned,
    pairs,
    query_rows,
    upstream_rows,
    deltas,
    logs,
    sums,
    kv_sums,
):
    i = pl.program_id(0)
    block = place_ref[0] * (TOK_DEV // BLK) + i
    tiles = kv_ref.shape[0] // TILE

    @pl.when(i == 0)
    def _():
        transpose_kv(kv_ref, turned, tiles)

        def clear(t, carry):
            kv_sums[:, pl.ds(pl.multiple_of(t * TILE, TILE), TILE), :] = jnp.zeros(
                (KEY_VALUE_HEADS, TILE, 128), f32
            )
            return carry

        lax.fori_loop(0, tiles, clear, 0)

    blank = jnp.zeros((HEAD_SIZE, WIDE), bf16)
    for h in range(KEY_VALUE_HEADS):
        query = heads_beside(query_ref, h)
        upstream = heads_beside(upstream_ref, h)
        pairs[h, :HEAD_SIZE, :WIDE] = query
        pairs[h, HEAD_SIZE:, :WIDE] = blank
        pairs[h, :HEAD_SIZE, WIDE:] = blank
        pairs[h, HEAD_SIZE:, WIDE:] = upstream
        query_rows[h] = pairs[h, :, :WIDE].T
        upstream_rows[h] = pairs[h, :, WIDE:].T
        deltas[h] = jnp.sum(
            upstream.astype(f32) * heads_beside(mixed_ref, h).astype(f32), axis=0, keepdims=True
        )
        logs[h] = jnp.concatenate(
            [log_ref[GROUPED * h + g : GROUPED * h + g + 1, :] for g in range(GROUPED)], axis=1
        )
    sums[...] = jnp.zeros(sums.shape, f32)

    def step(tile, allowed):
        rows = pl.ds(pl.multiple_of(tile * TILE, TILE), TILE)
        for h in range(KEY_VALUE_HEADS):
            both = jnp.dot(
                kv_ref[rows, 128 * h : 128 * h + 128], pairs[h], preferred_element_type=f32
            )
            scores = both[:, :WIDE]
            if allowed is not None:
                scores = jnp.where(allowed, scores, masked_value)
            probs = jnp.exp(scores - logs[h])
            d_scores = (probs * (both[:, WIDE:] - deltas[h])).astype(bf16)
            kv_sums[h, rows, :] += jnp.dot(
                d_scores, query_rows[h], preferred_element_type=f32
            ) + jnp.dot(probs.astype(bf16), upstream_rows[h], preferred_element_type=f32)
            sums[h] += jnp.dot(
                turned[tile, 128 * h : 128 * h + HEAD_SIZE, :], d_scores, preferred_element_type=f32
            )

    over_tiles(tile_range(starts_ref, fills_ref, block), block, step)
    cosine = cosine_ref[...]
    sine = sine_ref[...]
    half = HEAD_SIZE // 2
    for h in range(KEY_VALUE_HEADS):
        for g in range(GROUPED):
            head = GROUPED * h + g
            front = sums[h, :half, BLK * g : BLK * (g + 1)] * score_scale
            back = sums[h, half:, BLK * g : BLK * (g + 1)] * score_scale
            d_query_ref[HEAD_SIZE * head : HEAD_SIZE * head + half, :] = (
                front * cosine + back * sine
            ).astype(bf16)
            d_query_ref[HEAD_SIZE * head + half : HEAD_SIZE * (head + 1), :] = (
                back * cosine - front * sine
            ).astype(bf16)

    @pl.when(i == pl.num_programs(0) - 1)
    def _():
        def emit(t, carry):
            rows = pl.ds(pl.multiple_of(t * TILE, TILE), TILE)
            for h in range(KEY_VALUE_HEADS):
                d_kv_ref[rows, 128 * h : 128 * h + 128] = kv_sums[h, rows, :].astype(bf16)
            return carry

        lax.fori_loop(0, tiles, emit, 0)


def attention_backward(starts, fills, place, query, upstream, mixed, logs, cosine, sine, kv):
    group = kv.shape[0]
    half = HEAD_SIZE // 2
    return pl.pallas_call(
        attention_backward_kernel,
        grid_spec=pltpu.PrefetchScalarGridSpec(
            num_scalar_prefetch=3,
            grid=(TOK_DEV // BLK,),
            in_specs=[
                token_block(MODEL_WIDTH),
                token_block(MODEL_WIDTH),
                token_block(MODEL_WIDTH),
                token_block(16),
                token_block(half),
                token_block(half),
                whole((group, 2 * KV_WIDTH)),
            ],
            out_specs=[token_block(MODEL_WIDTH), whole((group, 2 * KV_WIDTH))],
            scratch_shapes=[
                pltpu.VMEM((group // TILE, 2 * KV_WIDTH, TILE), bf16),
                pltpu.VMEM((KEY_VALUE_HEADS, 2 * HEAD_SIZE, 2 * WIDE), bf16),
                pltpu.VMEM((KEY_VALUE_HEADS, WIDE, 128), bf16),
                pltpu.VMEM((KEY_VALUE_HEADS, WIDE, 128), bf16),
                pltpu.VMEM((KEY_VALUE_HEADS, 1, WIDE), f32),
                pltpu.VMEM((KEY_VALUE_HEADS, 1, WIDE), f32),
                pltpu.VMEM((KEY_VALUE_HEADS, HEAD_SIZE, WIDE), f32),
                pltpu.VMEM((KEY_VALUE_HEADS, group, 128), f32),
            ],
        ),
        out_shape=[
            jax.ShapeDtypeStruct((MODEL_WIDTH, TOK_DEV), bf16),
            jax.ShapeDtypeStruct((group, 2 * KV_WIDTH), bf16),
        ],
        name="attention_backward",
    )(starts, fills, place, query, upstream, mixed, logs, cosine, sine, kv)


def dot_of(left, right, left_dim, right_dim):
    return lax.dot_general(
        left, right, (((left_dim,), (right_dim,)), ((), ())), preferred_element_type=f32
    )


SLOTS = 3
FORM = 640
PIECES = (240, 240, 160)
GAIN_LINE = 560
PAD_WIDTH = 1024
CHUNK = 640
CORE_BIT = ("shard", 1)
NEAR_BITS = (("shard", 2), ("dp", 1), ("dp", 2))
FAR_BITS = (("dp", 4),)


def stages(colour):
    return (CORE_BIT,) + NEAR_BITS[colour:] + NEAR_BITS[:colour] + FAR_BITS


def swap(value, bit):
    axis, mask = bit
    size = lax.axis_size(axis)
    return lax.ppermute(value, axis, [(i, i ^ mask) for i in range(size)])


def gather_colour(own, colour):
    held = own[None]
    for bit in reversed(stages(colour)[1:]):
        held = jnp.concatenate([held, swap(held, bit)], axis=0)
    return held, swap(held, CORE_BIT)


def scatter_colour(keep, send, colour):
    for bit in stages(colour):
        got = swap(send, bit)
        half = keep.shape[0] // 2
        if half == 0:
            return keep[0], got[0]
        send = keep[half:] + got[half:]
        keep = keep[:half] + got[:half]


def positions():
    device = jnp.arange(UNITS, dtype=jnp.int32)
    width = lax.axis_size("shard")
    apart = {
        "dp": (device // width) ^ lax.axis_index("dp").astype(jnp.int32),
        "shard": (device % width) ^ lax.axis_index("shard").astype(jnp.int32),
    }
    tables = []
    for colour in range(SLOTS):
        place = jnp.zeros((UNITS,), jnp.int32)
        for axis, mask in stages(colour):
            place = 2 * place + (apart[axis] & mask) // mask
        tables.append(place)
    return jnp.concatenate(tables)


def copy_from(halves, place, dst, sem, pick=lambda ref: ref):
    for number, ref in enumerate(halves):

        @pl.when(place // 16 == number)
        def _():
            pltpu.make_async_copy(pick(ref.at[lax.rem(place, 16)]), dst, sem).start()


def copy_to(src, halves, place, sem, pick=lambda ref: ref):
    for number, ref in enumerate(halves):

        @pl.when(place // 16 == number)
        def _():
            pltpu.make_async_copy(src, pick(ref.at[lax.rem(place, 16)]), sem).start()


def wait_for(ref, sem):
    pltpu.make_async_copy(ref, ref, sem).wait()


def form_attention_kernel(wide_ref, lines_ref, gains_ref, a_ref, b_ref, c_ref, mid, form):
    @pl.when(wide_ref[0] == 1)
    def _():
        def store(c, value):
            if c == 7:
                value = jnp.where(lane_low(80), value, 0.0)
            form[80 * c : 80 * c + 80, :] = value

        lines_to_rows_960(lines_ref, 0, 80, mid, store)

    @pl.when(wide_ref[0] == 0)
    def _():
        low = lane_low(120)
        line = [lines_ref[pl.ds(k, 120, stride=5), :] for k in range(5)]
        turned = [None, None] + [pltpu.roll(line[k], 64, 1) for k in range(2, 5)]
        form[pl.ds(0, 120, stride=2), :] = line[0]
        form[pl.ds(1, 120, stride=2), :] = jnp.where(low, turned[2], turned[3])
        form[pl.ds(240, 120, stride=2), :] = line[1]
        form[pl.ds(241, 120, stride=2), :] = jnp.where(low, turned[3], turned[4])
        mid[pl.ds(0, 120, stride=2), :] = line[2]
        mid[pl.ds(1, 120, stride=2), :] = turned[4]
        low = lane_low(80)
        form[480:560, :] = jnp.where(low, mid[0:80, :], pltpu.roll(mid[160:240, :], 64, 1))
        form[560:640, :] = jnp.where(low, mid[80:160, :], 0.0)

    form[GAIN_LINE : GAIN_LINE + 1, :] = jnp.where(
        lane_low(1), form[GAIN_LINE : GAIN_LINE + 1, :], gains_ref[...]
    )
    a_ref[...] = form[0:240, :].astype(bf16)
    b_ref[...] = form[240:480, :].astype(bf16)
    c_ref[...] = form[480:640, :].astype(bf16)


SMEM_SPEC = pl.BlockSpec(memory_space=pltpu.SMEM)
ANY_SPEC = pl.BlockSpec(memory_space=pl.ANY)


def form_attention(wide, lines, gains):
    return pl.pallas_call(
        form_attention_kernel,
        in_specs=[SMEM_SPEC, pl.BlockSpec((LINES, 128)), pl.BlockSpec((1, 128))],
        out_shape=[jax.ShapeDtypeStruct((n, 128), bf16) for n in PIECES],
        scratch_shapes=[pltpu.VMEM((240, 128), f32), pltpu.VMEM((FORM, 128), f32)],
        name="form_attention",
    )(wide, lines, gains)


def unform_attention_kernel(wide_ref, *refs):
    pieces, (lines_ref, gains_ref, mid, form) = refs[:6], refs[6:]
    base = 0
    for n, keep, got in zip(PIECES, pieces[0::2], pieces[1::2]):
        form[base : base + n, :] = keep[...].astype(f32) + got[...].astype(f32)
        base += n
    gains_ref[...] = form[GAIN_LINE : GAIN_LINE + 1, :]

    @pl.when(wide_ref[0] == 1)
    def _():
        rows_to_lines_960(lambda c: form[80 * c : 80 * c + 80, :], lines_ref, 0, 80, mid)

    @pl.when(wide_ref[0] == 0)
    def _():
        low = lane_low(120)
        mid[0:80, :] = form[480:560, :]
        mid[80:160, :] = form[560:640, :]
        mid[160:240, :] = pltpu.roll(form[480:560, :], 64, 1)
        even = [form[pl.ds(0, 120, stride=2), :], form[pl.ds(240, 120, stride=2), :]]
        odd = [form[pl.ds(1, 120, stride=2), :], form[pl.ds(241, 120, stride=2), :]]
        even.append(mid[pl.ds(0, 120, stride=2), :])
        odd.append(mid[pl.ds(1, 120, stride=2), :])
        odd = [pltpu.roll(value, 64, 1) for value in odd]
        lines_ref[pl.ds(0, 120, stride=5), :] = even[0]
        lines_ref[pl.ds(1, 120, stride=5), :] = even[1]
        lines_ref[pl.ds(2, 120, stride=5), :] = jnp.where(low, even[2], odd[0])
        lines_ref[pl.ds(3, 120, stride=5), :] = jnp.where(low, odd[0], odd[1])
        lines_ref[pl.ds(4, 120, stride=5), :] = jnp.where(low, odd[1], odd[2])


def unform_attention(wide, addends):
    return pl.pallas_call(
        unform_attention_kernel,
        in_specs=[SMEM_SPEC] + [pl.BlockSpec((n, 128)) for n in PIECES for _ in range(2)],
        out_shape=[jax.ShapeDtypeStruct((LINES, 128), f32), jax.ShapeDtypeStruct((1, 128), f32)],
        scratch_shapes=[pltpu.VMEM((240, 128), f32), pltpu.VMEM((FORM, 128), f32)],
        name="unform_attention",
    )(wide, *addends)


def wide_pieces(c):
    return [((80 * c + 16 * m) // 32, (80 * c + 16 * m) % 32, 16 * m) for m in range(5)]


def form_feedforward_kernel(narrow_ref, lines_ref, *refs):
    outs, mid = refs[:SLOTS], refs[SLOTS]
    for s, out in enumerate(outs):

        @pl.when(narrow_ref[s] == 1)
        def _():
            mid[30:32, :] = jnp.zeros((2, 128), f32)
            for c in range(20):
                mid[0:30, :] = lines_ref[pl.ds(LINES * s + c, 30, stride=20), :]
                out[c] = mid[0:32, :].astype(bf16)

        @pl.when(narrow_ref[s] == 0)
        def _():
            def store(c, value):
                if c == 7:
                    value = jnp.where(lane_low(80), value, 0.0)
                for k, r, m in wide_pieces(c):
                    out[k, r : r + 16, :] = value[m : m + 16].astype(bf16)

            lines_to_rows_960(lines_ref, LINES * s, 80, mid, store)


def form_feedforward(narrow, lines):
    return pl.pallas_call(
        form_feedforward_kernel,
        in_specs=[SMEM_SPEC, pl.BlockSpec((SLOTS * LINES, 128))],
        out_shape=[jax.ShapeDtypeStruct((20, 32, 128), bf16)] * SLOTS,
        scratch_shapes=[pltpu.VMEM((80, 128), f32)],
        name="form_feedforward",
    )(narrow, lines)


def unform_feedforward_kernel(narrow_ref, *refs):
    pieces, (lines_ref, mid) = refs[: 2 * SLOTS], refs[2 * SLOTS :]
    for s in range(SLOTS):
        keep, got = pieces[2 * s], pieces[2 * s + 1]

        @pl.when(narrow_ref[s] == 1)
        def _():
            for c in range(20):
                mid[0:32, :] = keep[c].astype(f32) + got[c].astype(f32)
                lines_ref[pl.ds(LINES * s + c, 30, stride=20), :] = mid[0:30, :]

        @pl.when(narrow_ref[s] == 0)
        def _():
            def load(c):
                return jnp.concatenate(
                    [
                        keep[k, r : r + 16, :].astype(f32) + got[k, r : r + 16, :].astype(f32)
                        for k, r, m in wide_pieces(c)
                    ],
                    axis=0,
                )

            rows_to_lines_960(load, lines_ref, LINES * s, 80, mid)


def unform_feedforward(narrow, addends):
    return pl.pallas_call(
        unform_feedforward_kernel,
        in_specs=[SMEM_SPEC] + [pl.BlockSpec((20, 32, 128))] * (2 * SLOTS),
        out_shape=jax.ShapeDtypeStruct((SLOTS * LINES, 128), f32),
        scratch_shapes=[pltpu.VMEM((80, 128), f32)],
        name="unform_feedforward",
    )(narrow, *addends)


def place_attention_kernel(table_ref, *refs):
    halves = [refs[2 * k : 2 * k + 2] for k in range(SLOTS)]
    query_ref, kv_ref, out_ref, gains_ref, units, sem = refs[2 * SLOTS :]

    def start(d, carry):
        base = 0
        for k, n in enumerate(PIECES):
            copy_from(halves[k], table_ref[UNITS * k + d], units.at[d, base : base + n, :], sem)
            base += n
        return carry

    lax.fori_loop(0, UNITS, start, 0)
    wait_for(units, sem)

    def wide(out, first):
        def body(u, carry):
            rows = pl.ds(pl.multiple_of(80 * u, 16), 80)
            for c in range(7):
                out[rows, 128 * c : 128 * c + 128] = units[first + u, 80 * c : 80 * c + 80, :]
            out[rows, 896:960] = units[first + u, 560:640, :64]
            return carry

        lax.fori_loop(0, 12, body, 0)

    def keyed(j, carry):
        low = lane_low(240)
        chunks = []
        for first in (12, 16):
            unit = units[first + j].astype(f32)
            last = jnp.concatenate(
                [unit[480:640], pltpu.roll(unit[480:560], 64, 1)], axis=0
            )
            lines = (unit[0:240], unit[240:480], last)
            chunks.append([(lines[h // 2], h % 2) for h in range(KEY_VALUE_HEADS)])
        rows = pl.ds(pl.multiple_of(240 * j, 16), 240)
        for h in range(KEY_VALUE_HEADS):
            kv_ref[rows, 128 * h : 128 * h + 128] = jnp.where(
                low, placed(chunks[0][h], 0), placed(chunks[1][h], 1)
            ).astype(bf16)
        return carry

    lax.fori_loop(0, 4, keyed, 0)
    wide(query_ref, 0)
    wide(out_ref, 20)
    for u in range(UNITS):
        gains_ref[u : u + 1, :] = units[u, GAIN_LINE : GAIN_LINE + 1, :].astype(f32)


def place_attention(table, gathered):
    return pl.pallas_call(
        place_attention_kernel,
        in_specs=[SMEM_SPEC] + [ANY_SPEC] * (2 * SLOTS),
        out_shape=[
            jax.ShapeDtypeStruct((MODEL_WIDTH, MODEL_WIDTH), bf16),
            jax.ShapeDtypeStruct((MODEL_WIDTH, 2 * KV_WIDTH), bf16),
            jax.ShapeDtypeStruct((MODEL_WIDTH, MODEL_WIDTH), bf16),
            jax.ShapeDtypeStruct((UNITS, 128), f32),
        ],
        scratch_shapes=[pltpu.VMEM((UNITS, FORM, 128), bf16), pltpu.SemaphoreType.DMA],
        name="place_attention",
    )(table, *gathered)


def split_attention_kernel(table_ref, query_ref, kv_ref, out_ref, gains_ref, *refs):
    halves = [refs[2 * k : 2 * k + 2] for k in range(SLOTS)]
    units, sem = refs[2 * SLOTS :]

    def send(d):
        row = lax.broadcasted_iota(jnp.int32, (16, 128), 0)
        lane = lax.broadcasted_iota(jnp.int32, (16, 128), 1)
        block = units[d, GAIN_LINE : GAIN_LINE + 16, :].astype(f32)
        units[d, GAIN_LINE : GAIN_LINE + 16, :] = jnp.where(
            jnp.logical_and(row == 0, lane >= 64), gains_ref[pl.ds(d, 1), :], block
        ).astype(bf16)
        base = 0
        for k, n in enumerate(PIECES):
            copy_to(units.at[d, base : base + n, :], halves[k], table_ref[UNITS * k + d], sem)
            base += n

    def wide(source, first):
        def body(u, carry):
            rows = pl.ds(pl.multiple_of(80 * u, 16), 80)
            for c in range(7):
                units[first + u, 80 * c : 80 * c + 80, :] = source[rows, 128 * c : 128 * c + 128]
            tail = source[rows, 896:960]
            units[first + u, 560:640, :] = jnp.concatenate([tail, jnp.zeros_like(tail)], axis=1)
            send(first + u)
            return carry

        lax.fori_loop(0, 12, body, 0)

    def keyed(j, carry):
        low = lane_low(240)
        rows = pl.ds(pl.multiple_of(240 * j, 16), 240)
        for upper, first in ((0, 12), (1, 16)):
            heads = [
                (kv_ref[rows, 128 * h : 128 * h + 128].astype(f32), upper)
                for h in range(KEY_VALUE_HEADS)
            ]
            for c in range(2):
                units[first + j, 240 * c : 240 * c + 240, :] = jnp.where(
                    low, placed(heads[2 * c], 0), placed(heads[2 * c + 1], 1)
                ).astype(bf16)
            last = placed(heads[4], 0)
            turned = placed(heads[4], 1)
            units[first + j, 480:560, :] = jnp.where(
                lane_low(80), last[0:80], turned[160:240]
            ).astype(bf16)
            units[first + j, 560:640, :] = jnp.where(lane_low(80), last[80:160], 0.0).astype(bf16)
            send(first + j)
        return carry

    lax.fori_loop(0, 4, keyed, 0)
    wide(query_ref, 0)
    wide(out_ref, 20)
    wait_for(units, sem)


def split_attention(table, d_query, d_kv, d_out, gains):
    return pl.pallas_call(
        split_attention_kernel,
        in_specs=[
            SMEM_SPEC,
            pl.BlockSpec((MODEL_WIDTH, MODEL_WIDTH)),
            pl.BlockSpec((MODEL_WIDTH, 2 * KV_WIDTH)),
            pl.BlockSpec((MODEL_WIDTH, MODEL_WIDTH)),
            pl.BlockSpec((UNITS, 128)),
        ],
        out_specs=[ANY_SPEC] * (2 * SLOTS),
        out_shape=[jax.ShapeDtypeStruct((16, n, 128), bf16) for n in PIECES for _ in range(2)],
        scratch_shapes=[pltpu.VMEM((UNITS, FORM, 128), bf16), pltpu.SemaphoreType.DMA],
        name="split_attention",
    )(table, d_query, d_kv, d_out, gains)


def feedforward_kernel(table_ref, hidden_ref, turned_ref, grad_ref, *refs):
    sources = [refs[2 * s : 2 * s + 2] for s in range(SLOTS)]
    out_ref, d_hidden_ref = refs[6:8]
    targets = [refs[8 + 2 * s : 10 + 2 * s] for s in range(SLOTS)]
    (
        both_in,
        down_in,
        down,
        inner_rows,
        inner_turned,
        d_both,
        both_out,
        down_out,
        in_sem,
        out_sem,
    ) = refs[14:]
    q = pl.program_id(0)
    chunks = pl.num_programs(0)
    slot = lax.rem(q, 2)

    def narrow_units(move, chunk, buffer):
        columns = lambda ref: ref.at[pl.ds(5 * chunk, 5)]
        for u in range(2 * UNITS):
            device, s = divmod(u, SLOTS)
            piece = buffer.at[pl.ds(5 * (u // UNITS), 5), pl.ds(32 * (u % UNITS), 32), :]
            move(s, table_ref[UNITS * s + device], piece, columns)

    def down_units(move, chunk, buffer):
        for v in range(8):
            unit = 2 * UNITS + 8 * chunk + v
            device = unit // SLOTS
            for s in range(SLOTS):

                @pl.when(unit - SLOTS * device == s)
                def _():
                    move(s, table_ref[UNITS * s + device], buffer.at[v], lambda ref: ref)

    def start_in(chunk, carry):
        side = lax.rem(chunk, 2)
        narrow_units(
            lambda s, place, piece, pick: copy_from(
                sources[s], place, piece, in_sem.at[side, 0], pick
            ),
            chunk,
            both_in.at[side],
        )
        down_units(
            lambda s, place, piece, pick: copy_from(
                sources[s], place, piece, in_sem.at[side, 1], pick
            ),
            chunk,
            down_in.at[side],
        )
        return carry

    lax.fori_loop(jnp.where(q == 0, 0, q + 1), jnp.minimum(q + 2, chunks), start_in, 0)
    wait_for(both_in.at[slot], in_sem.at[slot, 0])
    wait_for(down_in.at[slot], in_sem.at[slot, 1])

    for v in range(8):
        for c in range(8):
            for k, r, m in wide_pieces(c):
                down[80 * v + m : 80 * v + m + 16, 128 * c : 128 * c + 128] = down_in[
                    slot, v, k, r : r + 16, :
                ]

    @pl.when(q == 0)
    def _():
        out_ref[...] = jnp.zeros(out_ref.shape, f32)
        d_hidden_ref[...] = jnp.zeros(d_hidden_ref.shape, f32)

    def rows_step(i, carry):
        rows = pl.ds(pl.multiple_of(256 * i, 256), 256)
        weights = jnp.concatenate([both_in[slot, c] for c in range(10)], axis=1)
        both = jnp.dot(hidden_ref[rows, :], weights, preferred_element_type=f32)
        gate, upper = both[:, :CHUNK], both[:, CHUNK:]
        sigmoid_gate = jax.nn.sigmoid(gate)
        activated = gate * sigmoid_gate
        inner = (activated * upper).astype(bf16)
        inner_rows[rows, :] = inner
        out_ref[rows, :] += jnp.dot(inner, down[...], preferred_element_type=f32)
        d_inner = dot_of(grad_ref[rows, :], down[...], 1, 1)
        d_gate = d_inner * upper * sigmoid_gate * (1.0 + gate * (1.0 - sigmoid_gate))
        d_upper = d_inner * activated
        d_pair = jnp.concatenate([d_gate, d_upper], axis=1).astype(bf16)
        d_both[rows, :] = d_pair
        d_hidden_ref[rows, :] += dot_of(d_pair, weights, 1, 1)
        return carry

    lax.fori_loop(0, 2, rows_step, 0)
    inner_turned[...] = inner_rows[...].T

    @pl.when(q >= 2)
    def _():
        wait_for(both_out.at[slot], out_sem.at[slot, 0])
        wait_for(down_out.at[slot], out_sem.at[slot, 1])

    def both_step(i, carry):
        rows = pl.ds(pl.multiple_of(256 * i, 256), 256)
        terms = jnp.dot(turned_ref[rows, :], d_both[...], preferred_element_type=f32)
        for c in range(10):
            both_out[slot, c, rows, :] = terms[:, 128 * c : 128 * c + 128].astype(bf16)
        return carry

    lax.fori_loop(0, 4, both_step, 0)

    def down_step(i, carry):
        rows = pl.ds(pl.multiple_of(320 * i, 16), 320)
        terms = jnp.dot(
            inner_turned[rows, :], grad_ref[...], preferred_element_type=f32
        ).astype(bf16)
        for v in range(4):
            for c in range(8):
                for k, r, m in wide_pieces(c):
                    down_out[slot, 4 * i + v, k, r : r + 16, :] = terms[
                        80 * v + m : 80 * v + m + 16, 128 * c : 128 * c + 128
                    ]
        return carry

    lax.fori_loop(0, 2, down_step, 0)
    narrow_units(
        lambda s, place, piece, pick: copy_to(
            piece, targets[s], place, out_sem.at[slot, 0], pick
        ),
        q,
        both_out.at[slot],
    )
    down_units(
        lambda s, place, piece, pick: copy_to(
            piece, targets[s], place, out_sem.at[slot, 1], pick
        ),
        q,
        down_out.at[slot],
    )

    @pl.when(q == chunks - 1)
    def _():
        for side in range(2):
            wait_for(both_out.at[side], out_sem.at[side, 0])
            wait_for(down_out.at[side], out_sem.at[side, 1])


def feedforward(table, hidden, turned, grad, gathered):
    block = jax.ShapeDtypeStruct((16, 20, 32, 128), bf16)
    full = lambda shape: pl.BlockSpec(shape, lambda q: (0, 0))
    return pl.pallas_call(
        feedforward_kernel,
        grid=(FF // CHUNK,),
        in_specs=[
            SMEM_SPEC,
            full((TOK_DEV, PAD_WIDTH)),
            full((PAD_WIDTH, TOK_DEV)),
            full((TOK_DEV, PAD_WIDTH)),
        ]
        + [ANY_SPEC] * (2 * SLOTS),
        out_specs=[full((TOK_DEV, PAD_WIDTH))] * 2 + [ANY_SPEC] * (2 * SLOTS),
        out_shape=[jax.ShapeDtypeStruct((TOK_DEV, PAD_WIDTH), f32)] * 2 + [block] * (2 * SLOTS),
        scratch_shapes=[
            pltpu.VMEM((2, 10, PAD_WIDTH, 128), bf16),
            pltpu.VMEM((2, 8, 20, 32, 128), bf16),
            pltpu.VMEM((CHUNK, PAD_WIDTH), bf16),
            pltpu.VMEM((TOK_DEV, CHUNK), bf16),
            pltpu.VMEM((CHUNK, TOK_DEV), bf16),
            pltpu.VMEM((TOK_DEV, 2 * CHUNK), bf16),
            pltpu.VMEM((2, 10, PAD_WIDTH, 128), bf16),
            pltpu.VMEM((2, 8, 20, 32, 128), bf16),
            pltpu.SemaphoreType.DMA((2, 2)),
            pltpu.SemaphoreType.DMA((2, 2)),
        ],
        compiler_params=pltpu.CompilerParams(vmem_limit_bytes=60 * 2**20),
        name="feedforward",
    )(table, hidden, turned, grad, *gathered)


def spread_matrix():
    column = jnp.arange(PAD_WIDTH, dtype=jnp.int32)
    entry = jnp.where(column % 32 < 30, 30 * (column // 32) + column % 32, -1)
    return (jnp.arange(MODEL_WIDTH, dtype=jnp.int32)[:, None] == entry[None, :]).astype(bf16)


def rope_tables(positions):
    steps = jnp.arange(HEAD_SIZE // 2, dtype=f32) * (2.0 / HEAD_SIZE)
    inverse = jnp.exp(-math.log(10000.0) * steps)
    angles = inverse[:, None] * positions.astype(f32)[None, :]
    return (jnp.cos(angles), jnp.sin(angles))


def norm_scale(field):
    return lax.rsqrt(jnp.mean(field * field, axis=1, keepdims=True) + epsilon)


def norm_back(upstream, normed, scale, gain):
    scaled = upstream * gain[None, :]
    return scale * (scaled - normed * jnp.mean(scaled * normed, axis=1, keepdims=True))


def adam_step(grad, moment, second, master):
    moment_new = 0.9 * moment + 0.1 * grad
    second_new = 0.999 * second + 0.001 * grad * grad
    corrected = moment_new / (1.0 - 0.9**ADAM_STEP)
    scaled = second_new / (1.0 - 0.999**ADAM_STEP)
    update = -learning_rate * (corrected / (jnp.sqrt(scaled) + 1e-08) + weight_decay * master)
    return (moment_new, second_new, update)


def gather_lines(block):
    return lax.all_gather(block, ALL_AXES, axis=0, tiled=True)


def scatter_lines(lines):
    return lax.psum_scatter(lines, ALL_AXES, scatter_dimension=0, tiled=True)


def local(
    layer_input,
    cotangent,
    master_attention,
    master_feedforward,
    master_gains,
    first_attention,
    second_attention,
    first_feedforward,
    second_feedforward,
    first_gains,
    second_gains,
    block_start,
    block_fill,
):
    devices = lax.axis_size(ALL_AXES)
    attention_lines = master_attention.shape[0] // 128
    feedforward_lines = master_feedforward.shape[0] // 128
    gain_count = master_gains.shape[0]
    padded = (attention_lines // 16 + 1) * 16

    in_units = devices == UNITS
    if in_units:
        table = positions()
        device = (
            lax.axis_index("dp") * lax.axis_size("shard") + lax.axis_index("shard")
        ).astype(jnp.int32)
        wide = jnp.logical_or(device < 12, device >= 20).astype(jnp.int32)[None]
        narrow = (SLOTS * device + jnp.arange(SLOTS, dtype=jnp.int32) < 2 * UNITS).astype(jnp.int32)
        gain_row = jnp.pad(
            master_gains.reshape(1, gain_count), ((0, 0), (64, 64 - gain_count))
        )
        pieces = form_attention(wide, master_attention.reshape(LINES, 128), gain_row)
        gathered = [half for k in range(SLOTS) for half in gather_colour(pieces[k], k)]
        forms = form_feedforward(narrow, master_feedforward.reshape(SLOTS * LINES, 128))
        feedforward_all = [half for k in range(SLOTS) for half in gather_colour(forms[k], k)]
        query_weight, kv_weight, out_weight, gain_rows = place_attention(table, gathered)
        gains_all = gain_rows[:, 64 : 64 + gain_count].reshape(-1)
    else:
        gain_lines = jnp.pad(
            master_gains.astype(bf16).reshape(1, gain_count),
            ((0, padded - attention_lines - 1), (0, 128 - gain_count)),
        )
        attention_block = jnp.concatenate(
            [master_attention.astype(bf16).reshape(attention_lines, 128), gain_lines], axis=0
        )
        by_device = gather_lines(attention_block).reshape(devices, padded, 128)
        feedforward_all = gather_lines(
            master_feedforward.astype(bf16).reshape(feedforward_lines, 128)
        )
        gains_all = by_device[:, attention_lines, :gain_count].reshape(-1).astype(f32)
        units = by_device[:, :attention_lines].reshape(UNITS, LINES, 128)
        query_weight = unpack_wide(units, 0)
        kv_weight = unpack_kv(units)
        out_weight = unpack_wide(units, 20)
    gain_one, gain_two = gains_all[:MODEL_WIDTH], gains_all[MODEL_WIDTH:]

    shard = lax.axis_index("shard").astype(jnp.int32)
    place = shard[None]
    first_row = shard * TOK_DEV
    first_block = shard * (TOK_DEV // BLK)
    local_slots = first_row + jnp.arange(TOK_DEV, dtype=jnp.int32)
    local_starts = lax.dynamic_slice_in_dim(block_start, first_block, TOK_DEV // BLK)
    local_fills = lax.dynamic_slice_in_dim(block_fill, first_block, TOK_DEV // BLK)
    live_rows = local_slots % BLK < jnp.repeat(local_fills, BLK)
    cosine_table, sine_table = rope_tables(local_slots - jnp.repeat(local_starts, BLK) * BLK)

    def rotate(field, scale):
        heads = field.shape[0]
        front = field[:, : HEAD_SIZE // 2]
        back = field[:, HEAD_SIZE // 2 :]
        return (
            jnp.concatenate(
                [
                    front * cosine_table[None] - back * sine_table[None],
                    back * cosine_table[None] + front * sine_table[None],
                ],
                axis=1,
            ).astype(bf16)
            * bf16(scale)
        ).reshape(heads * HEAD_SIZE, TOK_DEV)

    inputs = layer_input.astype(f32)
    scale_one = norm_scale(inputs)
    normed_one = inputs * scale_one
    first_hidden = (normed_one * gain_one[None, :]).astype(bf16)
    kv_turned = dot_of(kv_weight, first_hidden, 0, 1).reshape(
        KEY_VALUE_HEADS, 2, HEAD_SIZE, TOK_DEV
    )
    keys = rotate(kv_turned[:, 0], 1.0).reshape(KEY_VALUE_HEADS, 1, HEAD_SIZE, TOK_DEV)
    values = kv_turned[:, 1:].astype(bf16)
    kv_rows = jnp.concatenate([keys, values], axis=1).reshape(2 * KV_WIDTH, TOK_DEV).T
    kv_all = lax.all_gather(kv_rows, "shard", axis=0, tiled=True)
    query_turned = rotate(
        dot_of(query_weight, first_hidden, 0, 1).reshape(QUERY_HEADS, HEAD_SIZE, TOK_DEV),
        score_scale,
    )
    mixed_turned, logs = attention_forward(block_start, block_fill, place, query_turned, kv_all)
    middle = inputs + dot_of(mixed_turned, out_weight, 0, 0)
    scale_two = norm_scale(middle)
    normed_two = middle * scale_two
    hidden_two = (normed_two * gain_two[None, :]).astype(bf16)

    grad_out = cotangent.astype(f32) * live_rows[:, None].astype(f32)
    grad_low = grad_out.astype(bf16)
    if in_units:
        spread = spread_matrix()
        outcome, d_spread, *ff_terms = feedforward(
            table,
            dot_of(hidden_two, spread, 1, 0).astype(bf16),
            dot_of(spread, hidden_two, 0, 1).astype(bf16),
            jnp.pad(grad_low, ((0, 0), (0, PAD_WIDTH - MODEL_WIDTH))),
            feedforward_all,
        )
        layer_output = middle + outcome[:, :MODEL_WIDTH]
        d_coarse = lax.reduce_precision(d_spread, 8, 7)
        d_hidden_two = dot_of(d_coarse.astype(bf16), spread, 1, 1) + dot_of(
            (d_spread - d_coarse).astype(bf16), spread, 1, 1
        )
        ff_addends = [
            addend
            for k in range(SLOTS)
            for addend in scatter_colour(ff_terms[2 * k], ff_terms[2 * k + 1], k)
        ]
        feedforward_gradient = unform_feedforward(narrow, ff_addends).reshape(-1)
    else:
        gate_weight, up_weight, down_weight = unpack_ff(feedforward_all)
        gate = dot_of(hidden_two, gate_weight, 1, 0)
        upper = dot_of(hidden_two, up_weight, 1, 0)
        sigmoid_gate = jax.nn.sigmoid(gate)
        activated = gate * sigmoid_gate
        inner = (activated * upper).astype(bf16)
        layer_output = middle + dot_of(inner, down_weight, 1, 0)
        d_down_weight = dot_of(inner, grad_low, 0, 0).astype(bf16)
        d_inner = dot_of(grad_low, down_weight, 1, 1)
        d_gate = (
            d_inner * upper * sigmoid_gate * (1.0 + gate * (1.0 - sigmoid_gate))
        ).astype(bf16)
        d_upper = (d_inner * activated).astype(bf16)
        d_gate_weight = dot_of(hidden_two, d_gate, 0, 0).astype(bf16)
        d_up_weight = dot_of(hidden_two, d_upper, 0, 0).astype(bf16)
        d_hidden_two = dot_of(d_gate, gate_weight, 1, 1) + dot_of(d_upper, up_weight, 1, 1)
        feedforward_gradient = (
            scatter_lines(pack_ff(d_gate_weight, d_up_weight, d_down_weight))
            .astype(f32)
            .reshape(-1)
        )

    d_gain_two = jnp.sum(d_hidden_two * normed_two, axis=0)
    d_middle = grad_out + norm_back(d_hidden_two, normed_two, scale_two, gain_two)

    d_branch = d_middle.astype(bf16)
    d_out_weight = dot_of(mixed_turned, d_branch, 1, 0).astype(bf16)
    d_mixed = dot_of(out_weight, d_branch, 1, 1).astype(bf16)
    d_query, d_kv = attention_backward(
        block_start,
        block_fill,
        place,
        query_turned,
        d_mixed,
        mixed_turned,
        logs,
        cosine_table,
        sine_table,
        kv_all,
    )
    d_kv_rows = lax.psum_scatter(d_kv, "shard", scatter_dimension=0, tiled=True)
    d_kv_turned = d_kv_rows.T.reshape(KEY_VALUE_HEADS, 2, HEAD_SIZE, TOK_DEV)
    d_front = d_kv_turned[:, 0, : HEAD_SIZE // 2].astype(f32)
    d_back = d_kv_turned[:, 0, HEAD_SIZE // 2 :].astype(f32)
    d_keys = jnp.concatenate(
        [
            d_front * cosine_table[None] + d_back * sine_table[None],
            d_back * cosine_table[None] - d_front * sine_table[None],
        ],
        axis=1,
    ).astype(bf16)
    d_kv_lin = jnp.concatenate([d_keys[:, None], d_kv_turned[:, 1:]], axis=1).reshape(
        2 * KV_WIDTH, TOK_DEV
    )
    d_query_weight = dot_of(first_hidden, d_query, 0, 1).astype(bf16)
    d_kv_weight = dot_of(first_hidden, d_kv_lin, 0, 1).astype(bf16)
    d_hidden_one = dot_of(d_query, query_weight, 0, 1) + dot_of(d_kv_lin, kv_weight, 0, 1)
    d_gain_one = jnp.sum(d_hidden_one * normed_one, axis=0)
    input_gradient = d_middle + norm_back(d_hidden_one, normed_one, scale_one, gain_one)

    gain_terms = jnp.concatenate([d_gain_one, d_gain_two])
    if in_units:
        gain_rows = jnp.pad(
            gain_terms.reshape(UNITS, gain_count), ((0, 0), (64, 64 - gain_count))
        )
        terms = split_attention(table, d_query_weight, d_kv_weight, d_out_weight, gain_rows)
        addends = [
            addend
            for k in range(SLOTS)
            for addend in scatter_colour(terms[2 * k], terms[2 * k + 1], k)
        ]
        attention_sum, gain_sum = unform_attention(wide, addends)
        attention_gradient = attention_sum.reshape(-1)
        gains_gradient = gain_sum[0, 64 : 64 + gain_count]
    else:
        no_gains = jnp.zeros((UNITS, GAIN_LINES, 128), bf16)
        terms = pack_attention(d_query_weight, d_kv_weight, d_out_weight, no_gains)
        terms = jnp.concatenate(
            [
                terms[:, :LINES].reshape(devices, attention_lines, 128),
                jnp.pad(
                    gain_terms.astype(bf16).reshape(devices, 1, gain_count),
                    ((0, 0), (0, padded - attention_lines - 1), (0, 128 - gain_count)),
                ),
            ],
            axis=1,
        )
        summed = scatter_lines(terms.reshape(devices * padded, 128)).astype(f32)
        attention_gradient = summed[:attention_lines].reshape(-1)
        gains_gradient = summed[attention_lines, :gain_count]

    attention_first, attention_second, attention_update = adam_step(
        attention_gradient, first_attention, second_attention, master_attention
    )
    feedforward_first, feedforward_second, feedforward_update = adam_step(
        feedforward_gradient, first_feedforward, second_feedforward, master_feedforward
    )
    gains_first, gains_second, gains_update = adam_step(
        gains_gradient, first_gains, second_gains, master_gains
    )
    return (
        layer_output,
        input_gradient,
        attention_gradient,
        feedforward_gradient,
        gains_gradient,
        attention_first,
        attention_second,
        feedforward_first,
        feedforward_second,
        gains_first,
        gains_second,
        attention_update,
        feedforward_update,
        gains_update,
    )


def solution(mesh):
    rows = P(ALL_AXES, None)
    flat = P(ALL_AXES)
    return jax.shard_map(
        local,
        mesh=mesh,
        in_specs=(rows, rows) + (flat,) * 9 + (P("dp"), P("dp")),
        out_specs=(rows, rows) + (flat,) * 12,
        check_vma=False,
    )
```

```python
import functools
import math

import jax
import jax.numpy as jnp
from jax import lax
from jax.experimental import pallas as pl
from jax.experimental.pallas import tpu as pltpu
from jax.sharding import PartitionSpec as P

MODEL_WIDTH = 960
QUERY_HEADS = 15
KEY_VALUE_HEADS = 5
GROUPED = QUERY_HEADS // KEY_VALUE_HEADS
HEAD_SIZE = 64
FF = 2560
BLK = 128
ADAM_STEP = 10
TOK_DEV = 512
KV_WIDTH = KEY_VALUE_HEADS * HEAD_SIZE
TILE = 256
WIDE = GROUPED * BLK
UNITS = 32
LINES = 600
GAIN_LINES = 8
ALL_AXES = ("dp", "shard")

epsilon = 1e-05
masked_value = -1e30
learning_rate = 0.03
weight_decay = 0.1
score_scale = 1.0 / math.sqrt(HEAD_SIZE)
f32 = jnp.float32
bf16 = jnp.bfloat16


def lines_to_rows_2560(scratch, base, rows, store):
    for c in range(20):
        store(c, scratch[pl.ds(base + c, rows, stride=20), :])


def rows_to_lines_2560(load, scratch, base, rows):
    for c in range(20):
        scratch[pl.ds(base + c, rows, stride=20), :] = load(c)


def lane_low(rows):
    return lax.broadcasted_iota(jnp.int32, (rows, 128), 1) < 64


def lines_to_rows_960(scratch, base, rows, mid, store):
    half = rows // 2
    low = lane_low(half)
    line = [scratch[pl.ds(base + k, half, stride=15), :] for k in range(15)]
    turned = [None] * 7 + [pltpu.roll(line[k], 64, 1) for k in range(7, 15)]
    for c in range(8):
        mid[pl.ds(0, half, stride=2), :] = line[c]
        odd = jnp.where(low, turned[7 + c], turned[8 + c]) if c < 7 else turned[14]
        mid[pl.ds(1, half, stride=2), :] = odd
        store(c, mid[pl.ds(0, rows), :])


def rows_to_lines_960(load, scratch, base, rows, mid):
    half = rows // 2
    low = lane_low(half)
    odds = []
    for c in range(8):
        mid[pl.ds(0, rows), :] = load(c)
        even = mid[pl.ds(0, half, stride=2), :]
        odd = pltpu.roll(mid[pl.ds(1, half, stride=2), :], 64, 1)
        odds.append(odd)
        if c < 7:
            scratch[pl.ds(base + c, half, stride=15), :] = even
        else:
            scratch[pl.ds(base + 7, half, stride=15), :] = jnp.where(low, even, odds[0])
        if c > 0:
            scratch[pl.ds(base + 7 + c, half, stride=15), :] = jnp.where(low, odds[c - 1], odd)


def half_chunks(lines):
    even = [(lines[0], 0), (lines[0], 1), (lines[1], 0), (lines[1], 1), (lines[2], 0)]
    odd = [(lines[2], 1), (lines[3], 0), (lines[3], 1), (lines[4], 0), (lines[4], 1)]
    return even, odd


def placed(chunk, upper):
    line, side = chunk
    return line if side == upper else pltpu.roll(line, 64, 1)


def unpack_ff_kernel(lines_ref, gate_ref, up_ref, down_ref, scratch, mid):
    phase = pl.program_id(0)
    scratch[...] = lines_ref[...].astype(f32)
    for number, out in ((0, gate_ref), (1, up_ref)):

        @pl.when(phase == number)
        def _():
            def store(c, value):
                out[:, 128 * c : 128 * c + 128] = value.astype(bf16)

            lines_to_rows_2560(scratch, 0, 96, store)

    @pl.when(phase == 2)
    def _():
        def store(c, value):
            if c < 7:
                down_ref[:, 128 * c : 128 * c + 128] = value.astype(bf16)
            else:
                down_ref[:, 896:960] = value[:, :64].astype(bf16)

        lines_to_rows_960(scratch, 0, 256, mid, store)


def pinned(phase):
    def index(p, j):
        return (jnp.where(p == phase, j, jnp.where(p < phase, 0, 9)), 0)

    return index


def unpack_ff(lines):
    return pl.pallas_call(
        unpack_ff_kernel,
        grid=(3, 10),
        in_specs=[pl.BlockSpec((1920, 128), lambda p, j: (p * 10 + j, 0))],
        out_specs=[
            pl.BlockSpec((96, FF), pinned(0)),
            pl.BlockSpec((96, FF), pinned(1)),
            pl.BlockSpec((256, MODEL_WIDTH), pinned(2)),
        ],
        out_shape=[
            jax.ShapeDtypeStruct((MODEL_WIDTH, FF), bf16),
            jax.ShapeDtypeStruct((MODEL_WIDTH, FF), bf16),
            jax.ShapeDtypeStruct((FF, MODEL_WIDTH), bf16),
        ],
        scratch_shapes=[pltpu.VMEM((1920, 128), f32), pltpu.VMEM((256, 128), f32)],
        name="unpack_feedforward",
    )(lines)


def pack_ff_kernel(gate_ref, up_ref, down_ref, lines_ref, scratch, mid):
    phase = pl.program_id(0)
    for number, source in ((0, gate_ref), (1, up_ref)):

        @pl.when(phase == number)
        def _():
            rows_to_lines_2560(
                lambda c: source[:, 128 * c : 128 * c + 128].astype(f32), scratch, 0, 96
            )

    @pl.when(phase == 2)
    def _():
        def load(c):
            if c < 7:
                return down_ref[:, 128 * c : 128 * c + 128].astype(f32)
            tail = down_ref[:, 896:960].astype(f32)
            return jnp.concatenate([tail, tail], axis=1)

        rows_to_lines_960(load, scratch, 0, 256, mid)

    lines_ref[...] = scratch[...].astype(bf16)


def pack_ff(gate, up, down):
    return pl.pallas_call(
        pack_ff_kernel,
        grid=(3, 10),
        in_specs=[
            pl.BlockSpec((96, FF), pinned(0)),
            pl.BlockSpec((96, FF), pinned(1)),
            pl.BlockSpec((256, MODEL_WIDTH), pinned(2)),
        ],
        out_specs=pl.BlockSpec((1920, 128), lambda p, j: (p * 10 + j, 0)),
        out_shape=jax.ShapeDtypeStruct((3 * 19200, 128), bf16),
        scratch_shapes=[pltpu.VMEM((1920, 128), f32), pltpu.VMEM((256, 128), f32)],
        name="pack_feedforward",
    )(gate, up, down)


def unpack_wide_kernel(lines_ref, out_ref, scratch, mid):
    for u in range(4):
        scratch[...] = lines_ref[u].astype(f32)
        base = u * 80

        def store(c, value):
            if c < 7:
                out_ref[base : base + 80, 128 * c : 128 * c + 128] = value.astype(bf16)
            else:
                out_ref[base : base + 80, 896:960] = value[:, :64].astype(bf16)

        lines_to_rows_960(scratch, 0, 80, mid, store)


def unpack_wide(lines, first):
    depth = lines.shape[1]
    return pl.pallas_call(
        unpack_wide_kernel,
        grid=(3,),
        in_specs=[pl.BlockSpec((4, depth, 128), lambda j: (first // 4 + j, 0, 0))],
        out_specs=pl.BlockSpec((320, MODEL_WIDTH), lambda j: (j, 0)),
        out_shape=jax.ShapeDtypeStruct((MODEL_WIDTH, MODEL_WIDTH), bf16),
        scratch_shapes=[pltpu.VMEM((depth, 128), f32), pltpu.VMEM((80, 128), f32)],
        name="unpack_attention",
    )(lines)


def unpack_kv_kernel(key_ref, value_ref, out_ref, key_lines, value_lines, mid):
    low = lane_low(120)
    key_lines[...] = key_ref[0].astype(f32)
    value_lines[...] = value_ref[0].astype(f32)
    keys = half_chunks([key_lines[pl.ds(k, 120, stride=5), :] for k in range(5)])
    values = half_chunks([value_lines[pl.ds(k, 120, stride=5), :] for k in range(5)])
    for h in range(KEY_VALUE_HEADS):
        for parity in range(2):
            mid[pl.ds(parity, 120, stride=2), :] = jnp.where(
                low, placed(keys[parity][h], 0), placed(values[parity][h], 1)
            )
        out_ref[:, 128 * h : 128 * h + 128] = mid[...].astype(bf16)


def unpack_kv(lines):
    depth = lines.shape[1]
    return pl.pallas_call(
        unpack_kv_kernel,
        grid=(4,),
        in_specs=[
            pl.BlockSpec((1, depth, 128), lambda j: (12 + j, 0, 0)),
            pl.BlockSpec((1, depth, 128), lambda j: (16 + j, 0, 0)),
        ],
        out_specs=pl.BlockSpec((240, 2 * KV_WIDTH), lambda j: (j, 0)),
        out_shape=jax.ShapeDtypeStruct((MODEL_WIDTH, 2 * KV_WIDTH), bf16),
        scratch_shapes=[
            pltpu.VMEM((depth, 128), f32),
            pltpu.VMEM((depth, 128), f32),
            pltpu.VMEM((240, 128), f32),
        ],
        name="unpack_key_value",
    )(lines, lines)


def pack_attention_kernel(query_ref, kv_ref, out_weight_ref, gains_ref, lines_ref, scratch, mid):
    step = pl.program_id(0)

    def wide(source):
        for u in range(4):
            base = u * 80

            def load(c):
                if c < 7:
                    return source[base : base + 80, 128 * c : 128 * c + 128].astype(f32)
                tail = source[base : base + 80, 896:960].astype(f32)
                return jnp.concatenate([tail, tail], axis=1)

            rows_to_lines_960(load, scratch, 0, 80, mid)
            lines_ref[u, :LINES, :] = scratch[...].astype(bf16)

    @pl.when(step < 3)
    def _():
        wide(query_ref)

    @pl.when(step >= 5)
    def _():
        wide(out_weight_ref)

    for number, upper in ((3, 0), (4, 1)):

        @pl.when(step == number)
        def _():
            low = lane_low(120)
            for u in range(4):
                evens, odds = [], []
                for h in range(KEY_VALUE_HEADS):
                    mid[...] = kv_ref[
                        240 * u : 240 * u + 240, 128 * h : 128 * h + 128
                    ].astype(f32)
                    evens.append((mid[pl.ds(0, 120, stride=2), :], upper))
                    odds.append((mid[pl.ds(1, 120, stride=2), :], upper))
                run = evens + odds
                for k in range(5):
                    scratch[pl.ds(k, 120, stride=5), :] = jnp.where(
                        low, placed(run[2 * k], 0), placed(run[2 * k + 1], 1)
                    )
                lines_ref[u, :LINES, :] = scratch[...].astype(bf16)

    for u in range(4):
        lines_ref[u, LINES:, :] = gains_ref[u]


def pack_attention(d_query, d_kv, d_out, gains):
    return pl.pallas_call(
        pack_attention_kernel,
        grid=(8,),
        in_specs=[
            pl.BlockSpec((320, MODEL_WIDTH), lambda s: (jnp.minimum(s, 2), 0)),
            pl.BlockSpec((MODEL_WIDTH, 2 * KV_WIDTH), lambda s: (0, 0)),
            pl.BlockSpec((320, MODEL_WIDTH), lambda s: (jnp.maximum(s - 5, 0), 0)),
            pl.BlockSpec((4, GAIN_LINES, 128), lambda s: (s, 0, 0)),
        ],
        out_specs=pl.BlockSpec((4, LINES + GAIN_LINES, 128), lambda s: (s, 0, 0)),
        out_shape=jax.ShapeDtypeStruct((UNITS, LINES + GAIN_LINES, 128), bf16),
        scratch_shapes=[pltpu.VMEM((LINES, 128), f32), pltpu.VMEM((240, 128), f32)],
        name="pack_attention",
    )(d_query, d_kv, d_out, gains)


def tile_range(starts_ref, fills_ref, block):
    first_slot = starts_ref[block] * BLK
    last_slot = block * BLK + fills_ref[block]
    tile_first = first_slot // TILE
    tile_last = (block * BLK) // TILE
    ragged_first = jnp.logical_and(first_slot % TILE != 0, tile_first < tile_last)
    return first_slot, last_slot, tile_first, tile_last, ragged_first.astype(jnp.int32)


def allowed_pairs(tile, block, first_slot, last_slot):
    key_slot = tile * TILE + lax.broadcasted_iota(jnp.int32, (TILE, WIDE), 0)
    lane = lax.broadcasted_iota(jnp.int32, (TILE, WIDE), 1)
    query_slot = block * BLK + lax.rem(lane, BLK)
    return jnp.logical_and(
        jnp.logical_and(key_slot >= first_slot, key_slot <= query_slot),
        jnp.logical_or(key_slot < last_slot, key_slot == query_slot),
    )


def over_tiles(span, block, step):
    first_slot, last_slot, tile_first, tile_last, ragged = span

    def masked(tile):
        step(tile, allowed_pairs(tile, block, first_slot, last_slot))

    def edge(k, carry):
        masked(jnp.where(k == ragged, tile_last, tile_first))
        return carry

    lax.fori_loop(0, 1 + ragged, edge, 0)

    def inner(tile, carry):
        step(tile, None)
        return carry

    lax.fori_loop(tile_first + ragged, tile_last, inner, 0)


def transpose_kv(kv_ref, turned, tiles):
    def body(t, carry):
        rows = pl.ds(pl.multiple_of(t * TILE, TILE), TILE)
        for h in range(KEY_VALUE_HEADS):
            turned[t, 128 * h : 128 * h + 128, :] = kv_ref[rows, 128 * h : 128 * h + 128].T
        return carry

    lax.fori_loop(0, tiles, body, 0)


def lay_out_kv(blocks, kv_ref, place):
    size = blocks[0].shape[0]
    for apart, block in enumerate(blocks):
        spot = apart if len(blocks) == 1 else place ^ apart
        kv_ref[pl.ds(pl.multiple_of(spot * size, TILE), size), :] = block[...]


def heads_beside(ref, h):
    return jnp.concatenate(
        [
            ref[HEAD_SIZE * (GROUPED * h + g) : HEAD_SIZE * (GROUPED * h + g + 1), :]
            for g in range(GROUPED)
        ],
        axis=1,
    )


def attention_forward_kernel(
    starts_ref, fills_ref, place_ref, query_ref, *refs
):
    kv_blocks = refs[:-8]
    mixed_ref, log_ref, kv_ref, turned, pairs, tops, totals, sums = refs[-8:]
    i = pl.program_id(0)
    block = place_ref[0] * (TOK_DEV // BLK) + i

    @pl.when(i == 0)
    def _():
        lay_out_kv(kv_blocks, kv_ref, place_ref[0])
        transpose_kv(kv_ref, turned, kv_ref.shape[0] // TILE)

    for h in range(KEY_VALUE_HEADS):
        pairs[h, :HEAD_SIZE, :] = heads_beside(query_ref, h)
        pairs[h, HEAD_SIZE:, :] = jnp.zeros((HEAD_SIZE, WIDE), bf16)
    tops[...] = jnp.full(tops.shape, masked_value, f32)
    totals[...] = jnp.zeros(totals.shape, f32)
    sums[...] = jnp.zeros(sums.shape, f32)

    def step(tile, allowed):
        rows = pl.ds(pl.multiple_of(tile * TILE, TILE), TILE)
        for h in range(KEY_VALUE_HEADS):
            scores = jnp.dot(
                kv_ref[rows, 128 * h : 128 * h + 128], pairs[h], preferred_element_type=f32
            )
            if allowed is not None:
                scores = jnp.where(allowed, scores, masked_value)
            top_old = tops[h]
            top = jnp.maximum(top_old, jnp.max(scores, axis=0, keepdims=True))
            weights = jnp.exp(scores - top)
            shrink = jnp.exp(top_old - top)
            tops[h] = top
            totals[h] = totals[h] * shrink + jnp.sum(weights, axis=0, keepdims=True)
            sums[h] = sums[h] * shrink + jnp.dot(
                turned[tile, 128 * h + HEAD_SIZE : 128 * h + 128, :],
                weights.astype(bf16),
                preferred_element_type=f32,
            )

    over_tiles(tile_range(starts_ref, fills_ref, block), block, step)
    for h in range(KEY_VALUE_HEADS):
        outcome = (sums[h] / totals[h]).astype(bf16)
        log_total = tops[h] + jnp.log(totals[h])
        for g in range(GROUPED):
            head = GROUPED * h + g
            mixed_ref[HEAD_SIZE * head : HEAD_SIZE * (head + 1), :] = outcome[:, BLK * g : BLK * (g + 1)]
            log_ref[head : head + 1, :] = log_total[:, BLK * g : BLK * (g + 1)]
    log_ref[QUERY_HEADS:, :] = jnp.zeros((1, BLK), f32)


def token_block(rows):
    return pl.BlockSpec((rows, BLK), lambda i, *_: (0, i))


def whole(shape):
    return pl.BlockSpec(shape, lambda i, *_: (0,) * len(shape))


def attention_forward(starts, fills, place, query, kv):
    group = sum(block.shape[0] for block in kv)
    return pl.pallas_call(
        attention_forward_kernel,
        grid_spec=pltpu.PrefetchScalarGridSpec(
            num_scalar_prefetch=3,
            grid=(TOK_DEV // BLK,),
            in_specs=[token_block(MODEL_WIDTH)] + [whole(block.shape) for block in kv],
            out_specs=[token_block(MODEL_WIDTH), token_block(16)],
            scratch_shapes=[
                pltpu.VMEM((group, 2 * KV_WIDTH), bf16),
                pltpu.VMEM((group // TILE, 2 * KV_WIDTH, TILE), bf16),
                pltpu.VMEM((KEY_VALUE_HEADS, 2 * HEAD_SIZE, WIDE), bf16),
                pltpu.VMEM((KEY_VALUE_HEADS, 1, WIDE), f32),
                pltpu.VMEM((KEY_VALUE_HEADS, 1, WIDE), f32),
                pltpu.VMEM((KEY_VALUE_HEADS, HEAD_SIZE, WIDE), f32),
            ],
        ),
        out_shape=[
            jax.ShapeDtypeStruct((MODEL_WIDTH, TOK_DEV), bf16),
            jax.ShapeDtypeStruct((16, TOK_DEV), f32),
        ],
        name="attention_forward",
    )(starts, fills, place, query, *kv)


def attention_backward_kernel(
    starts_ref,
    fills_ref,
    place_ref,
    query_ref,
    upstream_ref,
    mixed_ref,
    log_ref,
    cosine_ref,
    sine_ref,
    *refs,
):
    count = (len(refs) - 10) // 2
    kv_blocks, d_query_ref, d_kv_blocks = refs[:count], refs[count], refs[count + 1 : 2 * count + 1]
    (
        kv_ref,
        turned,
        pairs,
        query_rows,
        upstream_rows,
        deltas,
        logs,
        sums,
        kv_sums,
    ) = refs[2 * count + 1 :]
    i = pl.program_id(0)
    block = place_ref[0] * (TOK_DEV // BLK) + i
    tiles = kv_ref.shape[0] // TILE

    @pl.when(i == 0)
    def _():
        lay_out_kv(kv_blocks, kv_ref, place_ref[0])
        transpose_kv(kv_ref, turned, tiles)

        def clear(t, carry):
            kv_sums[:, pl.ds(pl.multiple_of(t * TILE, TILE), TILE), :] = jnp.zeros(
                (KEY_VALUE_HEADS, TILE, 128), f32
            )
            return carry

        lax.fori_loop(0, tiles, clear, 0)

    blank = jnp.zeros((HEAD_SIZE, WIDE), bf16)
    for h in range(KEY_VALUE_HEADS):
        query = heads_beside(query_ref, h)
        upstream = heads_beside(upstream_ref, h)
        pairs[h, :HEAD_SIZE, :WIDE] = query
        pairs[h, HEAD_SIZE:, :WIDE] = blank
        pairs[h, :HEAD_SIZE, WIDE:] = blank
        pairs[h, HEAD_SIZE:, WIDE:] = upstream
        query_rows[h] = pairs[h, :, :WIDE].T
        upstream_rows[h] = pairs[h, :, WIDE:].T
        deltas[h] = jnp.sum(
            upstream.astype(f32) * heads_beside(mixed_ref, h).astype(f32), axis=0, keepdims=True
        )
        logs[h] = jnp.concatenate(
            [log_ref[GROUPED * h + g : GROUPED * h + g + 1, :] for g in range(GROUPED)], axis=1
        )
    sums[...] = jnp.zeros(sums.shape, f32)

    def step(tile, allowed):
        rows = pl.ds(pl.multiple_of(tile * TILE, TILE), TILE)
        for h in range(KEY_VALUE_HEADS):
            both = jnp.dot(
                kv_ref[rows, 128 * h : 128 * h + 128], pairs[h], preferred_element_type=f32
            )
            scores = both[:, :WIDE]
            if allowed is not None:
                scores = jnp.where(allowed, scores, masked_value)
            probs = jnp.exp(scores - logs[h])
            d_scores = (probs * (both[:, WIDE:] - deltas[h])).astype(bf16)
            kv_sums[h, rows, :] += jnp.dot(
                d_scores, query_rows[h], preferred_element_type=f32
            ) + jnp.dot(probs.astype(bf16), upstream_rows[h], preferred_element_type=f32)
            sums[h] += jnp.dot(
                turned[tile, 128 * h : 128 * h + HEAD_SIZE, :], d_scores, preferred_element_type=f32
            )

    over_tiles(tile_range(starts_ref, fills_ref, block), block, step)
    cosine = cosine_ref[...]
    sine = sine_ref[...]
    half = HEAD_SIZE // 2
    for h in range(KEY_VALUE_HEADS):
        for g in range(GROUPED):
            head = GROUPED * h + g
            front = sums[h, :half, BLK * g : BLK * (g + 1)] * score_scale
            back = sums[h, half:, BLK * g : BLK * (g + 1)] * score_scale
            d_query_ref[HEAD_SIZE * head : HEAD_SIZE * head + half, :] = (
                front * cosine + back * sine
            ).astype(bf16)
            d_query_ref[HEAD_SIZE * head + half : HEAD_SIZE * (head + 1), :] = (
                back * cosine - front * sine
            ).astype(bf16)

    @pl.when(i == pl.num_programs(0) - 1)
    def _():
        size = kv_blocks[0].shape[0]
        for apart, block in enumerate(d_kv_blocks):
            spot = apart if count == 1 else place_ref[0] ^ apart

            def emit(t, carry):
                rows = pl.ds(pl.multiple_of(spot * size + t * TILE, TILE), TILE)
                for h in range(KEY_VALUE_HEADS):
                    block[pl.ds(pl.multiple_of(t * TILE, TILE), TILE), 128 * h : 128 * h + 128] = (
                        kv_sums[h, rows, :].astype(bf16)
                    )
                return carry

            lax.fori_loop(0, size // TILE, emit, 0)


def attention_backward(starts, fills, place, query, upstream, mixed, logs, cosine, sine, kv):
    group = sum(block.shape[0] for block in kv)
    half = HEAD_SIZE // 2
    return pl.pallas_call(
        attention_backward_kernel,
        grid_spec=pltpu.PrefetchScalarGridSpec(
            num_scalar_prefetch=3,
            grid=(TOK_DEV // BLK,),
            in_specs=[
                token_block(MODEL_WIDTH),
                token_block(MODEL_WIDTH),
                token_block(MODEL_WIDTH),
                token_block(16),
                token_block(half),
                token_block(half),
            ]
            + [whole(block.shape) for block in kv],
            out_specs=[token_block(MODEL_WIDTH)] + [whole(block.shape) for block in kv],
            scratch_shapes=[
                pltpu.VMEM((group, 2 * KV_WIDTH), bf16),
                pltpu.VMEM((group // TILE, 2 * KV_WIDTH, TILE), bf16),
                pltpu.VMEM((KEY_VALUE_HEADS, 2 * HEAD_SIZE, 2 * WIDE), bf16),
                pltpu.VMEM((KEY_VALUE_HEADS, WIDE, 128), bf16),
                pltpu.VMEM((KEY_VALUE_HEADS, WIDE, 128), bf16),
                pltpu.VMEM((KEY_VALUE_HEADS, 1, WIDE), f32),
                pltpu.VMEM((KEY_VALUE_HEADS, 1, WIDE), f32),
                pltpu.VMEM((KEY_VALUE_HEADS, HEAD_SIZE, WIDE), f32),
                pltpu.VMEM((KEY_VALUE_HEADS, group, 128), f32),
            ],
        ),
        out_shape=[
            jax.ShapeDtypeStruct((MODEL_WIDTH, TOK_DEV), bf16),
        ]
        + [jax.ShapeDtypeStruct(block.shape, bf16) for block in kv],
        name="attention_backward",
    )(starts, fills, place, query, upstream, mixed, logs, cosine, sine, *kv)


def dot_of(left, right, left_dim, right_dim):
    return lax.dot_general(
        left, right, (((left_dim,), (right_dim,)), ((), ())), preferred_element_type=f32
    )


SLOTS = 3
FORM = 640
PIECES = (240, 240, 160)
GAIN_LINE = 560
PAD_WIDTH = 1024
CHUNK = 640
CORE_BIT = ("shard", 1)
ROW_BIT = ("shard", 2)
NEAR_BITS = (ROW_BIT, ("dp", 1), ("dp", 2))
FAR_BITS = (("dp", 4),)


def stages(colour):
    return (CORE_BIT,) + NEAR_BITS[colour:] + NEAR_BITS[:colour] + FAR_BITS


def swap(value, bit):
    axis, mask = bit
    size = lax.axis_size(axis)
    return lax.ppermute(value, axis, [(i, i ^ mask) for i in range(size)])


def gather_colour(own, colour):
    held = own[None]
    for bit in reversed(stages(colour)[1:]):
        held = jnp.concatenate([held, swap(held, bit)], axis=0)
    return held, swap(held, CORE_BIT)


def scatter_colour(keep, send, colour):
    for bit in stages(colour):
        got = swap(send, bit)
        half = keep.shape[0] // 2
        if half == 0:
            return keep[0], got[0]
        send = keep[half:] + got[half:]
        keep = keep[:half] + got[:half]


def positions():
    device = jnp.arange(UNITS, dtype=jnp.int32)
    width = lax.axis_size("shard")
    apart = {
        "dp": (device // width) ^ lax.axis_index("dp").astype(jnp.int32),
        "shard": (device % width) ^ lax.axis_index("shard").astype(jnp.int32),
    }
    tables = []
    for colour in range(SLOTS):
        place = jnp.zeros((UNITS,), jnp.int32)
        for axis, mask in stages(colour):
            place = 2 * place + (apart[axis] & mask) // mask
        tables.append(place)
    return jnp.concatenate(tables)


def copy_from(halves, place, dst, sem, pick=lambda ref: ref):
    for number, ref in enumerate(halves):

        @pl.when(place // 16 == number)
        def _():
            pltpu.make_async_copy(pick(ref.at[lax.rem(place, 16)]), dst, sem).start()


def copy_to(src, halves, place, sem, pick=lambda ref: ref):
    for number, ref in enumerate(halves):

        @pl.when(place // 16 == number)
        def _():
            pltpu.make_async_copy(src, pick(ref.at[lax.rem(place, 16)]), sem).start()


def wait_for(ref, sem):
    pltpu.make_async_copy(ref, ref, sem).wait()


def form_attention_kernel(wide_ref, lines_ref, gains_ref, a_ref, b_ref, c_ref, mid, form):
    @pl.when(wide_ref[0] == 1)
    def _():
        def store(c, value):
            if c == 7:
                value = jnp.where(lane_low(80), value, 0.0)
            form[80 * c : 80 * c + 80, :] = value

        lines_to_rows_960(lines_ref, 0, 80, mid, store)

    @pl.when(wide_ref[0] == 0)
    def _():
        low = lane_low(120)
        line = [lines_ref[pl.ds(k, 120, stride=5), :] for k in range(5)]
        turned = [None, None] + [pltpu.roll(line[k], 64, 1) for k in range(2, 5)]
        form[pl.ds(0, 120, stride=2), :] = line[0]
        form[pl.ds(1, 120, stride=2), :] = jnp.where(low, turned[2], turned[3])
        form[pl.ds(240, 120, stride=2), :] = line[1]
        form[pl.ds(241, 120, stride=2), :] = jnp.where(low, turned[3], turned[4])
        mid[pl.ds(0, 120, stride=2), :] = line[2]
        mid[pl.ds(1, 120, stride=2), :] = turned[4]
        low = lane_low(80)
        form[480:560, :] = jnp.where(low, mid[0:80, :], pltpu.roll(mid[160:240, :], 64, 1))
        form[560:640, :] = jnp.where(low, mid[80:160, :], 0.0)

    form[GAIN_LINE : GAIN_LINE + 1, :] = jnp.where(
        lane_low(1), form[GAIN_LINE : GAIN_LINE + 1, :], gains_ref[...]
    )
    a_ref[...] = form[0:240, :].astype(bf16)
    b_ref[...] = form[240:480, :].astype(bf16)
    c_ref[...] = form[480:640, :].astype(bf16)


SMEM_SPEC = pl.BlockSpec(memory_space=pltpu.SMEM)
ANY_SPEC = pl.BlockSpec(memory_space=pl.ANY)


def form_attention(wide, lines, gains):
    return pl.pallas_call(
        form_attention_kernel,
        in_specs=[SMEM_SPEC, pl.BlockSpec((LINES, 128)), pl.BlockSpec((1, 128))],
        out_shape=[jax.ShapeDtypeStruct((n, 128), bf16) for n in PIECES],
        scratch_shapes=[pltpu.VMEM((240, 128), f32), pltpu.VMEM((FORM, 128), f32)],
        name="form_attention",
    )(wide, lines, gains)


def unform_attention_kernel(wide_ref, *refs):
    pieces, (lines_ref, gains_ref, mid, form) = refs[:6], refs[6:]
    base = 0
    for n, keep, got in zip(PIECES, pieces[0::2], pieces[1::2]):
        form[base : base + n, :] = keep[...].astype(f32) + got[...].astype(f32)
        base += n
    gains_ref[...] = form[GAIN_LINE : GAIN_LINE + 1, :]

    @pl.when(wide_ref[0] == 1)
    def _():
        rows_to_lines_960(lambda c: form[80 * c : 80 * c + 80, :], lines_ref, 0, 80, mid)

    @pl.when(wide_ref[0] == 0)
    def _():
        low = lane_low(120)
        mid[0:80, :] = form[480:560, :]
        mid[80:160, :] = form[560:640, :]
        mid[160:240, :] = pltpu.roll(form[480:560, :], 64, 1)
        even = [form[pl.ds(0, 120, stride=2), :], form[pl.ds(240, 120, stride=2), :]]
        odd = [form[pl.ds(1, 120, stride=2), :], form[pl.ds(241, 120, stride=2), :]]
        even.append(mid[pl.ds(0, 120, stride=2), :])
        odd.append(mid[pl.ds(1, 120, stride=2), :])
        odd = [pltpu.roll(value, 64, 1) for value in odd]
        lines_ref[pl.ds(0, 120, stride=5), :] = even[0]
        lines_ref[pl.ds(1, 120, stride=5), :] = even[1]
        lines_ref[pl.ds(2, 120, stride=5), :] = jnp.where(low, even[2], odd[0])
        lines_ref[pl.ds(3, 120, stride=5), :] = jnp.where(low, odd[0], odd[1])
        lines_ref[pl.ds(4, 120, stride=5), :] = jnp.where(low, odd[1], odd[2])


def unform_attention(wide, addends):
    return pl.pallas_call(
        unform_attention_kernel,
        in_specs=[SMEM_SPEC] + [pl.BlockSpec((n, 128)) for n in PIECES for _ in range(2)],
        out_shape=[jax.ShapeDtypeStruct((LINES, 128), f32), jax.ShapeDtypeStruct((1, 128), f32)],
        scratch_shapes=[pltpu.VMEM((240, 128), f32), pltpu.VMEM((FORM, 128), f32)],
        name="unform_attention",
    )(wide, *addends)


def wide_pieces(c):
    return [((80 * c + 16 * m) // 32, (80 * c + 16 * m) % 32, 16 * m) for m in range(5)]


def form_feedforward_kernel(narrow_ref, lines_ref, out, mid):
    for s in range(SLOTS):

        @pl.when(narrow_ref[s] == 1)
        def _():
            mid[30:32, :] = jnp.zeros((2, 128), f32)
            for c in range(20):
                mid[0:30, :] = lines_ref[pl.ds(LINES * s + c, 30, stride=20), :]
                out[s, c] = mid[0:32, :].astype(bf16)

        @pl.when(narrow_ref[s] == 0)
        def _():
            def store(c, value):
                if c == 7:
                    value = jnp.where(lane_low(80), value, 0.0)
                for k, r, m in wide_pieces(c):
                    out[s, k, r : r + 16, :] = value[m : m + 16].astype(bf16)

            lines_to_rows_960(lines_ref, LINES * s, 80, mid, store)


def form_feedforward(narrow, lines):
    return pl.pallas_call(
        form_feedforward_kernel,
        in_specs=[SMEM_SPEC, pl.BlockSpec((SLOTS * LINES, 128))],
        out_shape=jax.ShapeDtypeStruct((SLOTS, 20, 32, 128), bf16),
        scratch_shapes=[pltpu.VMEM((80, 128), f32)],
        name="form_feedforward",
    )(narrow, lines)


def unform_feedforward_kernel(narrow_ref, terms, lines_ref, mid):
    for s in range(SLOTS):

        @pl.when(narrow_ref[s] == 1)
        def _():
            for c in range(20):
                mid[0:32, :] = terms[s, c].astype(f32)
                lines_ref[pl.ds(LINES * s + c, 30, stride=20), :] = mid[0:30, :]

        @pl.when(narrow_ref[s] == 0)
        def _():
            def load(c):
                return jnp.concatenate(
                    [terms[s, k, r : r + 16, :].astype(f32) for k, r, m in wide_pieces(c)], axis=0
                )

            rows_to_lines_960(load, lines_ref, LINES * s, 80, mid)


def unform_feedforward(narrow, terms):
    return pl.pallas_call(
        unform_feedforward_kernel,
        in_specs=[SMEM_SPEC, pl.BlockSpec((SLOTS, 20, 32, 128))],
        out_shape=jax.ShapeDtypeStruct((SLOTS * LINES, 128), f32),
        scratch_shapes=[pltpu.VMEM((80, 128), f32)],
        name="unform_feedforward",
    )(narrow, terms)


def place_attention_kernel(table_ref, *refs):
    halves = [refs[2 * k : 2 * k + 2] for k in range(SLOTS)]
    query_ref, kv_ref, out_ref, gains_ref, units, sem = refs[2 * SLOTS :]

    def start(d, carry):
        base = 0
        for k, n in enumerate(PIECES):
            copy_from(halves[k], table_ref[UNITS * k + d], units.at[d, base : base + n, :], sem)
            base += n
        return carry

    lax.fori_loop(0, UNITS, start, 0)
    wait_for(units, sem)

    def wide(out, first):
        def body(u, carry):
            rows = pl.ds(pl.multiple_of(80 * u, 16), 80)
            for c in range(7):
                out[rows, 128 * c : 128 * c + 128] = units[first + u, 80 * c : 80 * c + 80, :]
            out[rows, 896:960] = units[first + u, 560:640, :64]
            return carry

        lax.fori_loop(0, 12, body, 0)

    def keyed(j, carry):
        low = lane_low(240)
        chunks = []
        for first in (12, 16):
            unit = units[first + j].astype(f32)
            last = jnp.concatenate(
                [unit[480:640], pltpu.roll(unit[480:560], 64, 1)], axis=0
            )
            lines = (unit[0:240], unit[240:480], last)
            chunks.append([(lines[h // 2], h % 2) for h in range(KEY_VALUE_HEADS)])
        rows = pl.ds(pl.multiple_of(240 * j, 16), 240)
        for h in range(KEY_VALUE_HEADS):
            kv_ref[rows, 128 * h : 128 * h + 128] = jnp.where(
                low, placed(chunks[0][h], 0), placed(chunks[1][h], 1)
            ).astype(bf16)
        return carry

    lax.fori_loop(0, 4, keyed, 0)
    wide(query_ref, 0)
    wide(out_ref, 20)
    for u in range(UNITS):
        gains_ref[u : u + 1, :] = units[u, GAIN_LINE : GAIN_LINE + 1, :].astype(f32)


def place_attention(table, gathered):
    return pl.pallas_call(
        place_attention_kernel,
        in_specs=[SMEM_SPEC] + [ANY_SPEC] * (2 * SLOTS),
        out_shape=[
            jax.ShapeDtypeStruct((MODEL_WIDTH, MODEL_WIDTH), bf16),
            jax.ShapeDtypeStruct((MODEL_WIDTH, 2 * KV_WIDTH), bf16),
            jax.ShapeDtypeStruct((MODEL_WIDTH, MODEL_WIDTH), bf16),
            jax.ShapeDtypeStruct((UNITS, 128), f32),
        ],
        scratch_shapes=[pltpu.VMEM((UNITS, FORM, 128), bf16), pltpu.SemaphoreType.DMA],
        name="place_attention",
    )(table, *gathered)


def split_attention_kernel(table_ref, query_ref, kv_ref, out_ref, gains_ref, *refs):
    halves = [refs[2 * k : 2 * k + 2] for k in range(SLOTS)]
    units, sem = refs[2 * SLOTS :]

    def send(d):
        row = lax.broadcasted_iota(jnp.int32, (16, 128), 0)
        lane = lax.broadcasted_iota(jnp.int32, (16, 128), 1)
        block = units[d, GAIN_LINE : GAIN_LINE + 16, :].astype(f32)
        units[d, GAIN_LINE : GAIN_LINE + 16, :] = jnp.where(
            jnp.logical_and(row == 0, lane >= 64), gains_ref[pl.ds(d, 1), :], block
        ).astype(bf16)
        base = 0
        for k, n in enumerate(PIECES):
            copy_to(units.at[d, base : base + n, :], halves[k], table_ref[UNITS * k + d], sem)
            base += n

    def wide(source, first):
        def body(u, carry):
            rows = pl.ds(pl.multiple_of(80 * u, 16), 80)
            for c in range(7):
                units[first + u, 80 * c : 80 * c + 80, :] = source[rows, 128 * c : 128 * c + 128]
            tail = source[rows, 896:960]
            units[first + u, 560:640, :] = jnp.concatenate([tail, jnp.zeros_like(tail)], axis=1)
            send(first + u)
            return carry

        lax.fori_loop(0, 12, body, 0)

    def keyed(j, carry):
        low = lane_low(240)
        rows = pl.ds(pl.multiple_of(240 * j, 16), 240)
        for upper, first in ((0, 12), (1, 16)):
            heads = [
                (kv_ref[rows, 128 * h : 128 * h + 128].astype(f32), upper)
                for h in range(KEY_VALUE_HEADS)
            ]
            for c in range(2):
                units[first + j, 240 * c : 240 * c + 240, :] = jnp.where(
                    low, placed(heads[2 * c], 0), placed(heads[2 * c + 1], 1)
                ).astype(bf16)
            last = placed(heads[4], 0)
            turned = placed(heads[4], 1)
            units[first + j, 480:560, :] = jnp.where(
                lane_low(80), last[0:80], turned[160:240]
            ).astype(bf16)
            units[first + j, 560:640, :] = jnp.where(lane_low(80), last[80:160], 0.0).astype(bf16)
            send(first + j)
        return carry

    lax.fori_loop(0, 4, keyed, 0)
    wide(query_ref, 0)
    wide(out_ref, 20)
    wait_for(units, sem)


def split_attention(table, d_query, d_kv, d_out, gains):
    return pl.pallas_call(
        split_attention_kernel,
        in_specs=[
            SMEM_SPEC,
            pl.BlockSpec((MODEL_WIDTH, MODEL_WIDTH)),
            pl.BlockSpec((MODEL_WIDTH, 2 * KV_WIDTH)),
            pl.BlockSpec((MODEL_WIDTH, MODEL_WIDTH)),
            pl.BlockSpec((UNITS, 128)),
        ],
        out_specs=[ANY_SPEC] * (2 * SLOTS),
        out_shape=[jax.ShapeDtypeStruct((16, n, 128), bf16) for n in PIECES for _ in range(2)],
        scratch_shapes=[pltpu.VMEM((UNITS, FORM, 128), bf16), pltpu.SemaphoreType.DMA],
        name="split_attention",
    )(table, d_query, d_kv, d_out, gains)


def feedforward_kernel(
    hidden_ref,
    turned_ref,
    grad_ref,
    gate_ref,
    up_ref,
    down_ref,
    out_ref,
    d_hidden_ref,
    terms_ref,
    down,
    inner_rows,
    inner_turned,
    d_both,
    both_out,
    down_out,
    sems,
):
    q = pl.program_id(0)
    chunks = pl.num_programs(0)
    slot = lax.rem(q, 2)

    def copies(side, chunk):
        columns = pl.ds(5 * chunk, 5)
        return (
            pltpu.make_async_copy(
                both_out.at[side, 0], terms_ref.at[pl.ds(0, 32), columns], sems.at[side, 0]
            ),
            pltpu.make_async_copy(
                both_out.at[side, 1], terms_ref.at[pl.ds(32, 32), columns], sems.at[side, 1]
            ),
            pltpu.make_async_copy(
                down_out.at[side], terms_ref.at[pl.ds(64 + 8 * chunk, 8)], sems.at[side, 2]
            ),
        )

    for v in range(8):
        for c in range(8):
            for k, r, m in wide_pieces(c):
                down[80 * v + m : 80 * v + m + 16, 128 * c : 128 * c + 128] = down_ref[
                    v, k, r : r + 16, :
                ]

    @pl.when(q == 0)
    def _():
        out_ref[...] = jnp.zeros(out_ref.shape, f32)
        d_hidden_ref[...] = jnp.zeros(d_hidden_ref.shape, f32)

    def rows_step(i, carry):
        rows = pl.ds(pl.multiple_of(256 * i, 256), 256)
        weights = jnp.concatenate(
            [ref[:, c].reshape(PAD_WIDTH, 128) for ref in (gate_ref, up_ref) for c in range(5)],
            axis=1,
        )
        both = jnp.dot(hidden_ref[rows, :], weights, preferred_element_type=f32)
        gate, upper = both[:, :CHUNK], both[:, CHUNK:]
        sigmoid_gate = jax.nn.sigmoid(gate)
        activated = gate * sigmoid_gate
        inner = (activated * upper).astype(bf16)
        inner_rows[rows, :] = inner
        out_ref[rows, :] += jnp.dot(inner, down[...], preferred_element_type=f32)
        d_inner = dot_of(grad_ref[rows, :], down[...], 1, 1)
        d_gate = d_inner * upper * sigmoid_gate * (1.0 + gate * (1.0 - sigmoid_gate))
        d_upper = d_inner * activated
        d_pair = jnp.concatenate([d_gate, d_upper], axis=1).astype(bf16)
        d_both[rows, :] = d_pair
        d_hidden_ref[rows, :] += dot_of(d_pair, weights, 1, 1)
        return carry

    lax.fori_loop(0, 2, rows_step, 0)
    inner_turned[...] = inner_rows[...].T

    @pl.when(q >= 2)
    def _():
        for copy in copies(slot, q - 2):
            copy.wait()

    def both_step(i, carry):
        rows = pl.ds(pl.multiple_of(256 * i, 256), 256)
        terms = jnp.dot(turned_ref[rows, :], d_both[...], preferred_element_type=f32).astype(bf16)
        units = pl.ds(8 * i, 8)
        for c in range(10):
            both_out[slot, c // 5, units, c % 5] = terms[:, 128 * c : 128 * c + 128].reshape(
                8, 32, 128
            )
        return carry

    lax.fori_loop(0, 4, both_step, 0)

    def down_step(i, carry):
        rows = pl.ds(pl.multiple_of(320 * i, 16), 320)
        terms = jnp.dot(
            inner_turned[rows, :], grad_ref[...], preferred_element_type=f32
        ).astype(bf16)
        for v in range(4):
            for c in range(8):
                for k, r, m in wide_pieces(c):
                    down_out[slot, 4 * i + v, k, r : r + 16, :] = terms[
                        80 * v + m : 80 * v + m + 16, 128 * c : 128 * c + 128
                    ]
        return carry

    lax.fori_loop(0, 2, down_step, 0)
    for copy in copies(slot, q):
        copy.start()

    @pl.when(q == chunks - 1)
    def _():
        for copy in copies(1 - slot, q - 1) + copies(slot, q):
            copy.wait()


def feedforward(hidden, turned, grad, weights):
    full = lambda shape: pl.BlockSpec(shape, lambda q: (0, 0))
    return pl.pallas_call(
        feedforward_kernel,
        grid=(FF // CHUNK,),
        in_specs=[
            full((TOK_DEV, PAD_WIDTH)),
            full((PAD_WIDTH, TOK_DEV)),
            full((TOK_DEV, PAD_WIDTH)),
            pl.BlockSpec((32, 5, 32, 128), lambda q: (0, q, 0, 0)),
            pl.BlockSpec((32, 5, 32, 128), lambda q: (1, q, 0, 0)),
            pl.BlockSpec((8, 20, 32, 128), lambda q: (8 + q, 0, 0, 0)),
        ],
        out_specs=[full((TOK_DEV, PAD_WIDTH))] * 2 + [ANY_SPEC],
        out_shape=[jax.ShapeDtypeStruct((TOK_DEV, PAD_WIDTH), f32)] * 2
        + [jax.ShapeDtypeStruct((3 * UNITS, 20, 32, 128), bf16)],
        scratch_shapes=[
            pltpu.VMEM((CHUNK, PAD_WIDTH), bf16),
            pltpu.VMEM((TOK_DEV, CHUNK), bf16),
            pltpu.VMEM((CHUNK, TOK_DEV), bf16),
            pltpu.VMEM((TOK_DEV, 2 * CHUNK), bf16),
            pltpu.VMEM((2, 2, 32, 5, 32, 128), bf16),
            pltpu.VMEM((2, 8, 20, 32, 128), bf16),
            pltpu.SemaphoreType.DMA((2, 3)),
        ],
        compiler_params=pltpu.CompilerParams(vmem_limit_bytes=60 * 2**20),
        name="feedforward",
    )(hidden, turned, grad, weights, weights, weights)


def spread_matrix():
    column = jnp.arange(PAD_WIDTH, dtype=jnp.int32)
    entry = jnp.where(column % 32 < 30, 30 * (column // 32) + column % 32, -1)
    return (jnp.arange(MODEL_WIDTH, dtype=jnp.int32)[:, None] == entry[None, :]).astype(bf16)


def rope_tables(positions):
    steps = jnp.arange(HEAD_SIZE // 2, dtype=f32) * (2.0 / HEAD_SIZE)
    inverse = jnp.exp(-math.log(10000.0) * steps)
    angles = inverse[:, None] * positions.astype(f32)[None, :]
    return (jnp.cos(angles), jnp.sin(angles))


def norm_scale(field):
    return lax.rsqrt(jnp.mean(field * field, axis=1, keepdims=True) + epsilon)


def norm_back(upstream, normed, scale, gain):
    scaled = upstream * gain[None, :]
    return scale * (scaled - normed * jnp.mean(scaled * normed, axis=1, keepdims=True))


def adam_step(grad, moment, second, master):
    moment_new = 0.9 * moment + 0.1 * grad
    second_new = 0.999 * second + 0.001 * grad * grad
    corrected = moment_new / (1.0 - 0.9**ADAM_STEP)
    scaled = second_new / (1.0 - 0.999**ADAM_STEP)
    update = -learning_rate * (corrected / (jnp.sqrt(scaled) + 1e-08) + weight_decay * master)
    return (moment_new, second_new, update)


def gather_lines(block):
    return lax.all_gather(block, ALL_AXES, axis=0, tiled=True)


def scatter_lines(lines):
    return lax.psum_scatter(lines, ALL_AXES, scatter_dimension=0, tiled=True)


def local(
    layer_input,
    cotangent,
    master_attention,
    master_feedforward,
    master_gains,
    first_attention,
    second_attention,
    first_feedforward,
    second_feedforward,
    first_gains,
    second_gains,
    block_start,
    block_fill,
):
    devices = lax.axis_size(ALL_AXES)
    attention_lines = master_attention.shape[0] // 128
    feedforward_lines = master_feedforward.shape[0] // 128
    gain_count = master_gains.shape[0]
    padded = (attention_lines // 16 + 1) * 16

    in_units = devices == UNITS
    if in_units:
        table = positions()
        device = (
            lax.axis_index("dp") * lax.axis_size("shard") + lax.axis_index("shard")
        ).astype(jnp.int32)
        wide = jnp.logical_or(device < 12, device >= 20).astype(jnp.int32)[None]
        narrow = (SLOTS * device + jnp.arange(SLOTS, dtype=jnp.int32) < 2 * UNITS).astype(jnp.int32)
        gain_row = jnp.pad(
            master_gains.reshape(1, gain_count), ((0, 0), (64, 64 - gain_count))
        )
        pieces = form_attention(wide, master_attention.reshape(LINES, 128), gain_row)
        gathered = [half for k in range(SLOTS) for half in gather_colour(pieces[k], k)]
        forms = form_feedforward(narrow, master_feedforward.reshape(SLOTS * LINES, 128))
        feedforward_all = gather_lines(forms.reshape(SLOTS * FORM, 128))
        query_weight, kv_weight, out_weight, gain_rows = place_attention(table, gathered)
        gains_all = gain_rows[:, 64 : 64 + gain_count].reshape(-1)
    else:
        gain_lines = jnp.pad(
            master_gains.astype(bf16).reshape(1, gain_count),
            ((0, padded - attention_lines - 1), (0, 128 - gain_count)),
        )
        attention_block = jnp.concatenate(
            [master_attention.astype(bf16).reshape(attention_lines, 128), gain_lines], axis=0
        )
        by_device = gather_lines(attention_block).reshape(devices, padded, 128)
        feedforward_all = gather_lines(
            master_feedforward.astype(bf16).reshape(feedforward_lines, 128)
        )
        gains_all = by_device[:, attention_lines, :gain_count].reshape(-1).astype(f32)
        units = by_device[:, :attention_lines].reshape(UNITS, LINES, 128)
        query_weight = unpack_wide(units, 0)
        kv_weight = unpack_kv(units)
        out_weight = unpack_wide(units, 20)
    gain_one, gain_two = gains_all[:MODEL_WIDTH], gains_all[MODEL_WIDTH:]

    shard = lax.axis_index("shard").astype(jnp.int32)
    place = shard[None]
    first_row = shard * TOK_DEV
    first_block = shard * (TOK_DEV // BLK)
    local_slots = first_row + jnp.arange(TOK_DEV, dtype=jnp.int32)
    local_starts = lax.dynamic_slice_in_dim(block_start, first_block, TOK_DEV // BLK)
    local_fills = lax.dynamic_slice_in_dim(block_fill, first_block, TOK_DEV // BLK)
    live_rows = local_slots % BLK < jnp.repeat(local_fills, BLK)
    cosine_table, sine_table = rope_tables(local_slots - jnp.repeat(local_starts, BLK) * BLK)

    def rotate(field, scale):
        heads = field.shape[0]
        front = field[:, : HEAD_SIZE // 2]
        back = field[:, HEAD_SIZE // 2 :]
        return (
            jnp.concatenate(
                [
                    front * cosine_table[None] - back * sine_table[None],
                    back * cosine_table[None] + front * sine_table[None],
                ],
                axis=1,
            ).astype(bf16)
            * bf16(scale)
        ).reshape(heads * HEAD_SIZE, TOK_DEV)

    inputs = layer_input.astype(f32)
    scale_one = norm_scale(inputs)
    normed_one = inputs * scale_one
    first_hidden = (normed_one * gain_one[None, :]).astype(bf16)
    kv_turned = dot_of(kv_weight, first_hidden, 0, 1).reshape(
        KEY_VALUE_HEADS, 2, HEAD_SIZE, TOK_DEV
    )
    keys = rotate(kv_turned[:, 0], 1.0).reshape(KEY_VALUE_HEADS, 1, HEAD_SIZE, TOK_DEV)
    values = kv_turned[:, 1:].astype(bf16)
    kv_rows = jnp.concatenate([keys, values], axis=1).reshape(2 * KV_WIDTH, TOK_DEV).T
    if in_units:
        across = swap(kv_rows, ROW_BIT)
        kv_all = [kv_rows, swap(kv_rows, CORE_BIT), across, swap(across, CORE_BIT)]
    else:
        kv_all = [lax.all_gather(kv_rows, "shard", axis=0, tiled=True)]
    query_turned = rotate(
        dot_of(query_weight, first_hidden, 0, 1).reshape(QUERY_HEADS, HEAD_SIZE, TOK_DEV),
        score_scale,
    )
    mixed_turned, logs = attention_forward(block_start, block_fill, place, query_turned, kv_all)
    middle = inputs + dot_of(mixed_turned, out_weight, 0, 0)
    scale_two = norm_scale(middle)
    normed_two = middle * scale_two
    hidden_two = (normed_two * gain_two[None, :]).astype(bf16)

    grad_out = cotangent.astype(f32) * live_rows[:, None].astype(f32)
    grad_low = grad_out.astype(bf16)
    if in_units:
        spread = spread_matrix()
        outcome, d_spread, ff_terms = feedforward(
            dot_of(hidden_two, spread, 1, 0).astype(bf16),
            dot_of(spread, hidden_two, 0, 1).astype(bf16),
            jnp.pad(grad_low, ((0, 0), (0, PAD_WIDTH - MODEL_WIDTH))),
            feedforward_all.reshape(3 * UNITS, 20, 32, 128),
        )
        layer_output = middle + outcome[:, :MODEL_WIDTH]
        d_coarse = lax.reduce_precision(d_spread, 8, 7)
        d_hidden_two = dot_of(d_coarse.astype(bf16), spread, 1, 1) + dot_of(
            (d_spread - d_coarse).astype(bf16), spread, 1, 1
        )
        ff_sum = scatter_lines(ff_terms.reshape(SLOTS * UNITS * FORM, 128))
        feedforward_gradient = unform_feedforward(narrow, ff_sum.reshape(SLOTS, 20, 32, 128)).reshape(-1)
    else:
        gate_weight, up_weight, down_weight = unpack_ff(feedforward_all)
        gate = dot_of(hidden_two, gate_weight, 1, 0)
        upper = dot_of(hidden_two, up_weight, 1, 0)
        sigmoid_gate = jax.nn.sigmoid(gate)
        activated = gate * sigmoid_gate
        inner = (activated * upper).astype(bf16)
        layer_output = middle + dot_of(inner, down_weight, 1, 0)
        d_down_weight = dot_of(inner, grad_low, 0, 0).astype(bf16)
        d_inner = dot_of(grad_low, down_weight, 1, 1)
        d_gate = (
            d_inner * upper * sigmoid_gate * (1.0 + gate * (1.0 - sigmoid_gate))
        ).astype(bf16)
        d_upper = (d_inner * activated).astype(bf16)
        d_gate_weight = dot_of(hidden_two, d_gate, 0, 0).astype(bf16)
        d_up_weight = dot_of(hidden_two, d_upper, 0, 0).astype(bf16)
        d_hidden_two = dot_of(d_gate, gate_weight, 1, 1) + dot_of(d_upper, up_weight, 1, 1)
        feedforward_gradient = (
            scatter_lines(pack_ff(d_gate_weight, d_up_weight, d_down_weight))
            .astype(f32)
            .reshape(-1)
        )

    d_gain_two = jnp.sum(d_hidden_two * normed_two, axis=0)
    d_middle = grad_out + norm_back(d_hidden_two, normed_two, scale_two, gain_two)

    d_branch = d_middle.astype(bf16)
    d_out_weight = dot_of(mixed_turned, d_branch, 1, 0).astype(bf16)
    d_mixed = dot_of(out_weight, d_branch, 1, 1).astype(bf16)
    d_query, *d_kv = attention_backward(
        block_start,
        block_fill,
        place,
        query_turned,
        d_mixed,
        mixed_turned,
        logs,
        cosine_table,
        sine_table,
        kv_all,
    )
    if in_units:
        across = d_kv[2] + swap(d_kv[3], CORE_BIT)
        d_kv_rows = d_kv[0] + swap(d_kv[1], CORE_BIT) + swap(across, ROW_BIT)
    else:
        d_kv_rows = lax.psum_scatter(d_kv[0], "shard", scatter_dimension=0, tiled=True)
    d_kv_turned = d_kv_rows.T.reshape(KEY_VALUE_HEADS, 2, HEAD_SIZE, TOK_DEV)
    d_front = d_kv_turned[:, 0, : HEAD_SIZE // 2].astype(f32)
    d_back = d_kv_turned[:, 0, HEAD_SIZE // 2 :].astype(f32)
    d_keys = jnp.concatenate(
        [
            d_front * cosine_table[None] + d_back * sine_table[None],
            d_back * cosine_table[None] - d_front * sine_table[None],
        ],
        axis=1,
    ).astype(bf16)
    d_kv_lin = jnp.concatenate([d_keys[:, None], d_kv_turned[:, 1:]], axis=1).reshape(
        2 * KV_WIDTH, TOK_DEV
    )
    d_query_weight = dot_of(first_hidden, d_query, 0, 1).astype(bf16)
    d_kv_weight = dot_of(first_hidden, d_kv_lin, 0, 1).astype(bf16)
    d_hidden_one = dot_of(d_query, query_weight, 0, 1) + dot_of(d_kv_lin, kv_weight, 0, 1)
    d_gain_one = jnp.sum(d_hidden_one * normed_one, axis=0)
    input_gradient = d_middle + norm_back(d_hidden_one, normed_one, scale_one, gain_one)

    gain_terms = jnp.concatenate([d_gain_one, d_gain_two])
    if in_units:
        gain_rows = jnp.pad(
            gain_terms.reshape(UNITS, gain_count), ((0, 0), (64, 64 - gain_count))
        )
        terms = split_attention(table, d_query_weight, d_kv_weight, d_out_weight, gain_rows)
        addends = [
            addend
            for k in range(SLOTS)
            for addend in scatter_colour(terms[2 * k], terms[2 * k + 1], k)
        ]
        attention_sum, gain_sum = unform_attention(wide, addends)
        attention_gradient = attention_sum.reshape(-1)
        gains_gradient = gain_sum[0, 64 : 64 + gain_count]
    else:
        no_gains = jnp.zeros((UNITS, GAIN_LINES, 128), bf16)
        terms = pack_attention(d_query_weight, d_kv_weight, d_out_weight, no_gains)
        terms = jnp.concatenate(
            [
                terms[:, :LINES].reshape(devices, attention_lines, 128),
                jnp.pad(
                    gain_terms.astype(bf16).reshape(devices, 1, gain_count),
                    ((0, 0), (0, padded - attention_lines - 1), (0, 128 - gain_count)),
                ),
            ],
            axis=1,
        )
        summed = scatter_lines(terms.reshape(devices * padded, 128)).astype(f32)
        attention_gradient = summed[:attention_lines].reshape(-1)
        gains_gradient = summed[attention_lines, :gain_count]

    attention_first, attention_second, attention_update = adam_step(
        attention_gradient, first_attention, second_attention, master_attention
    )
    feedforward_first, feedforward_second, feedforward_update = adam_step(
        feedforward_gradient, first_feedforward, second_feedforward, master_feedforward
    )
    gains_first, gains_second, gains_update = adam_step(
        gains_gradient, first_gains, second_gains, master_gains
    )
    return (
        layer_output,
        input_gradient,
        attention_gradient,
        feedforward_gradient,
        gains_gradient,
        attention_first,
        attention_second,
        feedforward_first,
        feedforward_second,
        gains_first,
        gains_second,
        attention_update,
        feedforward_update,
        gains_update,
    )


def solution(mesh):
    rows = P(ALL_AXES, None)
    flat = P(ALL_AXES)
    return jax.shard_map(
        local,
        mesh=mesh,
        in_specs=(rows, rows) + (flat,) * 9 + (P("dp"), P("dp")),
        out_specs=(rows, rows) + (flat,) * 12,
        check_vma=False,
    )
```

```python
import functools
import math

import jax
import jax.numpy as jnp
from jax import lax
from jax.experimental import pallas as pl
from jax.experimental.pallas import tpu as pltpu
from jax.sharding import PartitionSpec as P

MODEL_WIDTH = 960
QUERY_HEADS = 15
KEY_VALUE_HEADS = 5
GROUPED = QUERY_HEADS // KEY_VALUE_HEADS
HEAD_SIZE = 64
FF = 2560
BLK = 128
ADAM_STEP = 10
TOK_DEV = 512
KV_WIDTH = KEY_VALUE_HEADS * HEAD_SIZE
TILE = 256
WIDE = GROUPED * BLK
UNITS = 32
LINES = 600
GAIN_LINES = 8
ALL_AXES = ("dp", "shard")

epsilon = 1e-05
masked_value = -1e30
learning_rate = 0.03
weight_decay = 0.1
score_scale = 1.0 / math.sqrt(HEAD_SIZE)
f32 = jnp.float32
bf16 = jnp.bfloat16


def lines_to_rows_2560(scratch, base, rows, store):
    for c in range(20):
        store(c, scratch[pl.ds(base + c, rows, stride=20), :])


def rows_to_lines_2560(load, scratch, base, rows):
    for c in range(20):
        scratch[pl.ds(base + c, rows, stride=20), :] = load(c)


def lane_low(rows):
    return lax.broadcasted_iota(jnp.int32, (rows, 128), 1) < 64


def lines_to_rows_960(scratch, base, rows, mid, store):
    half = rows // 2
    low = lane_low(half)
    line = [scratch[pl.ds(base + k, half, stride=15), :] for k in range(15)]
    turned = [None] * 7 + [pltpu.roll(line[k], 64, 1) for k in range(7, 15)]
    for c in range(8):
        mid[pl.ds(0, half, stride=2), :] = line[c]
        odd = jnp.where(low, turned[7 + c], turned[8 + c]) if c < 7 else turned[14]
        mid[pl.ds(1, half, stride=2), :] = odd
        store(c, mid[pl.ds(0, rows), :])


def rows_to_lines_960(load, scratch, base, rows, mid):
    half = rows // 2
    low = lane_low(half)
    odds = []
    for c in range(8):
        mid[pl.ds(0, rows), :] = load(c)
        even = mid[pl.ds(0, half, stride=2), :]
        odd = pltpu.roll(mid[pl.ds(1, half, stride=2), :], 64, 1)
        odds.append(odd)
        if c < 7:
            scratch[pl.ds(base + c, half, stride=15), :] = even
        else:
            scratch[pl.ds(base + 7, half, stride=15), :] = jnp.where(low, even, odds[0])
        if c > 0:
            scratch[pl.ds(base + 7 + c, half, stride=15), :] = jnp.where(low, odds[c - 1], odd)


def half_chunks(lines):
    even = [(lines[0], 0), (lines[0], 1), (lines[1], 0), (lines[1], 1), (lines[2], 0)]
    odd = [(lines[2], 1), (lines[3], 0), (lines[3], 1), (lines[4], 0), (lines[4], 1)]
    return even, odd


def placed(chunk, upper):
    line, side = chunk
    return line if side == upper else pltpu.roll(line, 64, 1)


def unpack_ff_kernel(lines_ref, gate_ref, up_ref, down_ref, scratch, mid):
    phase = pl.program_id(0)
    scratch[...] = lines_ref[...].astype(f32)
    for number, out in ((0, gate_ref), (1, up_ref)):

        @pl.when(phase == number)
        def _():
            def store(c, value):
                out[:, 128 * c : 128 * c + 128] = value.astype(bf16)

            lines_to_rows_2560(scratch, 0, 96, store)

    @pl.when(phase == 2)
    def _():
        def store(c, value):
            if c < 7:
                down_ref[:, 128 * c : 128 * c + 128] = value.astype(bf16)
            else:
                down_ref[:, 896:960] = value[:, :64].astype(bf16)

        lines_to_rows_960(scratch, 0, 256, mid, store)


def pinned(phase):
    def index(p, j):
        return (jnp.where(p == phase, j, jnp.where(p < phase, 0, 9)), 0)

    return index


def unpack_ff(lines):
    return pl.pallas_call(
        unpack_ff_kernel,
        grid=(3, 10),
        in_specs=[pl.BlockSpec((1920, 128), lambda p, j: (p * 10 + j, 0))],
        out_specs=[
            pl.BlockSpec((96, FF), pinned(0)),
            pl.BlockSpec((96, FF), pinned(1)),
            pl.BlockSpec((256, MODEL_WIDTH), pinned(2)),
        ],
        out_shape=[
            jax.ShapeDtypeStruct((MODEL_WIDTH, FF), bf16),
            jax.ShapeDtypeStruct((MODEL_WIDTH, FF), bf16),
            jax.ShapeDtypeStruct((FF, MODEL_WIDTH), bf16),
        ],
        scratch_shapes=[pltpu.VMEM((1920, 128), f32), pltpu.VMEM((256, 128), f32)],
        name="unpack_feedforward",
    )(lines)


def pack_ff_kernel(gate_ref, up_ref, down_ref, lines_ref, scratch, mid):
    phase = pl.program_id(0)
    for number, source in ((0, gate_ref), (1, up_ref)):

        @pl.when(phase == number)
        def _():
            rows_to_lines_2560(
                lambda c: source[:, 128 * c : 128 * c + 128].astype(f32), scratch, 0, 96
            )

    @pl.when(phase == 2)
    def _():
        def load(c):
            if c < 7:
                return down_ref[:, 128 * c : 128 * c + 128].astype(f32)
            tail = down_ref[:, 896:960].astype(f32)
            return jnp.concatenate([tail, tail], axis=1)

        rows_to_lines_960(load, scratch, 0, 256, mid)

    lines_ref[...] = scratch[...].astype(bf16)


def pack_ff(gate, up, down):
    return pl.pallas_call(
        pack_ff_kernel,
        grid=(3, 10),
        in_specs=[
            pl.BlockSpec((96, FF), pinned(0)),
            pl.BlockSpec((96, FF), pinned(1)),
            pl.BlockSpec((256, MODEL_WIDTH), pinned(2)),
        ],
        out_specs=pl.BlockSpec((1920, 128), lambda p, j: (p * 10 + j, 0)),
        out_shape=jax.ShapeDtypeStruct((3 * 19200, 128), bf16),
        scratch_shapes=[pltpu.VMEM((1920, 128), f32), pltpu.VMEM((256, 128), f32)],
        name="pack_feedforward",
    )(gate, up, down)


def unpack_wide_kernel(lines_ref, out_ref, scratch, mid):
    for u in range(4):
        scratch[...] = lines_ref[u].astype(f32)
        base = u * 80

        def store(c, value):
            if c < 7:
                out_ref[base : base + 80, 128 * c : 128 * c + 128] = value.astype(bf16)
            else:
                out_ref[base : base + 80, 896:960] = value[:, :64].astype(bf16)

        lines_to_rows_960(scratch, 0, 80, mid, store)


def unpack_wide(lines, first):
    depth = lines.shape[1]
    return pl.pallas_call(
        unpack_wide_kernel,
        grid=(3,),
        in_specs=[pl.BlockSpec((4, depth, 128), lambda j: (first // 4 + j, 0, 0))],
        out_specs=pl.BlockSpec((320, MODEL_WIDTH), lambda j: (j, 0)),
        out_shape=jax.ShapeDtypeStruct((MODEL_WIDTH, MODEL_WIDTH), bf16),
        scratch_shapes=[pltpu.VMEM((depth, 128), f32), pltpu.VMEM((80, 128), f32)],
        name="unpack_attention",
    )(lines)


def unpack_kv_kernel(key_ref, value_ref, out_ref, key_lines, value_lines, mid):
    low = lane_low(120)
    key_lines[...] = key_ref[0].astype(f32)
    value_lines[...] = value_ref[0].astype(f32)
    keys = half_chunks([key_lines[pl.ds(k, 120, stride=5), :] for k in range(5)])
    values = half_chunks([value_lines[pl.ds(k, 120, stride=5), :] for k in range(5)])
    for h in range(KEY_VALUE_HEADS):
        for parity in range(2):
            mid[pl.ds(parity, 120, stride=2), :] = jnp.where(
                low, placed(keys[parity][h], 0), placed(values[parity][h], 1)
            )
        out_ref[:, 128 * h : 128 * h + 128] = mid[...].astype(bf16)


def unpack_kv(lines):
    depth = lines.shape[1]
    return pl.pallas_call(
        unpack_kv_kernel,
        grid=(4,),
        in_specs=[
            pl.BlockSpec((1, depth, 128), lambda j: (12 + j, 0, 0)),
            pl.BlockSpec((1, depth, 128), lambda j: (16 + j, 0, 0)),
        ],
        out_specs=pl.BlockSpec((240, 2 * KV_WIDTH), lambda j: (j, 0)),
        out_shape=jax.ShapeDtypeStruct((MODEL_WIDTH, 2 * KV_WIDTH), bf16),
        scratch_shapes=[
            pltpu.VMEM((depth, 128), f32),
            pltpu.VMEM((depth, 128), f32),
            pltpu.VMEM((240, 128), f32),
        ],
        name="unpack_key_value",
    )(lines, lines)


def pack_attention_kernel(query_ref, kv_ref, out_weight_ref, gains_ref, lines_ref, scratch, mid):
    step = pl.program_id(0)

    def wide(source):
        for u in range(4):
            base = u * 80

            def load(c):
                if c < 7:
                    return source[base : base + 80, 128 * c : 128 * c + 128].astype(f32)
                tail = source[base : base + 80, 896:960].astype(f32)
                return jnp.concatenate([tail, tail], axis=1)

            rows_to_lines_960(load, scratch, 0, 80, mid)
            lines_ref[u, :LINES, :] = scratch[...].astype(bf16)

    @pl.when(step < 3)
    def _():
        wide(query_ref)

    @pl.when(step >= 5)
    def _():
        wide(out_weight_ref)

    for number, upper in ((3, 0), (4, 1)):

        @pl.when(step == number)
        def _():
            low = lane_low(120)
            for u in range(4):
                evens, odds = [], []
                for h in range(KEY_VALUE_HEADS):
                    mid[...] = kv_ref[
                        240 * u : 240 * u + 240, 128 * h : 128 * h + 128
                    ].astype(f32)
                    evens.append((mid[pl.ds(0, 120, stride=2), :], upper))
                    odds.append((mid[pl.ds(1, 120, stride=2), :], upper))
                run = evens + odds
                for k in range(5):
                    scratch[pl.ds(k, 120, stride=5), :] = jnp.where(
                        low, placed(run[2 * k], 0), placed(run[2 * k + 1], 1)
                    )
                lines_ref[u, :LINES, :] = scratch[...].astype(bf16)

    for u in range(4):
        lines_ref[u, LINES:, :] = gains_ref[u]


def pack_attention(d_query, d_kv, d_out, gains):
    return pl.pallas_call(
        pack_attention_kernel,
        grid=(8,),
        in_specs=[
            pl.BlockSpec((320, MODEL_WIDTH), lambda s: (jnp.minimum(s, 2), 0)),
            pl.BlockSpec((MODEL_WIDTH, 2 * KV_WIDTH), lambda s: (0, 0)),
            pl.BlockSpec((320, MODEL_WIDTH), lambda s: (jnp.maximum(s - 5, 0), 0)),
            pl.BlockSpec((4, GAIN_LINES, 128), lambda s: (s, 0, 0)),
        ],
        out_specs=pl.BlockSpec((4, LINES + GAIN_LINES, 128), lambda s: (s, 0, 0)),
        out_shape=jax.ShapeDtypeStruct((UNITS, LINES + GAIN_LINES, 128), bf16),
        scratch_shapes=[pltpu.VMEM((LINES, 128), f32), pltpu.VMEM((240, 128), f32)],
        name="pack_attention",
    )(d_query, d_kv, d_out, gains)


def tile_range(starts_ref, fills_ref, block):
    first_slot = starts_ref[block] * BLK
    last_slot = block * BLK + fills_ref[block]
    tile_first = first_slot // TILE
    tile_last = (block * BLK) // TILE
    ragged_first = jnp.logical_and(first_slot % TILE != 0, tile_first < tile_last)
    return first_slot, last_slot, tile_first, tile_last, ragged_first.astype(jnp.int32)


def allowed_pairs(tile, block, first_slot, last_slot):
    key_slot = tile * TILE + lax.broadcasted_iota(jnp.int32, (TILE, WIDE), 0)
    lane = lax.broadcasted_iota(jnp.int32, (TILE, WIDE), 1)
    query_slot = block * BLK + lax.rem(lane, BLK)
    return jnp.logical_and(
        jnp.logical_and(key_slot >= first_slot, key_slot <= query_slot),
        jnp.logical_or(key_slot < last_slot, key_slot == query_slot),
    )


def over_tiles(span, block, step):
    first_slot, last_slot, tile_first, tile_last, ragged = span

    def masked(tile):
        step(tile, allowed_pairs(tile, block, first_slot, last_slot))

    def edge(k, carry):
        masked(jnp.where(k == ragged, tile_last, tile_first))
        return carry

    lax.fori_loop(0, 1 + ragged, edge, 0)

    def inner(tile, carry):
        step(tile, None)
        return carry

    lax.fori_loop(tile_first + ragged, tile_last, inner, 0)


def transpose_kv(kv_ref, turned, tiles):
    def body(t, carry):
        rows = pl.ds(pl.multiple_of(t * TILE, TILE), TILE)
        for h in range(KEY_VALUE_HEADS):
            turned[t, 128 * h : 128 * h + 128, :] = kv_ref[rows, 128 * h : 128 * h + 128].T
        return carry

    lax.fori_loop(0, tiles, body, 0)


def lay_out_kv(blocks, kv_ref, place):
    size = blocks[0].shape[0]
    for apart, block in enumerate(blocks):
        spot = apart if len(blocks) == 1 else place ^ apart
        kv_ref[pl.ds(pl.multiple_of(spot * size, TILE), size), :] = block[...]


def heads_beside(ref, h):
    return jnp.concatenate(
        [
            ref[HEAD_SIZE * (GROUPED * h + g) : HEAD_SIZE * (GROUPED * h + g + 1), :]
            for g in range(GROUPED)
        ],
        axis=1,
    )


def attention_forward_kernel(
    starts_ref, fills_ref, place_ref, query_ref, *refs
):
    kv_blocks = refs[:-8]
    mixed_ref, log_ref, kv_ref, turned, pairs, tops, totals, sums = refs[-8:]
    i = pl.program_id(0)
    block = place_ref[0] * (TOK_DEV // BLK) + i

    @pl.when(i == 0)
    def _():
        lay_out_kv(kv_blocks, kv_ref, place_ref[0])
        transpose_kv(kv_ref, turned, kv_ref.shape[0] // TILE)

    for h in range(KEY_VALUE_HEADS):
        pairs[h, :HEAD_SIZE, :] = heads_beside(query_ref, h)
        pairs[h, HEAD_SIZE:, :] = jnp.zeros((HEAD_SIZE, WIDE), bf16)
    tops[...] = jnp.full(tops.shape, masked_value, f32)
    totals[...] = jnp.zeros(totals.shape, f32)
    sums[...] = jnp.zeros(sums.shape, f32)

    def step(tile, allowed):
        rows = pl.ds(pl.multiple_of(tile * TILE, TILE), TILE)
        for h in range(KEY_VALUE_HEADS):
            scores = jnp.dot(
                kv_ref[rows, 128 * h : 128 * h + 128], pairs[h], preferred_element_type=f32
            )
            if allowed is not None:
                scores = jnp.where(allowed, scores, masked_value)
            top_old = tops[h]
            top = jnp.maximum(top_old, jnp.max(scores, axis=0, keepdims=True))
            weights = jnp.exp(scores - top)
            shrink = jnp.exp(top_old - top)
            tops[h] = top
            totals[h] = totals[h] * shrink + jnp.sum(weights, axis=0, keepdims=True)
            sums[h] = sums[h] * shrink + jnp.dot(
                turned[tile, 128 * h + HEAD_SIZE : 128 * h + 128, :],
                weights.astype(bf16),
                preferred_element_type=f32,
            )

    over_tiles(tile_range(starts_ref, fills_ref, block), block, step)
    for h in range(KEY_VALUE_HEADS):
        outcome = (sums[h] / totals[h]).astype(bf16)
        log_total = tops[h] + jnp.log(totals[h])
        for g in range(GROUPED):
            head = GROUPED * h + g
            mixed_ref[HEAD_SIZE * head : HEAD_SIZE * (head + 1), :] = outcome[:, BLK * g : BLK * (g + 1)]
            log_ref[head : head + 1, :] = log_total[:, BLK * g : BLK * (g + 1)]
    log_ref[QUERY_HEADS:, :] = jnp.zeros((1, BLK), f32)


def token_block(rows):
    return pl.BlockSpec((rows, BLK), lambda i, *_: (0, i))


def whole(shape):
    return pl.BlockSpec(shape, lambda i, *_: (0,) * len(shape))


def attention_forward(starts, fills, place, query, kv):
    group = sum(block.shape[0] for block in kv)
    return pl.pallas_call(
        attention_forward_kernel,
        grid_spec=pltpu.PrefetchScalarGridSpec(
            num_scalar_prefetch=3,
            grid=(TOK_DEV // BLK,),
            in_specs=[token_block(MODEL_WIDTH)] + [whole(block.shape) for block in kv],
            out_specs=[token_block(MODEL_WIDTH), token_block(16)],
            scratch_shapes=[
                pltpu.VMEM((group, 2 * KV_WIDTH), bf16),
                pltpu.VMEM((group // TILE, 2 * KV_WIDTH, TILE), bf16),
                pltpu.VMEM((KEY_VALUE_HEADS, 2 * HEAD_SIZE, WIDE), bf16),
                pltpu.VMEM((KEY_VALUE_HEADS, 1, WIDE), f32),
                pltpu.VMEM((KEY_VALUE_HEADS, 1, WIDE), f32),
                pltpu.VMEM((KEY_VALUE_HEADS, HEAD_SIZE, WIDE), f32),
            ],
        ),
        out_shape=[
            jax.ShapeDtypeStruct((MODEL_WIDTH, TOK_DEV), bf16),
            jax.ShapeDtypeStruct((16, TOK_DEV), f32),
        ],
        name="attention_forward",
    )(starts, fills, place, query, *kv)


def attention_backward_kernel(
    first,
    blocks,
    starts_ref,
    fills_ref,
    place_ref,
    query_ref,
    upstream_ref,
    mixed_ref,
    log_ref,
    cosine_ref,
    sine_ref,
    *refs,
):
    kv_blocks, refs = refs[:blocks], refs[-(blocks + 10) :]
    d_query_ref, d_kv_blocks = refs[0], refs[1 : blocks + 1]
    kv_ref, turned, pairs, query_rows, upstream_rows, deltas, logs, sums, kv_sums = refs[blocks + 1 :]
    count = kv_sums.shape[0]
    i = pl.program_id(0)
    block = place_ref[0] * (TOK_DEV // BLK) + i
    tiles = kv_ref.shape[0] // TILE

    @pl.when(i == 0)
    def _():
        for apart, source in enumerate(kv_blocks):
            size = source.shape[0]
            spot = apart if blocks == 1 else place_ref[0] ^ apart
            kv_ref[pl.ds(pl.multiple_of(spot * size, TILE), size), :] = source[
                :, 128 * first : 128 * (first + count)
            ]

        def prepare(t, carry):
            rows = pl.ds(pl.multiple_of(t * TILE, TILE), TILE)
            for h in range(count):
                turned[t, HEAD_SIZE * h : HEAD_SIZE * (h + 1), :] = kv_ref[
                    rows, 128 * h : 128 * h + 128
                ].T[:HEAD_SIZE]
            kv_sums[:, rows, :] = jnp.zeros((count, TILE, 128), f32)
            return carry

        lax.fori_loop(0, tiles, prepare, 0)

    blank = jnp.zeros((HEAD_SIZE, WIDE), bf16)
    for h in range(count):
        query = heads_beside(query_ref, first + h)
        upstream = heads_beside(upstream_ref, first + h)
        pairs[h, :HEAD_SIZE, :WIDE] = query
        pairs[h, HEAD_SIZE:, :WIDE] = blank
        pairs[h, :HEAD_SIZE, WIDE:] = blank
        pairs[h, HEAD_SIZE:, WIDE:] = upstream
        query_rows[h] = pairs[h, :, :WIDE].T
        upstream_rows[h] = pairs[h, :, WIDE:].T
        deltas[h] = jnp.sum(
            upstream.astype(f32) * heads_beside(mixed_ref, first + h).astype(f32),
            axis=0,
            keepdims=True,
        )
        line = GROUPED * (first + h)
        logs[h] = jnp.concatenate(
            [log_ref[line + g : line + g + 1, :] for g in range(GROUPED)], axis=1
        )
    sums[...] = jnp.zeros(sums.shape, f32)

    def step(tile, allowed):
        rows = pl.ds(pl.multiple_of(tile * TILE, TILE), TILE)
        for h in range(count):
            both = jnp.dot(
                kv_ref[rows, 128 * h : 128 * h + 128], pairs[h], preferred_element_type=f32
            )
            scores = both[:, :WIDE]
            if allowed is not None:
                scores = jnp.where(allowed, scores, masked_value)
            probs = jnp.exp(scores - logs[h])
            d_scores = (probs * (both[:, WIDE:] - deltas[h])).astype(bf16)
            kv_sums[h, rows, :] += jnp.dot(
                d_scores, query_rows[h], preferred_element_type=f32
            ) + jnp.dot(probs.astype(bf16), upstream_rows[h], preferred_element_type=f32)
            sums[h] += jnp.dot(
                turned[tile, HEAD_SIZE * h : HEAD_SIZE * (h + 1), :],
                d_scores,
                preferred_element_type=f32,
            )

    over_tiles(tile_range(starts_ref, fills_ref, block), block, step)
    cosine = cosine_ref[...]
    sine = sine_ref[...]
    half = HEAD_SIZE // 2
    for h in range(count):
        for g in range(GROUPED):
            head = GROUPED * h + g
            front = sums[h, :half, BLK * g : BLK * (g + 1)] * score_scale
            back = sums[h, half:, BLK * g : BLK * (g + 1)] * score_scale
            d_query_ref[HEAD_SIZE * head : HEAD_SIZE * head + half, :] = (
                front * cosine + back * sine
            ).astype(bf16)
            d_query_ref[HEAD_SIZE * head + half : HEAD_SIZE * (head + 1), :] = (
                back * cosine - front * sine
            ).astype(bf16)

    @pl.when(i == pl.num_programs(0) - 1)
    def _():
        size = kv_blocks[0].shape[0]
        for apart, out in enumerate(d_kv_blocks):
            spot = apart if blocks == 1 else place_ref[0] ^ apart

            def emit(t, carry):
                rows = pl.ds(pl.multiple_of(spot * size + t * TILE, TILE), TILE)
                for h in range(count):
                    out[pl.ds(pl.multiple_of(t * TILE, TILE), TILE), 128 * h : 128 * h + 128] = (
                        kv_sums[h, rows, :].astype(bf16)
                    )
                return carry

            lax.fori_loop(0, size // TILE, emit, 0)


def attention_backward(
    first, count, starts, fills, place, query, upstream, mixed, logs, cosine, sine, kv, after=()
):
    group = sum(block.shape[0] for block in kv)
    half = HEAD_SIZE // 2
    outs = [(block.shape[0], 128 * count) for block in kv]
    return pl.pallas_call(
        functools.partial(attention_backward_kernel, first, len(kv)),
        grid_spec=pltpu.PrefetchScalarGridSpec(
            num_scalar_prefetch=3,
            grid=(TOK_DEV // BLK,),
            in_specs=[
                token_block(MODEL_WIDTH),
                token_block(MODEL_WIDTH),
                token_block(MODEL_WIDTH),
                token_block(16),
                token_block(half),
                token_block(half),
            ]
            + [whole(block.shape) for block in kv]
            + [pl.BlockSpec(memory_space=pl.ANY)] * len(after),
            out_specs=[token_block(GROUPED * HEAD_SIZE * count)] + [whole(shape) for shape in outs],
            scratch_shapes=[
                pltpu.VMEM((group, 128 * count), bf16),
                pltpu.VMEM((group // TILE, HEAD_SIZE * count, TILE), bf16),
                pltpu.VMEM((count, 2 * HEAD_SIZE, 2 * WIDE), bf16),
                pltpu.VMEM((count, WIDE, 128), bf16),
                pltpu.VMEM((count, WIDE, 128), bf16),
                pltpu.VMEM((count, 1, WIDE), f32),
                pltpu.VMEM((count, 1, WIDE), f32),
                pltpu.VMEM((count, HEAD_SIZE, WIDE), f32),
                pltpu.VMEM((count, group, 128), f32),
            ],
        ),
        out_shape=[jax.ShapeDtypeStruct((GROUPED * HEAD_SIZE * count, TOK_DEV), bf16)]
        + [jax.ShapeDtypeStruct(shape, bf16) for shape in outs],
        name="attention_backward",
    )(starts, fills, place, query, upstream, mixed, logs, cosine, sine, *kv, *after)


def dot_of(left, right, left_dim, right_dim):
    return lax.dot_general(
        left, right, (((left_dim,), (right_dim,)), ((), ())), preferred_element_type=f32
    )


SLOTS = 3
FORM = 640
PERMUTED = 1
COLOURS = 2
SLABS = 20 // COLOURS
PIECES = (240, 240, 160)
GAIN_LINE = 560
PAD_WIDTH = 1024
CHUNK = 640
CORE_BIT = ("shard", 1)
ROW_BIT = ("shard", 2)
NEAR_BITS = (ROW_BIT, ("dp", 1), ("dp", 2))
FAR_BITS = (("dp", 4),)
BACKWARD_CALLS = ((0, 5),)


def stages(colour):
    return (CORE_BIT,) + NEAR_BITS[colour:] + NEAR_BITS[:colour] + FAR_BITS


def swap(value, bit):
    axis, mask = bit
    size = lax.axis_size(axis)
    return lax.ppermute(value, axis, [(i, i ^ mask) for i in range(size)])


def gather_colour(own, colour):
    held = own[None]
    for bit in reversed(stages(colour)[1:]):
        held = jnp.concatenate([held, swap(held, bit)], axis=0)
    return held, swap(held, CORE_BIT)


def scatter_stage(held, number):
    outcome = []
    total = lambda parts: sum(part.astype(f32) for part in parts)
    for colour, (parts, send) in enumerate(held):
        got = swap(send, stages(colour)[number])
        half = got.shape[0] // 2
        if half == 0:
            outcome.append((total(parts)[0].astype(bf16), got[0]))
        else:
            parts = parts + [got]
            outcome.append(
                ([part[:half] for part in parts], total([part[half:] for part in parts]).astype(bf16))
            )
    return outcome


def positions():
    device = jnp.arange(UNITS, dtype=jnp.int32)
    width = lax.axis_size("shard")
    apart = {
        "dp": (device // width) ^ lax.axis_index("dp").astype(jnp.int32),
        "shard": (device % width) ^ lax.axis_index("shard").astype(jnp.int32),
    }
    tables = []
    for colour in range(SLOTS):
        place = jnp.zeros((UNITS,), jnp.int32)
        for axis, mask in stages(colour):
            place = 2 * place + (apart[axis] & mask) // mask
        tables.append(place)
    return jnp.concatenate(tables)


def copy_from(halves, place, dst, sem, pick=lambda ref: ref):
    for number, ref in enumerate(halves):

        @pl.when(place // 16 == number)
        def _():
            pltpu.make_async_copy(pick(ref.at[lax.rem(place, 16)]), dst, sem).start()


def copy_to(src, halves, place, sem, pick=lambda ref: ref):
    for number, ref in enumerate(halves):

        @pl.when(place // 16 == number)
        def _():
            pltpu.make_async_copy(src, pick(ref.at[lax.rem(place, 16)]), sem).start()


def wait_for(ref, sem):
    pltpu.make_async_copy(ref, ref, sem).wait()


def form_attention_kernel(wide_ref, lines_ref, gains_ref, a_ref, b_ref, c_ref, mid, form):
    @pl.when(wide_ref[0] == 1)
    def _():
        def store(c, value):
            if c == 7:
                value = jnp.where(lane_low(80), value, 0.0)
            form[80 * c : 80 * c + 80, :] = value

        lines_to_rows_960(lines_ref, 0, 80, mid, store)

    @pl.when(wide_ref[0] == 0)
    def _():
        low = lane_low(120)
        line = [lines_ref[pl.ds(k, 120, stride=5), :] for k in range(5)]
        turned = [None, None] + [pltpu.roll(line[k], 64, 1) for k in range(2, 5)]
        form[pl.ds(0, 120, stride=2), :] = line[0]
        form[pl.ds(1, 120, stride=2), :] = jnp.where(low, turned[2], turned[3])
        form[pl.ds(240, 120, stride=2), :] = line[1]
        form[pl.ds(241, 120, stride=2), :] = jnp.where(low, turned[3], turned[4])
        mid[pl.ds(0, 120, stride=2), :] = line[2]
        mid[pl.ds(1, 120, stride=2), :] = turned[4]
        low = lane_low(80)
        form[480:560, :] = jnp.where(low, mid[0:80, :], pltpu.roll(mid[160:240, :], 64, 1))
        form[560:640, :] = jnp.where(low, mid[80:160, :], 0.0)

    form[GAIN_LINE : GAIN_LINE + 1, :] = jnp.where(
        lane_low(1), form[GAIN_LINE : GAIN_LINE + 1, :], gains_ref[...]
    )
    a_ref[...] = form[0:240, :].astype(bf16)
    b_ref[...] = form[240:480, :].astype(bf16)
    c_ref[...] = form[480:640, :].astype(bf16)


SMEM_SPEC = pl.BlockSpec(memory_space=pltpu.SMEM)
ANY_SPEC = pl.BlockSpec(memory_space=pl.ANY)


def form_attention(wide, lines, gains):
    return pl.pallas_call(
        form_attention_kernel,
        in_specs=[SMEM_SPEC, pl.BlockSpec((LINES, 128)), pl.BlockSpec((1, 128))],
        out_shape=[jax.ShapeDtypeStruct((n, 128), bf16) for n in PIECES],
        scratch_shapes=[pltpu.VMEM((240, 128), f32), pltpu.VMEM((FORM, 128), f32)],
        name="form_attention",
    )(wide, lines, gains)


def unform_attention_kernel(wide_ref, *refs):
    pieces, (lines_ref, gains_ref, mid, form) = refs[:6], refs[6:]
    base = 0
    for n, keep, got in zip(PIECES, pieces[0::2], pieces[1::2]):
        form[base : base + n, :] = keep[...].astype(f32) + got[...].astype(f32)
        base += n
    gains_ref[...] = form[GAIN_LINE : GAIN_LINE + 1, :]

    @pl.when(wide_ref[0] == 1)
    def _():
        rows_to_lines_960(lambda c: form[80 * c : 80 * c + 80, :], lines_ref, 0, 80, mid)

    @pl.when(wide_ref[0] == 0)
    def _():
        low = lane_low(120)
        mid[0:80, :] = form[480:560, :]
        mid[80:160, :] = form[560:640, :]
        mid[160:240, :] = pltpu.roll(form[480:560, :], 64, 1)
        even = [form[pl.ds(0, 120, stride=2), :], form[pl.ds(240, 120, stride=2), :]]
        odd = [form[pl.ds(1, 120, stride=2), :], form[pl.ds(241, 120, stride=2), :]]
        even.append(mid[pl.ds(0, 120, stride=2), :])
        odd.append(mid[pl.ds(1, 120, stride=2), :])
        odd = [pltpu.roll(value, 64, 1) for value in odd]
        lines_ref[pl.ds(0, 120, stride=5), :] = even[0]
        lines_ref[pl.ds(1, 120, stride=5), :] = even[1]
        lines_ref[pl.ds(2, 120, stride=5), :] = jnp.where(low, even[2], odd[0])
        lines_ref[pl.ds(3, 120, stride=5), :] = jnp.where(low, odd[0], odd[1])
        lines_ref[pl.ds(4, 120, stride=5), :] = jnp.where(low, odd[1], odd[2])


def unform_attention(wide, addends):
    return pl.pallas_call(
        unform_attention_kernel,
        in_specs=[SMEM_SPEC] + [pl.BlockSpec((n, 128)) for n in PIECES for _ in range(2)],
        out_shape=[jax.ShapeDtypeStruct((LINES, 128), f32), jax.ShapeDtypeStruct((1, 128), f32)],
        scratch_shapes=[pltpu.VMEM((240, 128), f32), pltpu.VMEM((FORM, 128), f32)],
        name="unform_attention",
    )(wide, *addends)


def wide_pieces(c):
    return [((80 * c + 16 * m) // 32, (80 * c + 16 * m) % 32, 16 * m) for m in range(5)]


def form_feedforward_kernel(narrow_ref, lines_ref, out, mid):
    for s in range(SLOTS):

        @pl.when(narrow_ref[s] == 1)
        def _():
            mid[30:32, :] = jnp.zeros((2, 128), f32)
            for c in range(20):
                mid[0:30, :] = lines_ref[pl.ds(LINES * s + c, 30, stride=20), :]
                out[s, c] = mid[0:32, :].astype(bf16)

        @pl.when(narrow_ref[s] == 0)
        def _():
            def store(c, value):
                if c == 7:
                    value = jnp.where(lane_low(80), value, 0.0)
                for k, r, m in wide_pieces(c):
                    out[s, k, r : r + 16, :] = value[m : m + 16].astype(bf16)

            lines_to_rows_960(lines_ref, LINES * s, 80, mid, store)


def form_feedforward(narrow, lines):
    return pl.pallas_call(
        form_feedforward_kernel,
        in_specs=[SMEM_SPEC, pl.BlockSpec((SLOTS * LINES, 128))],
        out_shape=jax.ShapeDtypeStruct((SLOTS, 20, 32, 128), bf16),
        scratch_shapes=[pltpu.VMEM((80, 128), f32)],
        name="form_feedforward",
    )(narrow, lines)


def unform_feedforward_kernel(narrow_ref, *refs):
    addends, (terms, lines_ref, mid) = refs[: 2 * COLOURS], refs[2 * COLOURS :]

    def term(s, k, rows):
        if s >= PERMUTED:
            return terms[s - PERMUTED, k, rows, :].astype(f32)
        keep, got = addends[2 * (k // SLABS) : 2 * (k // SLABS) + 2]
        return keep[k % SLABS, rows, :].astype(f32) + got[k % SLABS, rows, :].astype(f32)

    for s in range(SLOTS):

        @pl.when(narrow_ref[s] == 1)
        def _():
            for c in range(20):
                mid[0:32, :] = term(s, c, slice(0, 32))
                lines_ref[pl.ds(LINES * s + c, 30, stride=20), :] = mid[0:30, :]

        @pl.when(narrow_ref[s] == 0)
        def _():
            def load(c):
                return jnp.concatenate(
                    [term(s, k, slice(r, r + 16)) for k, r, m in wide_pieces(c)], axis=0
                )

            rows_to_lines_960(load, lines_ref, LINES * s, 80, mid)


def unform_feedforward(narrow, addends, terms):
    return pl.pallas_call(
        unform_feedforward_kernel,
        in_specs=[SMEM_SPEC]
        + [pl.BlockSpec((SLABS, 32, 128))] * (2 * COLOURS)
        + [pl.BlockSpec((SLOTS - PERMUTED, 20, 32, 128))],
        out_shape=jax.ShapeDtypeStruct((SLOTS * LINES, 128), f32),
        scratch_shapes=[pltpu.VMEM((80, 128), f32)],
        name="unform_feedforward",
    )(narrow, *addends, terms)


def place_attention_kernel(table_ref, *refs):
    halves = [refs[2 * k : 2 * k + 2] for k in range(SLOTS)]
    query_ref, kv_ref, out_ref, gains_ref, units, sem = refs[2 * SLOTS :]

    def start(d, carry):
        base = 0
        for k, n in enumerate(PIECES):
            copy_from(halves[k], table_ref[UNITS * k + d], units.at[d, base : base + n, :], sem)
            base += n
        return carry

    lax.fori_loop(0, UNITS, start, 0)
    wait_for(units, sem)

    def wide(out, first):
        def body(u, carry):
            rows = pl.ds(pl.multiple_of(80 * u, 16), 80)
            for c in range(7):
                out[rows, 128 * c : 128 * c + 128] = units[first + u, 80 * c : 80 * c + 80, :]
            out[rows, 896:960] = units[first + u, 560:640, :64]
            return carry

        lax.fori_loop(0, 12, body, 0)

    def keyed(j, carry):
        low = lane_low(240)
        chunks = []
        for first in (12, 16):
            unit = units[first + j].astype(f32)
            last = jnp.concatenate(
                [unit[480:640], pltpu.roll(unit[480:560], 64, 1)], axis=0
            )
            lines = (unit[0:240], unit[240:480], last)
            chunks.append([(lines[h // 2], h % 2) for h in range(KEY_VALUE_HEADS)])
        rows = pl.ds(pl.multiple_of(240 * j, 16), 240)
        for h in range(KEY_VALUE_HEADS):
            kv_ref[rows, 128 * h : 128 * h + 128] = jnp.where(
                low, placed(chunks[0][h], 0), placed(chunks[1][h], 1)
            ).astype(bf16)
        return carry

    lax.fori_loop(0, 4, keyed, 0)
    wide(query_ref, 0)
    wide(out_ref, 20)
    for u in range(UNITS):
        gains_ref[u : u + 1, :] = units[u, GAIN_LINE : GAIN_LINE + 1, :].astype(f32)


def place_attention(table, gathered):
    return pl.pallas_call(
        place_attention_kernel,
        in_specs=[SMEM_SPEC] + [ANY_SPEC] * (2 * SLOTS),
        out_shape=[
            jax.ShapeDtypeStruct((MODEL_WIDTH, MODEL_WIDTH), bf16),
            jax.ShapeDtypeStruct((MODEL_WIDTH, 2 * KV_WIDTH), bf16),
            jax.ShapeDtypeStruct((MODEL_WIDTH, MODEL_WIDTH), bf16),
            jax.ShapeDtypeStruct((UNITS, 128), f32),
        ],
        scratch_shapes=[pltpu.VMEM((UNITS, FORM, 128), bf16), pltpu.SemaphoreType.DMA],
        name="place_attention",
    )(table, *gathered)


def split_attention_kernel(table_ref, query_ref, kv_ref, out_ref, gains_ref, *refs):
    halves = [refs[2 * k : 2 * k + 2] for k in range(SLOTS)]
    units, sem = refs[2 * SLOTS :]

    def send(d):
        row = lax.broadcasted_iota(jnp.int32, (16, 128), 0)
        lane = lax.broadcasted_iota(jnp.int32, (16, 128), 1)
        block = units[d, GAIN_LINE : GAIN_LINE + 16, :].astype(f32)
        units[d, GAIN_LINE : GAIN_LINE + 16, :] = jnp.where(
            jnp.logical_and(row == 0, lane >= 64), gains_ref[pl.ds(d, 1), :], block
        ).astype(bf16)
        base = 0
        for k, n in enumerate(PIECES):
            copy_to(units.at[d, base : base + n, :], halves[k], table_ref[UNITS * k + d], sem)
            base += n

    def wide(source, first):
        def body(u, carry):
            rows = pl.ds(pl.multiple_of(80 * u, 16), 80)
            for c in range(7):
                units[first + u, 80 * c : 80 * c + 80, :] = source[rows, 128 * c : 128 * c + 128]
            tail = source[rows, 896:960]
            units[first + u, 560:640, :] = jnp.concatenate([tail, jnp.zeros_like(tail)], axis=1)
            send(first + u)
            return carry

        lax.fori_loop(0, 12, body, 0)

    def keyed(j, carry):
        low = lane_low(240)
        rows = pl.ds(pl.multiple_of(240 * j, 16), 240)
        for upper, first in ((0, 12), (1, 16)):
            heads = [
                (kv_ref[rows, 128 * h : 128 * h + 128].astype(f32), upper)
                for h in range(KEY_VALUE_HEADS)
            ]
            for c in range(2):
                units[first + j, 240 * c : 240 * c + 240, :] = jnp.where(
                    low, placed(heads[2 * c], 0), placed(heads[2 * c + 1], 1)
                ).astype(bf16)
            last = placed(heads[4], 0)
            turned = placed(heads[4], 1)
            units[first + j, 480:560, :] = jnp.where(
                lane_low(80), last[0:80], turned[160:240]
            ).astype(bf16)
            units[first + j, 560:640, :] = jnp.where(lane_low(80), last[80:160], 0.0).astype(bf16)
            send(first + j)
        return carry

    lax.fori_loop(0, 4, keyed, 0)
    wide(query_ref, 0)
    wide(out_ref, 20)
    wait_for(units, sem)


def split_attention(table, d_query, d_kv, d_out, gains):
    return pl.pallas_call(
        split_attention_kernel,
        in_specs=[
            SMEM_SPEC,
            pl.BlockSpec((MODEL_WIDTH, MODEL_WIDTH)),
            pl.BlockSpec((MODEL_WIDTH, 2 * KV_WIDTH)),
            pl.BlockSpec((MODEL_WIDTH, MODEL_WIDTH)),
            pl.BlockSpec((UNITS, 128)),
        ],
        out_specs=[ANY_SPEC] * (2 * SLOTS),
        out_shape=[jax.ShapeDtypeStruct((16, n, 128), bf16) for n in PIECES for _ in range(2)],
        scratch_shapes=[pltpu.VMEM((UNITS, FORM, 128), bf16), pltpu.SemaphoreType.DMA],
        name="split_attention",
    )(table, d_query, d_kv, d_out, gains)


def feedforward_kernel(
    table_ref,
    hidden_ref,
    turned_ref,
    grad_ref,
    gate_ref,
    up_ref,
    down_ref,
    out_ref,
    d_hidden_ref,
    *refs,
):
    targets = [refs[2 * k : 2 * k + 2] for k in range(COLOURS)]
    terms_ref, down, inner_rows, inner_turned, d_both, both_out, down_out, sems = refs[2 * COLOURS :]
    q = pl.program_id(0)
    chunks = pl.num_programs(0)
    slot = lax.rem(q, 2)

    def send_terms():
        columns = pl.ds(5 * q, 5)
        for u in range(2 * UNITS):
            device, s = divmod(u, SLOTS)
            source = both_out.at[slot, u // UNITS, u % UNITS]
            if s >= PERMUTED:
                place = (SLOTS - PERMUTED) * device + s - PERMUTED
                pltpu.make_async_copy(source, terms_ref.at[place, columns], sems.at[slot, 0]).start()
                continue
            for k in range(COLOURS):

                @pl.when(5 * q // SLABS == k)
                def _():
                    copy_to(
                        source,
                        targets[k],
                        table_ref[UNITS * k + device],
                        sems.at[slot, 0],
                        lambda ref: ref.at[pl.ds(5 * q - SLABS * k, 5)],
                    )

        for v in range(8):
            unit = 2 * UNITS + 8 * q + v
            device = unit // SLOTS
            s = unit - SLOTS * device
            source = down_out.at[slot, v]

            @pl.when(s >= PERMUTED)
            def _():
                place = (SLOTS - PERMUTED) * device + s - PERMUTED
                pltpu.make_async_copy(source, terms_ref.at[place], sems.at[slot, 1]).start()

            @pl.when(s < PERMUTED)
            def _():
                for k in range(COLOURS):
                    copy_to(
                        source.at[pl.ds(SLABS * k, SLABS)],
                        targets[k],
                        table_ref[UNITS * k + device],
                        sems.at[slot, 1],
                    )

    def wait_terms(side):
        wait_for(both_out.at[side], sems.at[side, 0])
        wait_for(down_out.at[side], sems.at[side, 1])

    for v in range(8):
        for c in range(8):
            for k, r, m in wide_pieces(c):
                down[80 * v + m : 80 * v + m + 16, 128 * c : 128 * c + 128] = down_ref[
                    v, k, r : r + 16, :
                ]

    @pl.when(q == 0)
    def _():
        out_ref[...] = jnp.zeros(out_ref.shape, f32)
        d_hidden_ref[...] = jnp.zeros(d_hidden_ref.shape, f32)

    def rows_step(i, carry):
        rows = pl.ds(pl.multiple_of(256 * i, 256), 256)
        weights = jnp.concatenate(
            [ref[:, c].reshape(PAD_WIDTH, 128) for ref in (gate_ref, up_ref) for c in range(5)],
            axis=1,
        )
        both = jnp.dot(hidden_ref[rows, :], weights, preferred_element_type=f32)
        gate, upper = both[:, :CHUNK], both[:, CHUNK:]
        sigmoid_gate = jax.nn.sigmoid(gate)
        activated = gate * sigmoid_gate
        inner = (activated * upper).astype(bf16)
        inner_rows[rows, :] = inner
        out_ref[rows, :] += jnp.dot(inner, down[...], preferred_element_type=f32)
        d_inner = dot_of(grad_ref[rows, :], down[...], 1, 1)
        d_gate = d_inner * upper * sigmoid_gate * (1.0 + gate * (1.0 - sigmoid_gate))
        d_upper = d_inner * activated
        d_pair = jnp.concatenate([d_gate, d_upper], axis=1).astype(bf16)
        d_both[rows, :] = d_pair
        d_hidden_ref[rows, :] += dot_of(d_pair, weights, 1, 1)
        return carry

    lax.fori_loop(0, 2, rows_step, 0)
    inner_turned[...] = inner_rows[...].T

    @pl.when(q >= 2)
    def _():
        wait_terms(slot)

    def both_step(i, carry):
        rows = pl.ds(pl.multiple_of(256 * i, 256), 256)
        terms = jnp.dot(turned_ref[rows, :], d_both[...], preferred_element_type=f32).astype(bf16)
        units = pl.ds(8 * i, 8)
        for c in range(10):
            both_out[slot, c // 5, units, c % 5] = terms[:, 128 * c : 128 * c + 128].reshape(
                8, 32, 128
            )
        return carry

    lax.fori_loop(0, 4, both_step, 0)

    def down_step(i, carry):
        rows = pl.ds(pl.multiple_of(320 * i, 16), 320)
        terms = jnp.dot(
            inner_turned[rows, :], grad_ref[...], preferred_element_type=f32
        ).astype(bf16)
        for v in range(4):
            for c in range(8):
                for k, r, m in wide_pieces(c):
                    down_out[slot, 4 * i + v, k, r : r + 16, :] = terms[
                        80 * v + m : 80 * v + m + 16, 128 * c : 128 * c + 128
                    ]
        return carry

    lax.fori_loop(0, 2, down_step, 0)
    send_terms()

    @pl.when(q == chunks - 1)
    def _():
        for side in range(2):
            wait_terms(side)


def feedforward(table, hidden, turned, grad, weights):
    block = jax.ShapeDtypeStruct((16, SLABS, 32, 128), bf16)
    full = lambda shape: pl.BlockSpec(shape, lambda q: (0, 0))
    return pl.pallas_call(
        feedforward_kernel,
        grid=(FF // CHUNK,),
        in_specs=[
            SMEM_SPEC,
            full((TOK_DEV, PAD_WIDTH)),
            full((PAD_WIDTH, TOK_DEV)),
            full((TOK_DEV, PAD_WIDTH)),
            pl.BlockSpec((32, 5, 32, 128), lambda q: (0, q, 0, 0)),
            pl.BlockSpec((32, 5, 32, 128), lambda q: (1, q, 0, 0)),
            pl.BlockSpec((8, 20, 32, 128), lambda q: (8 + q, 0, 0, 0)),
        ],
        out_specs=[full((TOK_DEV, PAD_WIDTH))] * 2 + [ANY_SPEC] * (2 * COLOURS + 1),
        out_shape=[jax.ShapeDtypeStruct((TOK_DEV, PAD_WIDTH), f32)] * 2
        + [block] * (2 * COLOURS)
        + [jax.ShapeDtypeStruct(((SLOTS - PERMUTED) * UNITS, 20, 32, 128), bf16)],
        scratch_shapes=[
            pltpu.VMEM((CHUNK, PAD_WIDTH), bf16),
            pltpu.VMEM((TOK_DEV, CHUNK), bf16),
            pltpu.VMEM((CHUNK, TOK_DEV), bf16),
            pltpu.VMEM((TOK_DEV, 2 * CHUNK), bf16),
            pltpu.VMEM((2, 2, 32, 5, 32, 128), bf16),
            pltpu.VMEM((2, 8, 20, 32, 128), bf16),
            pltpu.SemaphoreType.DMA((2, 2)),
        ],
        compiler_params=pltpu.CompilerParams(vmem_limit_bytes=60 * 2**20),
        name="feedforward",
    )(table, hidden, turned, grad, weights, weights, weights)


def spread_matrix():
    column = jnp.arange(PAD_WIDTH, dtype=jnp.int32)
    entry = jnp.where(column % 32 < 30, 30 * (column // 32) + column % 32, -1)
    return (jnp.arange(MODEL_WIDTH, dtype=jnp.int32)[:, None] == entry[None, :]).astype(bf16)


def rope_tables(positions):
    steps = jnp.arange(HEAD_SIZE // 2, dtype=f32) * (2.0 / HEAD_SIZE)
    inverse = jnp.exp(-math.log(10000.0) * steps)
    angles = inverse[:, None] * positions.astype(f32)[None, :]
    return (jnp.cos(angles), jnp.sin(angles))


def norm_scale(field):
    return lax.rsqrt(jnp.mean(field * field, axis=1, keepdims=True) + epsilon)


def norm_back(upstream, normed, scale, gain):
    scaled = upstream * gain[None, :]
    return scale * (scaled - normed * jnp.mean(scaled * normed, axis=1, keepdims=True))


def adam_step(grad, moment, second, master):
    moment_new = 0.9 * moment + 0.1 * grad
    second_new = 0.999 * second + 0.001 * grad * grad
    corrected = moment_new / (1.0 - 0.9**ADAM_STEP)
    scaled = second_new / (1.0 - 0.999**ADAM_STEP)
    update = -learning_rate * (corrected / (jnp.sqrt(scaled) + 1e-08) + weight_decay * master)
    return (moment_new, second_new, update)


def gather_lines(block):
    return lax.all_gather(block, ALL_AXES, axis=0, tiled=True)


def scatter_lines(lines):
    return lax.psum_scatter(lines, ALL_AXES, scatter_dimension=0, tiled=True)


def local(
    layer_input,
    cotangent,
    master_attention,
    master_feedforward,
    master_gains,
    first_attention,
    second_attention,
    first_feedforward,
    second_feedforward,
    first_gains,
    second_gains,
    block_start,
    block_fill,
):
    devices = lax.axis_size(ALL_AXES)
    attention_lines = master_attention.shape[0] // 128
    feedforward_lines = master_feedforward.shape[0] // 128
    gain_count = master_gains.shape[0]
    padded = (attention_lines // 16 + 1) * 16

    in_units = devices == UNITS
    if in_units:
        table = positions()
        device = (
            lax.axis_index("dp") * lax.axis_size("shard") + lax.axis_index("shard")
        ).astype(jnp.int32)
        wide = jnp.logical_or(device < 12, device >= 20).astype(jnp.int32)[None]
        narrow = (SLOTS * device + jnp.arange(SLOTS, dtype=jnp.int32) < 2 * UNITS).astype(jnp.int32)
        gain_row = jnp.pad(
            master_gains.reshape(1, gain_count), ((0, 0), (64, 64 - gain_count))
        )
        pieces = form_attention(wide, master_attention.reshape(LINES, 128), gain_row)
        gathered = [half for k in range(SLOTS) for half in gather_colour(pieces[k], k)]
        forms = form_feedforward(narrow, master_feedforward.reshape(SLOTS * LINES, 128))
        feedforward_all = gather_lines(forms.reshape(SLOTS * FORM, 128))
        query_weight, kv_weight, out_weight, gain_rows = place_attention(table, gathered)
        gains_all = gain_rows[:, 64 : 64 + gain_count].reshape(-1)
    else:
        gain_lines = jnp.pad(
            master_gains.astype(bf16).reshape(1, gain_count),
            ((0, padded - attention_lines - 1), (0, 128 - gain_count)),
        )
        attention_block = jnp.concatenate(
            [master_attention.astype(bf16).reshape(attention_lines, 128), gain_lines], axis=0
        )
        by_device = gather_lines(attention_block).reshape(devices, padded, 128)
        feedforward_all = gather_lines(
            master_feedforward.astype(bf16).reshape(feedforward_lines, 128)
        )
        gains_all = by_device[:, attention_lines, :gain_count].reshape(-1).astype(f32)
        units = by_device[:, :attention_lines].reshape(UNITS, LINES, 128)
        query_weight = unpack_wide(units, 0)
        kv_weight = unpack_kv(units)
        out_weight = unpack_wide(units, 20)
    gain_one, gain_two = gains_all[:MODEL_WIDTH], gains_all[MODEL_WIDTH:]

    shard = lax.axis_index("shard").astype(jnp.int32)
    place = shard[None]
    first_row = shard * TOK_DEV
    first_block = shard * (TOK_DEV // BLK)
    local_slots = first_row + jnp.arange(TOK_DEV, dtype=jnp.int32)
    local_starts = lax.dynamic_slice_in_dim(block_start, first_block, TOK_DEV // BLK)
    local_fills = lax.dynamic_slice_in_dim(block_fill, first_block, TOK_DEV // BLK)
    live_rows = local_slots % BLK < jnp.repeat(local_fills, BLK)
    cosine_table, sine_table = rope_tables(local_slots - jnp.repeat(local_starts, BLK) * BLK)

    def rotate(field, scale):
        heads = field.shape[0]
        front = field[:, : HEAD_SIZE // 2]
        back = field[:, HEAD_SIZE // 2 :]
        return (
            jnp.concatenate(
                [
                    front * cosine_table[None] - back * sine_table[None],
                    back * cosine_table[None] + front * sine_table[None],
                ],
                axis=1,
            ).astype(bf16)
            * bf16(scale)
        ).reshape(heads * HEAD_SIZE, TOK_DEV)

    inputs = layer_input.astype(f32)
    scale_one = norm_scale(inputs)
    normed_one = inputs * scale_one
    first_hidden = (normed_one * gain_one[None, :]).astype(bf16)
    kv_turned = dot_of(kv_weight, first_hidden, 0, 1).reshape(
        KEY_VALUE_HEADS, 2, HEAD_SIZE, TOK_DEV
    )
    keys = rotate(kv_turned[:, 0], 1.0).reshape(KEY_VALUE_HEADS, 1, HEAD_SIZE, TOK_DEV)
    values = kv_turned[:, 1:].astype(bf16)
    kv_rows = jnp.concatenate([keys, values], axis=1).reshape(2 * KV_WIDTH, TOK_DEV).T
    if in_units:
        across = swap(kv_rows, ROW_BIT)
        kv_all = [kv_rows, swap(kv_rows, CORE_BIT), across, swap(across, CORE_BIT)]
    else:
        kv_all = [lax.all_gather(kv_rows, "shard", axis=0, tiled=True)]
    query_turned = rotate(
        dot_of(query_weight, first_hidden, 0, 1).reshape(QUERY_HEADS, HEAD_SIZE, TOK_DEV),
        score_scale,
    )
    mixed_turned, logs = attention_forward(block_start, block_fill, place, query_turned, kv_all)
    middle = inputs + dot_of(mixed_turned, out_weight, 0, 0)
    scale_two = norm_scale(middle)
    normed_two = middle * scale_two
    hidden_two = (normed_two * gain_two[None, :]).astype(bf16)

    grad_out = cotangent.astype(f32) * live_rows[:, None].astype(f32)
    grad_low = grad_out.astype(bf16)
    if in_units:
        spread = spread_matrix()
        outcome, d_spread, *ff_terms, ff_rest = feedforward(
            table,
            dot_of(hidden_two, spread, 1, 0).astype(bf16),
            dot_of(spread, hidden_two, 0, 1).astype(bf16),
            jnp.pad(grad_low, ((0, 0), (0, PAD_WIDTH - MODEL_WIDTH))),
            feedforward_all.reshape(3 * UNITS, 20, 32, 128),
        )
        layer_output = middle + outcome[:, :MODEL_WIDTH]
        d_coarse = lax.reduce_precision(d_spread, 8, 7)
        d_hidden_two = dot_of(d_coarse.astype(bf16), spread, 1, 1) + dot_of(
            (d_spread - d_coarse).astype(bf16), spread, 1, 1
        )
        ff_held = [([ff_terms[2 * k]], ff_terms[2 * k + 1]) for k in range(COLOURS)]
        ff_sum = scatter_lines(ff_rest.reshape(-1, 128))
    else:
        gate_weight, up_weight, down_weight = unpack_ff(feedforward_all)
        gate = dot_of(hidden_two, gate_weight, 1, 0)
        upper = dot_of(hidden_two, up_weight, 1, 0)
        sigmoid_gate = jax.nn.sigmoid(gate)
        activated = gate * sigmoid_gate
        inner = (activated * upper).astype(bf16)
        layer_output = middle + dot_of(inner, down_weight, 1, 0)
        d_down_weight = dot_of(inner, grad_low, 0, 0).astype(bf16)
        d_inner = dot_of(grad_low, down_weight, 1, 1)
        d_gate = (
            d_inner * upper * sigmoid_gate * (1.0 + gate * (1.0 - sigmoid_gate))
        ).astype(bf16)
        d_upper = (d_inner * activated).astype(bf16)
        d_gate_weight = dot_of(hidden_two, d_gate, 0, 0).astype(bf16)
        d_up_weight = dot_of(hidden_two, d_upper, 0, 0).astype(bf16)
        d_hidden_two = dot_of(d_gate, gate_weight, 1, 1) + dot_of(d_upper, up_weight, 1, 1)
        feedforward_gradient = (
            scatter_lines(pack_ff(d_gate_weight, d_up_weight, d_down_weight))
            .astype(f32)
            .reshape(-1)
        )

    d_gain_two = jnp.sum(d_hidden_two * normed_two, axis=0)
    d_middle = grad_out + norm_back(d_hidden_two, normed_two, scale_two, gain_two)

    d_branch = d_middle.astype(bf16)
    d_out_weight = dot_of(mixed_turned, d_branch, 1, 0).astype(bf16)
    d_mixed = dot_of(out_weight, d_branch, 1, 1).astype(bf16)
    backward_of = lambda first, count, after: attention_backward(
        first,
        count,
        block_start,
        block_fill,
        place,
        query_turned,
        d_mixed,
        mixed_turned,
        logs,
        cosine_table,
        sine_table,
        kv_all,
        after,
    )
    if in_units:
        d_query, d_kv_rows = [], []
        for number, (first, count) in enumerate(BACKWARD_CALLS):
            ff_held = scatter_stage(ff_held, number)
            d_query_part, *d_kv = backward_of(first, count, [send for _, send in ff_held])
            across = d_kv[2] + swap(d_kv[3], CORE_BIT)
            d_query.append(d_query_part)
            d_kv_rows.append(d_kv[0] + swap(d_kv[1], CORE_BIT) + swap(across, ROW_BIT))
        d_query = jnp.concatenate(d_query, axis=0)
        d_kv_rows = jnp.concatenate(d_kv_rows, axis=1)
        for number in range(len(BACKWARD_CALLS), len(stages(0))):
            ff_held = scatter_stage(ff_held, number)
        ff_addends = [addend for pair in ff_held for addend in pair]
        feedforward_gradient = unform_feedforward(
            narrow, ff_addends, ff_sum.reshape(SLOTS - PERMUTED, 20, 32, 128)
        ).reshape(-1)
    else:
        d_query, d_kv = backward_of(0, KEY_VALUE_HEADS, ())
        d_kv_rows = lax.psum_scatter(d_kv, "shard", scatter_dimension=0, tiled=True)
    d_kv_turned = d_kv_rows.T.reshape(KEY_VALUE_HEADS, 2, HEAD_SIZE, TOK_DEV)
    d_front = d_kv_turned[:, 0, : HEAD_SIZE // 2].astype(f32)
    d_back = d_kv_turned[:, 0, HEAD_SIZE // 2 :].astype(f32)
    d_keys = jnp.concatenate(
        [
            d_front * cosine_table[None] + d_back * sine_table[None],
            d_back * cosine_table[None] - d_front * sine_table[None],
        ],
        axis=1,
    ).astype(bf16)
    d_kv_lin = jnp.concatenate([d_keys[:, None], d_kv_turned[:, 1:]], axis=1).reshape(
        2 * KV_WIDTH, TOK_DEV
    )
    d_query_weight = dot_of(first_hidden, d_query, 0, 1).astype(bf16)
    d_kv_weight = dot_of(first_hidden, d_kv_lin, 0, 1).astype(bf16)
    d_hidden_one = dot_of(d_query, query_weight, 0, 1) + dot_of(d_kv_lin, kv_weight, 0, 1)
    d_gain_one = jnp.sum(d_hidden_one * normed_one, axis=0)
    input_gradient = d_middle + norm_back(d_hidden_one, normed_one, scale_one, gain_one)

    gain_terms = jnp.concatenate([d_gain_one, d_gain_two])
    if in_units:
        gain_rows = jnp.pad(
            gain_terms.reshape(UNITS, gain_count), ((0, 0), (64, 64 - gain_count))
        )
        terms = split_attention(table, d_query_weight, d_kv_weight, d_out_weight, gain_rows)
        held = [([terms[2 * k]], terms[2 * k + 1]) for k in range(SLOTS)]
        for number in range(len(stages(0))):
            held = scatter_stage(held, number)
        addends = [addend for pair in held for addend in pair]
        attention_sum, gain_sum = unform_attention(wide, addends)
        attention_gradient = attention_sum.reshape(-1)
        gains_gradient = gain_sum[0, 64 : 64 + gain_count]
    else:
        no_gains = jnp.zeros((UNITS, GAIN_LINES, 128), bf16)
        terms = pack_attention(d_query_weight, d_kv_weight, d_out_weight, no_gains)
        terms = jnp.concatenate(
            [
                terms[:, :LINES].reshape(devices, attention_lines, 128),
                jnp.pad(
                    gain_terms.astype(bf16).reshape(devices, 1, gain_count),
                    ((0, 0), (0, padded - attention_lines - 1), (0, 128 - gain_count)),
                ),
            ],
            axis=1,
        )
        summed = scatter_lines(terms.reshape(devices * padded, 128)).astype(f32)
        attention_gradient = summed[:attention_lines].reshape(-1)
        gains_gradient = summed[attention_lines, :gain_count]

    attention_first, attention_second, attention_update = adam_step(
        attention_gradient, first_attention, second_attention, master_attention
    )
    feedforward_first, feedforward_second, feedforward_update = adam_step(
        feedforward_gradient, first_feedforward, second_feedforward, master_feedforward
    )
    gains_first, gains_second, gains_update = adam_step(
        gains_gradient, first_gains, second_gains, master_gains
    )
    return (
        layer_output,
        input_gradient,
        attention_gradient,
        feedforward_gradient,
        gains_gradient,
        attention_first,
        attention_second,
        feedforward_first,
        feedforward_second,
        gains_first,
        gains_second,
        attention_update,
        feedforward_update,
        gains_update,
    )


def solution(mesh):
    rows = P(ALL_AXES, None)
    flat = P(ALL_AXES)
    return jax.shard_map(
        local,
        mesh=mesh,
        in_specs=(rows, rows) + (flat,) * 9 + (P("dp"), P("dp")),
        out_specs=(rows, rows) + (flat,) * 12,
        check_vma=False,
    )
```

```python
import functools
import math

import jax
import jax.numpy as jnp
from jax import lax
from jax.experimental import pallas as pl
from jax.experimental.pallas import tpu as pltpu
from jax.sharding import PartitionSpec as P

MODEL_WIDTH = 960
QUERY_HEADS = 15
KEY_VALUE_HEADS = 5
GROUPED = QUERY_HEADS // KEY_VALUE_HEADS
HEAD_SIZE = 64
FF = 2560
BLK = 128
ADAM_STEP = 10
TOK_DEV = 512
KV_WIDTH = KEY_VALUE_HEADS * HEAD_SIZE
TILE = 256
WIDE = GROUPED * BLK
UNITS = 32
LINES = 600
GAIN_LINES = 8
ALL_AXES = ("dp", "shard")

epsilon = 1e-05
masked_value = -1e30
learning_rate = 0.03
weight_decay = 0.1
score_scale = 1.0 / math.sqrt(HEAD_SIZE)
f32 = jnp.float32
bf16 = jnp.bfloat16


def lines_to_rows_2560(scratch, base, rows, store):
    for c in range(20):
        store(c, scratch[pl.ds(base + c, rows, stride=20), :])


def rows_to_lines_2560(load, scratch, base, rows):
    for c in range(20):
        scratch[pl.ds(base + c, rows, stride=20), :] = load(c)


def lane_low(rows):
    return lax.broadcasted_iota(jnp.int32, (rows, 128), 1) < 64


def lines_to_rows_960(scratch, base, rows, mid, store):
    half = rows // 2
    low = lane_low(half)
    line = [scratch[pl.ds(base + k, half, stride=15), :] for k in range(15)]
    turned = [None] * 7 + [pltpu.roll(line[k], 64, 1) for k in range(7, 15)]
    for c in range(8):
        mid[pl.ds(0, half, stride=2), :] = line[c]
        odd = jnp.where(low, turned[7 + c], turned[8 + c]) if c < 7 else turned[14]
        mid[pl.ds(1, half, stride=2), :] = odd
        store(c, mid[pl.ds(0, rows), :])


def rows_to_lines_960(load, scratch, base, rows, mid):
    half = rows // 2
    low = lane_low(half)
    odds = []
    for c in range(8):
        mid[pl.ds(0, rows), :] = load(c)
        even = mid[pl.ds(0, half, stride=2), :]
        odd = pltpu.roll(mid[pl.ds(1, half, stride=2), :], 64, 1)
        odds.append(odd)
        if c < 7:
            scratch[pl.ds(base + c, half, stride=15), :] = even
        else:
            scratch[pl.ds(base + 7, half, stride=15), :] = jnp.where(low, even, odds[0])
        if c > 0:
            scratch[pl.ds(base + 7 + c, half, stride=15), :] = jnp.where(low, odds[c - 1], odd)


def half_chunks(lines):
    even = [(lines[0], 0), (lines[0], 1), (lines[1], 0), (lines[1], 1), (lines[2], 0)]
    odd = [(lines[2], 1), (lines[3], 0), (lines[3], 1), (lines[4], 0), (lines[4], 1)]
    return even, odd


def placed(chunk, upper):
    line, side = chunk
    return line if side == upper else pltpu.roll(line, 64, 1)


def unpack_ff_kernel(lines_ref, gate_ref, up_ref, down_ref, scratch, mid):
    phase = pl.program_id(0)
    scratch[...] = lines_ref[...].astype(f32)
    for number, out in ((0, gate_ref), (1, up_ref)):

        @pl.when(phase == number)
        def _():
            def store(c, value):
                out[:, 128 * c : 128 * c + 128] = value.astype(bf16)

            lines_to_rows_2560(scratch, 0, 96, store)

    @pl.when(phase == 2)
    def _():
        def store(c, value):
            if c < 7:
                down_ref[:, 128 * c : 128 * c + 128] = value.astype(bf16)
            else:
                down_ref[:, 896:960] = value[:, :64].astype(bf16)

        lines_to_rows_960(scratch, 0, 256, mid, store)


def pinned(phase):
    def index(p, j):
        return (jnp.where(p == phase, j, jnp.where(p < phase, 0, 9)), 0)

    return index


def unpack_ff(lines):
    return pl.pallas_call(
        unpack_ff_kernel,
        grid=(3, 10),
        in_specs=[pl.BlockSpec((1920, 128), lambda p, j: (p * 10 + j, 0))],
        out_specs=[
            pl.BlockSpec((96, FF), pinned(0)),
            pl.BlockSpec((96, FF), pinned(1)),
            pl.BlockSpec((256, MODEL_WIDTH), pinned(2)),
        ],
        out_shape=[
            jax.ShapeDtypeStruct((MODEL_WIDTH, FF), bf16),
            jax.ShapeDtypeStruct((MODEL_WIDTH, FF), bf16),
            jax.ShapeDtypeStruct((FF, MODEL_WIDTH), bf16),
        ],
        scratch_shapes=[pltpu.VMEM((1920, 128), f32), pltpu.VMEM((256, 128), f32)],
        name="unpack_feedforward",
    )(lines)


def pack_ff_kernel(gate_ref, up_ref, down_ref, lines_ref, scratch, mid):
    phase = pl.program_id(0)
    for number, source in ((0, gate_ref), (1, up_ref)):

        @pl.when(phase == number)
        def _():
            rows_to_lines_2560(
                lambda c: source[:, 128 * c : 128 * c + 128].astype(f32), scratch, 0, 96
            )

    @pl.when(phase == 2)
    def _():
        def load(c):
            if c < 7:
                return down_ref[:, 128 * c : 128 * c + 128].astype(f32)
            tail = down_ref[:, 896:960].astype(f32)
            return jnp.concatenate([tail, tail], axis=1)

        rows_to_lines_960(load, scratch, 0, 256, mid)

    lines_ref[...] = scratch[...].astype(bf16)


def pack_ff(gate, up, down):
    return pl.pallas_call(
        pack_ff_kernel,
        grid=(3, 10),
        in_specs=[
            pl.BlockSpec((96, FF), pinned(0)),
            pl.BlockSpec((96, FF), pinned(1)),
            pl.BlockSpec((256, MODEL_WIDTH), pinned(2)),
        ],
        out_specs=pl.BlockSpec((1920, 128), lambda p, j: (p * 10 + j, 0)),
        out_shape=jax.ShapeDtypeStruct((3 * 19200, 128), bf16),
        scratch_shapes=[pltpu.VMEM((1920, 128), f32), pltpu.VMEM((256, 128), f32)],
        name="pack_feedforward",
    )(gate, up, down)


def unpack_wide_kernel(lines_ref, out_ref, scratch, mid):
    for u in range(4):
        scratch[...] = lines_ref[u].astype(f32)
        base = u * 80

        def store(c, value):
            if c < 7:
                out_ref[base : base + 80, 128 * c : 128 * c + 128] = value.astype(bf16)
            else:
                out_ref[base : base + 80, 896:960] = value[:, :64].astype(bf16)

        lines_to_rows_960(scratch, 0, 80, mid, store)


def unpack_wide(lines, first):
    depth = lines.shape[1]
    return pl.pallas_call(
        unpack_wide_kernel,
        grid=(3,),
        in_specs=[pl.BlockSpec((4, depth, 128), lambda j: (first // 4 + j, 0, 0))],
        out_specs=pl.BlockSpec((320, MODEL_WIDTH), lambda j: (j, 0)),
        out_shape=jax.ShapeDtypeStruct((MODEL_WIDTH, MODEL_WIDTH), bf16),
        scratch_shapes=[pltpu.VMEM((depth, 128), f32), pltpu.VMEM((80, 128), f32)],
        name="unpack_attention",
    )(lines)


def unpack_kv_kernel(key_ref, value_ref, out_ref, key_lines, value_lines, mid):
    low = lane_low(120)
    key_lines[...] = key_ref[0].astype(f32)
    value_lines[...] = value_ref[0].astype(f32)
    keys = half_chunks([key_lines[pl.ds(k, 120, stride=5), :] for k in range(5)])
    values = half_chunks([value_lines[pl.ds(k, 120, stride=5), :] for k in range(5)])
    for h in range(KEY_VALUE_HEADS):
        for parity in range(2):
            mid[pl.ds(parity, 120, stride=2), :] = jnp.where(
                low, placed(keys[parity][h], 0), placed(values[parity][h], 1)
            )
        out_ref[:, 128 * h : 128 * h + 128] = mid[...].astype(bf16)


def unpack_kv(lines):
    depth = lines.shape[1]
    return pl.pallas_call(
        unpack_kv_kernel,
        grid=(4,),
        in_specs=[
            pl.BlockSpec((1, depth, 128), lambda j: (12 + j, 0, 0)),
            pl.BlockSpec((1, depth, 128), lambda j: (16 + j, 0, 0)),
        ],
        out_specs=pl.BlockSpec((240, 2 * KV_WIDTH), lambda j: (j, 0)),
        out_shape=jax.ShapeDtypeStruct((MODEL_WIDTH, 2 * KV_WIDTH), bf16),
        scratch_shapes=[
            pltpu.VMEM((depth, 128), f32),
            pltpu.VMEM((depth, 128), f32),
            pltpu.VMEM((240, 128), f32),
        ],
        name="unpack_key_value",
    )(lines, lines)


def pack_attention_kernel(query_ref, kv_ref, out_weight_ref, gains_ref, lines_ref, scratch, mid):
    step = pl.program_id(0)

    def wide(source):
        for u in range(4):
            base = u * 80

            def load(c):
                if c < 7:
                    return source[base : base + 80, 128 * c : 128 * c + 128].astype(f32)
                tail = source[base : base + 80, 896:960].astype(f32)
                return jnp.concatenate([tail, tail], axis=1)

            rows_to_lines_960(load, scratch, 0, 80, mid)
            lines_ref[u, :LINES, :] = scratch[...].astype(bf16)

    @pl.when(step < 3)
    def _():
        wide(query_ref)

    @pl.when(step >= 5)
    def _():
        wide(out_weight_ref)

    for number, upper in ((3, 0), (4, 1)):

        @pl.when(step == number)
        def _():
            low = lane_low(120)
            for u in range(4):
                evens, odds = [], []
                for h in range(KEY_VALUE_HEADS):
                    mid[...] = kv_ref[
                        240 * u : 240 * u + 240, 128 * h : 128 * h + 128
                    ].astype(f32)
                    evens.append((mid[pl.ds(0, 120, stride=2), :], upper))
                    odds.append((mid[pl.ds(1, 120, stride=2), :], upper))
                run = evens + odds
                for k in range(5):
                    scratch[pl.ds(k, 120, stride=5), :] = jnp.where(
                        low, placed(run[2 * k], 0), placed(run[2 * k + 1], 1)
                    )
                lines_ref[u, :LINES, :] = scratch[...].astype(bf16)

    for u in range(4):
        lines_ref[u, LINES:, :] = gains_ref[u]


def pack_attention(d_query, d_kv, d_out, gains):
    return pl.pallas_call(
        pack_attention_kernel,
        grid=(8,),
        in_specs=[
            pl.BlockSpec((320, MODEL_WIDTH), lambda s: (jnp.minimum(s, 2), 0)),
            pl.BlockSpec((MODEL_WIDTH, 2 * KV_WIDTH), lambda s: (0, 0)),
            pl.BlockSpec((320, MODEL_WIDTH), lambda s: (jnp.maximum(s - 5, 0), 0)),
            pl.BlockSpec((4, GAIN_LINES, 128), lambda s: (s, 0, 0)),
        ],
        out_specs=pl.BlockSpec((4, LINES + GAIN_LINES, 128), lambda s: (s, 0, 0)),
        out_shape=jax.ShapeDtypeStruct((UNITS, LINES + GAIN_LINES, 128), bf16),
        scratch_shapes=[pltpu.VMEM((LINES, 128), f32), pltpu.VMEM((240, 128), f32)],
        name="pack_attention",
    )(d_query, d_kv, d_out, gains)


def tile_range(starts_ref, fills_ref, block):
    first_slot = starts_ref[block] * BLK
    last_slot = block * BLK + fills_ref[block]
    tile_first = first_slot // TILE
    tile_last = (block * BLK) // TILE
    ragged_first = jnp.logical_and(first_slot % TILE != 0, tile_first < tile_last)
    return first_slot, last_slot, tile_first, tile_last, ragged_first.astype(jnp.int32)


def allowed_pairs(tile, block, first_slot, last_slot):
    key_slot = tile * TILE + lax.broadcasted_iota(jnp.int32, (TILE, WIDE), 0)
    lane = lax.broadcasted_iota(jnp.int32, (TILE, WIDE), 1)
    query_slot = block * BLK + lax.rem(lane, BLK)
    return jnp.logical_and(
        jnp.logical_and(key_slot >= first_slot, key_slot <= query_slot),
        jnp.logical_or(key_slot < last_slot, key_slot == query_slot),
    )


def over_tiles(span, block, step):
    first_slot, last_slot, tile_first, tile_last, ragged = span

    def masked(tile):
        step(tile, allowed_pairs(tile, block, first_slot, last_slot))

    def edge(k, carry):
        masked(jnp.where(k == ragged, tile_last, tile_first))
        return carry

    lax.fori_loop(0, 1 + ragged, edge, 0)

    def inner(tile, carry):
        step(tile, None)
        return carry

    lax.fori_loop(tile_first + ragged, tile_last, inner, 0)


def transpose_kv(kv_ref, turned, tiles):
    def body(t, carry):
        rows = pl.ds(pl.multiple_of(t * TILE, TILE), TILE)
        for h in range(KEY_VALUE_HEADS):
            turned[t, 128 * h : 128 * h + 128, :] = kv_ref[rows, 128 * h : 128 * h + 128].T
        return carry

    lax.fori_loop(0, tiles, body, 0)


def lay_out_kv(blocks, kv_ref, place):
    size = blocks[0].shape[0]
    for apart, block in enumerate(blocks):
        spot = apart if len(blocks) == 1 else place ^ apart
        kv_ref[pl.ds(pl.multiple_of(spot * size, TILE), size), :] = block[...]


def heads_beside(ref, h):
    return jnp.concatenate(
        [
            ref[HEAD_SIZE * (GROUPED * h + g) : HEAD_SIZE * (GROUPED * h + g + 1), :]
            for g in range(GROUPED)
        ],
        axis=1,
    )


def attention_forward_kernel(
    starts_ref, fills_ref, place_ref, query_ref, *refs
):
    kv_blocks = refs[:-8]
    mixed_ref, log_ref, kv_ref, turned, pairs, tops, totals, sums = refs[-8:]
    i = pl.program_id(0)
    block = place_ref[0] * (TOK_DEV // BLK) + i

    @pl.when(i == 0)
    def _():
        lay_out_kv(kv_blocks, kv_ref, place_ref[0])
        transpose_kv(kv_ref, turned, kv_ref.shape[0] // TILE)

    for h in range(KEY_VALUE_HEADS):
        pairs[h, :HEAD_SIZE, :] = heads_beside(query_ref, h)
        pairs[h, HEAD_SIZE:, :] = jnp.zeros((HEAD_SIZE, WIDE), bf16)
    tops[...] = jnp.full(tops.shape, masked_value, f32)
    totals[...] = jnp.zeros(totals.shape, f32)
    sums[...] = jnp.zeros(sums.shape, f32)

    def step(tile, allowed):
        rows = pl.ds(pl.multiple_of(tile * TILE, TILE), TILE)

        def score(h):
            return jnp.dot(
                kv_ref[rows, 128 * h : 128 * h + 128], pairs[h], preferred_element_type=f32
            )

        def weigh(h, scores):
            if allowed is not None:
                scores = jnp.where(allowed, scores, masked_value)
            top_old = tops[h]
            top = jnp.maximum(top_old, jnp.max(scores, axis=0, keepdims=True))
            weights = jnp.exp(scores - top)
            shrink = jnp.exp(top_old - top)
            tops[h] = top
            totals[h] = totals[h] * shrink + jnp.sum(weights, axis=0, keepdims=True)
            return weights.astype(bf16), shrink

        def gather(h, weights, shrink):
            sums[h] = sums[h] * shrink + jnp.dot(
                turned[tile, 128 * h + HEAD_SIZE : 128 * h + 128, :],
                weights,
                preferred_element_type=f32,
            )

        scores = [score(h) for h in range(KEY_VALUE_HEADS)]
        held = None
        for h in range(KEY_VALUE_HEADS):
            weighed = weigh(h, scores[h])
            if held is not None:
                gather(h - 1, *held)
            held = weighed
        gather(KEY_VALUE_HEADS - 1, *held)

    over_tiles(tile_range(starts_ref, fills_ref, block), block, step)
    for h in range(KEY_VALUE_HEADS):
        outcome = (sums[h] / totals[h]).astype(bf16)
        log_total = tops[h] + jnp.log(totals[h])
        for g in range(GROUPED):
            head = GROUPED * h + g
            mixed_ref[HEAD_SIZE * head : HEAD_SIZE * (head + 1), :] = outcome[:, BLK * g : BLK * (g + 1)]
            log_ref[head : head + 1, :] = log_total[:, BLK * g : BLK * (g + 1)]
    log_ref[QUERY_HEADS:, :] = jnp.zeros((1, BLK), f32)


def token_block(rows):
    return pl.BlockSpec((rows, BLK), lambda i, *_: (0, i))


def whole(shape):
    return pl.BlockSpec(shape, lambda i, *_: (0,) * len(shape))


def attention_forward(starts, fills, place, query, kv):
    group = sum(block.shape[0] for block in kv)
    return pl.pallas_call(
        attention_forward_kernel,
        grid_spec=pltpu.PrefetchScalarGridSpec(
            num_scalar_prefetch=3,
            grid=(TOK_DEV // BLK,),
            in_specs=[token_block(MODEL_WIDTH)] + [whole(block.shape) for block in kv],
            out_specs=[token_block(MODEL_WIDTH), token_block(16)],
            scratch_shapes=[
                pltpu.VMEM((group, 2 * KV_WIDTH), bf16),
                pltpu.VMEM((group // TILE, 2 * KV_WIDTH, TILE), bf16),
                pltpu.VMEM((KEY_VALUE_HEADS, 2 * HEAD_SIZE, WIDE), bf16),
                pltpu.VMEM((KEY_VALUE_HEADS, 1, WIDE), f32),
                pltpu.VMEM((KEY_VALUE_HEADS, 1, WIDE), f32),
                pltpu.VMEM((KEY_VALUE_HEADS, HEAD_SIZE, WIDE), f32),
            ],
        ),
        out_shape=[
            jax.ShapeDtypeStruct((MODEL_WIDTH, TOK_DEV), bf16),
            jax.ShapeDtypeStruct((16, TOK_DEV), f32),
        ],
        name="attention_forward",
    )(starts, fills, place, query, *kv)


def attention_backward_kernel(
    starts_ref,
    fills_ref,
    place_ref,
    query_ref,
    upstream_ref,
    mixed_ref,
    log_ref,
    cosine_ref,
    sine_ref,
    *refs,
):
    count = (len(refs) - 10) // 2
    kv_blocks, d_query_ref, d_kv_blocks = refs[:count], refs[count], refs[count + 1 : 2 * count + 1]
    (
        kv_ref,
        turned,
        pairs,
        query_rows,
        upstream_rows,
        deltas,
        logs,
        sums,
        kv_sums,
    ) = refs[2 * count + 1 :]
    i = pl.program_id(0)
    block = place_ref[0] * (TOK_DEV // BLK) + i
    tiles = kv_ref.shape[0] // TILE

    @pl.when(i == 0)
    def _():
        lay_out_kv(kv_blocks, kv_ref, place_ref[0])
        transpose_kv(kv_ref, turned, tiles)

        def clear(t, carry):
            kv_sums[:, pl.ds(pl.multiple_of(t * TILE, TILE), TILE), :] = jnp.zeros(
                (KEY_VALUE_HEADS, TILE, 128), f32
            )
            return carry

        lax.fori_loop(0, tiles, clear, 0)

    blank = jnp.zeros((HEAD_SIZE, WIDE), bf16)
    for h in range(KEY_VALUE_HEADS):
        query = heads_beside(query_ref, h)
        upstream = heads_beside(upstream_ref, h)
        pairs[h, :HEAD_SIZE, :WIDE] = query
        pairs[h, HEAD_SIZE:, :WIDE] = blank
        pairs[h, :HEAD_SIZE, WIDE:] = blank
        pairs[h, HEAD_SIZE:, WIDE:] = upstream
        query_rows[h] = pairs[h, :, :WIDE].T
        upstream_rows[h] = pairs[h, :, WIDE:].T
        deltas[h] = jnp.sum(
            upstream.astype(f32) * heads_beside(mixed_ref, h).astype(f32), axis=0, keepdims=True
        )
        logs[h] = jnp.concatenate(
            [log_ref[GROUPED * h + g : GROUPED * h + g + 1, :] for g in range(GROUPED)], axis=1
        )
    sums[...] = jnp.zeros(sums.shape, f32)

    def step(tile, allowed):
        rows = pl.ds(pl.multiple_of(tile * TILE, TILE), TILE)

        def score(h):
            return jnp.dot(
                kv_ref[rows, 128 * h : 128 * h + 128], pairs[h], preferred_element_type=f32
            )

        def weigh(h, both):
            scores = both[:, :WIDE]
            if allowed is not None:
                scores = jnp.where(allowed, scores, masked_value)
            probs = jnp.exp(scores - logs[h])
            d_scores = (probs * (both[:, WIDE:] - deltas[h])).astype(bf16)
            return probs.astype(bf16), d_scores

        def gather(h, probs, d_scores):
            kv_sums[h, rows, :] += jnp.dot(
                d_scores, query_rows[h], preferred_element_type=f32
            ) + jnp.dot(probs, upstream_rows[h], preferred_element_type=f32)
            sums[h] += jnp.dot(
                turned[tile, 128 * h : 128 * h + HEAD_SIZE, :], d_scores, preferred_element_type=f32
            )

        following = score(0)
        held = None
        for h in range(KEY_VALUE_HEADS):
            both = following
            if h + 1 < KEY_VALUE_HEADS:
                following = score(h + 1)
            weighed = weigh(h, both)
            if held is not None:
                gather(h - 1, *held)
            held = weighed
        gather(KEY_VALUE_HEADS - 1, *held)

    over_tiles(tile_range(starts_ref, fills_ref, block), block, step)
    cosine = cosine_ref[...]
    sine = sine_ref[...]
    half = HEAD_SIZE // 2
    for h in range(KEY_VALUE_HEADS):
        for g in range(GROUPED):
            head = GROUPED * h + g
            front = sums[h, :half, BLK * g : BLK * (g + 1)] * score_scale
            back = sums[h, half:, BLK * g : BLK * (g + 1)] * score_scale
            d_query_ref[HEAD_SIZE * head : HEAD_SIZE * head + half, :] = (
                front * cosine + back * sine
            ).astype(bf16)
            d_query_ref[HEAD_SIZE * head + half : HEAD_SIZE * (head + 1), :] = (
                back * cosine - front * sine
            ).astype(bf16)

    @pl.when(i == pl.num_programs(0) - 1)
    def _():
        size = kv_blocks[0].shape[0]
        for apart, block in enumerate(d_kv_blocks):
            spot = apart if count == 1 else place_ref[0] ^ apart

            def emit(t, carry):
                rows = pl.ds(pl.multiple_of(spot * size + t * TILE, TILE), TILE)
                for h in range(KEY_VALUE_HEADS):
                    block[pl.ds(pl.multiple_of(t * TILE, TILE), TILE), 128 * h : 128 * h + 128] = (
                        kv_sums[h, rows, :].astype(bf16)
                    )
                return carry

            lax.fori_loop(0, size // TILE, emit, 0)


def attention_backward(starts, fills, place, query, upstream, mixed, logs, cosine, sine, kv):
    group = sum(block.shape[0] for block in kv)
    half = HEAD_SIZE // 2
    return pl.pallas_call(
        attention_backward_kernel,
        grid_spec=pltpu.PrefetchScalarGridSpec(
            num_scalar_prefetch=3,
            grid=(TOK_DEV // BLK,),
            in_specs=[
                token_block(MODEL_WIDTH),
                token_block(MODEL_WIDTH),
                token_block(MODEL_WIDTH),
                token_block(16),
                token_block(half),
                token_block(half),
            ]
            + [whole(block.shape) for block in kv],
            out_specs=[token_block(MODEL_WIDTH)] + [whole(block.shape) for block in kv],
            scratch_shapes=[
                pltpu.VMEM((group, 2 * KV_WIDTH), bf16),
                pltpu.VMEM((group // TILE, 2 * KV_WIDTH, TILE), bf16),
                pltpu.VMEM((KEY_VALUE_HEADS, 2 * HEAD_SIZE, 2 * WIDE), bf16),
                pltpu.VMEM((KEY_VALUE_HEADS, WIDE, 128), bf16),
                pltpu.VMEM((KEY_VALUE_HEADS, WIDE, 128), bf16),
                pltpu.VMEM((KEY_VALUE_HEADS, 1, WIDE), f32),
                pltpu.VMEM((KEY_VALUE_HEADS, 1, WIDE), f32),
                pltpu.VMEM((KEY_VALUE_HEADS, HEAD_SIZE, WIDE), f32),
                pltpu.VMEM((KEY_VALUE_HEADS, group, 128), f32),
            ],
        ),
        out_shape=[
            jax.ShapeDtypeStruct((MODEL_WIDTH, TOK_DEV), bf16),
        ]
        + [jax.ShapeDtypeStruct(block.shape, bf16) for block in kv],
        name="attention_backward",
    )(starts, fills, place, query, upstream, mixed, logs, cosine, sine, *kv)


def dot_of(left, right, left_dim, right_dim):
    return lax.dot_general(
        left, right, (((left_dim,), (right_dim,)), ((), ())), preferred_element_type=f32
    )


SLOTS = 3
FORM = 640
PIECES = (240, 240, 160)
GAIN_LINE = 560
PAD_WIDTH = 1024
CHUNK = 640
CORE_BIT = ("shard", 1)
ROW_BIT = ("shard", 2)
NEAR_BITS = (ROW_BIT, ("dp", 1), ("dp", 2))
FAR_BITS = (("dp", 4),)


def stages(colour):
    return (CORE_BIT,) + NEAR_BITS[colour:] + NEAR_BITS[:colour] + FAR_BITS


def swap(value, bit):
    axis, mask = bit
    size = lax.axis_size(axis)
    return lax.ppermute(value, axis, [(i, i ^ mask) for i in range(size)])


def gather_colour(own, colour):
    held = own[None]
    for bit in reversed(stages(colour)[1:]):
        held = jnp.concatenate([held, swap(held, bit)], axis=0)
    return held, swap(held, CORE_BIT)


def scatter_colour(keep, send, colour):
    for bit in stages(colour):
        got = swap(send, bit)
        half = keep.shape[0] // 2
        if half == 0:
            return keep[0], got[0]
        send = keep[half:] + got[half:]
        keep = keep[:half] + got[:half]


def positions():
    device = jnp.arange(UNITS, dtype=jnp.int32)
    width = lax.axis_size("shard")
    apart = {
        "dp": (device // width) ^ lax.axis_index("dp").astype(jnp.int32),
        "shard": (device % width) ^ lax.axis_index("shard").astype(jnp.int32),
    }
    tables = []
    for colour in range(SLOTS):
        place = jnp.zeros((UNITS,), jnp.int32)
        for axis, mask in stages(colour):
            place = 2 * place + (apart[axis] & mask) // mask
        tables.append(place)
    return jnp.concatenate(tables)


def copy_from(halves, place, dst, sem, pick=lambda ref: ref):
    for number, ref in enumerate(halves):

        @pl.when(place // 16 == number)
        def _():
            pltpu.make_async_copy(pick(ref.at[lax.rem(place, 16)]), dst, sem).start()


def copy_to(src, halves, place, sem, pick=lambda ref: ref):
    for number, ref in enumerate(halves):

        @pl.when(place // 16 == number)
        def _():
            pltpu.make_async_copy(src, pick(ref.at[lax.rem(place, 16)]), sem).start()


def wait_for(ref, sem):
    pltpu.make_async_copy(ref, ref, sem).wait()


def form_attention_kernel(wide_ref, lines_ref, gains_ref, a_ref, b_ref, c_ref, mid, form):
    @pl.when(wide_ref[0] == 1)
    def _():
        def store(c, value):
            if c == 7:
                value = jnp.where(lane_low(80), value, 0.0)
            form[80 * c : 80 * c + 80, :] = value

        lines_to_rows_960(lines_ref, 0, 80, mid, store)

    @pl.when(wide_ref[0] == 0)
    def _():
        low = lane_low(120)
        line = [lines_ref[pl.ds(k, 120, stride=5), :] for k in range(5)]
        turned = [None, None] + [pltpu.roll(line[k], 64, 1) for k in range(2, 5)]
        form[pl.ds(0, 120, stride=2), :] = line[0]
        form[pl.ds(1, 120, stride=2), :] = jnp.where(low, turned[2], turned[3])
        form[pl.ds(240, 120, stride=2), :] = line[1]
        form[pl.ds(241, 120, stride=2), :] = jnp.where(low, turned[3], turned[4])
        mid[pl.ds(0, 120, stride=2), :] = line[2]
        mid[pl.ds(1, 120, stride=2), :] = turned[4]
        low = lane_low(80)
        form[480:560, :] = jnp.where(low, mid[0:80, :], pltpu.roll(mid[160:240, :], 64, 1))
        form[560:640, :] = jnp.where(low, mid[80:160, :], 0.0)

    form[GAIN_LINE : GAIN_LINE + 1, :] = jnp.where(
        lane_low(1), form[GAIN_LINE : GAIN_LINE + 1, :], gains_ref[...]
    )
    a_ref[...] = form[0:240, :].astype(bf16)
    b_ref[...] = form[240:480, :].astype(bf16)
    c_ref[...] = form[480:640, :].astype(bf16)


SMEM_SPEC = pl.BlockSpec(memory_space=pltpu.SMEM)
ANY_SPEC = pl.BlockSpec(memory_space=pl.ANY)


def form_attention(wide, lines, gains):
    return pl.pallas_call(
        form_attention_kernel,
        in_specs=[SMEM_SPEC, pl.BlockSpec((LINES, 128)), pl.BlockSpec((1, 128))],
        out_shape=[jax.ShapeDtypeStruct((n, 128), bf16) for n in PIECES],
        scratch_shapes=[pltpu.VMEM((240, 128), f32), pltpu.VMEM((FORM, 128), f32)],
        name="form_attention",
    )(wide, lines, gains)


def unform_attention_kernel(wide_ref, *refs):
    pieces, (lines_ref, gains_ref, mid, form) = refs[:6], refs[6:]
    base = 0
    for n, keep, got in zip(PIECES, pieces[0::2], pieces[1::2]):
        form[base : base + n, :] = keep[...].astype(f32) + got[...].astype(f32)
        base += n
    gains_ref[...] = form[GAIN_LINE : GAIN_LINE + 1, :]

    @pl.when(wide_ref[0] == 1)
    def _():
        rows_to_lines_960(lambda c: form[80 * c : 80 * c + 80, :], lines_ref, 0, 80, mid)

    @pl.when(wide_ref[0] == 0)
    def _():
        low = lane_low(120)
        mid[0:80, :] = form[480:560, :]
        mid[80:160, :] = form[560:640, :]
        mid[160:240, :] = pltpu.roll(form[480:560, :], 64, 1)
        even = [form[pl.ds(0, 120, stride=2), :], form[pl.ds(240, 120, stride=2), :]]
        odd = [form[pl.ds(1, 120, stride=2), :], form[pl.ds(241, 120, stride=2), :]]
        even.append(mid[pl.ds(0, 120, stride=2), :])
        odd.append(mid[pl.ds(1, 120, stride=2), :])
        odd = [pltpu.roll(value, 64, 1) for value in odd]
        lines_ref[pl.ds(0, 120, stride=5), :] = even[0]
        lines_ref[pl.ds(1, 120, stride=5), :] = even[1]
        lines_ref[pl.ds(2, 120, stride=5), :] = jnp.where(low, even[2], odd[0])
        lines_ref[pl.ds(3, 120, stride=5), :] = jnp.where(low, odd[0], odd[1])
        lines_ref[pl.ds(4, 120, stride=5), :] = jnp.where(low, odd[1], odd[2])


def unform_attention(wide, addends):
    return pl.pallas_call(
        unform_attention_kernel,
        in_specs=[SMEM_SPEC] + [pl.BlockSpec((n, 128)) for n in PIECES for _ in range(2)],
        out_shape=[jax.ShapeDtypeStruct((LINES, 128), f32), jax.ShapeDtypeStruct((1, 128), f32)],
        scratch_shapes=[pltpu.VMEM((240, 128), f32), pltpu.VMEM((FORM, 128), f32)],
        name="unform_attention",
    )(wide, *addends)


def wide_pieces(c):
    return [((80 * c + 16 * m) // 32, (80 * c + 16 * m) % 32, 16 * m) for m in range(5)]


def form_feedforward_kernel(narrow_ref, lines_ref, out, mid):
    for s in range(SLOTS):

        @pl.when(narrow_ref[s] == 1)
        def _():
            mid[30:32, :] = jnp.zeros((2, 128), f32)
            for c in range(20):
                mid[0:30, :] = lines_ref[pl.ds(LINES * s + c, 30, stride=20), :]
                out[s, c] = mid[0:32, :].astype(bf16)

        @pl.when(narrow_ref[s] == 0)
        def _():
            def store(c, value):
                if c == 7:
                    value = jnp.where(lane_low(80), value, 0.0)
                for k, r, m in wide_pieces(c):
                    out[s, k, r : r + 16, :] = value[m : m + 16].astype(bf16)

            lines_to_rows_960(lines_ref, LINES * s, 80, mid, store)


def form_feedforward(narrow, lines):
    return pl.pallas_call(
        form_feedforward_kernel,
        in_specs=[SMEM_SPEC, pl.BlockSpec((SLOTS * LINES, 128))],
        out_shape=jax.ShapeDtypeStruct((SLOTS, 20, 32, 128), bf16),
        scratch_shapes=[pltpu.VMEM((80, 128), f32)],
        name="form_feedforward",
    )(narrow, lines)


def unform_feedforward_kernel(narrow_ref, terms, lines_ref, mid):
    for s in range(SLOTS):

        @pl.when(narrow_ref[s] == 1)
        def _():
            for c in range(20):
                mid[0:32, :] = terms[s, c].astype(f32)
                lines_ref[pl.ds(LINES * s + c, 30, stride=20), :] = mid[0:30, :]

        @pl.when(narrow_ref[s] == 0)
        def _():
            def load(c):
                return jnp.concatenate(
                    [terms[s, k, r : r + 16, :].astype(f32) for k, r, m in wide_pieces(c)], axis=0
                )

            rows_to_lines_960(load, lines_ref, LINES * s, 80, mid)


def unform_feedforward(narrow, terms):
    return pl.pallas_call(
        unform_feedforward_kernel,
        in_specs=[SMEM_SPEC, pl.BlockSpec((SLOTS, 20, 32, 128))],
        out_shape=jax.ShapeDtypeStruct((SLOTS * LINES, 128), f32),
        scratch_shapes=[pltpu.VMEM((80, 128), f32)],
        name="unform_feedforward",
    )(narrow, terms)


def place_attention_kernel(table_ref, *refs):
    halves = [refs[2 * k : 2 * k + 2] for k in range(SLOTS)]
    query_ref, kv_ref, out_ref, gains_ref, units, sem = refs[2 * SLOTS :]

    def start(d, carry):
        base = 0
        for k, n in enumerate(PIECES):
            copy_from(halves[k], table_ref[UNITS * k + d], units.at[d, base : base + n, :], sem)
            base += n
        return carry

    lax.fori_loop(0, UNITS, start, 0)
    wait_for(units, sem)

    def wide(out, first):
        def body(u, carry):
            rows = pl.ds(pl.multiple_of(80 * u, 16), 80)
            for c in range(7):
                out[rows, 128 * c : 128 * c + 128] = units[first + u, 80 * c : 80 * c + 80, :]
            out[rows, 896:960] = units[first + u, 560:640, :64]
            return carry

        lax.fori_loop(0, 12, body, 0)

    def keyed(j, carry):
        low = lane_low(240)
        chunks = []
        for first in (12, 16):
            unit = units[first + j].astype(f32)
            last = jnp.concatenate(
                [unit[480:640], pltpu.roll(unit[480:560], 64, 1)], axis=0
            )
            lines = (unit[0:240], unit[240:480], last)
            chunks.append([(lines[h // 2], h % 2) for h in range(KEY_VALUE_HEADS)])
        rows = pl.ds(pl.multiple_of(240 * j, 16), 240)
        for h in range(KEY_VALUE_HEADS):
            kv_ref[rows, 128 * h : 128 * h + 128] = jnp.where(
                low, placed(chunks[0][h], 0), placed(chunks[1][h], 1)
            ).astype(bf16)
        return carry

    lax.fori_loop(0, 4, keyed, 0)
    wide(query_ref, 0)
    wide(out_ref, 20)
    for u in range(UNITS):
        gains_ref[u : u + 1, :] = units[u, GAIN_LINE : GAIN_LINE + 1, :].astype(f32)


def place_attention(table, gathered):
    return pl.pallas_call(
        place_attention_kernel,
        in_specs=[SMEM_SPEC] + [ANY_SPEC] * (2 * SLOTS),
        out_shape=[
            jax.ShapeDtypeStruct((MODEL_WIDTH, MODEL_WIDTH), bf16),
            jax.ShapeDtypeStruct((MODEL_WIDTH, 2 * KV_WIDTH), bf16),
            jax.ShapeDtypeStruct((MODEL_WIDTH, MODEL_WIDTH), bf16),
            jax.ShapeDtypeStruct((UNITS, 128), f32),
        ],
        scratch_shapes=[pltpu.VMEM((UNITS, FORM, 128), bf16), pltpu.SemaphoreType.DMA],
        name="place_attention",
    )(table, *gathered)


def split_attention_kernel(table_ref, query_ref, kv_ref, out_ref, gains_ref, *refs):
    halves = [refs[2 * k : 2 * k + 2] for k in range(SLOTS)]
    units, sem = refs[2 * SLOTS :]

    def send(d):
        row = lax.broadcasted_iota(jnp.int32, (16, 128), 0)
        lane = lax.broadcasted_iota(jnp.int32, (16, 128), 1)
        block = units[d, GAIN_LINE : GAIN_LINE + 16, :].astype(f32)
        units[d, GAIN_LINE : GAIN_LINE + 16, :] = jnp.where(
            jnp.logical_and(row == 0, lane >= 64), gains_ref[pl.ds(d, 1), :], block
        ).astype(bf16)
        base = 0
        for k, n in enumerate(PIECES):
            copy_to(units.at[d, base : base + n, :], halves[k], table_ref[UNITS * k + d], sem)
            base += n

    def wide(source, first):
        def body(u, carry):
            rows = pl.ds(pl.multiple_of(80 * u, 16), 80)
            for c in range(7):
                units[first + u, 80 * c : 80 * c + 80, :] = source[rows, 128 * c : 128 * c + 128]
            tail = source[rows, 896:960]
            units[first + u, 560:640, :] = jnp.concatenate([tail, jnp.zeros_like(tail)], axis=1)
            send(first + u)
            return carry

        lax.fori_loop(0, 12, body, 0)

    def keyed(j, carry):
        low = lane_low(240)
        rows = pl.ds(pl.multiple_of(240 * j, 16), 240)
        for upper, first in ((0, 12), (1, 16)):
            heads = [
                (kv_ref[rows, 128 * h : 128 * h + 128].astype(f32), upper)
                for h in range(KEY_VALUE_HEADS)
            ]
            for c in range(2):
                units[first + j, 240 * c : 240 * c + 240, :] = jnp.where(
                    low, placed(heads[2 * c], 0), placed(heads[2 * c + 1], 1)
                ).astype(bf16)
            last = placed(heads[4], 0)
            turned = placed(heads[4], 1)
            units[first + j, 480:560, :] = jnp.where(
                lane_low(80), last[0:80], turned[160:240]
            ).astype(bf16)
            units[first + j, 560:640, :] = jnp.where(lane_low(80), last[80:160], 0.0).astype(bf16)
            send(first + j)
        return carry

    lax.fori_loop(0, 4, keyed, 0)
    wide(query_ref, 0)
    wide(out_ref, 20)
    wait_for(units, sem)


def split_attention(table, d_query, d_kv, d_out, gains):
    return pl.pallas_call(
        split_attention_kernel,
        in_specs=[
            SMEM_SPEC,
            pl.BlockSpec((MODEL_WIDTH, MODEL_WIDTH)),
            pl.BlockSpec((MODEL_WIDTH, 2 * KV_WIDTH)),
            pl.BlockSpec((MODEL_WIDTH, MODEL_WIDTH)),
            pl.BlockSpec((UNITS, 128)),
        ],
        out_specs=[ANY_SPEC] * (2 * SLOTS),
        out_shape=[jax.ShapeDtypeStruct((16, n, 128), bf16) for n in PIECES for _ in range(2)],
        scratch_shapes=[pltpu.VMEM((UNITS, FORM, 128), bf16), pltpu.SemaphoreType.DMA],
        name="split_attention",
    )(table, d_query, d_kv, d_out, gains)


def feedforward_kernel(
    hidden_ref,
    turned_ref,
    grad_ref,
    gate_ref,
    up_ref,
    down_ref,
    out_ref,
    d_hidden_ref,
    terms_ref,
    down,
    inner_rows,
    inner_turned,
    d_both,
    both_out,
    down_out,
    sems,
):
    q = pl.program_id(0)
    chunks = pl.num_programs(0)
    slot = lax.rem(q, 2)

    def copies(side, chunk):
        columns = pl.ds(5 * chunk, 5)
        return (
            pltpu.make_async_copy(
                both_out.at[side, 0], terms_ref.at[pl.ds(0, 32), columns], sems.at[side, 0]
            ),
            pltpu.make_async_copy(
                both_out.at[side, 1], terms_ref.at[pl.ds(32, 32), columns], sems.at[side, 1]
            ),
            pltpu.make_async_copy(
                down_out.at[side], terms_ref.at[pl.ds(64 + 8 * chunk, 8)], sems.at[side, 2]
            ),
        )

    for v in range(8):
        for c in range(8):
            for k, r, m in wide_pieces(c):
                down[80 * v + m : 80 * v + m + 16, 128 * c : 128 * c + 128] = down_ref[
                    v, k, r : r + 16, :
                ]

    @pl.when(q == 0)
    def _():
        out_ref[...] = jnp.zeros(out_ref.shape, f32)
        d_hidden_ref[...] = jnp.zeros(d_hidden_ref.shape, f32)

    def rows_step(i, carry):
        rows = pl.ds(pl.multiple_of(256 * i, 256), 256)
        weights = jnp.concatenate(
            [ref[:, c].reshape(PAD_WIDTH, 128) for ref in (gate_ref, up_ref) for c in range(5)],
            axis=1,
        )
        both = jnp.dot(hidden_ref[rows, :], weights, preferred_element_type=f32)
        gate, upper = both[:, :CHUNK], both[:, CHUNK:]
        sigmoid_gate = jax.nn.sigmoid(gate)
        activated = gate * sigmoid_gate
        inner = (activated * upper).astype(bf16)
        inner_rows[rows, :] = inner
        out_ref[rows, :] += jnp.dot(inner, down[...], preferred_element_type=f32)
        d_inner = dot_of(grad_ref[rows, :], down[...], 1, 1)
        d_gate = d_inner * upper * sigmoid_gate * (1.0 + gate * (1.0 - sigmoid_gate))
        d_upper = d_inner * activated
        d_pair = jnp.concatenate([d_gate, d_upper], axis=1).astype(bf16)
        d_both[rows, :] = d_pair
        d_hidden_ref[rows, :] += dot_of(d_pair, weights, 1, 1)
        return carry

    lax.fori_loop(0, 2, rows_step, 0)
    inner_turned[...] = inner_rows[...].T

    @pl.when(q >= 2)
    def _():
        for copy in copies(slot, q - 2):
            copy.wait()

    def both_step(i, carry):
        rows = pl.ds(pl.multiple_of(256 * i, 256), 256)
        terms = jnp.dot(turned_ref[rows, :], d_both[...], preferred_element_type=f32).astype(bf16)
        units = pl.ds(8 * i, 8)
        for c in range(10):
            both_out[slot, c // 5, units, c % 5] = terms[:, 128 * c : 128 * c + 128].reshape(
                8, 32, 128
            )
        return carry

    lax.fori_loop(0, 4, both_step, 0)

    def down_step(i, carry):
        rows = pl.ds(pl.multiple_of(320 * i, 16), 320)
        terms = jnp.dot(
            inner_turned[rows, :], grad_ref[...], preferred_element_type=f32
        ).astype(bf16)
        for v in range(4):
            for c in range(8):
                for k, r, m in wide_pieces(c):
                    down_out[slot, 4 * i + v, k, r : r + 16, :] = terms[
                        80 * v + m : 80 * v + m + 16, 128 * c : 128 * c + 128
                    ]
        return carry

    lax.fori_loop(0, 2, down_step, 0)
    for copy in copies(slot, q):
        copy.start()

    @pl.when(q == chunks - 1)
    def _():
        for copy in copies(1 - slot, q - 1) + copies(slot, q):
            copy.wait()


def feedforward(hidden, turned, grad, weights):
    full = lambda shape: pl.BlockSpec(shape, lambda q: (0, 0))
    return pl.pallas_call(
        feedforward_kernel,
        grid=(FF // CHUNK,),
        in_specs=[
            full((TOK_DEV, PAD_WIDTH)),
            full((PAD_WIDTH, TOK_DEV)),
            full((TOK_DEV, PAD_WIDTH)),
            pl.BlockSpec((32, 5, 32, 128), lambda q: (0, q, 0, 0)),
            pl.BlockSpec((32, 5, 32, 128), lambda q: (1, q, 0, 0)),
            pl.BlockSpec((8, 20, 32, 128), lambda q: (8 + q, 0, 0, 0)),
        ],
        out_specs=[full((TOK_DEV, PAD_WIDTH))] * 2 + [ANY_SPEC],
        out_shape=[jax.ShapeDtypeStruct((TOK_DEV, PAD_WIDTH), f32)] * 2
        + [jax.ShapeDtypeStruct((3 * UNITS, 20, 32, 128), bf16)],
        scratch_shapes=[
            pltpu.VMEM((CHUNK, PAD_WIDTH), bf16),
            pltpu.VMEM((TOK_DEV, CHUNK), bf16),
            pltpu.VMEM((CHUNK, TOK_DEV), bf16),
            pltpu.VMEM((TOK_DEV, 2 * CHUNK), bf16),
            pltpu.VMEM((2, 2, 32, 5, 32, 128), bf16),
            pltpu.VMEM((2, 8, 20, 32, 128), bf16),
            pltpu.SemaphoreType.DMA((2, 3)),
        ],
        compiler_params=pltpu.CompilerParams(vmem_limit_bytes=60 * 2**20),
        name="feedforward",
    )(hidden, turned, grad, weights, weights, weights)


def spread_matrix():
    column = jnp.arange(PAD_WIDTH, dtype=jnp.int32)
    entry = jnp.where(column % 32 < 30, 30 * (column // 32) + column % 32, -1)
    return (jnp.arange(MODEL_WIDTH, dtype=jnp.int32)[:, None] == entry[None, :]).astype(bf16)


def rope_tables(positions):
    steps = jnp.arange(HEAD_SIZE // 2, dtype=f32) * (2.0 / HEAD_SIZE)
    inverse = jnp.exp(-math.log(10000.0) * steps)
    angles = inverse[:, None] * positions.astype(f32)[None, :]
    return (jnp.cos(angles), jnp.sin(angles))


def norm_scale(field):
    return lax.rsqrt(jnp.mean(field * field, axis=1, keepdims=True) + epsilon)


def norm_back(upstream, normed, scale, gain):
    scaled = upstream * gain[None, :]
    return scale * (scaled - normed * jnp.mean(scaled * normed, axis=1, keepdims=True))


def adam_step(grad, moment, second, master):
    moment_new = 0.9 * moment + 0.1 * grad
    second_new = 0.999 * second + 0.001 * grad * grad
    corrected = moment_new / (1.0 - 0.9**ADAM_STEP)
    scaled = second_new / (1.0 - 0.999**ADAM_STEP)
    update = -learning_rate * (corrected / (jnp.sqrt(scaled) + 1e-08) + weight_decay * master)
    return (moment_new, second_new, update)


def gather_lines(block):
    return lax.all_gather(block, ALL_AXES, axis=0, tiled=True)


def scatter_lines(lines):
    return lax.psum_scatter(lines, ALL_AXES, scatter_dimension=0, tiled=True)


def local(
    layer_input,
    cotangent,
    master_attention,
    master_feedforward,
    master_gains,
    first_attention,
    second_attention,
    first_feedforward,
    second_feedforward,
    first_gains,
    second_gains,
    block_start,
    block_fill,
):
    devices = lax.axis_size(ALL_AXES)
    attention_lines = master_attention.shape[0] // 128
    feedforward_lines = master_feedforward.shape[0] // 128
    gain_count = master_gains.shape[0]
    padded = (attention_lines // 16 + 1) * 16

    in_units = devices == UNITS
    if in_units:
        table = positions()
        device = (
            lax.axis_index("dp") * lax.axis_size("shard") + lax.axis_index("shard")
        ).astype(jnp.int32)
        wide = jnp.logical_or(device < 12, device >= 20).astype(jnp.int32)[None]
        narrow = (SLOTS * device + jnp.arange(SLOTS, dtype=jnp.int32) < 2 * UNITS).astype(jnp.int32)
        gain_row = jnp.pad(
            master_gains.reshape(1, gain_count), ((0, 0), (64, 64 - gain_count))
        )
        pieces = form_attention(wide, master_attention.reshape(LINES, 128), gain_row)
        gathered = [half for k in range(SLOTS) for half in gather_colour(pieces[k], k)]
        forms = form_feedforward(narrow, master_feedforward.reshape(SLOTS * LINES, 128))
        feedforward_all = gather_lines(forms.reshape(SLOTS * FORM, 128))
        query_weight, kv_weight, out_weight, gain_rows = place_attention(table, gathered)
        gains_all = gain_rows[:, 64 : 64 + gain_count].reshape(-1)
    else:
        gain_lines = jnp.pad(
            master_gains.astype(bf16).reshape(1, gain_count),
            ((0, padded - attention_lines - 1), (0, 128 - gain_count)),
        )
        attention_block = jnp.concatenate(
            [master_attention.astype(bf16).reshape(attention_lines, 128), gain_lines], axis=0
        )
        by_device = gather_lines(attention_block).reshape(devices, padded, 128)
        feedforward_all = gather_lines(
            master_feedforward.astype(bf16).reshape(feedforward_lines, 128)
        )
        gains_all = by_device[:, attention_lines, :gain_count].reshape(-1).astype(f32)
        units = by_device[:, :attention_lines].reshape(UNITS, LINES, 128)
        query_weight = unpack_wide(units, 0)
        kv_weight = unpack_kv(units)
        out_weight = unpack_wide(units, 20)
    gain_one, gain_two = gains_all[:MODEL_WIDTH], gains_all[MODEL_WIDTH:]

    shard = lax.axis_index("shard").astype(jnp.int32)
    place = shard[None]
    first_row = shard * TOK_DEV
    first_block = shard * (TOK_DEV // BLK)
    local_slots = first_row + jnp.arange(TOK_DEV, dtype=jnp.int32)
    local_starts = lax.dynamic_slice_in_dim(block_start, first_block, TOK_DEV // BLK)
    local_fills = lax.dynamic_slice_in_dim(block_fill, first_block, TOK_DEV // BLK)
    live_rows = local_slots % BLK < jnp.repeat(local_fills, BLK)
    cosine_table, sine_table = rope_tables(local_slots - jnp.repeat(local_starts, BLK) * BLK)

    def rotate(field, scale):
        heads = field.shape[0]
        front = field[:, : HEAD_SIZE // 2]
        back = field[:, HEAD_SIZE // 2 :]
        return (
            jnp.concatenate(
                [
                    front * cosine_table[None] - back * sine_table[None],
                    back * cosine_table[None] + front * sine_table[None],
                ],
                axis=1,
            ).astype(bf16)
            * bf16(scale)
        ).reshape(heads * HEAD_SIZE, TOK_DEV)

    inputs = layer_input.astype(f32)
    scale_one = norm_scale(inputs)
    normed_one = inputs * scale_one
    first_hidden = (normed_one * gain_one[None, :]).astype(bf16)
    kv_turned = dot_of(kv_weight, first_hidden, 0, 1).reshape(
        KEY_VALUE_HEADS, 2, HEAD_SIZE, TOK_DEV
    )
    keys = rotate(kv_turned[:, 0], 1.0).reshape(KEY_VALUE_HEADS, 1, HEAD_SIZE, TOK_DEV)
    values = kv_turned[:, 1:].astype(bf16)
    kv_rows = jnp.concatenate([keys, values], axis=1).reshape(2 * KV_WIDTH, TOK_DEV).T
    if in_units:
        across = swap(kv_rows, ROW_BIT)
        kv_all = [kv_rows, swap(kv_rows, CORE_BIT), across, swap(across, CORE_BIT)]
    else:
        kv_all = [lax.all_gather(kv_rows, "shard", axis=0, tiled=True)]
    query_turned = rotate(
        dot_of(query_weight, first_hidden, 0, 1).reshape(QUERY_HEADS, HEAD_SIZE, TOK_DEV),
        score_scale,
    )
    mixed_turned, logs = attention_forward(block_start, block_fill, place, query_turned, kv_all)
    middle = inputs + dot_of(mixed_turned, out_weight, 0, 0)
    scale_two = norm_scale(middle)
    normed_two = middle * scale_two
    hidden_two = (normed_two * gain_two[None, :]).astype(bf16)

    grad_out = cotangent.astype(f32) * live_rows[:, None].astype(f32)
    grad_low = grad_out.astype(bf16)
    if in_units:
        spread = spread_matrix()
        outcome, d_spread, ff_terms = feedforward(
            dot_of(hidden_two, spread, 1, 0).astype(bf16),
            dot_of(spread, hidden_two, 0, 1).astype(bf16),
            jnp.pad(grad_low, ((0, 0), (0, PAD_WIDTH - MODEL_WIDTH))),
            feedforward_all.reshape(3 * UNITS, 20, 32, 128),
        )
        layer_output = middle + outcome[:, :MODEL_WIDTH]
        d_coarse = lax.reduce_precision(d_spread, 8, 7)
        d_hidden_two = dot_of(d_coarse.astype(bf16), spread, 1, 1) + dot_of(
            (d_spread - d_coarse).astype(bf16), spread, 1, 1
        )
        ff_sum = scatter_lines(ff_terms.reshape(SLOTS * UNITS * FORM, 128))
        feedforward_gradient = unform_feedforward(narrow, ff_sum.reshape(SLOTS, 20, 32, 128)).reshape(-1)
    else:
        gate_weight, up_weight, down_weight = unpack_ff(feedforward_all)
        gate = dot_of(hidden_two, gate_weight, 1, 0)
        upper = dot_of(hidden_two, up_weight, 1, 0)
        sigmoid_gate = jax.nn.sigmoid(gate)
        activated = gate * sigmoid_gate
        inner = (activated * upper).astype(bf16)
        layer_output = middle + dot_of(inner, down_weight, 1, 0)
        d_down_weight = dot_of(inner, grad_low, 0, 0).astype(bf16)
        d_inner = dot_of(grad_low, down_weight, 1, 1)
        d_gate = (
            d_inner * upper * sigmoid_gate * (1.0 + gate * (1.0 - sigmoid_gate))
        ).astype(bf16)
        d_upper = (d_inner * activated).astype(bf16)
        d_gate_weight = dot_of(hidden_two, d_gate, 0, 0).astype(bf16)
        d_up_weight = dot_of(hidden_two, d_upper, 0, 0).astype(bf16)
        d_hidden_two = dot_of(d_gate, gate_weight, 1, 1) + dot_of(d_upper, up_weight, 1, 1)
        feedforward_gradient = (
            scatter_lines(pack_ff(d_gate_weight, d_up_weight, d_down_weight))
            .astype(f32)
            .reshape(-1)
        )

    d_gain_two = jnp.sum(d_hidden_two * normed_two, axis=0)
    d_middle = grad_out + norm_back(d_hidden_two, normed_two, scale_two, gain_two)

    d_branch = d_middle.astype(bf16)
    d_out_weight = dot_of(mixed_turned, d_branch, 1, 0).astype(bf16)
    d_mixed = dot_of(out_weight, d_branch, 1, 1).astype(bf16)
    d_query, *d_kv = attention_backward(
        block_start,
        block_fill,
        place,
        query_turned,
        d_mixed,
        mixed_turned,
        logs,
        cosine_table,
        sine_table,
        kv_all,
    )
    if in_units:
        across = d_kv[2] + swap(d_kv[3], CORE_BIT)
        d_kv_rows = d_kv[0] + swap(d_kv[1], CORE_BIT) + swap(across, ROW_BIT)
    else:
        d_kv_rows = lax.psum_scatter(d_kv[0], "shard", scatter_dimension=0, tiled=True)
    d_kv_turned = d_kv_rows.T.reshape(KEY_VALUE_HEADS, 2, HEAD_SIZE, TOK_DEV)
    d_front = d_kv_turned[:, 0, : HEAD_SIZE // 2].astype(f32)
    d_back = d_kv_turned[:, 0, HEAD_SIZE // 2 :].astype(f32)
    d_keys = jnp.concatenate(
        [
            d_front * cosine_table[None] + d_back * sine_table[None],
            d_back * cosine_table[None] - d_front * sine_table[None],
        ],
        axis=1,
    ).astype(bf16)
    d_kv_lin = jnp.concatenate([d_keys[:, None], d_kv_turned[:, 1:]], axis=1).reshape(
        2 * KV_WIDTH, TOK_DEV
    )
    d_query_weight = dot_of(first_hidden, d_query, 0, 1).astype(bf16)
    d_kv_weight = dot_of(first_hidden, d_kv_lin, 0, 1).astype(bf16)
    d_hidden_one = dot_of(d_query, query_weight, 0, 1) + dot_of(d_kv_lin, kv_weight, 0, 1)
    d_gain_one = jnp.sum(d_hidden_one * normed_one, axis=0)
    input_gradient = d_middle + norm_back(d_hidden_one, normed_one, scale_one, gain_one)

    gain_terms = jnp.concatenate([d_gain_one, d_gain_two])
    if in_units:
        gain_rows = jnp.pad(
            gain_terms.reshape(UNITS, gain_count), ((0, 0), (64, 64 - gain_count))
        )
        terms = split_attention(table, d_query_weight, d_kv_weight, d_out_weight, gain_rows)
        addends = [
            addend
            for k in range(SLOTS)
            for addend in scatter_colour(terms[2 * k], terms[2 * k + 1], k)
        ]
        attention_sum, gain_sum = unform_attention(wide, addends)
        attention_gradient = attention_sum.reshape(-1)
        gains_gradient = gain_sum[0, 64 : 64 + gain_count]
    else:
        no_gains = jnp.zeros((UNITS, GAIN_LINES, 128), bf16)
        terms = pack_attention(d_query_weight, d_kv_weight, d_out_weight, no_gains)
        terms = jnp.concatenate(
            [
                terms[:, :LINES].reshape(devices, attention_lines, 128),
                jnp.pad(
                    gain_terms.astype(bf16).reshape(devices, 1, gain_count),
                    ((0, 0), (0, padded - attention_lines - 1), (0, 128 - gain_count)),
                ),
            ],
            axis=1,
        )
        summed = scatter_lines(terms.reshape(devices * padded, 128)).astype(f32)
        attention_gradient = summed[:attention_lines].reshape(-1)
        gains_gradient = summed[attention_lines, :gain_count]

    attention_first, attention_second, attention_update = adam_step(
        attention_gradient, first_attention, second_attention, master_attention
    )
    feedforward_first, feedforward_second, feedforward_update = adam_step(
        feedforward_gradient, first_feedforward, second_feedforward, master_feedforward
    )
    gains_first, gains_second, gains_update = adam_step(
        gains_gradient, first_gains, second_gains, master_gains
    )
    return (
        layer_output,
        input_gradient,
        attention_gradient,
        feedforward_gradient,
        gains_gradient,
        attention_first,
        attention_second,
        feedforward_first,
        feedforward_second,
        gains_first,
        gains_second,
        attention_update,
        feedforward_update,
        gains_update,
    )


def solution(mesh):
    rows = P(ALL_AXES, None)
    flat = P(ALL_AXES)
    return jax.shard_map(
        local,
        mesh=mesh,
        in_specs=(rows, rows) + (flat,) * 9 + (P("dp"), P("dp")),
        out_specs=(rows, rows) + (flat,) * 12,
        check_vma=False,
    )
```

```python
import functools
import math

import jax
import jax.numpy as jnp
from jax import lax
from jax.experimental import pallas as pl
from jax.experimental.pallas import tpu as pltpu
from jax.sharding import PartitionSpec as P

MODEL_WIDTH = 960
QUERY_HEADS = 15
KEY_VALUE_HEADS = 5
GROUPED = QUERY_HEADS // KEY_VALUE_HEADS
HEAD_SIZE = 64
FF = 2560
BLK = 128
ADAM_STEP = 10
TOK_DEV = 512
KV_WIDTH = KEY_VALUE_HEADS * HEAD_SIZE
TILE = 256
WIDE = GROUPED * BLK
UNITS = 32
LINES = 600
GAIN_LINES = 8
ALL_AXES = ("dp", "shard")

epsilon = 1e-05
masked_value = -1e30
learning_rate = 0.03
weight_decay = 0.1
score_scale = 1.0 / math.sqrt(HEAD_SIZE)
f32 = jnp.float32
bf16 = jnp.bfloat16


def lines_to_rows_2560(scratch, base, rows, store):
    for c in range(20):
        store(c, scratch[pl.ds(base + c, rows, stride=20), :])


def rows_to_lines_2560(load, scratch, base, rows):
    for c in range(20):
        scratch[pl.ds(base + c, rows, stride=20), :] = load(c)


def lane_low(rows):
    return lax.broadcasted_iota(jnp.int32, (rows, 128), 1) < 64


def lines_to_rows_960(scratch, base, rows, mid, store):
    half = rows // 2
    low = lane_low(half)
    line = [scratch[pl.ds(base + k, half, stride=15), :] for k in range(15)]
    turned = [None] * 7 + [pltpu.roll(line[k], 64, 1) for k in range(7, 15)]
    for c in range(8):
        mid[pl.ds(0, half, stride=2), :] = line[c]
        odd = jnp.where(low, turned[7 + c], turned[8 + c]) if c < 7 else turned[14]
        mid[pl.ds(1, half, stride=2), :] = odd
        store(c, mid[pl.ds(0, rows), :])


def rows_to_lines_960(load, scratch, base, rows, mid):
    half = rows // 2
    low = lane_low(half)
    odds = []
    for c in range(8):
        mid[pl.ds(0, rows), :] = load(c)
        even = mid[pl.ds(0, half, stride=2), :]
        odd = pltpu.roll(mid[pl.ds(1, half, stride=2), :], 64, 1)
        odds.append(odd)
        if c < 7:
            scratch[pl.ds(base + c, half, stride=15), :] = even
        else:
            scratch[pl.ds(base + 7, half, stride=15), :] = jnp.where(low, even, odds[0])
        if c > 0:
            scratch[pl.ds(base + 7 + c, half, stride=15), :] = jnp.where(low, odds[c - 1], odd)


def half_chunks(lines):
    even = [(lines[0], 0), (lines[0], 1), (lines[1], 0), (lines[1], 1), (lines[2], 0)]
    odd = [(lines[2], 1), (lines[3], 0), (lines[3], 1), (lines[4], 0), (lines[4], 1)]
    return even, odd


def placed(chunk, upper):
    line, side = chunk
    return line if side == upper else pltpu.roll(line, 64, 1)


def unpack_ff_kernel(lines_ref, gate_ref, up_ref, down_ref, scratch, mid):
    phase = pl.program_id(0)
    scratch[...] = lines_ref[...].astype(f32)
    for number, out in ((0, gate_ref), (1, up_ref)):

        @pl.when(phase == number)
        def _():
            def store(c, value):
                out[:, 128 * c : 128 * c + 128] = value.astype(bf16)

            lines_to_rows_2560(scratch, 0, 96, store)

    @pl.when(phase == 2)
    def _():
        def store(c, value):
            if c < 7:
                down_ref[:, 128 * c : 128 * c + 128] = value.astype(bf16)
            else:
                down_ref[:, 896:960] = value[:, :64].astype(bf16)

        lines_to_rows_960(scratch, 0, 256, mid, store)


def pinned(phase):
    def index(p, j):
        return (jnp.where(p == phase, j, jnp.where(p < phase, 0, 9)), 0)

    return index


def unpack_ff(lines):
    return pl.pallas_call(
        unpack_ff_kernel,
        grid=(3, 10),
        in_specs=[pl.BlockSpec((1920, 128), lambda p, j: (p * 10 + j, 0))],
        out_specs=[
            pl.BlockSpec((96, FF), pinned(0)),
            pl.BlockSpec((96, FF), pinned(1)),
            pl.BlockSpec((256, MODEL_WIDTH), pinned(2)),
        ],
        out_shape=[
            jax.ShapeDtypeStruct((MODEL_WIDTH, FF), bf16),
            jax.ShapeDtypeStruct((MODEL_WIDTH, FF), bf16),
            jax.ShapeDtypeStruct((FF, MODEL_WIDTH), bf16),
        ],
        scratch_shapes=[pltpu.VMEM((1920, 128), f32), pltpu.VMEM((256, 128), f32)],
        name="unpack_feedforward",
    )(lines)


def pack_ff_kernel(gate_ref, up_ref, down_ref, lines_ref, scratch, mid):
    phase = pl.program_id(0)
    for number, source in ((0, gate_ref), (1, up_ref)):

        @pl.when(phase == number)
        def _():
            rows_to_lines_2560(
                lambda c: source[:, 128 * c : 128 * c + 128].astype(f32), scratch, 0, 96
            )

    @pl.when(phase == 2)
    def _():
        def load(c):
            if c < 7:
                return down_ref[:, 128 * c : 128 * c + 128].astype(f32)
            tail = down_ref[:, 896:960].astype(f32)
            return jnp.concatenate([tail, tail], axis=1)

        rows_to_lines_960(load, scratch, 0, 256, mid)

    lines_ref[...] = scratch[...].astype(bf16)


def pack_ff(gate, up, down):
    return pl.pallas_call(
        pack_ff_kernel,
        grid=(3, 10),
        in_specs=[
            pl.BlockSpec((96, FF), pinned(0)),
            pl.BlockSpec((96, FF), pinned(1)),
            pl.BlockSpec((256, MODEL_WIDTH), pinned(2)),
        ],
        out_specs=pl.BlockSpec((1920, 128), lambda p, j: (p * 10 + j, 0)),
        out_shape=jax.ShapeDtypeStruct((3 * 19200, 128), bf16),
        scratch_shapes=[pltpu.VMEM((1920, 128), f32), pltpu.VMEM((256, 128), f32)],
        name="pack_feedforward",
    )(gate, up, down)


def unpack_wide_kernel(lines_ref, out_ref, scratch, mid):
    for u in range(4):
        scratch[...] = lines_ref[u].astype(f32)
        base = u * 80

        def store(c, value):
            if c < 7:
                out_ref[base : base + 80, 128 * c : 128 * c + 128] = value.astype(bf16)
            else:
                out_ref[base : base + 80, 896:960] = value[:, :64].astype(bf16)

        lines_to_rows_960(scratch, 0, 80, mid, store)


def unpack_wide(lines, first):
    depth = lines.shape[1]
    return pl.pallas_call(
        unpack_wide_kernel,
        grid=(3,),
        in_specs=[pl.BlockSpec((4, depth, 128), lambda j: (first // 4 + j, 0, 0))],
        out_specs=pl.BlockSpec((320, MODEL_WIDTH), lambda j: (j, 0)),
        out_shape=jax.ShapeDtypeStruct((MODEL_WIDTH, MODEL_WIDTH), bf16),
        scratch_shapes=[pltpu.VMEM((depth, 128), f32), pltpu.VMEM((80, 128), f32)],
        name="unpack_attention",
    )(lines)


def unpack_kv_kernel(key_ref, value_ref, out_ref, key_lines, value_lines, mid):
    low = lane_low(120)
    key_lines[...] = key_ref[0].astype(f32)
    value_lines[...] = value_ref[0].astype(f32)
    keys = half_chunks([key_lines[pl.ds(k, 120, stride=5), :] for k in range(5)])
    values = half_chunks([value_lines[pl.ds(k, 120, stride=5), :] for k in range(5)])
    for h in range(KEY_VALUE_HEADS):
        for parity in range(2):
            mid[pl.ds(parity, 120, stride=2), :] = jnp.where(
                low, placed(keys[parity][h], 0), placed(values[parity][h], 1)
            )
        out_ref[:, 128 * h : 128 * h + 128] = mid[...].astype(bf16)


def unpack_kv(lines):
    depth = lines.shape[1]
    return pl.pallas_call(
        unpack_kv_kernel,
        grid=(4,),
        in_specs=[
            pl.BlockSpec((1, depth, 128), lambda j: (12 + j, 0, 0)),
            pl.BlockSpec((1, depth, 128), lambda j: (16 + j, 0, 0)),
        ],
        out_specs=pl.BlockSpec((240, 2 * KV_WIDTH), lambda j: (j, 0)),
        out_shape=jax.ShapeDtypeStruct((MODEL_WIDTH, 2 * KV_WIDTH), bf16),
        scratch_shapes=[
            pltpu.VMEM((depth, 128), f32),
            pltpu.VMEM((depth, 128), f32),
            pltpu.VMEM((240, 128), f32),
        ],
        name="unpack_key_value",
    )(lines, lines)


def pack_attention_kernel(query_ref, kv_ref, out_weight_ref, gains_ref, lines_ref, scratch, mid):
    step = pl.program_id(0)

    def wide(source):
        for u in range(4):
            base = u * 80

            def load(c):
                if c < 7:
                    return source[base : base + 80, 128 * c : 128 * c + 128].astype(f32)
                tail = source[base : base + 80, 896:960].astype(f32)
                return jnp.concatenate([tail, tail], axis=1)

            rows_to_lines_960(load, scratch, 0, 80, mid)
            lines_ref[u, :LINES, :] = scratch[...].astype(bf16)

    @pl.when(step < 3)
    def _():
        wide(query_ref)

    @pl.when(step >= 5)
    def _():
        wide(out_weight_ref)

    for number, upper in ((3, 0), (4, 1)):

        @pl.when(step == number)
        def _():
            low = lane_low(120)
            for u in range(4):
                evens, odds = [], []
                for h in range(KEY_VALUE_HEADS):
                    mid[...] = kv_ref[
                        240 * u : 240 * u + 240, 128 * h : 128 * h + 128
                    ].astype(f32)
                    evens.append((mid[pl.ds(0, 120, stride=2), :], upper))
                    odds.append((mid[pl.ds(1, 120, stride=2), :], upper))
                run = evens + odds
                for k in range(5):
                    scratch[pl.ds(k, 120, stride=5), :] = jnp.where(
                        low, placed(run[2 * k], 0), placed(run[2 * k + 1], 1)
                    )
                lines_ref[u, :LINES, :] = scratch[...].astype(bf16)

    for u in range(4):
        lines_ref[u, LINES:, :] = gains_ref[u]


def pack_attention(d_query, d_kv, d_out, gains):
    return pl.pallas_call(
        pack_attention_kernel,
        grid=(8,),
        in_specs=[
            pl.BlockSpec((320, MODEL_WIDTH), lambda s: (jnp.minimum(s, 2), 0)),
            pl.BlockSpec((MODEL_WIDTH, 2 * KV_WIDTH), lambda s: (0, 0)),
            pl.BlockSpec((320, MODEL_WIDTH), lambda s: (jnp.maximum(s - 5, 0), 0)),
            pl.BlockSpec((4, GAIN_LINES, 128), lambda s: (s, 0, 0)),
        ],
        out_specs=pl.BlockSpec((4, LINES + GAIN_LINES, 128), lambda s: (s, 0, 0)),
        out_shape=jax.ShapeDtypeStruct((UNITS, LINES + GAIN_LINES, 128), bf16),
        scratch_shapes=[pltpu.VMEM((LINES, 128), f32), pltpu.VMEM((240, 128), f32)],
        name="pack_attention",
    )(d_query, d_kv, d_out, gains)


def tile_range(starts_ref, fills_ref, block):
    first_slot = starts_ref[block] * BLK
    last_slot = block * BLK + fills_ref[block]
    tile_first = first_slot // TILE
    tile_last = (block * BLK) // TILE
    ragged_first = jnp.logical_and(first_slot % TILE != 0, tile_first < tile_last)
    return first_slot, last_slot, tile_first, tile_last, ragged_first.astype(jnp.int32)


def allowed_pairs(tile, block, first_slot, last_slot):
    key_slot = tile * TILE + lax.broadcasted_iota(jnp.int32, (TILE, WIDE), 0)
    lane = lax.broadcasted_iota(jnp.int32, (TILE, WIDE), 1)
    query_slot = block * BLK + lax.rem(lane, BLK)
    return jnp.logical_and(
        jnp.logical_and(key_slot >= first_slot, key_slot <= query_slot),
        jnp.logical_or(key_slot < last_slot, key_slot == query_slot),
    )


def over_tiles(span, block, step):
    first_slot, last_slot, tile_first, tile_last, ragged = span

    def masked(tile):
        step(tile, allowed_pairs(tile, block, first_slot, last_slot))

    def edge(k, carry):
        masked(jnp.where(k == ragged, tile_last, tile_first))
        return carry

    lax.fori_loop(0, 1 + ragged, edge, 0)

    def inner(tile, carry):
        step(tile, None)
        return carry

    lax.fori_loop(tile_first + ragged, tile_last, inner, 0)


def transpose_kv(kv_ref, turned, tiles):
    def body(t, carry):
        rows = pl.ds(pl.multiple_of(t * TILE, TILE), TILE)
        for h in range(KEY_VALUE_HEADS):
            turned[t, 128 * h : 128 * h + 128, :] = kv_ref[rows, 128 * h : 128 * h + 128].T
        return carry

    lax.fori_loop(0, tiles, body, 0)


def lay_out_kv(blocks, kv_ref, place):
    size = blocks[0].shape[0]
    for apart, block in enumerate(blocks):
        spot = apart if len(blocks) == 1 else place ^ apart
        kv_ref[pl.ds(pl.multiple_of(spot * size, TILE), size), :] = block[...]


def heads_beside(ref, h):
    return jnp.concatenate(
        [
            ref[HEAD_SIZE * (GROUPED * h + g) : HEAD_SIZE * (GROUPED * h + g + 1), :]
            for g in range(GROUPED)
        ],
        axis=1,
    )


def attention_forward_kernel(
    starts_ref, fills_ref, place_ref, query_ref, *refs
):
    kv_blocks = refs[:-8]
    mixed_ref, log_ref, kv_ref, turned, pairs, tops, totals, sums = refs[-8:]
    i = pl.program_id(0)
    block = place_ref[0] * (TOK_DEV // BLK) + i

    @pl.when(i == 0)
    def _():
        lay_out_kv(kv_blocks, kv_ref, place_ref[0])
        transpose_kv(kv_ref, turned, kv_ref.shape[0] // TILE)

    for h in range(KEY_VALUE_HEADS):
        pairs[h, :HEAD_SIZE, :] = heads_beside(query_ref, h)
        pairs[h, HEAD_SIZE:, :] = jnp.zeros((HEAD_SIZE, WIDE), bf16)
    tops[...] = jnp.full(tops.shape, masked_value, f32)
    totals[...] = jnp.zeros(totals.shape, f32)
    sums[...] = jnp.zeros(sums.shape, f32)

    def step(tile, allowed):
        rows = pl.ds(pl.multiple_of(tile * TILE, TILE), TILE)

        def score(h):
            return jnp.dot(
                kv_ref[rows, 128 * h : 128 * h + 128], pairs[h], preferred_element_type=f32
            )

        def weigh(h, scores):
            if allowed is not None:
                scores = jnp.where(allowed, scores, masked_value)
            top_old = tops[h]
            top = jnp.maximum(top_old, jnp.max(scores, axis=0, keepdims=True))
            weights = jnp.exp(scores - top)
            shrink = jnp.exp(top_old - top)
            tops[h] = top
            totals[h] = totals[h] * shrink + jnp.sum(weights, axis=0, keepdims=True)
            return weights.astype(bf16), shrink

        def gather(h, weights, shrink):
            sums[h] = sums[h] * shrink + jnp.dot(
                turned[tile, 128 * h + HEAD_SIZE : 128 * h + 128, :],
                weights,
                preferred_element_type=f32,
            )

        scores = [score(h) for h in range(KEY_VALUE_HEADS)]
        held = None
        for h in range(KEY_VALUE_HEADS):
            weighed = weigh(h, scores[h])
            if held is not None:
                gather(h - 1, *held)
            held = weighed
        gather(KEY_VALUE_HEADS - 1, *held)

    over_tiles(tile_range(starts_ref, fills_ref, block), block, step)
    for h in range(KEY_VALUE_HEADS):
        outcome = (sums[h] / totals[h]).astype(bf16)
        log_total = tops[h] + jnp.log(totals[h])
        for g in range(GROUPED):
            head = GROUPED * h + g
            mixed_ref[HEAD_SIZE * head : HEAD_SIZE * (head + 1), :] = outcome[:, BLK * g : BLK * (g + 1)]
            log_ref[head : head + 1, :] = log_total[:, BLK * g : BLK * (g + 1)]
    log_ref[QUERY_HEADS:, :] = jnp.zeros((1, BLK), f32)


def token_block(rows):
    return pl.BlockSpec((rows, BLK), lambda i, *_: (0, i))


def whole(shape):
    return pl.BlockSpec(shape, lambda i, *_: (0,) * len(shape))


def attention_forward(starts, fills, place, query, kv):
    group = sum(block.shape[0] for block in kv)
    return pl.pallas_call(
        attention_forward_kernel,
        grid_spec=pltpu.PrefetchScalarGridSpec(
            num_scalar_prefetch=3,
            grid=(TOK_DEV // BLK,),
            in_specs=[token_block(MODEL_WIDTH)] + [whole(block.shape) for block in kv],
            out_specs=[token_block(MODEL_WIDTH), token_block(16)],
            scratch_shapes=[
                pltpu.VMEM((group, 2 * KV_WIDTH), bf16),
                pltpu.VMEM((group // TILE, 2 * KV_WIDTH, TILE), bf16),
                pltpu.VMEM((KEY_VALUE_HEADS, 2 * HEAD_SIZE, WIDE), bf16),
                pltpu.VMEM((KEY_VALUE_HEADS, 1, WIDE), f32),
                pltpu.VMEM((KEY_VALUE_HEADS, 1, WIDE), f32),
                pltpu.VMEM((KEY_VALUE_HEADS, HEAD_SIZE, WIDE), f32),
            ],
        ),
        out_shape=[
            jax.ShapeDtypeStruct((MODEL_WIDTH, TOK_DEV), bf16),
            jax.ShapeDtypeStruct((16, TOK_DEV), f32),
        ],
        name="attention_forward",
    )(starts, fills, place, query, *kv)


def attention_backward_kernel(
    first,
    blocks,
    starts_ref,
    fills_ref,
    place_ref,
    query_ref,
    upstream_ref,
    mixed_ref,
    log_ref,
    cosine_ref,
    sine_ref,
    *refs,
):
    kv_blocks, refs = refs[:blocks], refs[-(blocks + 10) :]
    d_query_ref, d_kv_blocks = refs[0], refs[1 : blocks + 1]
    kv_ref, turned, pairs, query_rows, upstream_rows, deltas, logs, sums, kv_sums = refs[blocks + 1 :]
    count = kv_sums.shape[0]
    i = pl.program_id(0)
    block = place_ref[0] * (TOK_DEV // BLK) + i
    tiles = kv_ref.shape[0] // TILE

    @pl.when(i == 0)
    def _():
        for apart, source in enumerate(kv_blocks):
            size = source.shape[0]
            spot = apart if blocks == 1 else place_ref[0] ^ apart
            kv_ref[pl.ds(pl.multiple_of(spot * size, TILE), size), :] = source[
                :, 128 * first : 128 * (first + count)
            ]

        def prepare(t, carry):
            rows = pl.ds(pl.multiple_of(t * TILE, TILE), TILE)
            for h in range(count):
                turned[t, HEAD_SIZE * h : HEAD_SIZE * (h + 1), :] = kv_ref[
                    rows, 128 * h : 128 * h + 128
                ].T[:HEAD_SIZE]
            kv_sums[:, rows, :] = jnp.zeros((count, TILE, 128), f32)
            return carry

        lax.fori_loop(0, tiles, prepare, 0)

    blank = jnp.zeros((HEAD_SIZE, WIDE), bf16)
    for h in range(count):
        query = heads_beside(query_ref, first + h)
        upstream = heads_beside(upstream_ref, first + h)
        pairs[h, :HEAD_SIZE, :WIDE] = query
        pairs[h, HEAD_SIZE:, :WIDE] = blank
        pairs[h, :HEAD_SIZE, WIDE:] = blank
        pairs[h, HEAD_SIZE:, WIDE:] = upstream
        query_rows[h] = pairs[h, :, :WIDE].T
        upstream_rows[h] = pairs[h, :, WIDE:].T
        deltas[h] = jnp.sum(
            upstream.astype(f32) * heads_beside(mixed_ref, first + h).astype(f32),
            axis=0,
            keepdims=True,
        )
        line = GROUPED * (first + h)
        logs[h] = jnp.concatenate(
            [log_ref[line + g : line + g + 1, :] for g in range(GROUPED)], axis=1
        )
    sums[...] = jnp.zeros(sums.shape, f32)

    def step(tile, allowed):
        rows = pl.ds(pl.multiple_of(tile * TILE, TILE), TILE)

        def score(h):
            return jnp.dot(
                kv_ref[rows, 128 * h : 128 * h + 128], pairs[h], preferred_element_type=f32
            )

        def weigh(h, both):
            scores = both[:, :WIDE]
            if allowed is not None:
                scores = jnp.where(allowed, scores, masked_value)
            probs = jnp.exp(scores - logs[h])
            d_scores = (probs * (both[:, WIDE:] - deltas[h])).astype(bf16)
            return probs.astype(bf16), d_scores

        def gather(h, probs, d_scores):
            kv_sums[h, rows, :] += jnp.dot(
                d_scores, query_rows[h], preferred_element_type=f32
            ) + jnp.dot(probs, upstream_rows[h], preferred_element_type=f32)
            sums[h] += jnp.dot(
                turned[tile, HEAD_SIZE * h : HEAD_SIZE * (h + 1), :],
                d_scores,
                preferred_element_type=f32,
            )

        following = score(0)
        held = None
        for h in range(count):
            both = following
            if h + 1 < count:
                following = score(h + 1)
            weighed = weigh(h, both)
            if held is not None:
                gather(h - 1, *held)
            held = weighed
        gather(count - 1, *held)

    over_tiles(tile_range(starts_ref, fills_ref, block), block, step)
    cosine = cosine_ref[...]
    sine = sine_ref[...]
    half = HEAD_SIZE // 2
    for h in range(count):
        for g in range(GROUPED):
            head = GROUPED * h + g
            front = sums[h, :half, BLK * g : BLK * (g + 1)] * score_scale
            back = sums[h, half:, BLK * g : BLK * (g + 1)] * score_scale
            d_query_ref[HEAD_SIZE * head : HEAD_SIZE * head + half, :] = (
                front * cosine + back * sine
            ).astype(bf16)
            d_query_ref[HEAD_SIZE * head + half : HEAD_SIZE * (head + 1), :] = (
                back * cosine - front * sine
            ).astype(bf16)

    @pl.when(i == pl.num_programs(0) - 1)
    def _():
        size = kv_blocks[0].shape[0]
        for apart, out in enumerate(d_kv_blocks):
            spot = apart if blocks == 1 else place_ref[0] ^ apart

            def emit(t, carry):
                rows = pl.ds(pl.multiple_of(spot * size + t * TILE, TILE), TILE)
                for h in range(count):
                    out[pl.ds(pl.multiple_of(t * TILE, TILE), TILE), 128 * h : 128 * h + 128] = (
                        kv_sums[h, rows, :].astype(bf16)
                    )
                return carry

            lax.fori_loop(0, size // TILE, emit, 0)


def attention_backward(
    first, count, starts, fills, place, query, upstream, mixed, logs, cosine, sine, kv, after=()
):
    group = sum(block.shape[0] for block in kv)
    half = HEAD_SIZE // 2
    outs = [(block.shape[0], 128 * count) for block in kv]
    return pl.pallas_call(
        functools.partial(attention_backward_kernel, first, len(kv)),
        grid_spec=pltpu.PrefetchScalarGridSpec(
            num_scalar_prefetch=3,
            grid=(TOK_DEV // BLK,),
            in_specs=[
                token_block(MODEL_WIDTH),
                token_block(MODEL_WIDTH),
                token_block(MODEL_WIDTH),
                token_block(16),
                token_block(half),
                token_block(half),
            ]
            + [whole(block.shape) for block in kv]
            + [pl.BlockSpec(memory_space=pl.ANY)] * len(after),
            out_specs=[token_block(GROUPED * HEAD_SIZE * count)] + [whole(shape) for shape in outs],
            scratch_shapes=[
                pltpu.VMEM((group, 128 * count), bf16),
                pltpu.VMEM((group // TILE, HEAD_SIZE * count, TILE), bf16),
                pltpu.VMEM((count, 2 * HEAD_SIZE, 2 * WIDE), bf16),
                pltpu.VMEM((count, WIDE, 128), bf16),
                pltpu.VMEM((count, WIDE, 128), bf16),
                pltpu.VMEM((count, 1, WIDE), f32),
                pltpu.VMEM((count, 1, WIDE), f32),
                pltpu.VMEM((count, HEAD_SIZE, WIDE), f32),
                pltpu.VMEM((count, group, 128), f32),
            ],
        ),
        out_shape=[jax.ShapeDtypeStruct((GROUPED * HEAD_SIZE * count, TOK_DEV), bf16)]
        + [jax.ShapeDtypeStruct(shape, bf16) for shape in outs],
        name="attention_backward",
    )(starts, fills, place, query, upstream, mixed, logs, cosine, sine, *kv, *after)


def dot_of(left, right, left_dim, right_dim):
    return lax.dot_general(
        left, right, (((left_dim,), (right_dim,)), ((), ())), preferred_element_type=f32
    )


SLOTS = 3
FORM = 640
PIECES = (240, 240, 160)
GAIN_LINE = 560
PAD_WIDTH = 1024
CHUNK = 640
CORE_BIT = ("shard", 1)
ROW_BIT = ("shard", 2)
NEAR_BITS = (ROW_BIT, ("dp", 1), ("dp", 2))
FAR_BITS = (("dp", 4),)
BACKWARD_CALLS = ((0, 3), (3, 2))


def stages(colour):
    return (CORE_BIT,) + NEAR_BITS[colour:] + NEAR_BITS[:colour] + FAR_BITS


def swap(value, bit):
    axis, mask = bit
    size = lax.axis_size(axis)
    return lax.ppermute(value, axis, [(i, i ^ mask) for i in range(size)])


def gather_colour(own, colour):
    held = own[None]
    for bit in reversed(stages(colour)[1:]):
        held = jnp.concatenate([held, swap(held, bit)], axis=0)
    return held, swap(held, CORE_BIT)


def scatter_stage(held, number):
    outcome = []
    total = lambda parts: sum(part.astype(f32) for part in parts)
    for colour, (parts, send) in enumerate(held):
        got = swap(send, stages(colour)[number])
        half = got.shape[0] // 2
        if half == 0:
            outcome.append((total(parts)[0].astype(bf16), got[0]))
        else:
            parts = parts + [got]
            outcome.append(
                ([part[:half] for part in parts], total([part[half:] for part in parts]).astype(bf16))
            )
    return outcome


def positions():
    device = jnp.arange(UNITS, dtype=jnp.int32)
    width = lax.axis_size("shard")
    apart = {
        "dp": (device // width) ^ lax.axis_index("dp").astype(jnp.int32),
        "shard": (device % width) ^ lax.axis_index("shard").astype(jnp.int32),
    }
    tables = []
    for colour in range(SLOTS):
        place = jnp.zeros((UNITS,), jnp.int32)
        for axis, mask in stages(colour):
            place = 2 * place + (apart[axis] & mask) // mask
        tables.append(place)
    return jnp.concatenate(tables)


def copy_from(halves, place, dst, sem, pick=lambda ref: ref):
    for number, ref in enumerate(halves):

        @pl.when(place // 16 == number)
        def _():
            pltpu.make_async_copy(pick(ref.at[lax.rem(place, 16)]), dst, sem).start()


def copy_to(src, halves, place, sem, pick=lambda ref: ref):
    for number, ref in enumerate(halves):

        @pl.when(place // 16 == number)
        def _():
            pltpu.make_async_copy(src, pick(ref.at[lax.rem(place, 16)]), sem).start()


def wait_for(ref, sem):
    pltpu.make_async_copy(ref, ref, sem).wait()


def form_attention_kernel(wide_ref, lines_ref, gains_ref, a_ref, b_ref, c_ref, mid, form):
    @pl.when(wide_ref[0] == 1)
    def _():
        def store(c, value):
            if c == 7:
                value = jnp.where(lane_low(80), value, 0.0)
            form[80 * c : 80 * c + 80, :] = value

        lines_to_rows_960(lines_ref, 0, 80, mid, store)

    @pl.when(wide_ref[0] == 0)
    def _():
        low = lane_low(120)
        line = [lines_ref[pl.ds(k, 120, stride=5), :] for k in range(5)]
        turned = [None, None] + [pltpu.roll(line[k], 64, 1) for k in range(2, 5)]
        form[pl.ds(0, 120, stride=2), :] = line[0]
        form[pl.ds(1, 120, stride=2), :] = jnp.where(low, turned[2], turned[3])
        form[pl.ds(240, 120, stride=2), :] = line[1]
        form[pl.ds(241, 120, stride=2), :] = jnp.where(low, turned[3], turned[4])
        mid[pl.ds(0, 120, stride=2), :] = line[2]
        mid[pl.ds(1, 120, stride=2), :] = turned[4]
        low = lane_low(80)
        form[480:560, :] = jnp.where(low, mid[0:80, :], pltpu.roll(mid[160:240, :], 64, 1))
        form[560:640, :] = jnp.where(low, mid[80:160, :], 0.0)

    form[GAIN_LINE : GAIN_LINE + 1, :] = jnp.where(
        lane_low(1), form[GAIN_LINE : GAIN_LINE + 1, :], gains_ref[...]
    )
    a_ref[...] = form[0:240, :].astype(bf16)
    b_ref[...] = form[240:480, :].astype(bf16)
    c_ref[...] = form[480:640, :].astype(bf16)


SMEM_SPEC = pl.BlockSpec(memory_space=pltpu.SMEM)
ANY_SPEC = pl.BlockSpec(memory_space=pl.ANY)


def form_attention(wide, lines, gains):
    return pl.pallas_call(
        form_attention_kernel,
        in_specs=[SMEM_SPEC, pl.BlockSpec((LINES, 128)), pl.BlockSpec((1, 128))],
        out_shape=[jax.ShapeDtypeStruct((n, 128), bf16) for n in PIECES],
        scratch_shapes=[pltpu.VMEM((240, 128), f32), pltpu.VMEM((FORM, 128), f32)],
        name="form_attention",
    )(wide, lines, gains)


def unform_attention_kernel(wide_ref, *refs):
    pieces, (lines_ref, gains_ref, mid, form) = refs[:6], refs[6:]
    base = 0
    for n, keep, got in zip(PIECES, pieces[0::2], pieces[1::2]):
        form[base : base + n, :] = keep[...].astype(f32) + got[...].astype(f32)
        base += n
    gains_ref[...] = form[GAIN_LINE : GAIN_LINE + 1, :]

    @pl.when(wide_ref[0] == 1)
    def _():
        rows_to_lines_960(lambda c: form[80 * c : 80 * c + 80, :], lines_ref, 0, 80, mid)

    @pl.when(wide_ref[0] == 0)
    def _():
        low = lane_low(120)
        mid[0:80, :] = form[480:560, :]
        mid[80:160, :] = form[560:640, :]
        mid[160:240, :] = pltpu.roll(form[480:560, :], 64, 1)
        even = [form[pl.ds(0, 120, stride=2), :], form[pl.ds(240, 120, stride=2), :]]
        odd = [form[pl.ds(1, 120, stride=2), :], form[pl.ds(241, 120, stride=2), :]]
        even.append(mid[pl.ds(0, 120, stride=2), :])
        odd.append(mid[pl.ds(1, 120, stride=2), :])
        odd = [pltpu.roll(value, 64, 1) for value in odd]
        lines_ref[pl.ds(0, 120, stride=5), :] = even[0]
        lines_ref[pl.ds(1, 120, stride=5), :] = even[1]
        lines_ref[pl.ds(2, 120, stride=5), :] = jnp.where(low, even[2], odd[0])
        lines_ref[pl.ds(3, 120, stride=5), :] = jnp.where(low, odd[0], odd[1])
        lines_ref[pl.ds(4, 120, stride=5), :] = jnp.where(low, odd[1], odd[2])


def unform_attention(wide, addends):
    return pl.pallas_call(
        unform_attention_kernel,
        in_specs=[SMEM_SPEC] + [pl.BlockSpec((n, 128)) for n in PIECES for _ in range(2)],
        out_shape=[jax.ShapeDtypeStruct((LINES, 128), f32), jax.ShapeDtypeStruct((1, 128), f32)],
        scratch_shapes=[pltpu.VMEM((240, 128), f32), pltpu.VMEM((FORM, 128), f32)],
        name="unform_attention",
    )(wide, *addends)


def wide_pieces(c):
    return [((80 * c + 16 * m) // 32, (80 * c + 16 * m) % 32, 16 * m) for m in range(5)]


def form_feedforward_kernel(narrow_ref, lines_ref, out, mid):
    for s in range(SLOTS):

        @pl.when(narrow_ref[s] == 1)
        def _():
            mid[30:32, :] = jnp.zeros((2, 128), f32)
            for c in range(20):
                mid[0:30, :] = lines_ref[pl.ds(LINES * s + c, 30, stride=20), :]
                out[s, c] = mid[0:32, :].astype(bf16)

        @pl.when(narrow_ref[s] == 0)
        def _():
            def store(c, value):
                if c == 7:
                    value = jnp.where(lane_low(80), value, 0.0)
                for k, r, m in wide_pieces(c):
                    out[s, k, r : r + 16, :] = value[m : m + 16].astype(bf16)

            lines_to_rows_960(lines_ref, LINES * s, 80, mid, store)


def form_feedforward(narrow, lines):
    return pl.pallas_call(
        form_feedforward_kernel,
        in_specs=[SMEM_SPEC, pl.BlockSpec((SLOTS * LINES, 128))],
        out_shape=jax.ShapeDtypeStruct((SLOTS, 20, 32, 128), bf16),
        scratch_shapes=[pltpu.VMEM((80, 128), f32)],
        name="form_feedforward",
    )(narrow, lines)


def unform_feedforward_kernel(narrow_ref, *refs):
    pieces, (lines_ref, mid) = refs[: 2 * SLOTS], refs[2 * SLOTS :]
    for s in range(SLOTS):
        keep, got = pieces[2 * s], pieces[2 * s + 1]

        @pl.when(narrow_ref[s] == 1)
        def _():
            for c in range(20):
                mid[0:32, :] = keep[c].astype(f32) + got[c].astype(f32)
                lines_ref[pl.ds(LINES * s + c, 30, stride=20), :] = mid[0:30, :]

        @pl.when(narrow_ref[s] == 0)
        def _():
            def load(c):
                return jnp.concatenate(
                    [
                        keep[k, r : r + 16, :].astype(f32) + got[k, r : r + 16, :].astype(f32)
                        for k, r, m in wide_pieces(c)
                    ],
                    axis=0,
                )

            rows_to_lines_960(load, lines_ref, LINES * s, 80, mid)


def unform_feedforward(narrow, addends):
    return pl.pallas_call(
        unform_feedforward_kernel,
        in_specs=[SMEM_SPEC] + [pl.BlockSpec((20, 32, 128))] * (2 * SLOTS),
        out_shape=jax.ShapeDtypeStruct((SLOTS * LINES, 128), f32),
        scratch_shapes=[pltpu.VMEM((80, 128), f32)],
        name="unform_feedforward",
    )(narrow, *addends)


def place_attention_kernel(table_ref, *refs):
    halves = [refs[2 * k : 2 * k + 2] for k in range(SLOTS)]
    query_ref, kv_ref, out_ref, gains_ref, units, sem = refs[2 * SLOTS :]

    def start(d, carry):
        base = 0
        for k, n in enumerate(PIECES):
            copy_from(halves[k], table_ref[UNITS * k + d], units.at[d, base : base + n, :], sem)
            base += n
        return carry

    lax.fori_loop(0, UNITS, start, 0)
    wait_for(units, sem)

    def wide(out, first):
        def body(u, carry):
            rows = pl.ds(pl.multiple_of(80 * u, 16), 80)
            for c in range(7):
                out[rows, 128 * c : 128 * c + 128] = units[first + u, 80 * c : 80 * c + 80, :]
            out[rows, 896:960] = units[first + u, 560:640, :64]
            return carry

        lax.fori_loop(0, 12, body, 0)

    def keyed(j, carry):
        low = lane_low(240)
        chunks = []
        for first in (12, 16):
            unit = units[first + j].astype(f32)
            last = jnp.concatenate(
                [unit[480:640], pltpu.roll(unit[480:560], 64, 1)], axis=0
            )
            lines = (unit[0:240], unit[240:480], last)
            chunks.append([(lines[h // 2], h % 2) for h in range(KEY_VALUE_HEADS)])
        rows = pl.ds(pl.multiple_of(240 * j, 16), 240)
        for h in range(KEY_VALUE_HEADS):
            kv_ref[rows, 128 * h : 128 * h + 128] = jnp.where(
                low, placed(chunks[0][h], 0), placed(chunks[1][h], 1)
            ).astype(bf16)
        return carry

    lax.fori_loop(0, 4, keyed, 0)
    wide(query_ref, 0)
    wide(out_ref, 20)
    for u in range(UNITS):
        gains_ref[u : u + 1, :] = units[u, GAIN_LINE : GAIN_LINE + 1, :].astype(f32)


def place_attention(table, gathered):
    return pl.pallas_call(
        place_attention_kernel,
        in_specs=[SMEM_SPEC] + [ANY_SPEC] * (2 * SLOTS),
        out_shape=[
            jax.ShapeDtypeStruct((MODEL_WIDTH, MODEL_WIDTH), bf16),
            jax.ShapeDtypeStruct((MODEL_WIDTH, 2 * KV_WIDTH), bf16),
            jax.ShapeDtypeStruct((MODEL_WIDTH, MODEL_WIDTH), bf16),
            jax.ShapeDtypeStruct((UNITS, 128), f32),
        ],
        scratch_shapes=[pltpu.VMEM((UNITS, FORM, 128), bf16), pltpu.SemaphoreType.DMA],
        name="place_attention",
    )(table, *gathered)


def split_attention_kernel(table_ref, query_ref, kv_ref, out_ref, gains_ref, *refs):
    halves = [refs[2 * k : 2 * k + 2] for k in range(SLOTS)]
    units, sem = refs[2 * SLOTS :]

    def send(d):
        row = lax.broadcasted_iota(jnp.int32, (16, 128), 0)
        lane = lax.broadcasted_iota(jnp.int32, (16, 128), 1)
        block = units[d, GAIN_LINE : GAIN_LINE + 16, :].astype(f32)
        units[d, GAIN_LINE : GAIN_LINE + 16, :] = jnp.where(
            jnp.logical_and(row == 0, lane >= 64), gains_ref[pl.ds(d, 1), :], block
        ).astype(bf16)
        base = 0
        for k, n in enumerate(PIECES):
            copy_to(units.at[d, base : base + n, :], halves[k], table_ref[UNITS * k + d], sem)
            base += n

    def wide(source, first):
        def body(u, carry):
            rows = pl.ds(pl.multiple_of(80 * u, 16), 80)
            for c in range(7):
                units[first + u, 80 * c : 80 * c + 80, :] = source[rows, 128 * c : 128 * c + 128]
            tail = source[rows, 896:960]
            units[first + u, 560:640, :] = jnp.concatenate([tail, jnp.zeros_like(tail)], axis=1)
            send(first + u)
            return carry

        lax.fori_loop(0, 12, body, 0)

    def keyed(j, carry):
        low = lane_low(240)
        rows = pl.ds(pl.multiple_of(240 * j, 16), 240)
        for upper, first in ((0, 12), (1, 16)):
            heads = [
                (kv_ref[rows, 128 * h : 128 * h + 128].astype(f32), upper)
                for h in range(KEY_VALUE_HEADS)
            ]
            for c in range(2):
                units[first + j, 240 * c : 240 * c + 240, :] = jnp.where(
                    low, placed(heads[2 * c], 0), placed(heads[2 * c + 1], 1)
                ).astype(bf16)
            last = placed(heads[4], 0)
            turned = placed(heads[4], 1)
            units[first + j, 480:560, :] = jnp.where(
                lane_low(80), last[0:80], turned[160:240]
            ).astype(bf16)
            units[first + j, 560:640, :] = jnp.where(lane_low(80), last[80:160], 0.0).astype(bf16)
            send(first + j)
        return carry

    lax.fori_loop(0, 4, keyed, 0)
    wide(query_ref, 0)
    wide(out_ref, 20)
    wait_for(units, sem)


def split_attention(table, d_query, d_kv, d_out, gains):
    return pl.pallas_call(
        split_attention_kernel,
        in_specs=[
            SMEM_SPEC,
            pl.BlockSpec((MODEL_WIDTH, MODEL_WIDTH)),
            pl.BlockSpec((MODEL_WIDTH, 2 * KV_WIDTH)),
            pl.BlockSpec((MODEL_WIDTH, MODEL_WIDTH)),
            pl.BlockSpec((UNITS, 128)),
        ],
        out_specs=[ANY_SPEC] * (2 * SLOTS),
        out_shape=[jax.ShapeDtypeStruct((16, n, 128), bf16) for n in PIECES for _ in range(2)],
        scratch_shapes=[pltpu.VMEM((UNITS, FORM, 128), bf16), pltpu.SemaphoreType.DMA],
        name="split_attention",
    )(table, d_query, d_kv, d_out, gains)


def feedforward_kernel(
    table_ref,
    hidden_ref,
    turned_ref,
    grad_ref,
    gate_ref,
    up_ref,
    down_ref,
    out_ref,
    d_hidden_ref,
    *refs,
):
    targets = [refs[2 * s : 2 * s + 2] for s in range(SLOTS)]
    down, inner_rows, inner_turned, d_both, both_out, down_out, sems = refs[2 * SLOTS :]
    q = pl.program_id(0)
    chunks = pl.num_programs(0)
    slot = lax.rem(q, 2)

    def send_terms():
        for u in range(2 * UNITS):
            device, s = divmod(u, SLOTS)
            copy_to(
                both_out.at[slot, u // UNITS, u % UNITS],
                targets[s],
                table_ref[UNITS * s + device],
                sems.at[slot, 0],
                lambda ref: ref.at[pl.ds(5 * q, 5)],
            )
        for v in range(8):
            unit = 2 * UNITS + 8 * q + v
            device = unit // SLOTS
            for s in range(SLOTS):

                @pl.when(unit - SLOTS * device == s)
                def _():
                    copy_to(
                        down_out.at[slot, v],
                        targets[s],
                        table_ref[UNITS * s + device],
                        sems.at[slot, 1],
                    )

    def wait_terms(side):
        wait_for(both_out.at[side], sems.at[side, 0])
        wait_for(down_out.at[side], sems.at[side, 1])

    for v in range(8):
        for c in range(8):
            for k, r, m in wide_pieces(c):
                down[80 * v + m : 80 * v + m + 16, 128 * c : 128 * c + 128] = down_ref[
                    v, k, r : r + 16, :
                ]

    @pl.when(q == 0)
    def _():
        out_ref[...] = jnp.zeros(out_ref.shape, f32)
        d_hidden_ref[...] = jnp.zeros(d_hidden_ref.shape, f32)

    def rows_step(i, carry):
        rows = pl.ds(pl.multiple_of(256 * i, 256), 256)
        weights = jnp.concatenate(
            [ref[:, c].reshape(PAD_WIDTH, 128) for ref in (gate_ref, up_ref) for c in range(5)],
            axis=1,
        )
        both = jnp.dot(hidden_ref[rows, :], weights, preferred_element_type=f32)
        gate, upper = both[:, :CHUNK], both[:, CHUNK:]
        sigmoid_gate = jax.nn.sigmoid(gate)
        activated = gate * sigmoid_gate
        inner = (activated * upper).astype(bf16)
        inner_rows[rows, :] = inner
        out_ref[rows, :] += jnp.dot(inner, down[...], preferred_element_type=f32)
        d_inner = dot_of(grad_ref[rows, :], down[...], 1, 1)
        d_gate = d_inner * upper * sigmoid_gate * (1.0 + gate * (1.0 - sigmoid_gate))
        d_upper = d_inner * activated
        d_pair = jnp.concatenate([d_gate, d_upper], axis=1).astype(bf16)
        d_both[rows, :] = d_pair
        d_hidden_ref[rows, :] += dot_of(d_pair, weights, 1, 1)
        return carry

    lax.fori_loop(0, 2, rows_step, 0)
    inner_turned[...] = inner_rows[...].T

    @pl.when(q >= 2)
    def _():
        wait_terms(slot)

    def both_step(i, carry):
        rows = pl.ds(pl.multiple_of(256 * i, 256), 256)
        terms = jnp.dot(turned_ref[rows, :], d_both[...], preferred_element_type=f32).astype(bf16)
        units = pl.ds(8 * i, 8)
        for c in range(10):
            both_out[slot, c // 5, units, c % 5] = terms[:, 128 * c : 128 * c + 128].reshape(
                8, 32, 128
            )
        return carry

    lax.fori_loop(0, 4, both_step, 0)

    def down_step(i, carry):
        rows = pl.ds(pl.multiple_of(320 * i, 16), 320)
        terms = jnp.dot(
            inner_turned[rows, :], grad_ref[...], preferred_element_type=f32
        ).astype(bf16)
        for v in range(4):
            for c in range(8):
                for k, r, m in wide_pieces(c):
                    down_out[slot, 4 * i + v, k, r : r + 16, :] = terms[
                        80 * v + m : 80 * v + m + 16, 128 * c : 128 * c + 128
                    ]
        return carry

    lax.fori_loop(0, 2, down_step, 0)
    send_terms()

    @pl.when(q == chunks - 1)
    def _():
        for side in range(2):
            wait_terms(side)


def feedforward(table, hidden, turned, grad, weights):
    block = jax.ShapeDtypeStruct((16, 20, 32, 128), bf16)
    full = lambda shape: pl.BlockSpec(shape, lambda q: (0, 0))
    return pl.pallas_call(
        feedforward_kernel,
        grid=(FF // CHUNK,),
        in_specs=[
            SMEM_SPEC,
            full((TOK_DEV, PAD_WIDTH)),
            full((PAD_WIDTH, TOK_DEV)),
            full((TOK_DEV, PAD_WIDTH)),
            pl.BlockSpec((32, 5, 32, 128), lambda q: (0, q, 0, 0)),
            pl.BlockSpec((32, 5, 32, 128), lambda q: (1, q, 0, 0)),
            pl.BlockSpec((8, 20, 32, 128), lambda q: (8 + q, 0, 0, 0)),
        ],
        out_specs=[full((TOK_DEV, PAD_WIDTH))] * 2 + [ANY_SPEC] * (2 * SLOTS),
        out_shape=[jax.ShapeDtypeStruct((TOK_DEV, PAD_WIDTH), f32)] * 2 + [block] * (2 * SLOTS),
        scratch_shapes=[
            pltpu.VMEM((CHUNK, PAD_WIDTH), bf16),
            pltpu.VMEM((TOK_DEV, CHUNK), bf16),
            pltpu.VMEM((CHUNK, TOK_DEV), bf16),
            pltpu.VMEM((TOK_DEV, 2 * CHUNK), bf16),
            pltpu.VMEM((2, 2, 32, 5, 32, 128), bf16),
            pltpu.VMEM((2, 8, 20, 32, 128), bf16),
            pltpu.SemaphoreType.DMA((2, 2)),
        ],
        compiler_params=pltpu.CompilerParams(vmem_limit_bytes=60 * 2**20),
        name="feedforward",
    )(table, hidden, turned, grad, weights, weights, weights)


def spread_matrix():
    column = jnp.arange(PAD_WIDTH, dtype=jnp.int32)
    entry = jnp.where(column % 32 < 30, 30 * (column // 32) + column % 32, -1)
    return (jnp.arange(MODEL_WIDTH, dtype=jnp.int32)[:, None] == entry[None, :]).astype(bf16)


def rope_tables(positions):
    steps = jnp.arange(HEAD_SIZE // 2, dtype=f32) * (2.0 / HEAD_SIZE)
    inverse = jnp.exp(-math.log(10000.0) * steps)
    angles = inverse[:, None] * positions.astype(f32)[None, :]
    return (jnp.cos(angles), jnp.sin(angles))


def norm_scale(field):
    return lax.rsqrt(jnp.mean(field * field, axis=1, keepdims=True) + epsilon)


def norm_back(upstream, normed, scale, gain):
    scaled = upstream * gain[None, :]
    return scale * (scaled - normed * jnp.mean(scaled * normed, axis=1, keepdims=True))


def adam_step(grad, moment, second, master):
    moment_new = 0.9 * moment + 0.1 * grad
    second_new = 0.999 * second + 0.001 * grad * grad
    corrected = moment_new / (1.0 - 0.9**ADAM_STEP)
    scaled = second_new / (1.0 - 0.999**ADAM_STEP)
    update = -learning_rate * (corrected / (jnp.sqrt(scaled) + 1e-08) + weight_decay * master)
    return (moment_new, second_new, update)


def gather_lines(block):
    return lax.all_gather(block, ALL_AXES, axis=0, tiled=True)


def scatter_lines(lines):
    return lax.psum_scatter(lines, ALL_AXES, scatter_dimension=0, tiled=True)


def local(
    layer_input,
    cotangent,
    master_attention,
    master_feedforward,
    master_gains,
    first_attention,
    second_attention,
    first_feedforward,
    second_feedforward,
    first_gains,
    second_gains,
    block_start,
    block_fill,
):
    devices = lax.axis_size(ALL_AXES)
    attention_lines = master_attention.shape[0] // 128
    feedforward_lines = master_feedforward.shape[0] // 128
    gain_count = master_gains.shape[0]
    padded = (attention_lines // 16 + 1) * 16

    in_units = devices == UNITS
    if in_units:
        table = positions()
        device = (
            lax.axis_index("dp") * lax.axis_size("shard") + lax.axis_index("shard")
        ).astype(jnp.int32)
        wide = jnp.logical_or(device < 12, device >= 20).astype(jnp.int32)[None]
        narrow = (SLOTS * device + jnp.arange(SLOTS, dtype=jnp.int32) < 2 * UNITS).astype(jnp.int32)
        gain_row = jnp.pad(
            master_gains.reshape(1, gain_count), ((0, 0), (64, 64 - gain_count))
        )
        pieces = form_attention(wide, master_attention.reshape(LINES, 128), gain_row)
        gathered = [half for k in range(SLOTS) for half in gather_colour(pieces[k], k)]
        forms = form_feedforward(narrow, master_feedforward.reshape(SLOTS * LINES, 128))
        feedforward_all = gather_lines(forms.reshape(SLOTS * FORM, 128))
        query_weight, kv_weight, out_weight, gain_rows = place_attention(table, gathered)
        gains_all = gain_rows[:, 64 : 64 + gain_count].reshape(-1)
    else:
        gain_lines = jnp.pad(
            master_gains.astype(bf16).reshape(1, gain_count),
            ((0, padded - attention_lines - 1), (0, 128 - gain_count)),
        )
        attention_block = jnp.concatenate(
            [master_attention.astype(bf16).reshape(attention_lines, 128), gain_lines], axis=0
        )
        by_device = gather_lines(attention_block).reshape(devices, padded, 128)
        feedforward_all = gather_lines(
            master_feedforward.astype(bf16).reshape(feedforward_lines, 128)
        )
        gains_all = by_device[:, attention_lines, :gain_count].reshape(-1).astype(f32)
        units = by_device[:, :attention_lines].reshape(UNITS, LINES, 128)
        query_weight = unpack_wide(units, 0)
        kv_weight = unpack_kv(units)
        out_weight = unpack_wide(units, 20)
    gain_one, gain_two = gains_all[:MODEL_WIDTH], gains_all[MODEL_WIDTH:]

    shard = lax.axis_index("shard").astype(jnp.int32)
    place = shard[None]
    first_row = shard * TOK_DEV
    first_block = shard * (TOK_DEV // BLK)
    local_slots = first_row + jnp.arange(TOK_DEV, dtype=jnp.int32)
    local_starts = lax.dynamic_slice_in_dim(block_start, first_block, TOK_DEV // BLK)
    local_fills = lax.dynamic_slice_in_dim(block_fill, first_block, TOK_DEV // BLK)
    live_rows = local_slots % BLK < jnp.repeat(local_fills, BLK)
    cosine_table, sine_table = rope_tables(local_slots - jnp.repeat(local_starts, BLK) * BLK)

    def rotate(field, scale):
        heads = field.shape[0]
        front = field[:, : HEAD_SIZE // 2]
        back = field[:, HEAD_SIZE // 2 :]
        return (
            jnp.concatenate(
                [
                    front * cosine_table[None] - back * sine_table[None],
                    back * cosine_table[None] + front * sine_table[None],
                ],
                axis=1,
            ).astype(bf16)
            * bf16(scale)
        ).reshape(heads * HEAD_SIZE, TOK_DEV)

    inputs = layer_input.astype(f32)
    scale_one = norm_scale(inputs)
    normed_one = inputs * scale_one
    first_hidden = (normed_one * gain_one[None, :]).astype(bf16)
    kv_turned = dot_of(kv_weight, first_hidden, 0, 1).reshape(
        KEY_VALUE_HEADS, 2, HEAD_SIZE, TOK_DEV
    )
    keys = rotate(kv_turned[:, 0], 1.0).reshape(KEY_VALUE_HEADS, 1, HEAD_SIZE, TOK_DEV)
    values = kv_turned[:, 1:].astype(bf16)
    kv_rows = jnp.concatenate([keys, values], axis=1).reshape(2 * KV_WIDTH, TOK_DEV).T
    if in_units:
        across = swap(kv_rows, ROW_BIT)
        kv_all = [kv_rows, swap(kv_rows, CORE_BIT), across, swap(across, CORE_BIT)]
    else:
        kv_all = [lax.all_gather(kv_rows, "shard", axis=0, tiled=True)]
    query_turned = rotate(
        dot_of(query_weight, first_hidden, 0, 1).reshape(QUERY_HEADS, HEAD_SIZE, TOK_DEV),
        score_scale,
    )
    mixed_turned, logs = attention_forward(block_start, block_fill, place, query_turned, kv_all)
    middle = inputs + dot_of(mixed_turned, out_weight, 0, 0)
    scale_two = norm_scale(middle)
    normed_two = middle * scale_two
    hidden_two = (normed_two * gain_two[None, :]).astype(bf16)

    grad_out = cotangent.astype(f32) * live_rows[:, None].astype(f32)
    grad_low = grad_out.astype(bf16)
    if in_units:
        spread = spread_matrix()
        outcome, d_spread, *ff_terms = feedforward(
            table,
            dot_of(hidden_two, spread, 1, 0).astype(bf16),
            dot_of(spread, hidden_two, 0, 1).astype(bf16),
            jnp.pad(grad_low, ((0, 0), (0, PAD_WIDTH - MODEL_WIDTH))),
            feedforward_all.reshape(3 * UNITS, 20, 32, 128),
        )
        layer_output = middle + outcome[:, :MODEL_WIDTH]
        d_coarse = lax.reduce_precision(d_spread, 8, 7)
        d_hidden_two = dot_of(d_coarse.astype(bf16), spread, 1, 1) + dot_of(
            (d_spread - d_coarse).astype(bf16), spread, 1, 1
        )
        ff_held = [([ff_terms[2 * k]], ff_terms[2 * k + 1]) for k in range(SLOTS)]
    else:
        gate_weight, up_weight, down_weight = unpack_ff(feedforward_all)
        gate = dot_of(hidden_two, gate_weight, 1, 0)
        upper = dot_of(hidden_two, up_weight, 1, 0)
        sigmoid_gate = jax.nn.sigmoid(gate)
        activated = gate * sigmoid_gate
        inner = (activated * upper).astype(bf16)
        layer_output = middle + dot_of(inner, down_weight, 1, 0)
        d_down_weight = dot_of(inner, grad_low, 0, 0).astype(bf16)
        d_inner = dot_of(grad_low, down_weight, 1, 1)
        d_gate = (
            d_inner * upper * sigmoid_gate * (1.0 + gate * (1.0 - sigmoid_gate))
        ).astype(bf16)
        d_upper = (d_inner * activated).astype(bf16)
        d_gate_weight = dot_of(hidden_two, d_gate, 0, 0).astype(bf16)
        d_up_weight = dot_of(hidden_two, d_upper, 0, 0).astype(bf16)
        d_hidden_two = dot_of(d_gate, gate_weight, 1, 1) + dot_of(d_upper, up_weight, 1, 1)
        feedforward_gradient = (
            scatter_lines(pack_ff(d_gate_weight, d_up_weight, d_down_weight))
            .astype(f32)
            .reshape(-1)
        )

    d_gain_two = jnp.sum(d_hidden_two * normed_two, axis=0)
    d_middle = grad_out + norm_back(d_hidden_two, normed_two, scale_two, gain_two)

    d_branch = d_middle.astype(bf16)
    d_out_weight = dot_of(mixed_turned, d_branch, 1, 0).astype(bf16)
    d_mixed = dot_of(out_weight, d_branch, 1, 1).astype(bf16)
    backward_of = lambda first, count, after: attention_backward(
        first,
        count,
        block_start,
        block_fill,
        place,
        query_turned,
        d_mixed,
        mixed_turned,
        logs,
        cosine_table,
        sine_table,
        kv_all,
        after,
    )
    if in_units:
        d_query, d_kv_rows = [], []
        for number, (first, count) in enumerate(BACKWARD_CALLS):
            ff_held = scatter_stage(ff_held, number)
            d_query_part, *d_kv = backward_of(first, count, [send for _, send in ff_held])
            across = d_kv[2] + swap(d_kv[3], CORE_BIT)
            d_query.append(d_query_part)
            d_kv_rows.append(d_kv[0] + swap(d_kv[1], CORE_BIT) + swap(across, ROW_BIT))
        d_query = jnp.concatenate(d_query, axis=0)
        d_kv_rows = jnp.concatenate(d_kv_rows, axis=1)
        for number in range(len(BACKWARD_CALLS), len(stages(0))):
            ff_held = scatter_stage(ff_held, number)
        ff_addends = [addend for pair in ff_held for addend in pair]
        feedforward_gradient = unform_feedforward(narrow, ff_addends).reshape(-1)
    else:
        d_query, d_kv = backward_of(0, KEY_VALUE_HEADS, ())
        d_kv_rows = lax.psum_scatter(d_kv, "shard", scatter_dimension=0, tiled=True)
    d_kv_turned = d_kv_rows.T.reshape(KEY_VALUE_HEADS, 2, HEAD_SIZE, TOK_DEV)
    d_front = d_kv_turned[:, 0, : HEAD_SIZE // 2].astype(f32)
    d_back = d_kv_turned[:, 0, HEAD_SIZE // 2 :].astype(f32)
    d_keys = jnp.concatenate(
        [
            d_front * cosine_table[None] + d_back * sine_table[None],
            d_back * cosine_table[None] - d_front * sine_table[None],
        ],
        axis=1,
    ).astype(bf16)
    d_kv_lin = jnp.concatenate([d_keys[:, None], d_kv_turned[:, 1:]], axis=1).reshape(
        2 * KV_WIDTH, TOK_DEV
    )
    d_query_weight = dot_of(first_hidden, d_query, 0, 1).astype(bf16)
    d_kv_weight = dot_of(first_hidden, d_kv_lin, 0, 1).astype(bf16)
    d_hidden_one = dot_of(d_query, query_weight, 0, 1) + dot_of(d_kv_lin, kv_weight, 0, 1)
    d_gain_one = jnp.sum(d_hidden_one * normed_one, axis=0)
    input_gradient = d_middle + norm_back(d_hidden_one, normed_one, scale_one, gain_one)

    gain_terms = jnp.concatenate([d_gain_one, d_gain_two])
    if in_units:
        gain_rows = jnp.pad(
            gain_terms.reshape(UNITS, gain_count), ((0, 0), (64, 64 - gain_count))
        )
        terms = split_attention(table, d_query_weight, d_kv_weight, d_out_weight, gain_rows)
        held = [([terms[2 * k]], terms[2 * k + 1]) for k in range(SLOTS)]
        for number in range(len(stages(0))):
            held = scatter_stage(held, number)
        addends = [addend for pair in held for addend in pair]
        attention_sum, gain_sum = unform_attention(wide, addends)
        attention_gradient = attention_sum.reshape(-1)
        gains_gradient = gain_sum[0, 64 : 64 + gain_count]
    else:
        no_gains = jnp.zeros((UNITS, GAIN_LINES, 128), bf16)
        terms = pack_attention(d_query_weight, d_kv_weight, d_out_weight, no_gains)
        terms = jnp.concatenate(
            [
                terms[:, :LINES].reshape(devices, attention_lines, 128),
                jnp.pad(
                    gain_terms.astype(bf16).reshape(devices, 1, gain_count),
                    ((0, 0), (0, padded - attention_lines - 1), (0, 128 - gain_count)),
                ),
            ],
            axis=1,
        )
        summed = scatter_lines(terms.reshape(devices * padded, 128)).astype(f32)
        attention_gradient = summed[:attention_lines].reshape(-1)
        gains_gradient = summed[attention_lines, :gain_count]

    attention_first, attention_second, attention_update = adam_step(
        attention_gradient, first_attention, second_attention, master_attention
    )
    feedforward_first, feedforward_second, feedforward_update = adam_step(
        feedforward_gradient, first_feedforward, second_feedforward, master_feedforward
    )
    gains_first, gains_second, gains_update = adam_step(
        gains_gradient, first_gains, second_gains, master_gains
    )
    return (
        layer_output,
        input_gradient,
        attention_gradient,
        feedforward_gradient,
        gains_gradient,
        attention_first,
        attention_second,
        feedforward_first,
        feedforward_second,
        gains_first,
        gains_second,
        attention_update,
        feedforward_update,
        gains_update,
    )


def solution(mesh):
    rows = P(ALL_AXES, None)
    flat = P(ALL_AXES)
    return jax.shard_map(
        local,
        mesh=mesh,
        in_specs=(rows, rows) + (flat,) * 9 + (P("dp"), P("dp")),
        out_specs=(rows, rows) + (flat,) * 12,
        check_vma=False,
    )
```

```python
import functools
import math

import jax
import jax.numpy as jnp
from jax import lax
from jax.experimental import pallas as pl
from jax.experimental.pallas import tpu as pltpu
from jax.sharding import PartitionSpec as P

MODEL_WIDTH = 960
QUERY_HEADS = 15
KEY_VALUE_HEADS = 5
GROUPED = QUERY_HEADS // KEY_VALUE_HEADS
HEAD_SIZE = 64
FF = 2560
BLK = 128
ADAM_STEP = 10
TOK_DEV = 512
KV_WIDTH = KEY_VALUE_HEADS * HEAD_SIZE
TILE = 256
WIDE = GROUPED * BLK
UNITS = 32
LINES = 600
GAIN_LINES = 8
ALL_AXES = ("dp", "shard")

epsilon = 1e-05
masked_value = -1e30
learning_rate = 0.03
weight_decay = 0.1
score_scale = 1.0 / math.sqrt(HEAD_SIZE)
f32 = jnp.float32
bf16 = jnp.bfloat16


def lines_to_rows_2560(scratch, base, rows, store):
    for c in range(20):
        store(c, scratch[pl.ds(base + c, rows, stride=20), :])


def rows_to_lines_2560(load, scratch, base, rows):
    for c in range(20):
        scratch[pl.ds(base + c, rows, stride=20), :] = load(c)


def lane_low(rows):
    return lax.broadcasted_iota(jnp.int32, (rows, 128), 1) < 64


def lines_to_rows_960(scratch, base, rows, mid, store):
    half = rows // 2
    low = lane_low(half)
    line = [scratch[pl.ds(base + k, half, stride=15), :] for k in range(15)]
    turned = [None] * 7 + [pltpu.roll(line[k], 64, 1) for k in range(7, 15)]
    for c in range(8):
        mid[pl.ds(0, half, stride=2), :] = line[c]
        odd = jnp.where(low, turned[7 + c], turned[8 + c]) if c < 7 else turned[14]
        mid[pl.ds(1, half, stride=2), :] = odd
        store(c, mid[pl.ds(0, rows), :])


def rows_to_lines_960(load, scratch, base, rows, mid):
    half = rows // 2
    low = lane_low(half)
    odds = []
    for c in range(8):
        mid[pl.ds(0, rows), :] = load(c)
        even = mid[pl.ds(0, half, stride=2), :]
        odd = pltpu.roll(mid[pl.ds(1, half, stride=2), :], 64, 1)
        odds.append(odd)
        if c < 7:
            scratch[pl.ds(base + c, half, stride=15), :] = even
        else:
            scratch[pl.ds(base + 7, half, stride=15), :] = jnp.where(low, even, odds[0])
        if c > 0:
            scratch[pl.ds(base + 7 + c, half, stride=15), :] = jnp.where(low, odds[c - 1], odd)


def half_chunks(lines):
    even = [(lines[0], 0), (lines[0], 1), (lines[1], 0), (lines[1], 1), (lines[2], 0)]
    odd = [(lines[2], 1), (lines[3], 0), (lines[3], 1), (lines[4], 0), (lines[4], 1)]
    return even, odd


def placed(chunk, upper):
    line, side = chunk
    return line if side == upper else pltpu.roll(line, 64, 1)


def unpack_ff_kernel(lines_ref, gate_ref, up_ref, down_ref, scratch, mid):
    phase = pl.program_id(0)
    scratch[...] = lines_ref[...].astype(f32)
    for number, out in ((0, gate_ref), (1, up_ref)):

        @pl.when(phase == number)
        def _():
            def store(c, value):
                out[:, 128 * c : 128 * c + 128] = value.astype(bf16)

            lines_to_rows_2560(scratch, 0, 96, store)

    @pl.when(phase == 2)
    def _():
        def store(c, value):
            if c < 7:
                down_ref[:, 128 * c : 128 * c + 128] = value.astype(bf16)
            else:
                down_ref[:, 896:960] = value[:, :64].astype(bf16)

        lines_to_rows_960(scratch, 0, 256, mid, store)


def pinned(phase):
    def index(p, j):
        return (jnp.where(p == phase, j, jnp.where(p < phase, 0, 9)), 0)

    return index


def unpack_ff(lines):
    return pl.pallas_call(
        unpack_ff_kernel,
        grid=(3, 10),
        in_specs=[pl.BlockSpec((1920, 128), lambda p, j: (p * 10 + j, 0))],
        out_specs=[
            pl.BlockSpec((96, FF), pinned(0)),
            pl.BlockSpec((96, FF), pinned(1)),
            pl.BlockSpec((256, MODEL_WIDTH), pinned(2)),
        ],
        out_shape=[
            jax.ShapeDtypeStruct((MODEL_WIDTH, FF), bf16),
            jax.ShapeDtypeStruct((MODEL_WIDTH, FF), bf16),
            jax.ShapeDtypeStruct((FF, MODEL_WIDTH), bf16),
        ],
        scratch_shapes=[pltpu.VMEM((1920, 128), f32), pltpu.VMEM((256, 128), f32)],
        name="unpack_feedforward",
    )(lines)


def pack_ff_kernel(gate_ref, up_ref, down_ref, lines_ref, scratch, mid):
    phase = pl.program_id(0)
    for number, source in ((0, gate_ref), (1, up_ref)):

        @pl.when(phase == number)
        def _():
            rows_to_lines_2560(
                lambda c: source[:, 128 * c : 128 * c + 128].astype(f32), scratch, 0, 96
            )

    @pl.when(phase == 2)
    def _():
        def load(c):
            if c < 7:
                return down_ref[:, 128 * c : 128 * c + 128].astype(f32)
            tail = down_ref[:, 896:960].astype(f32)
            return jnp.concatenate([tail, tail], axis=1)

        rows_to_lines_960(load, scratch, 0, 256, mid)

    lines_ref[...] = scratch[...].astype(bf16)


def pack_ff(gate, up, down):
    return pl.pallas_call(
        pack_ff_kernel,
        grid=(3, 10),
        in_specs=[
            pl.BlockSpec((96, FF), pinned(0)),
            pl.BlockSpec((96, FF), pinned(1)),
            pl.BlockSpec((256, MODEL_WIDTH), pinned(2)),
        ],
        out_specs=pl.BlockSpec((1920, 128), lambda p, j: (p * 10 + j, 0)),
        out_shape=jax.ShapeDtypeStruct((3 * 19200, 128), bf16),
        scratch_shapes=[pltpu.VMEM((1920, 128), f32), pltpu.VMEM((256, 128), f32)],
        name="pack_feedforward",
    )(gate, up, down)


def unpack_wide_kernel(lines_ref, out_ref, scratch, mid):
    for u in range(4):
        scratch[...] = lines_ref[u].astype(f32)
        base = u * 80

        def store(c, value):
            if c < 7:
                out_ref[base : base + 80, 128 * c : 128 * c + 128] = value.astype(bf16)
            else:
                out_ref[base : base + 80, 896:960] = value[:, :64].astype(bf16)

        lines_to_rows_960(scratch, 0, 80, mid, store)


def unpack_wide(lines, first):
    depth = lines.shape[1]
    return pl.pallas_call(
        unpack_wide_kernel,
        grid=(3,),
        in_specs=[pl.BlockSpec((4, depth, 128), lambda j: (first // 4 + j, 0, 0))],
        out_specs=pl.BlockSpec((320, MODEL_WIDTH), lambda j: (j, 0)),
        out_shape=jax.ShapeDtypeStruct((MODEL_WIDTH, MODEL_WIDTH), bf16),
        scratch_shapes=[pltpu.VMEM((depth, 128), f32), pltpu.VMEM((80, 128), f32)],
        name="unpack_attention",
    )(lines)


def unpack_kv_kernel(key_ref, value_ref, out_ref, key_lines, value_lines, mid):
    low = lane_low(120)
    key_lines[...] = key_ref[0].astype(f32)
    value_lines[...] = value_ref[0].astype(f32)
    keys = half_chunks([key_lines[pl.ds(k, 120, stride=5), :] for k in range(5)])
    values = half_chunks([value_lines[pl.ds(k, 120, stride=5), :] for k in range(5)])
    for h in range(KEY_VALUE_HEADS):
        for parity in range(2):
            mid[pl.ds(parity, 120, stride=2), :] = jnp.where(
                low, placed(keys[parity][h], 0), placed(values[parity][h], 1)
            )
        out_ref[:, 128 * h : 128 * h + 128] = mid[...].astype(bf16)


def unpack_kv(lines):
    depth = lines.shape[1]
    return pl.pallas_call(
        unpack_kv_kernel,
        grid=(4,),
        in_specs=[
            pl.BlockSpec((1, depth, 128), lambda j: (12 + j, 0, 0)),
            pl.BlockSpec((1, depth, 128), lambda j: (16 + j, 0, 0)),
        ],
        out_specs=pl.BlockSpec((240, 2 * KV_WIDTH), lambda j: (j, 0)),
        out_shape=jax.ShapeDtypeStruct((MODEL_WIDTH, 2 * KV_WIDTH), bf16),
        scratch_shapes=[
            pltpu.VMEM((depth, 128), f32),
            pltpu.VMEM((depth, 128), f32),
            pltpu.VMEM((240, 128), f32),
        ],
        name="unpack_key_value",
    )(lines, lines)


def pack_attention_kernel(query_ref, kv_ref, out_weight_ref, gains_ref, lines_ref, scratch, mid):
    step = pl.program_id(0)

    def wide(source):
        for u in range(4):
            base = u * 80

            def load(c):
                if c < 7:
                    return source[base : base + 80, 128 * c : 128 * c + 128].astype(f32)
                tail = source[base : base + 80, 896:960].astype(f32)
                return jnp.concatenate([tail, tail], axis=1)

            rows_to_lines_960(load, scratch, 0, 80, mid)
            lines_ref[u, :LINES, :] = scratch[...].astype(bf16)

    @pl.when(step < 3)
    def _():
        wide(query_ref)

    @pl.when(step >= 5)
    def _():
        wide(out_weight_ref)

    for number, upper in ((3, 0), (4, 1)):

        @pl.when(step == number)
        def _():
            low = lane_low(120)
            for u in range(4):
                evens, odds = [], []
                for h in range(KEY_VALUE_HEADS):
                    mid[...] = kv_ref[
                        240 * u : 240 * u + 240, 128 * h : 128 * h + 128
                    ].astype(f32)
                    evens.append((mid[pl.ds(0, 120, stride=2), :], upper))
                    odds.append((mid[pl.ds(1, 120, stride=2), :], upper))
                run = evens + odds
                for k in range(5):
                    scratch[pl.ds(k, 120, stride=5), :] = jnp.where(
                        low, placed(run[2 * k], 0), placed(run[2 * k + 1], 1)
                    )
                lines_ref[u, :LINES, :] = scratch[...].astype(bf16)

    for u in range(4):
        lines_ref[u, LINES:, :] = gains_ref[u]


def pack_attention(d_query, d_kv, d_out, gains):
    return pl.pallas_call(
        pack_attention_kernel,
        grid=(8,),
        in_specs=[
            pl.BlockSpec((320, MODEL_WIDTH), lambda s: (jnp.minimum(s, 2), 0)),
            pl.BlockSpec((MODEL_WIDTH, 2 * KV_WIDTH), lambda s: (0, 0)),
            pl.BlockSpec((320, MODEL_WIDTH), lambda s: (jnp.maximum(s - 5, 0), 0)),
            pl.BlockSpec((4, GAIN_LINES, 128), lambda s: (s, 0, 0)),
        ],
        out_specs=pl.BlockSpec((4, LINES + GAIN_LINES, 128), lambda s: (s, 0, 0)),
        out_shape=jax.ShapeDtypeStruct((UNITS, LINES + GAIN_LINES, 128), bf16),
        scratch_shapes=[pltpu.VMEM((LINES, 128), f32), pltpu.VMEM((240, 128), f32)],
        name="pack_attention",
    )(d_query, d_kv, d_out, gains)


def tile_range(starts_ref, fills_ref, block):
    first_slot = starts_ref[block] * BLK
    last_slot = block * BLK + fills_ref[block]
    tile_first = first_slot // TILE
    tile_last = (block * BLK) // TILE
    ragged_first = jnp.logical_and(first_slot % TILE != 0, tile_first < tile_last)
    return first_slot, last_slot, tile_first, tile_last, ragged_first.astype(jnp.int32)


def allowed_pairs(tile, block, first_slot, last_slot):
    key_slot = tile * TILE + lax.broadcasted_iota(jnp.int32, (TILE, WIDE), 0)
    lane = lax.broadcasted_iota(jnp.int32, (TILE, WIDE), 1)
    query_slot = block * BLK + lax.rem(lane, BLK)
    return jnp.logical_and(
        jnp.logical_and(key_slot >= first_slot, key_slot <= query_slot),
        jnp.logical_or(key_slot < last_slot, key_slot == query_slot),
    )


def over_tiles(span, block, step):
    first_slot, last_slot, tile_first, tile_last, ragged = span

    def masked(tile):
        step(tile, allowed_pairs(tile, block, first_slot, last_slot))

    def edge(k, carry):
        masked(jnp.where(k == ragged, tile_last, tile_first))
        return carry

    lax.fori_loop(0, 1 + ragged, edge, 0)

    def inner(tile, carry):
        step(tile, None)
        return carry

    lax.fori_loop(tile_first + ragged, tile_last, inner, 0)


def transpose_kv(kv_ref, turned, tiles):
    def body(t, carry):
        rows = pl.ds(pl.multiple_of(t * TILE, TILE), TILE)
        for h in range(KEY_VALUE_HEADS):
            turned[t, 128 * h : 128 * h + 128, :] = kv_ref[rows, 128 * h : 128 * h + 128].T
        return carry

    lax.fori_loop(0, tiles, body, 0)


def lay_out_kv(blocks, kv_ref, place):
    size = blocks[0].shape[0]
    for apart, block in enumerate(blocks):
        spot = apart if len(blocks) == 1 else place ^ apart
        kv_ref[pl.ds(pl.multiple_of(spot * size, TILE), size), :] = block[...]


def heads_beside(ref, h):
    return jnp.concatenate(
        [
            ref[HEAD_SIZE * (GROUPED * h + g) : HEAD_SIZE * (GROUPED * h + g + 1), :]
            for g in range(GROUPED)
        ],
        axis=1,
    )


def attention_forward_kernel(
    starts_ref, fills_ref, place_ref, query_ref, *refs
):
    kv_blocks = refs[:-8]
    mixed_ref, log_ref, kv_ref, turned, pairs, tops, totals, sums = refs[-8:]
    i = pl.program_id(0)
    block = place_ref[0] * (TOK_DEV // BLK) + i

    @pl.when(i == 0)
    def _():
        lay_out_kv(kv_blocks, kv_ref, place_ref[0])
        transpose_kv(kv_ref, turned, kv_ref.shape[0] // TILE)

    for h in range(KEY_VALUE_HEADS):
        pairs[h, :HEAD_SIZE, :] = heads_beside(query_ref, h)
        pairs[h, HEAD_SIZE:, :] = jnp.zeros((HEAD_SIZE, WIDE), bf16)
    tops[...] = jnp.full(tops.shape, masked_value, f32)
    totals[...] = jnp.zeros(totals.shape, f32)
    sums[...] = jnp.zeros(sums.shape, f32)

    def step(tile, allowed):
        rows = pl.ds(pl.multiple_of(tile * TILE, TILE), TILE)

        def score(h):
            return jnp.dot(
                kv_ref[rows, 128 * h : 128 * h + 128], pairs[h], preferred_element_type=f32
            )

        def weigh(h, scores):
            if allowed is not None:
                scores = jnp.where(allowed, scores, masked_value)
            top_old = tops[h]
            top = jnp.maximum(top_old, jnp.max(scores, axis=0, keepdims=True))
            weights = jnp.exp(scores - top)
            shrink = jnp.exp(top_old - top)
            tops[h] = top
            totals[h] = totals[h] * shrink + jnp.sum(weights, axis=0, keepdims=True)
            return weights.astype(bf16), shrink

        def gather(h, weights, shrink):
            sums[h] = sums[h] * shrink + jnp.dot(
                turned[tile, 128 * h + HEAD_SIZE : 128 * h + 128, :],
                weights,
                preferred_element_type=f32,
            )

        scores = [score(h) for h in range(KEY_VALUE_HEADS)]
        held = None
        for h in range(KEY_VALUE_HEADS):
            weighed = weigh(h, scores[h])
            if held is not None:
                gather(h - 1, *held)
            held = weighed
        gather(KEY_VALUE_HEADS - 1, *held)

    over_tiles(tile_range(starts_ref, fills_ref, block), block, step)
    for h in range(KEY_VALUE_HEADS):
        outcome = (sums[h] / totals[h]).astype(bf16)
        log_total = tops[h] + jnp.log(totals[h])
        for g in range(GROUPED):
            head = GROUPED * h + g
            mixed_ref[HEAD_SIZE * head : HEAD_SIZE * (head + 1), :] = outcome[:, BLK * g : BLK * (g + 1)]
            log_ref[head : head + 1, :] = log_total[:, BLK * g : BLK * (g + 1)]
    log_ref[QUERY_HEADS:, :] = jnp.zeros((1, BLK), f32)


def token_block(rows):
    return pl.BlockSpec((rows, BLK), lambda i, *_: (0, i))


def whole(shape):
    return pl.BlockSpec(shape, lambda i, *_: (0,) * len(shape))


def attention_forward(starts, fills, place, query, kv):
    group = sum(block.shape[0] for block in kv)
    return pl.pallas_call(
        attention_forward_kernel,
        grid_spec=pltpu.PrefetchScalarGridSpec(
            num_scalar_prefetch=3,
            grid=(TOK_DEV // BLK,),
            in_specs=[token_block(MODEL_WIDTH)] + [whole(block.shape) for block in kv],
            out_specs=[token_block(MODEL_WIDTH), token_block(16)],
            scratch_shapes=[
                pltpu.VMEM((group, 2 * KV_WIDTH), bf16),
                pltpu.VMEM((group // TILE, 2 * KV_WIDTH, TILE), bf16),
                pltpu.VMEM((KEY_VALUE_HEADS, 2 * HEAD_SIZE, WIDE), bf16),
                pltpu.VMEM((KEY_VALUE_HEADS, 1, WIDE), f32),
                pltpu.VMEM((KEY_VALUE_HEADS, 1, WIDE), f32),
                pltpu.VMEM((KEY_VALUE_HEADS, HEAD_SIZE, WIDE), f32),
            ],
        ),
        out_shape=[
            jax.ShapeDtypeStruct((MODEL_WIDTH, TOK_DEV), bf16),
            jax.ShapeDtypeStruct((16, TOK_DEV), f32),
        ],
        name="attention_forward",
    )(starts, fills, place, query, *kv)


def attention_backward_kernel(
    first,
    blocks,
    starts_ref,
    fills_ref,
    place_ref,
    query_ref,
    upstream_ref,
    mixed_ref,
    log_ref,
    cosine_ref,
    sine_ref,
    *refs,
):
    kv_blocks, refs = refs[:blocks], refs[-(blocks + 10) :]
    d_query_ref, d_kv_blocks = refs[0], refs[1 : blocks + 1]
    kv_ref, turned, pairs, query_rows, upstream_rows, deltas, logs, sums, kv_sums = refs[blocks + 1 :]
    count = kv_sums.shape[0]
    i = pl.program_id(0)
    block = place_ref[0] * (TOK_DEV // BLK) + i
    tiles = kv_ref.shape[0] // TILE

    @pl.when(i == 0)
    def _():
        for apart, source in enumerate(kv_blocks):
            size = source.shape[0]
            spot = apart if blocks == 1 else place_ref[0] ^ apart
            kv_ref[pl.ds(pl.multiple_of(spot * size, TILE), size), :] = source[
                :, 128 * first : 128 * (first + count)
            ]

        def prepare(t, carry):
            rows = pl.ds(pl.multiple_of(t * TILE, TILE), TILE)
            for h in range(count):
                turned[t, HEAD_SIZE * h : HEAD_SIZE * (h + 1), :] = kv_ref[
                    rows, 128 * h : 128 * h + 128
                ].T[:HEAD_SIZE]
            kv_sums[:, rows, :] = jnp.zeros((count, TILE, 128), f32)
            return carry

        lax.fori_loop(0, tiles, prepare, 0)

    blank = jnp.zeros((HEAD_SIZE, WIDE), bf16)
    for h in range(count):
        query = heads_beside(query_ref, first + h)
        upstream = heads_beside(upstream_ref, first + h)
        pairs[h, :HEAD_SIZE, :WIDE] = query
        pairs[h, HEAD_SIZE:, :WIDE] = blank
        pairs[h, :HEAD_SIZE, WIDE:] = blank
        pairs[h, HEAD_SIZE:, WIDE:] = upstream
        query_rows[h] = pairs[h, :, :WIDE].T
        upstream_rows[h] = pairs[h, :, WIDE:].T
        deltas[h] = jnp.sum(
            upstream.astype(f32) * heads_beside(mixed_ref, first + h).astype(f32),
            axis=0,
            keepdims=True,
        )
        line = GROUPED * (first + h)
        logs[h] = jnp.concatenate(
            [log_ref[line + g : line + g + 1, :] for g in range(GROUPED)], axis=1
        )
    sums[...] = jnp.zeros(sums.shape, f32)

    def step(tile, allowed):
        rows = pl.ds(pl.multiple_of(tile * TILE, TILE), TILE)

        def score(h):
            return jnp.dot(
                kv_ref[rows, 128 * h : 128 * h + 128], pairs[h], preferred_element_type=f32
            )

        def weigh(h, both):
            scores = both[:, :WIDE]
            if allowed is not None:
                scores = jnp.where(allowed, scores, masked_value)
            probs = jnp.exp(scores - logs[h])
            d_scores = (probs * (both[:, WIDE:] - deltas[h])).astype(bf16)
            return probs.astype(bf16), d_scores

        def gather(h, probs, d_scores):
            kv_sums[h, rows, :] += jnp.dot(
                d_scores, query_rows[h], preferred_element_type=f32
            ) + jnp.dot(probs, upstream_rows[h], preferred_element_type=f32)
            sums[h] += jnp.dot(
                turned[tile, HEAD_SIZE * h : HEAD_SIZE * (h + 1), :],
                d_scores,
                preferred_element_type=f32,
            )

        following = score(0)
        held = None
        for h in range(count):
            both = following
            if h + 1 < count:
                following = score(h + 1)
            weighed = weigh(h, both)
            if held is not None:
                gather(h - 1, *held)
            held = weighed
        gather(count - 1, *held)

    over_tiles(tile_range(starts_ref, fills_ref, block), block, step)
    cosine = cosine_ref[...]
    sine = sine_ref[...]
    half = HEAD_SIZE // 2
    for h in range(count):
        for g in range(GROUPED):
            head = GROUPED * h + g
            front = sums[h, :half, BLK * g : BLK * (g + 1)] * score_scale
            back = sums[h, half:, BLK * g : BLK * (g + 1)] * score_scale
            d_query_ref[HEAD_SIZE * head : HEAD_SIZE * head + half, :] = (
                front * cosine + back * sine
            ).astype(bf16)
            d_query_ref[HEAD_SIZE * head + half : HEAD_SIZE * (head + 1), :] = (
                back * cosine - front * sine
            ).astype(bf16)

    @pl.when(i == pl.num_programs(0) - 1)
    def _():
        size = kv_blocks[0].shape[0]
        for apart, out in enumerate(d_kv_blocks):
            spot = apart if blocks == 1 else place_ref[0] ^ apart

            def emit(t, carry):
                rows = pl.ds(pl.multiple_of(spot * size + t * TILE, TILE), TILE)
                for h in range(count):
                    out[pl.ds(pl.multiple_of(t * TILE, TILE), TILE), 128 * h : 128 * h + 128] = (
                        kv_sums[h, rows, :].astype(bf16)
                    )
                return carry

            lax.fori_loop(0, size // TILE, emit, 0)


def attention_backward(
    first, count, starts, fills, place, query, upstream, mixed, logs, cosine, sine, kv, after=()
):
    group = sum(block.shape[0] for block in kv)
    half = HEAD_SIZE // 2
    outs = [(block.shape[0], 128 * count) for block in kv]
    return pl.pallas_call(
        functools.partial(attention_backward_kernel, first, len(kv)),
        grid_spec=pltpu.PrefetchScalarGridSpec(
            num_scalar_prefetch=3,
            grid=(TOK_DEV // BLK,),
            in_specs=[
                token_block(MODEL_WIDTH),
                token_block(MODEL_WIDTH),
                token_block(MODEL_WIDTH),
                token_block(16),
                token_block(half),
                token_block(half),
            ]
            + [whole(block.shape) for block in kv]
            + [pl.BlockSpec(memory_space=pl.ANY)] * len(after),
            out_specs=[token_block(GROUPED * HEAD_SIZE * count)] + [whole(shape) for shape in outs],
            scratch_shapes=[
                pltpu.VMEM((group, 128 * count), bf16),
                pltpu.VMEM((group // TILE, HEAD_SIZE * count, TILE), bf16),
                pltpu.VMEM((count, 2 * HEAD_SIZE, 2 * WIDE), bf16),
                pltpu.VMEM((count, WIDE, 128), bf16),
                pltpu.VMEM((count, WIDE, 128), bf16),
                pltpu.VMEM((count, 1, WIDE), f32),
                pltpu.VMEM((count, 1, WIDE), f32),
                pltpu.VMEM((count, HEAD_SIZE, WIDE), f32),
                pltpu.VMEM((count, group, 128), f32),
            ],
        ),
        out_shape=[jax.ShapeDtypeStruct((GROUPED * HEAD_SIZE * count, TOK_DEV), bf16)]
        + [jax.ShapeDtypeStruct(shape, bf16) for shape in outs],
        name="attention_backward",
    )(starts, fills, place, query, upstream, mixed, logs, cosine, sine, *kv, *after)


def dot_of(left, right, left_dim, right_dim):
    return lax.dot_general(
        left, right, (((left_dim,), (right_dim,)), ((), ())), preferred_element_type=f32
    )


SLOTS = 3
FORM = 640
PIECES = (240, 240, 160)
GAIN_LINE = 560
PAD_WIDTH = 1024
CHUNK = 640
CORE_BIT = ("shard", 1)
ROW_BIT = ("shard", 2)
NEAR_BITS = (ROW_BIT, ("dp", 1), ("dp", 2))
FAR_BITS = (("dp", 4),)
BACKWARD_CALLS = ((0, 5),)


def stages(colour):
    return (CORE_BIT,) + NEAR_BITS[colour:] + NEAR_BITS[:colour] + FAR_BITS


def swap(value, bit):
    axis, mask = bit
    size = lax.axis_size(axis)
    return lax.ppermute(value, axis, [(i, i ^ mask) for i in range(size)])


def gather_colour(own, colour):
    held = own[None]
    for bit in reversed(stages(colour)[1:]):
        held = jnp.concatenate([held, swap(held, bit)], axis=0)
    return held, swap(held, CORE_BIT)


def scatter_stage(held, number, arrived=None):
    outcome = []
    total = lambda parts: sum(part.astype(f32) for part in parts)
    bits = [stages(colour)[number] for colour in range(len(held))]
    if arrived is None and len(set(bits)) == 1:
        flat = [send.reshape(-1, 128) for _, send in held]
        merged = swap(jnp.concatenate(flat, axis=0), bits[0])
        arrived, base = [], 0
        for (_, send), lines in zip(held, flat):
            arrived.append(merged[base : base + lines.shape[0]].reshape(send.shape))
            base += lines.shape[0]
    if arrived is None:
        arrived = [swap(send, bit) for (_, send), bit in zip(held, bits)]
    for (parts, _), got in zip(held, arrived):
        half = got.shape[0] // 2
        if half == 0:
            outcome.append((total(parts)[0].astype(bf16), got[0]))
        else:
            parts = parts + [got]
            outcome.append(
                ([part[:half] for part in parts], total([part[half:] for part in parts]).astype(bf16))
            )
    return outcome


def positions():
    device = jnp.arange(UNITS, dtype=jnp.int32)
    width = lax.axis_size("shard")
    apart = {
        "dp": (device // width) ^ lax.axis_index("dp").astype(jnp.int32),
        "shard": (device % width) ^ lax.axis_index("shard").astype(jnp.int32),
    }
    tables = []
    for colour in range(SLOTS):
        place = jnp.zeros((UNITS,), jnp.int32)
        for axis, mask in stages(colour):
            place = 2 * place + (apart[axis] & mask) // mask
        tables.append(place)
    return jnp.concatenate(tables)


def copy_from(halves, place, dst, sem, pick=lambda ref: ref):
    for number, ref in enumerate(halves):

        @pl.when(place // 16 == number)
        def _():
            pltpu.make_async_copy(pick(ref.at[lax.rem(place, 16)]), dst, sem).start()


def copy_to(src, keep, send, place, sem):
    for number, pick in enumerate((keep, send)):

        @pl.when(place // 16 == number)
        def _():
            pltpu.make_async_copy(src, pick(lax.rem(place, 16)), sem).start()


def wait_for(ref, sem):
    pltpu.make_async_copy(ref, ref, sem).wait()


def form_attention_kernel(wide_ref, lines_ref, gains_ref, a_ref, b_ref, c_ref, mid, form):
    @pl.when(wide_ref[0] == 1)
    def _():
        def store(c, value):
            if c == 7:
                value = jnp.where(lane_low(80), value, 0.0)
            form[80 * c : 80 * c + 80, :] = value

        lines_to_rows_960(lines_ref, 0, 80, mid, store)

    @pl.when(wide_ref[0] == 0)
    def _():
        low = lane_low(120)
        line = [lines_ref[pl.ds(k, 120, stride=5), :] for k in range(5)]
        turned = [None, None] + [pltpu.roll(line[k], 64, 1) for k in range(2, 5)]
        form[pl.ds(0, 120, stride=2), :] = line[0]
        form[pl.ds(1, 120, stride=2), :] = jnp.where(low, turned[2], turned[3])
        form[pl.ds(240, 120, stride=2), :] = line[1]
        form[pl.ds(241, 120, stride=2), :] = jnp.where(low, turned[3], turned[4])
        mid[pl.ds(0, 120, stride=2), :] = line[2]
        mid[pl.ds(1, 120, stride=2), :] = turned[4]
        low = lane_low(80)
        form[480:560, :] = jnp.where(low, mid[0:80, :], pltpu.roll(mid[160:240, :], 64, 1))
        form[560:640, :] = jnp.where(low, mid[80:160, :], 0.0)

    form[GAIN_LINE : GAIN_LINE + 1, :] = jnp.where(
        lane_low(1), form[GAIN_LINE : GAIN_LINE + 1, :], gains_ref[...]
    )
    a_ref[...] = form[0:240, :].astype(bf16)
    b_ref[...] = form[240:480, :].astype(bf16)
    c_ref[...] = form[480:640, :].astype(bf16)


SMEM_SPEC = pl.BlockSpec(memory_space=pltpu.SMEM)
ANY_SPEC = pl.BlockSpec(memory_space=pl.ANY)


def form_attention(wide, lines, gains):
    return pl.pallas_call(
        form_attention_kernel,
        in_specs=[SMEM_SPEC, pl.BlockSpec((LINES, 128)), pl.BlockSpec((1, 128))],
        out_shape=[jax.ShapeDtypeStruct((n, 128), bf16) for n in PIECES],
        scratch_shapes=[pltpu.VMEM((240, 128), f32), pltpu.VMEM((FORM, 128), f32)],
        name="form_attention",
    )(wide, lines, gains)


def unform_attention_kernel(wide_ref, *refs):
    pieces, (lines_ref, gains_ref, mid, form) = refs[:6], refs[6:]
    base = 0
    for n, keep, got in zip(PIECES, pieces[0::2], pieces[1::2]):
        form[base : base + n, :] = keep[...].astype(f32) + got[...].astype(f32)
        base += n
    gains_ref[...] = form[GAIN_LINE : GAIN_LINE + 1, :]

    @pl.when(wide_ref[0] == 1)
    def _():
        rows_to_lines_960(lambda c: form[80 * c : 80 * c + 80, :], lines_ref, 0, 80, mid)

    @pl.when(wide_ref[0] == 0)
    def _():
        low = lane_low(120)
        mid[0:80, :] = form[480:560, :]
        mid[80:160, :] = form[560:640, :]
        mid[160:240, :] = pltpu.roll(form[480:560, :], 64, 1)
        even = [form[pl.ds(0, 120, stride=2), :], form[pl.ds(240, 120, stride=2), :]]
        odd = [form[pl.ds(1, 120, stride=2), :], form[pl.ds(241, 120, stride=2), :]]
        even.append(mid[pl.ds(0, 120, stride=2), :])
        odd.append(mid[pl.ds(1, 120, stride=2), :])
        odd = [pltpu.roll(value, 64, 1) for value in odd]
        lines_ref[pl.ds(0, 120, stride=5), :] = even[0]
        lines_ref[pl.ds(1, 120, stride=5), :] = even[1]
        lines_ref[pl.ds(2, 120, stride=5), :] = jnp.where(low, even[2], odd[0])
        lines_ref[pl.ds(3, 120, stride=5), :] = jnp.where(low, odd[0], odd[1])
        lines_ref[pl.ds(4, 120, stride=5), :] = jnp.where(low, odd[1], odd[2])


def unform_attention(wide, addends):
    return pl.pallas_call(
        unform_attention_kernel,
        in_specs=[SMEM_SPEC] + [pl.BlockSpec((n, 128)) for n in PIECES for _ in range(2)],
        out_shape=[jax.ShapeDtypeStruct((LINES, 128), f32), jax.ShapeDtypeStruct((1, 128), f32)],
        scratch_shapes=[pltpu.VMEM((240, 128), f32), pltpu.VMEM((FORM, 128), f32)],
        name="unform_attention",
    )(wide, *addends)


def wide_pieces(c):
    return [((80 * c + 16 * m) // 32, (80 * c + 16 * m) % 32, 16 * m) for m in range(5)]


def form_feedforward_kernel(narrow_ref, lines_ref, out, mid):
    for s in range(SLOTS):

        @pl.when(narrow_ref[s] == 1)
        def _():
            mid[30:32, :] = jnp.zeros((2, 128), f32)
            for c in range(20):
                mid[0:30, :] = lines_ref[pl.ds(LINES * s + c, 30, stride=20), :]
                out[s, c] = mid[0:32, :].astype(bf16)

        @pl.when(narrow_ref[s] == 0)
        def _():
            def store(c, value):
                if c == 7:
                    value = jnp.where(lane_low(80), value, 0.0)
                for k, r, m in wide_pieces(c):
                    out[s, k, r : r + 16, :] = value[m : m + 16].astype(bf16)

            lines_to_rows_960(lines_ref, LINES * s, 80, mid, store)


def form_feedforward(narrow, lines):
    return pl.pallas_call(
        form_feedforward_kernel,
        in_specs=[SMEM_SPEC, pl.BlockSpec((SLOTS * LINES, 128))],
        out_shape=jax.ShapeDtypeStruct((SLOTS, 20, 32, 128), bf16),
        scratch_shapes=[pltpu.VMEM((80, 128), f32)],
        name="form_feedforward",
    )(narrow, lines)


def unform_feedforward_kernel(narrow_ref, *refs):
    pieces, (lines_ref, mid) = refs[: 2 * SLOTS], refs[2 * SLOTS :]
    for s in range(SLOTS):
        keep, got = pieces[2 * s], pieces[2 * s + 1]

        @pl.when(narrow_ref[s] == 1)
        def _():
            for c in range(20):
                mid[0:32, :] = keep[c].astype(f32) + got[c].astype(f32)
                lines_ref[pl.ds(LINES * s + c, 30, stride=20), :] = mid[0:30, :]

        @pl.when(narrow_ref[s] == 0)
        def _():
            def load(c):
                return jnp.concatenate(
                    [
                        keep[k, r : r + 16, :].astype(f32) + got[k, r : r + 16, :].astype(f32)
                        for k, r, m in wide_pieces(c)
                    ],
                    axis=0,
                )

            rows_to_lines_960(load, lines_ref, LINES * s, 80, mid)


def unform_feedforward(narrow, addends):
    return pl.pallas_call(
        unform_feedforward_kernel,
        in_specs=[SMEM_SPEC] + [pl.BlockSpec((20, 32, 128))] * (2 * SLOTS),
        out_shape=jax.ShapeDtypeStruct((SLOTS * LINES, 128), f32),
        scratch_shapes=[pltpu.VMEM((80, 128), f32)],
        name="unform_feedforward",
    )(narrow, *addends)


def place_attention_kernel(table_ref, *refs):
    halves = [refs[2 * k : 2 * k + 2] for k in range(SLOTS)]
    query_ref, kv_ref, out_ref, gains_ref, units, sem = refs[2 * SLOTS :]

    def start(d, carry):
        base = 0
        for k, n in enumerate(PIECES):
            copy_from(halves[k], table_ref[UNITS * k + d], units.at[d, base : base + n, :], sem)
            base += n
        return carry

    lax.fori_loop(0, UNITS, start, 0)
    wait_for(units, sem)

    def wide(out, first):
        def body(u, carry):
            rows = pl.ds(pl.multiple_of(80 * u, 16), 80)
            for c in range(7):
                out[rows, 128 * c : 128 * c + 128] = units[first + u, 80 * c : 80 * c + 80, :]
            out[rows, 896:960] = units[first + u, 560:640, :64]
            return carry

        lax.fori_loop(0, 12, body, 0)

    def keyed(j, carry):
        low = lane_low(240)
        chunks = []
        for first in (12, 16):
            unit = units[first + j].astype(f32)
            last = jnp.concatenate(
                [unit[480:640], pltpu.roll(unit[480:560], 64, 1)], axis=0
            )
            lines = (unit[0:240], unit[240:480], last)
            chunks.append([(lines[h // 2], h % 2) for h in range(KEY_VALUE_HEADS)])
        rows = pl.ds(pl.multiple_of(240 * j, 16), 240)
        for h in range(KEY_VALUE_HEADS):
            kv_ref[rows, 128 * h : 128 * h + 128] = jnp.where(
                low, placed(chunks[0][h], 0), placed(chunks[1][h], 1)
            ).astype(bf16)
        return carry

    lax.fori_loop(0, 4, keyed, 0)
    wide(query_ref, 0)
    wide(out_ref, 20)
    for u in range(UNITS):
        gains_ref[u : u + 1, :] = units[u, GAIN_LINE : GAIN_LINE + 1, :].astype(f32)


def place_attention(table, gathered):
    return pl.pallas_call(
        place_attention_kernel,
        in_specs=[SMEM_SPEC] + [ANY_SPEC] * (2 * SLOTS),
        out_shape=[
            jax.ShapeDtypeStruct((MODEL_WIDTH, MODEL_WIDTH), bf16),
            jax.ShapeDtypeStruct((MODEL_WIDTH, 2 * KV_WIDTH), bf16),
            jax.ShapeDtypeStruct((MODEL_WIDTH, MODEL_WIDTH), bf16),
            jax.ShapeDtypeStruct((UNITS, 128), f32),
        ],
        scratch_shapes=[pltpu.VMEM((UNITS, FORM, 128), bf16), pltpu.SemaphoreType.DMA],
        name="place_attention",
    )(table, *gathered)


def split_attention_kernel(table_ref, query_ref, kv_ref, out_ref, gains_ref, *refs):
    *keeps, sent, units, sem = refs

    def send(d):
        row = lax.broadcasted_iota(jnp.int32, (16, 128), 0)
        lane = lax.broadcasted_iota(jnp.int32, (16, 128), 1)
        block = units[d, GAIN_LINE : GAIN_LINE + 16, :].astype(f32)
        units[d, GAIN_LINE : GAIN_LINE + 16, :] = jnp.where(
            jnp.logical_and(row == 0, lane >= 64), gains_ref[pl.ds(d, 1), :], block
        ).astype(bf16)
        base = 0
        for k, n in enumerate(PIECES):
            copy_to(
                units.at[d, base : base + n, :],
                lambda p: keeps[k].at[p],
                lambda p: sent.at[p, base : base + n, :],
                table_ref[UNITS * k + d],
                sem,
            )
            base += n

    def wide(source, first):
        def body(u, carry):
            rows = pl.ds(pl.multiple_of(80 * u, 16), 80)
            for c in range(7):
                units[first + u, 80 * c : 80 * c + 80, :] = source[rows, 128 * c : 128 * c + 128]
            tail = source[rows, 896:960]
            units[first + u, 560:640, :] = jnp.concatenate([tail, jnp.zeros_like(tail)], axis=1)
            send(first + u)
            return carry

        lax.fori_loop(0, 12, body, 0)

    def keyed(j, carry):
        low = lane_low(240)
        rows = pl.ds(pl.multiple_of(240 * j, 16), 240)
        for upper, first in ((0, 12), (1, 16)):
            heads = [
                (kv_ref[rows, 128 * h : 128 * h + 128].astype(f32), upper)
                for h in range(KEY_VALUE_HEADS)
            ]
            for c in range(2):
                units[first + j, 240 * c : 240 * c + 240, :] = jnp.where(
                    low, placed(heads[2 * c], 0), placed(heads[2 * c + 1], 1)
                ).astype(bf16)
            last = placed(heads[4], 0)
            turned = placed(heads[4], 1)
            units[first + j, 480:560, :] = jnp.where(
                lane_low(80), last[0:80], turned[160:240]
            ).astype(bf16)
            units[first + j, 560:640, :] = jnp.where(lane_low(80), last[80:160], 0.0).astype(bf16)
            send(first + j)
        return carry

    lax.fori_loop(0, 4, keyed, 0)
    wide(query_ref, 0)
    wide(out_ref, 20)
    wait_for(units, sem)


def split_attention(table, d_query, d_kv, d_out, gains):
    return pl.pallas_call(
        split_attention_kernel,
        in_specs=[
            SMEM_SPEC,
            pl.BlockSpec((MODEL_WIDTH, MODEL_WIDTH)),
            pl.BlockSpec((MODEL_WIDTH, 2 * KV_WIDTH)),
            pl.BlockSpec((MODEL_WIDTH, MODEL_WIDTH)),
            pl.BlockSpec((UNITS, 128)),
        ],
        out_specs=[ANY_SPEC] * (SLOTS + 1),
        out_shape=[jax.ShapeDtypeStruct((16, n, 128), bf16) for n in PIECES + (FORM,)],
        scratch_shapes=[pltpu.VMEM((UNITS, FORM, 128), bf16), pltpu.SemaphoreType.DMA],
        name="split_attention",
    )(table, d_query, d_kv, d_out, gains)


def feedforward_kernel(
    table_ref,
    hidden_ref,
    turned_ref,
    grad_ref,
    gate_ref,
    up_ref,
    down_ref,
    out_ref,
    d_hidden_ref,
    *refs,
):
    keeps, sent = refs[:SLOTS], refs[SLOTS]
    down, inner_rows, inner_turned, d_both, both_out, down_out, sems = refs[SLOTS + 1 :]
    q = pl.program_id(0)
    chunks = pl.num_programs(0)
    slot = lax.rem(q, 2)

    def send_terms():
        for u in range(2 * UNITS):
            device, s = divmod(u, SLOTS)
            copy_to(
                both_out.at[slot, u // UNITS, u % UNITS],
                lambda p: keeps[s].at[p, pl.ds(5 * q, 5)],
                lambda p: sent.at[s, p, pl.ds(5 * q, 5)],
                table_ref[UNITS * s + device],
                sems.at[slot, 0],
            )
        for v in range(8):
            unit = 2 * UNITS + 8 * q + v
            device = unit // SLOTS
            for s in range(SLOTS):

                @pl.when(unit - SLOTS * device == s)
                def _():
                    copy_to(
                        down_out.at[slot, v],
                        lambda p: keeps[s].at[p],
                        lambda p: sent.at[s, p],
                        table_ref[UNITS * s + device],
                        sems.at[slot, 1],
                    )

    def wait_terms(side):
        wait_for(both_out.at[side], sems.at[side, 0])
        wait_for(down_out.at[side], sems.at[side, 1])

    for v in range(8):
        for c in range(8):
            for k, r, m in wide_pieces(c):
                down[80 * v + m : 80 * v + m + 16, 128 * c : 128 * c + 128] = down_ref[
                    v, k, r : r + 16, :
                ]

    @pl.when(q == 0)
    def _():
        out_ref[...] = jnp.zeros(out_ref.shape, f32)
        d_hidden_ref[...] = jnp.zeros(d_hidden_ref.shape, f32)

    def rows_step(i, carry):
        rows = pl.ds(pl.multiple_of(256 * i, 256), 256)
        weights = jnp.concatenate(
            [ref[:, c].reshape(PAD_WIDTH, 128) for ref in (gate_ref, up_ref) for c in range(5)],
            axis=1,
        )
        both = jnp.dot(hidden_ref[rows, :], weights, preferred_element_type=f32)
        gate, upper = both[:, :CHUNK], both[:, CHUNK:]
        sigmoid_gate = jax.nn.sigmoid(gate)
        activated = gate * sigmoid_gate
        inner = (activated * upper).astype(bf16)
        inner_rows[rows, :] = inner
        out_ref[rows, :] += jnp.dot(inner, down[...], preferred_element_type=f32)
        d_inner = dot_of(grad_ref[rows, :], down[...], 1, 1)
        d_gate = d_inner * upper * sigmoid_gate * (1.0 + gate * (1.0 - sigmoid_gate))
        d_upper = d_inner * activated
        d_pair = jnp.concatenate([d_gate, d_upper], axis=1).astype(bf16)
        d_both[rows, :] = d_pair
        d_hidden_ref[rows, :] += dot_of(d_pair, weights, 1, 1)
        return carry

    lax.fori_loop(0, 2, rows_step, 0)
    inner_turned[...] = inner_rows[...].T

    @pl.when(q >= 2)
    def _():
        wait_terms(slot)

    def both_step(i, carry):
        rows = pl.ds(pl.multiple_of(256 * i, 256), 256)
        terms = jnp.dot(turned_ref[rows, :], d_both[...], preferred_element_type=f32).astype(bf16)
        units = pl.ds(8 * i, 8)
        for c in range(10):
            both_out[slot, c // 5, units, c % 5] = terms[:, 128 * c : 128 * c + 128].reshape(
                8, 32, 128
            )
        return carry

    lax.fori_loop(0, 4, both_step, 0)

    def down_step(i, carry):
        rows = pl.ds(pl.multiple_of(320 * i, 16), 320)
        terms = jnp.dot(
            inner_turned[rows, :], grad_ref[...], preferred_element_type=f32
        ).astype(bf16)
        for v in range(4):
            for c in range(8):
                for k, r, m in wide_pieces(c):
                    down_out[slot, 4 * i + v, k, r : r + 16, :] = terms[
                        80 * v + m : 80 * v + m + 16, 128 * c : 128 * c + 128
                    ]
        return carry

    lax.fori_loop(0, 2, down_step, 0)
    send_terms()

    @pl.when(q == chunks - 1)
    def _():
        for side in range(2):
            wait_terms(side)


def feedforward(table, hidden, turned, grad, weights):
    block = jax.ShapeDtypeStruct((16, 20, 32, 128), bf16)
    full = lambda shape: pl.BlockSpec(shape, lambda q: (0, 0))
    return pl.pallas_call(
        feedforward_kernel,
        grid=(FF // CHUNK,),
        in_specs=[
            SMEM_SPEC,
            full((TOK_DEV, PAD_WIDTH)),
            full((PAD_WIDTH, TOK_DEV)),
            full((TOK_DEV, PAD_WIDTH)),
            pl.BlockSpec((32, 5, 32, 128), lambda q: (0, q, 0, 0)),
            pl.BlockSpec((32, 5, 32, 128), lambda q: (1, q, 0, 0)),
            pl.BlockSpec((8, 20, 32, 128), lambda q: (8 + q, 0, 0, 0)),
        ],
        out_specs=[full((TOK_DEV, PAD_WIDTH))] * 2 + [ANY_SPEC] * (SLOTS + 1),
        out_shape=[jax.ShapeDtypeStruct((TOK_DEV, PAD_WIDTH), f32)] * 2
        + [block] * SLOTS
        + [jax.ShapeDtypeStruct((SLOTS,) + block.shape, bf16)],
        scratch_shapes=[
            pltpu.VMEM((CHUNK, PAD_WIDTH), bf16),
            pltpu.VMEM((TOK_DEV, CHUNK), bf16),
            pltpu.VMEM((CHUNK, TOK_DEV), bf16),
            pltpu.VMEM((TOK_DEV, 2 * CHUNK), bf16),
            pltpu.VMEM((2, 2, 32, 5, 32, 128), bf16),
            pltpu.VMEM((2, 8, 20, 32, 128), bf16),
            pltpu.SemaphoreType.DMA((2, 2)),
        ],
        compiler_params=pltpu.CompilerParams(vmem_limit_bytes=60 * 2**20),
        name="feedforward",
    )(table, hidden, turned, grad, weights, weights, weights)


def spread_matrix():
    column = jnp.arange(PAD_WIDTH, dtype=jnp.int32)
    entry = jnp.where(column % 32 < 30, 30 * (column // 32) + column % 32, -1)
    return (jnp.arange(MODEL_WIDTH, dtype=jnp.int32)[:, None] == entry[None, :]).astype(bf16)


def rope_tables(positions):
    steps = jnp.arange(HEAD_SIZE // 2, dtype=f32) * (2.0 / HEAD_SIZE)
    inverse = jnp.exp(-math.log(10000.0) * steps)
    angles = inverse[:, None] * positions.astype(f32)[None, :]
    return (jnp.cos(angles), jnp.sin(angles))


def norm_scale(field):
    return lax.rsqrt(jnp.mean(field * field, axis=1, keepdims=True) + epsilon)


def norm_back(upstream, normed, scale, gain):
    scaled = upstream * gain[None, :]
    return scale * (scaled - normed * jnp.mean(scaled * normed, axis=1, keepdims=True))


def adam_step(grad, moment, second, master):
    moment_new = 0.9 * moment + 0.1 * grad
    second_new = 0.999 * second + 0.001 * grad * grad
    corrected = moment_new / (1.0 - 0.9**ADAM_STEP)
    scaled = second_new / (1.0 - 0.999**ADAM_STEP)
    update = -learning_rate * (corrected / (jnp.sqrt(scaled) + 1e-08) + weight_decay * master)
    return (moment_new, second_new, update)


def gather_lines(block):
    return lax.all_gather(block, ALL_AXES, axis=0, tiled=True)


def scatter_lines(lines):
    return lax.psum_scatter(lines, ALL_AXES, scatter_dimension=0, tiled=True)


def local(
    layer_input,
    cotangent,
    master_attention,
    master_feedforward,
    master_gains,
    first_attention,
    second_attention,
    first_feedforward,
    second_feedforward,
    first_gains,
    second_gains,
    block_start,
    block_fill,
):
    devices = lax.axis_size(ALL_AXES)
    attention_lines = master_attention.shape[0] // 128
    feedforward_lines = master_feedforward.shape[0] // 128
    gain_count = master_gains.shape[0]
    padded = (attention_lines // 16 + 1) * 16

    in_units = devices == UNITS
    if in_units:
        table = positions()
        device = (
            lax.axis_index("dp") * lax.axis_size("shard") + lax.axis_index("shard")
        ).astype(jnp.int32)
        wide = jnp.logical_or(device < 12, device >= 20).astype(jnp.int32)[None]
        narrow = (SLOTS * device + jnp.arange(SLOTS, dtype=jnp.int32) < 2 * UNITS).astype(jnp.int32)
        gain_row = jnp.pad(
            master_gains.reshape(1, gain_count), ((0, 0), (64, 64 - gain_count))
        )
        pieces = form_attention(wide, master_attention.reshape(LINES, 128), gain_row)
        gathered = [half for k in range(SLOTS) for half in gather_colour(pieces[k], k)]
        forms = form_feedforward(narrow, master_feedforward.reshape(SLOTS * LINES, 128))
        feedforward_all = gather_lines(forms.reshape(SLOTS * FORM, 128))
        query_weight, kv_weight, out_weight, gain_rows = place_attention(table, gathered)
        gains_all = gain_rows[:, 64 : 64 + gain_count].reshape(-1)
    else:
        gain_lines = jnp.pad(
            master_gains.astype(bf16).reshape(1, gain_count),
            ((0, padded - attention_lines - 1), (0, 128 - gain_count)),
        )
        attention_block = jnp.concatenate(
            [master_attention.astype(bf16).reshape(attention_lines, 128), gain_lines], axis=0
        )
        by_device = gather_lines(attention_block).reshape(devices, padded, 128)
        feedforward_all = gather_lines(
            master_feedforward.astype(bf16).reshape(feedforward_lines, 128)
        )
        gains_all = by_device[:, attention_lines, :gain_count].reshape(-1).astype(f32)
        units = by_device[:, :attention_lines].reshape(UNITS, LINES, 128)
        query_weight = unpack_wide(units, 0)
        kv_weight = unpack_kv(units)
        out_weight = unpack_wide(units, 20)
    gain_one, gain_two = gains_all[:MODEL_WIDTH], gains_all[MODEL_WIDTH:]

    shard = lax.axis_index("shard").astype(jnp.int32)
    place = shard[None]
    first_row = shard * TOK_DEV
    first_block = shard * (TOK_DEV // BLK)
    local_slots = first_row + jnp.arange(TOK_DEV, dtype=jnp.int32)
    local_starts = lax.dynamic_slice_in_dim(block_start, first_block, TOK_DEV // BLK)
    local_fills = lax.dynamic_slice_in_dim(block_fill, first_block, TOK_DEV // BLK)
    live_rows = local_slots % BLK < jnp.repeat(local_fills, BLK)
    cosine_table, sine_table = rope_tables(local_slots - jnp.repeat(local_starts, BLK) * BLK)

    def rotate(field, scale):
        heads = field.shape[0]
        front = field[:, : HEAD_SIZE // 2]
        back = field[:, HEAD_SIZE // 2 :]
        return (
            jnp.concatenate(
                [
                    front * cosine_table[None] - back * sine_table[None],
                    back * cosine_table[None] + front * sine_table[None],
                ],
                axis=1,
            ).astype(bf16)
            * bf16(scale)
        ).reshape(heads * HEAD_SIZE, TOK_DEV)

    inputs = layer_input.astype(f32)
    scale_one = norm_scale(inputs)
    normed_one = inputs * scale_one
    first_hidden = (normed_one * gain_one[None, :]).astype(bf16)
    kv_turned = dot_of(kv_weight, first_hidden, 0, 1).reshape(
        KEY_VALUE_HEADS, 2, HEAD_SIZE, TOK_DEV
    )
    keys = rotate(kv_turned[:, 0], 1.0).reshape(KEY_VALUE_HEADS, 1, HEAD_SIZE, TOK_DEV)
    values = kv_turned[:, 1:].astype(bf16)
    kv_rows = jnp.concatenate([keys, values], axis=1).reshape(2 * KV_WIDTH, TOK_DEV).T
    if in_units:
        across = swap(kv_rows, ROW_BIT)
        kv_all = [kv_rows, swap(kv_rows, CORE_BIT), across, swap(across, CORE_BIT)]
    else:
        kv_all = [lax.all_gather(kv_rows, "shard", axis=0, tiled=True)]
    query_turned = rotate(
        dot_of(query_weight, first_hidden, 0, 1).reshape(QUERY_HEADS, HEAD_SIZE, TOK_DEV),
        score_scale,
    )
    mixed_turned, logs = attention_forward(block_start, block_fill, place, query_turned, kv_all)
    middle = inputs + dot_of(mixed_turned, out_weight, 0, 0)
    scale_two = norm_scale(middle)
    normed_two = middle * scale_two
    hidden_two = (normed_two * gain_two[None, :]).astype(bf16)

    grad_out = cotangent.astype(f32) * live_rows[:, None].astype(f32)
    grad_low = grad_out.astype(bf16)
    if in_units:
        spread = spread_matrix()
        outcome, d_spread, *ff_keeps, ff_sent = feedforward(
            table,
            dot_of(hidden_two, spread, 1, 0).astype(bf16),
            dot_of(spread, hidden_two, 0, 1).astype(bf16),
            jnp.pad(grad_low, ((0, 0), (0, PAD_WIDTH - MODEL_WIDTH))),
            feedforward_all.reshape(3 * UNITS, 20, 32, 128),
        )
        layer_output = middle + outcome[:, :MODEL_WIDTH]
        d_coarse = lax.reduce_precision(d_spread, 8, 7)
        d_hidden_two = dot_of(d_coarse.astype(bf16), spread, 1, 1) + dot_of(
            (d_spread - d_coarse).astype(bf16), spread, 1, 1
        )
        ff_sent = swap(ff_sent, CORE_BIT)
        ff_held = scatter_stage([([keep], None) for keep in ff_keeps], 0, list(ff_sent))
    else:
        gate_weight, up_weight, down_weight = unpack_ff(feedforward_all)
        gate = dot_of(hidden_two, gate_weight, 1, 0)
        upper = dot_of(hidden_two, up_weight, 1, 0)
        sigmoid_gate = jax.nn.sigmoid(gate)
        activated = gate * sigmoid_gate
        inner = (activated * upper).astype(bf16)
        layer_output = middle + dot_of(inner, down_weight, 1, 0)
        d_down_weight = dot_of(inner, grad_low, 0, 0).astype(bf16)
        d_inner = dot_of(grad_low, down_weight, 1, 1)
        d_gate = (
            d_inner * upper * sigmoid_gate * (1.0 + gate * (1.0 - sigmoid_gate))
        ).astype(bf16)
        d_upper = (d_inner * activated).astype(bf16)
        d_gate_weight = dot_of(hidden_two, d_gate, 0, 0).astype(bf16)
        d_up_weight = dot_of(hidden_two, d_upper, 0, 0).astype(bf16)
        d_hidden_two = dot_of(d_gate, gate_weight, 1, 1) + dot_of(d_upper, up_weight, 1, 1)
        feedforward_gradient = (
            scatter_lines(pack_ff(d_gate_weight, d_up_weight, d_down_weight))
            .astype(f32)
            .reshape(-1)
        )

    d_gain_two = jnp.sum(d_hidden_two * normed_two, axis=0)
    d_middle = grad_out + norm_back(d_hidden_two, normed_two, scale_two, gain_two)

    d_branch = d_middle.astype(bf16)
    d_out_weight = dot_of(mixed_turned, d_branch, 1, 0).astype(bf16)
    d_mixed = dot_of(out_weight, d_branch, 1, 1).astype(bf16)
    backward_of = lambda first, count, after: attention_backward(
        first,
        count,
        block_start,
        block_fill,
        place,
        query_turned,
        d_mixed,
        mixed_turned,
        logs,
        cosine_table,
        sine_table,
        kv_all,
        after,
    )
    if in_units:
        d_query, d_kv_rows = [], []
        for number, (first, count) in enumerate(BACKWARD_CALLS):
            ff_held = scatter_stage(ff_held, number) if number else ff_held
            d_query_part, *d_kv = backward_of(first, count, [send for _, send in ff_held])
            across = d_kv[2] + swap(d_kv[3], CORE_BIT)
            d_query.append(d_query_part)
            d_kv_rows.append(d_kv[0] + swap(d_kv[1], CORE_BIT) + swap(across, ROW_BIT))
        d_query = jnp.concatenate(d_query, axis=0)
        d_kv_rows = jnp.concatenate(d_kv_rows, axis=1)
        for number in range(len(BACKWARD_CALLS), len(stages(0))):
            ff_held = scatter_stage(ff_held, number)
        ff_addends = [addend for pair in ff_held for addend in pair]
        feedforward_gradient = unform_feedforward(narrow, ff_addends).reshape(-1)
    else:
        d_query, d_kv = backward_of(0, KEY_VALUE_HEADS, ())
        d_kv_rows = lax.psum_scatter(d_kv, "shard", scatter_dimension=0, tiled=True)
    d_kv_turned = d_kv_rows.T.reshape(KEY_VALUE_HEADS, 2, HEAD_SIZE, TOK_DEV)
    d_front = d_kv_turned[:, 0, : HEAD_SIZE // 2].astype(f32)
    d_back = d_kv_turned[:, 0, HEAD_SIZE // 2 :].astype(f32)
    d_keys = jnp.concatenate(
        [
            d_front * cosine_table[None] + d_back * sine_table[None],
            d_back * cosine_table[None] - d_front * sine_table[None],
        ],
        axis=1,
    ).astype(bf16)
    d_kv_lin = jnp.concatenate([d_keys[:, None], d_kv_turned[:, 1:]], axis=1).reshape(
        2 * KV_WIDTH, TOK_DEV
    )
    d_query_weight = dot_of(first_hidden, d_query, 0, 1).astype(bf16)
    d_kv_weight = dot_of(first_hidden, d_kv_lin, 0, 1).astype(bf16)
    d_hidden_one = dot_of(d_query, query_weight, 0, 1) + dot_of(d_kv_lin, kv_weight, 0, 1)
    d_gain_one = jnp.sum(d_hidden_one * normed_one, axis=0)
    input_gradient = d_middle + norm_back(d_hidden_one, normed_one, scale_one, gain_one)

    gain_terms = jnp.concatenate([d_gain_one, d_gain_two])
    if in_units:
        gain_rows = jnp.pad(
            gain_terms.reshape(UNITS, gain_count), ((0, 0), (64, 64 - gain_count))
        )
        *keeps, sent = split_attention(table, d_query_weight, d_kv_weight, d_out_weight, gain_rows)
        sent = swap(sent, CORE_BIT)
        arrived = [sent[:, sum(PIECES[:k]) : sum(PIECES[: k + 1])] for k in range(SLOTS)]
        held = scatter_stage([([keep], None) for keep in keeps], 0, arrived)
        for number in range(1, len(stages(0))):
            held = scatter_stage(held, number)
        addends = [addend for pair in held for addend in pair]
        attention_sum, gain_sum = unform_attention(wide, addends)
        attention_gradient = attention_sum.reshape(-1)
        gains_gradient = gain_sum[0, 64 : 64 + gain_count]
    else:
        no_gains = jnp.zeros((UNITS, GAIN_LINES, 128), bf16)
        terms = pack_attention(d_query_weight, d_kv_weight, d_out_weight, no_gains)
        terms = jnp.concatenate(
            [
                terms[:, :LINES].reshape(devices, attention_lines, 128),
                jnp.pad(
                    gain_terms.astype(bf16).reshape(devices, 1, gain_count),
                    ((0, 0), (0, padded - attention_lines - 1), (0, 128 - gain_count)),
                ),
            ],
            axis=1,
        )
        summed = scatter_lines(terms.reshape(devices * padded, 128)).astype(f32)
        attention_gradient = summed[:attention_lines].reshape(-1)
        gains_gradient = summed[attention_lines, :gain_count]

    attention_first, attention_second, attention_update = adam_step(
        attention_gradient, first_attention, second_attention, master_attention
    )
    feedforward_first, feedforward_second, feedforward_update = adam_step(
        feedforward_gradient, first_feedforward, second_feedforward, master_feedforward
    )
    gains_first, gains_second, gains_update = adam_step(
        gains_gradient, first_gains, second_gains, master_gains
    )
    return (
        layer_output,
        input_gradient,
        attention_gradient,
        feedforward_gradient,
        gains_gradient,
        attention_first,
        attention_second,
        feedforward_first,
        feedforward_second,
        gains_first,
        gains_second,
        attention_update,
        feedforward_update,
        gains_update,
    )


def solution(mesh):
    rows = P(ALL_AXES, None)
    flat = P(ALL_AXES)
    return jax.shard_map(
        local,
        mesh=mesh,
        in_specs=(rows, rows) + (flat,) * 9 + (P("dp"), P("dp")),
        out_specs=(rows, rows) + (flat,) * 12,
        check_vma=False,
    )
```

```python
import functools
import math

import jax
import jax.numpy as jnp
from jax import lax
from jax.experimental import pallas as pl
from jax.experimental.pallas import tpu as pltpu
from jax.sharding import PartitionSpec as P

MODEL_WIDTH = 960
QUERY_HEADS = 15
KEY_VALUE_HEADS = 5
GROUPED = QUERY_HEADS // KEY_VALUE_HEADS
HEAD_SIZE = 64
FF = 2560
BLK = 128
ADAM_STEP = 10
TOK_DEV = 512
KV_WIDTH = KEY_VALUE_HEADS * HEAD_SIZE
TILE = 256
WIDE = GROUPED * BLK
UNITS = 32
LINES = 600
GAIN_LINES = 8
ALL_AXES = ("dp", "shard")

epsilon = 1e-05
masked_value = -1e30
learning_rate = 0.03
weight_decay = 0.1
score_scale = 1.0 / math.sqrt(HEAD_SIZE)
f32 = jnp.float32
bf16 = jnp.bfloat16


def lines_to_rows_2560(scratch, base, rows, store):
    for c in range(20):
        store(c, scratch[pl.ds(base + c, rows, stride=20), :])


def rows_to_lines_2560(load, scratch, base, rows):
    for c in range(20):
        scratch[pl.ds(base + c, rows, stride=20), :] = load(c)


def lane_low(rows):
    return lax.broadcasted_iota(jnp.int32, (rows, 128), 1) < 64


def lines_to_rows_960(scratch, base, rows, mid, store):
    half = rows // 2
    low = lane_low(half)
    line = [scratch[pl.ds(base + k, half, stride=15), :] for k in range(15)]
    turned = [None] * 7 + [pltpu.roll(line[k], 64, 1) for k in range(7, 15)]
    for c in range(8):
        mid[pl.ds(0, half, stride=2), :] = line[c]
        odd = jnp.where(low, turned[7 + c], turned[8 + c]) if c < 7 else turned[14]
        mid[pl.ds(1, half, stride=2), :] = odd
        store(c, mid[pl.ds(0, rows), :])


def rows_to_lines_960(load, scratch, base, rows, mid):
    half = rows // 2
    low = lane_low(half)
    odds = []
    for c in range(8):
        mid[pl.ds(0, rows), :] = load(c)
        even = mid[pl.ds(0, half, stride=2), :]
        odd = pltpu.roll(mid[pl.ds(1, half, stride=2), :], 64, 1)
        odds.append(odd)
        if c < 7:
            scratch[pl.ds(base + c, half, stride=15), :] = even
        else:
            scratch[pl.ds(base + 7, half, stride=15), :] = jnp.where(low, even, odds[0])
        if c > 0:
            scratch[pl.ds(base + 7 + c, half, stride=15), :] = jnp.where(low, odds[c - 1], odd)


def half_chunks(lines):
    even = [(lines[0], 0), (lines[0], 1), (lines[1], 0), (lines[1], 1), (lines[2], 0)]
    odd = [(lines[2], 1), (lines[3], 0), (lines[3], 1), (lines[4], 0), (lines[4], 1)]
    return even, odd


def placed(chunk, upper):
    line, side = chunk
    return line if side == upper else pltpu.roll(line, 64, 1)


def unpack_ff_kernel(lines_ref, gate_ref, up_ref, down_ref, scratch, mid):
    phase = pl.program_id(0)
    scratch[...] = lines_ref[...].astype(f32)
    for number, out in ((0, gate_ref), (1, up_ref)):

        @pl.when(phase == number)
        def _():
            def store(c, value):
                out[:, 128 * c : 128 * c + 128] = value.astype(bf16)

            lines_to_rows_2560(scratch, 0, 96, store)

    @pl.when(phase == 2)
    def _():
        def store(c, value):
            if c < 7:
                down_ref[:, 128 * c : 128 * c + 128] = value.astype(bf16)
            else:
                down_ref[:, 896:960] = value[:, :64].astype(bf16)

        lines_to_rows_960(scratch, 0, 256, mid, store)


def pinned(phase):
    def index(p, j):
        return (jnp.where(p == phase, j, jnp.where(p < phase, 0, 9)), 0)

    return index


def unpack_ff(lines):
    return pl.pallas_call(
        unpack_ff_kernel,
        grid=(3, 10),
        in_specs=[pl.BlockSpec((1920, 128), lambda p, j: (p * 10 + j, 0))],
        out_specs=[
            pl.BlockSpec((96, FF), pinned(0)),
            pl.BlockSpec((96, FF), pinned(1)),
            pl.BlockSpec((256, MODEL_WIDTH), pinned(2)),
        ],
        out_shape=[
            jax.ShapeDtypeStruct((MODEL_WIDTH, FF), bf16),
            jax.ShapeDtypeStruct((MODEL_WIDTH, FF), bf16),
            jax.ShapeDtypeStruct((FF, MODEL_WIDTH), bf16),
        ],
        scratch_shapes=[pltpu.VMEM((1920, 128), f32), pltpu.VMEM((256, 128), f32)],
        name="unpack_feedforward",
    )(lines)


def pack_ff_kernel(gate_ref, up_ref, down_ref, lines_ref, scratch, mid):
    phase = pl.program_id(0)
    for number, source in ((0, gate_ref), (1, up_ref)):

        @pl.when(phase == number)
        def _():
            rows_to_lines_2560(
                lambda c: source[:, 128 * c : 128 * c + 128].astype(f32), scratch, 0, 96
            )

    @pl.when(phase == 2)
    def _():
        def load(c):
            if c < 7:
                return down_ref[:, 128 * c : 128 * c + 128].astype(f32)
            tail = down_ref[:, 896:960].astype(f32)
            return jnp.concatenate([tail, tail], axis=1)

        rows_to_lines_960(load, scratch, 0, 256, mid)

    lines_ref[...] = scratch[...].astype(bf16)


def pack_ff(gate, up, down):
    return pl.pallas_call(
        pack_ff_kernel,
        grid=(3, 10),
        in_specs=[
            pl.BlockSpec((96, FF), pinned(0)),
            pl.BlockSpec((96, FF), pinned(1)),
            pl.BlockSpec((256, MODEL_WIDTH), pinned(2)),
        ],
        out_specs=pl.BlockSpec((1920, 128), lambda p, j: (p * 10 + j, 0)),
        out_shape=jax.ShapeDtypeStruct((3 * 19200, 128), bf16),
        scratch_shapes=[pltpu.VMEM((1920, 128), f32), pltpu.VMEM((256, 128), f32)],
        name="pack_feedforward",
    )(gate, up, down)


def unpack_wide_kernel(lines_ref, out_ref, scratch, mid):
    for u in range(4):
        scratch[...] = lines_ref[u].astype(f32)
        base = u * 80

        def store(c, value):
            if c < 7:
                out_ref[base : base + 80, 128 * c : 128 * c + 128] = value.astype(bf16)
            else:
                out_ref[base : base + 80, 896:960] = value[:, :64].astype(bf16)

        lines_to_rows_960(scratch, 0, 80, mid, store)


def unpack_wide(lines, first):
    depth = lines.shape[1]
    return pl.pallas_call(
        unpack_wide_kernel,
        grid=(3,),
        in_specs=[pl.BlockSpec((4, depth, 128), lambda j: (first // 4 + j, 0, 0))],
        out_specs=pl.BlockSpec((320, MODEL_WIDTH), lambda j: (j, 0)),
        out_shape=jax.ShapeDtypeStruct((MODEL_WIDTH, MODEL_WIDTH), bf16),
        scratch_shapes=[pltpu.VMEM((depth, 128), f32), pltpu.VMEM((80, 128), f32)],
        name="unpack_attention",
    )(lines)


def unpack_kv_kernel(key_ref, value_ref, out_ref, key_lines, value_lines, mid):
    low = lane_low(120)
    key_lines[...] = key_ref[0].astype(f32)
    value_lines[...] = value_ref[0].astype(f32)
    keys = half_chunks([key_lines[pl.ds(k, 120, stride=5), :] for k in range(5)])
    values = half_chunks([value_lines[pl.ds(k, 120, stride=5), :] for k in range(5)])
    for h in range(KEY_VALUE_HEADS):
        for parity in range(2):
            mid[pl.ds(parity, 120, stride=2), :] = jnp.where(
                low, placed(keys[parity][h], 0), placed(values[parity][h], 1)
            )
        out_ref[:, 128 * h : 128 * h + 128] = mid[...].astype(bf16)


def unpack_kv(lines):
    depth = lines.shape[1]
    return pl.pallas_call(
        unpack_kv_kernel,
        grid=(4,),
        in_specs=[
            pl.BlockSpec((1, depth, 128), lambda j: (12 + j, 0, 0)),
            pl.BlockSpec((1, depth, 128), lambda j: (16 + j, 0, 0)),
        ],
        out_specs=pl.BlockSpec((240, 2 * KV_WIDTH), lambda j: (j, 0)),
        out_shape=jax.ShapeDtypeStruct((MODEL_WIDTH, 2 * KV_WIDTH), bf16),
        scratch_shapes=[
            pltpu.VMEM((depth, 128), f32),
            pltpu.VMEM((depth, 128), f32),
            pltpu.VMEM((240, 128), f32),
        ],
        name="unpack_key_value",
    )(lines, lines)


def pack_attention_kernel(query_ref, kv_ref, out_weight_ref, gains_ref, lines_ref, scratch, mid):
    step = pl.program_id(0)

    def wide(source):
        for u in range(4):
            base = u * 80

            def load(c):
                if c < 7:
                    return source[base : base + 80, 128 * c : 128 * c + 128].astype(f32)
                tail = source[base : base + 80, 896:960].astype(f32)
                return jnp.concatenate([tail, tail], axis=1)

            rows_to_lines_960(load, scratch, 0, 80, mid)
            lines_ref[u, :LINES, :] = scratch[...].astype(bf16)

    @pl.when(step < 3)
    def _():
        wide(query_ref)

    @pl.when(step >= 5)
    def _():
        wide(out_weight_ref)

    for number, upper in ((3, 0), (4, 1)):

        @pl.when(step == number)
        def _():
            low = lane_low(120)
            for u in range(4):
                evens, odds = [], []
                for h in range(KEY_VALUE_HEADS):
                    mid[...] = kv_ref[
                        240 * u : 240 * u + 240, 128 * h : 128 * h + 128
                    ].astype(f32)
                    evens.append((mid[pl.ds(0, 120, stride=2), :], upper))
                    odds.append((mid[pl.ds(1, 120, stride=2), :], upper))
                run = evens + odds
                for k in range(5):
                    scratch[pl.ds(k, 120, stride=5), :] = jnp.where(
                        low, placed(run[2 * k], 0), placed(run[2 * k + 1], 1)
                    )
                lines_ref[u, :LINES, :] = scratch[...].astype(bf16)

    for u in range(4):
        lines_ref[u, LINES:, :] = gains_ref[u]


def pack_attention(d_query, d_kv, d_out, gains):
    return pl.pallas_call(
        pack_attention_kernel,
        grid=(8,),
        in_specs=[
            pl.BlockSpec((320, MODEL_WIDTH), lambda s: (jnp.minimum(s, 2), 0)),
            pl.BlockSpec((MODEL_WIDTH, 2 * KV_WIDTH), lambda s: (0, 0)),
            pl.BlockSpec((320, MODEL_WIDTH), lambda s: (jnp.maximum(s - 5, 0), 0)),
            pl.BlockSpec((4, GAIN_LINES, 128), lambda s: (s, 0, 0)),
        ],
        out_specs=pl.BlockSpec((4, LINES + GAIN_LINES, 128), lambda s: (s, 0, 0)),
        out_shape=jax.ShapeDtypeStruct((UNITS, LINES + GAIN_LINES, 128), bf16),
        scratch_shapes=[pltpu.VMEM((LINES, 128), f32), pltpu.VMEM((240, 128), f32)],
        name="pack_attention",
    )(d_query, d_kv, d_out, gains)


def tile_range(starts_ref, fills_ref, block):
    first_slot = starts_ref[block] * BLK
    last_slot = block * BLK + fills_ref[block]
    tile_first = first_slot // TILE
    tile_last = (block * BLK) // TILE
    ragged_first = jnp.logical_and(first_slot % TILE != 0, tile_first < tile_last)
    return first_slot, last_slot, tile_first, tile_last, ragged_first.astype(jnp.int32)


def allowed_pairs(tile, block, first_slot, last_slot):
    key_slot = tile * TILE + lax.broadcasted_iota(jnp.int32, (TILE, WIDE), 0)
    lane = lax.broadcasted_iota(jnp.int32, (TILE, WIDE), 1)
    query_slot = block * BLK + lax.rem(lane, BLK)
    return jnp.logical_and(
        jnp.logical_and(key_slot >= first_slot, key_slot <= query_slot),
        jnp.logical_or(key_slot < last_slot, key_slot == query_slot),
    )


def over_tiles(span, block, step):
    first_slot, last_slot, tile_first, tile_last, ragged = span

    def masked(tile):
        step(tile, allowed_pairs(tile, block, first_slot, last_slot))

    def edge(k, carry):
        masked(jnp.where(k == ragged, tile_last, tile_first))
        return carry

    lax.fori_loop(0, 1 + ragged, edge, 0)

    def inner(tile, carry):
        step(tile, None)
        return carry

    lax.fori_loop(tile_first + ragged, tile_last, inner, 0)


def transpose_kv(kv_ref, turned, tiles):
    def body(t, carry):
        rows = pl.ds(pl.multiple_of(t * TILE, TILE), TILE)
        for h in range(KEY_VALUE_HEADS):
            turned[t, 128 * h : 128 * h + 128, :] = kv_ref[rows, 128 * h : 128 * h + 128].T
        return carry

    lax.fori_loop(0, tiles, body, 0)


def lay_out_kv(blocks, kv_ref, place):
    size = blocks[0].shape[0]
    for apart, block in enumerate(blocks):
        spot = apart if len(blocks) == 1 else place ^ apart
        kv_ref[pl.ds(pl.multiple_of(spot * size, TILE), size), :] = block[...]


def heads_beside(ref, h):
    return jnp.concatenate(
        [
            ref[HEAD_SIZE * (GROUPED * h + g) : HEAD_SIZE * (GROUPED * h + g + 1), :]
            for g in range(GROUPED)
        ],
        axis=1,
    )


def attention_forward_kernel(
    starts_ref, fills_ref, place_ref, query_ref, *refs
):
    kv_blocks = refs[:-8]
    mixed_ref, log_ref, kv_ref, turned, pairs, tops, totals, sums = refs[-8:]
    i = pl.program_id(0)
    block = place_ref[0] * (TOK_DEV // BLK) + i

    @pl.when(i == 0)
    def _():
        lay_out_kv(kv_blocks, kv_ref, place_ref[0])
        transpose_kv(kv_ref, turned, kv_ref.shape[0] // TILE)

    for h in range(KEY_VALUE_HEADS):
        pairs[h, :HEAD_SIZE, :] = heads_beside(query_ref, h)
        pairs[h, HEAD_SIZE:, :] = jnp.zeros((HEAD_SIZE, WIDE), bf16)
    tops[...] = jnp.full(tops.shape, masked_value, f32)
    totals[...] = jnp.zeros(totals.shape, f32)
    sums[...] = jnp.zeros(sums.shape, f32)

    def step(tile, allowed):
        rows = pl.ds(pl.multiple_of(tile * TILE, TILE), TILE)

        def score(h):
            return jnp.dot(
                kv_ref[rows, 128 * h : 128 * h + 128], pairs[h], preferred_element_type=f32
            )

        def weigh(h, scores):
            if allowed is not None:
                scores = jnp.where(allowed, scores, masked_value)
            top_old = tops[h]
            top = jnp.maximum(top_old, jnp.max(scores, axis=0, keepdims=True))
            weights = jnp.exp(scores - top)
            shrink = jnp.exp(top_old - top)
            tops[h] = top
            totals[h] = totals[h] * shrink + jnp.sum(weights, axis=0, keepdims=True)
            return weights.astype(bf16), shrink

        def gather(h, weights, shrink):
            sums[h] = sums[h] * shrink + jnp.dot(
                turned[tile, 128 * h + HEAD_SIZE : 128 * h + 128, :],
                weights,
                preferred_element_type=f32,
            )

        scores = [score(h) for h in range(KEY_VALUE_HEADS)]
        held = None
        for h in range(KEY_VALUE_HEADS):
            weighed = weigh(h, scores[h])
            if held is not None:
                gather(h - 1, *held)
            held = weighed
        gather(KEY_VALUE_HEADS - 1, *held)

    over_tiles(tile_range(starts_ref, fills_ref, block), block, step)
    for h in range(KEY_VALUE_HEADS):
        outcome = (sums[h] / totals[h]).astype(bf16)
        log_total = tops[h] + jnp.log(totals[h])
        for g in range(GROUPED):
            head = GROUPED * h + g
            mixed_ref[HEAD_SIZE * head : HEAD_SIZE * (head + 1), :] = outcome[:, BLK * g : BLK * (g + 1)]
            log_ref[head : head + 1, :] = log_total[:, BLK * g : BLK * (g + 1)]
    log_ref[QUERY_HEADS:, :] = jnp.zeros((1, BLK), f32)


def token_block(rows):
    return pl.BlockSpec((rows, BLK), lambda i, *_: (0, i))


def whole(shape):
    return pl.BlockSpec(shape, lambda i, *_: (0,) * len(shape))


def attention_forward(starts, fills, place, query, kv):
    group = sum(block.shape[0] for block in kv)
    return pl.pallas_call(
        attention_forward_kernel,
        grid_spec=pltpu.PrefetchScalarGridSpec(
            num_scalar_prefetch=3,
            grid=(TOK_DEV // BLK,),
            in_specs=[token_block(MODEL_WIDTH)] + [whole(block.shape) for block in kv],
            out_specs=[token_block(MODEL_WIDTH), token_block(16)],
            scratch_shapes=[
                pltpu.VMEM((group, 2 * KV_WIDTH), bf16),
                pltpu.VMEM((group // TILE, 2 * KV_WIDTH, TILE), bf16),
                pltpu.VMEM((KEY_VALUE_HEADS, 2 * HEAD_SIZE, WIDE), bf16),
                pltpu.VMEM((KEY_VALUE_HEADS, 1, WIDE), f32),
                pltpu.VMEM((KEY_VALUE_HEADS, 1, WIDE), f32),
                pltpu.VMEM((KEY_VALUE_HEADS, HEAD_SIZE, WIDE), f32),
            ],
        ),
        out_shape=[
            jax.ShapeDtypeStruct((MODEL_WIDTH, TOK_DEV), bf16),
            jax.ShapeDtypeStruct((16, TOK_DEV), f32),
        ],
        name="attention_forward",
    )(starts, fills, place, query, *kv)


def attention_backward_kernel(
    first,
    blocks,
    starts_ref,
    fills_ref,
    place_ref,
    query_ref,
    upstream_ref,
    mixed_ref,
    log_ref,
    cosine_ref,
    sine_ref,
    *refs,
):
    kv_blocks, refs = refs[:blocks], refs[-(blocks + 10) :]
    d_query_ref, d_kv_blocks = refs[0], refs[1 : blocks + 1]
    kv_ref, turned, pairs, query_rows, upstream_rows, deltas, logs, sums, kv_sums = refs[blocks + 1 :]
    count = kv_sums.shape[0]
    i = pl.program_id(0)
    block = place_ref[0] * (TOK_DEV // BLK) + i
    tiles = kv_ref.shape[0] // TILE

    @pl.when(i == 0)
    def _():
        for apart, source in enumerate(kv_blocks):
            size = source.shape[0]
            spot = apart if blocks == 1 else place_ref[0] ^ apart
            kv_ref[pl.ds(pl.multiple_of(spot * size, TILE), size), :] = source[
                :, 128 * first : 128 * (first + count)
            ]

        def prepare(t, carry):
            rows = pl.ds(pl.multiple_of(t * TILE, TILE), TILE)
            for h in range(count):
                turned[t, HEAD_SIZE * h : HEAD_SIZE * (h + 1), :] = kv_ref[
                    rows, 128 * h : 128 * h + 128
                ].T[:HEAD_SIZE]
            kv_sums[:, rows, :] = jnp.zeros((count, TILE, 128), f32)
            return carry

        lax.fori_loop(0, tiles, prepare, 0)

    blank = jnp.zeros((HEAD_SIZE, WIDE), bf16)
    for h in range(count):
        query = heads_beside(query_ref, first + h)
        upstream = heads_beside(upstream_ref, first + h)
        pairs[h, :HEAD_SIZE, :WIDE] = query
        pairs[h, HEAD_SIZE:, :WIDE] = blank
        pairs[h, :HEAD_SIZE, WIDE:] = blank
        pairs[h, HEAD_SIZE:, WIDE:] = upstream
        query_rows[h] = pairs[h, :, :WIDE].T
        upstream_rows[h] = pairs[h, :, WIDE:].T
        deltas[h] = jnp.sum(
            upstream.astype(f32) * heads_beside(mixed_ref, first + h).astype(f32),
            axis=0,
            keepdims=True,
        )
        line = GROUPED * (first + h)
        logs[h] = jnp.concatenate(
            [log_ref[line + g : line + g + 1, :] for g in range(GROUPED)], axis=1
        )
    sums[...] = jnp.zeros(sums.shape, f32)

    def step(tile, allowed):
        rows = pl.ds(pl.multiple_of(tile * TILE, TILE), TILE)

        def score(h):
            return jnp.dot(
                kv_ref[rows, 128 * h : 128 * h + 128], pairs[h], preferred_element_type=f32
            )

        def weigh(h, both):
            scores = both[:, :WIDE]
            if allowed is not None:
                scores = jnp.where(allowed, scores, masked_value)
            probs = jnp.exp(scores - logs[h])
            d_scores = (probs * (both[:, WIDE:] - deltas[h])).astype(bf16)
            return probs.astype(bf16), d_scores

        def gather(h, probs, d_scores):
            kv_sums[h, rows, :] += jnp.dot(
                d_scores, query_rows[h], preferred_element_type=f32
            ) + jnp.dot(probs, upstream_rows[h], preferred_element_type=f32)
            sums[h] += jnp.dot(
                turned[tile, HEAD_SIZE * h : HEAD_SIZE * (h + 1), :],
                d_scores,
                preferred_element_type=f32,
            )

        following = score(0)
        held = None
        for h in range(count):
            both = following
            if h + 1 < count:
                following = score(h + 1)
            weighed = weigh(h, both)
            if held is not None:
                gather(h - 1, *held)
            held = weighed
        gather(count - 1, *held)

    over_tiles(tile_range(starts_ref, fills_ref, block), block, step)
    cosine = cosine_ref[...]
    sine = sine_ref[...]
    half = HEAD_SIZE // 2
    for h in range(count):
        for g in range(GROUPED):
            head = GROUPED * h + g
            front = sums[h, :half, BLK * g : BLK * (g + 1)] * score_scale
            back = sums[h, half:, BLK * g : BLK * (g + 1)] * score_scale
            d_query_ref[HEAD_SIZE * head : HEAD_SIZE * head + half, :] = (
                front * cosine + back * sine
            ).astype(bf16)
            d_query_ref[HEAD_SIZE * head + half : HEAD_SIZE * (head + 1), :] = (
                back * cosine - front * sine
            ).astype(bf16)

    @pl.when(i == pl.num_programs(0) - 1)
    def _():
        size = kv_blocks[0].shape[0]
        for apart, out in enumerate(d_kv_blocks):
            spot = apart if blocks == 1 else place_ref[0] ^ apart

            def emit(t, carry):
                rows = pl.ds(pl.multiple_of(spot * size + t * TILE, TILE), TILE)
                for h in range(count):
                    out[pl.ds(pl.multiple_of(t * TILE, TILE), TILE), 128 * h : 128 * h + 128] = (
                        kv_sums[h, rows, :].astype(bf16)
                    )
                return carry

            lax.fori_loop(0, size // TILE, emit, 0)


def attention_backward(
    first, count, starts, fills, place, query, upstream, mixed, logs, cosine, sine, kv, after=()
):
    group = sum(block.shape[0] for block in kv)
    half = HEAD_SIZE // 2
    outs = [(block.shape[0], 128 * count) for block in kv]
    return pl.pallas_call(
        functools.partial(attention_backward_kernel, first, len(kv)),
        grid_spec=pltpu.PrefetchScalarGridSpec(
            num_scalar_prefetch=3,
            grid=(TOK_DEV // BLK,),
            in_specs=[
                token_block(MODEL_WIDTH),
                token_block(MODEL_WIDTH),
                token_block(MODEL_WIDTH),
                token_block(16),
                token_block(half),
                token_block(half),
            ]
            + [whole(block.shape) for block in kv]
            + [pl.BlockSpec(memory_space=pl.ANY)] * len(after),
            out_specs=[token_block(GROUPED * HEAD_SIZE * count)] + [whole(shape) for shape in outs],
            scratch_shapes=[
                pltpu.VMEM((group, 128 * count), bf16),
                pltpu.VMEM((group // TILE, HEAD_SIZE * count, TILE), bf16),
                pltpu.VMEM((count, 2 * HEAD_SIZE, 2 * WIDE), bf16),
                pltpu.VMEM((count, WIDE, 128), bf16),
                pltpu.VMEM((count, WIDE, 128), bf16),
                pltpu.VMEM((count, 1, WIDE), f32),
                pltpu.VMEM((count, 1, WIDE), f32),
                pltpu.VMEM((count, HEAD_SIZE, WIDE), f32),
                pltpu.VMEM((count, group, 128), f32),
            ],
        ),
        out_shape=[jax.ShapeDtypeStruct((GROUPED * HEAD_SIZE * count, TOK_DEV), bf16)]
        + [jax.ShapeDtypeStruct(shape, bf16) for shape in outs],
        name="attention_backward",
    )(starts, fills, place, query, upstream, mixed, logs, cosine, sine, *kv, *after)


def dot_of(left, right, left_dim, right_dim):
    return lax.dot_general(
        left, right, (((left_dim,), (right_dim,)), ((), ())), preferred_element_type=f32
    )


SLOTS = 3
FORM = 640
PIECES = (240, 240, 160)
GAIN_LINE = 560
PAD_WIDTH = 1024
CHUNK = 640
CORE_BIT = ("shard", 1)
ROW_BIT = ("shard", 2)
NEAR_BITS = (ROW_BIT, ("dp", 1), ("dp", 2))
FAR_BITS = (("dp", 4),)
BACKWARD_CALLS = ((0, 5),)


def stages(colour):
    return (CORE_BIT,) + NEAR_BITS[colour:] + NEAR_BITS[:colour] + FAR_BITS


def swap(value, bit):
    axis, mask = bit
    size = lax.axis_size(axis)
    return lax.ppermute(value, axis, [(i, i ^ mask) for i in range(size)])


def gather_colour(own, colour):
    held = own[None]
    for bit in reversed(stages(colour)[1:]):
        held = jnp.concatenate([held, swap(held, bit)], axis=0)
    return held, swap(held, CORE_BIT)


def scatter_stage(held, number, arrived=None):
    outcome = []
    total = lambda parts: sum(part.astype(f32) for part in parts)
    bits = [stages(colour)[number] for colour in range(len(held))]
    if arrived is None and len(set(bits)) == 1:
        flat = [send.reshape(-1, 128) for _, send in held]
        merged = swap(jnp.concatenate(flat, axis=0), bits[0])
        arrived, base = [], 0
        for (_, send), lines in zip(held, flat):
            arrived.append(merged[base : base + lines.shape[0]].reshape(send.shape))
            base += lines.shape[0]
    if arrived is None:
        arrived = [swap(send, bit) for (_, send), bit in zip(held, bits)]
    for (parts, _), got in zip(held, arrived):
        half = got.shape[0] // 2
        if half == 0:
            outcome.append((total(parts)[0].astype(bf16), got[0]))
        else:
            parts = parts + [got]
            outcome.append(
                ([part[:half] for part in parts], total([part[half:] for part in parts]).astype(bf16))
            )
    return outcome


def positions():
    device = jnp.arange(UNITS, dtype=jnp.int32)
    width = lax.axis_size("shard")
    apart = {
        "dp": (device // width) ^ lax.axis_index("dp").astype(jnp.int32),
        "shard": (device % width) ^ lax.axis_index("shard").astype(jnp.int32),
    }
    tables = []
    for colour in range(SLOTS):
        place = jnp.zeros((UNITS,), jnp.int32)
        for axis, mask in stages(colour):
            place = 2 * place + (apart[axis] & mask) // mask
        tables.append(place)
    return jnp.concatenate(tables)


def copy_from(halves, place, dst, sem, pick=lambda ref: ref):
    for number, ref in enumerate(halves):

        @pl.when(place // 16 == number)
        def _():
            pltpu.make_async_copy(pick(ref.at[lax.rem(place, 16)]), dst, sem).start()


def copy_to(src, keep, send, place, sem):
    for number, pick in enumerate((keep, send)):

        @pl.when(place // 16 == number)
        def _():
            pltpu.make_async_copy(src, pick(lax.rem(place, 16)), sem).start()


def wait_for(ref, sem):
    pltpu.make_async_copy(ref, ref, sem).wait()


def form_attention_kernel(wide_ref, lines_ref, gains_ref, a_ref, b_ref, c_ref, mid, form):
    @pl.when(wide_ref[0] == 1)
    def _():
        def store(c, value):
            if c == 7:
                value = jnp.where(lane_low(80), value, 0.0)
            form[80 * c : 80 * c + 80, :] = value

        lines_to_rows_960(lines_ref, 0, 80, mid, store)

    @pl.when(wide_ref[0] == 0)
    def _():
        low = lane_low(120)
        line = [lines_ref[pl.ds(k, 120, stride=5), :] for k in range(5)]
        turned = [None, None] + [pltpu.roll(line[k], 64, 1) for k in range(2, 5)]
        form[pl.ds(0, 120, stride=2), :] = line[0]
        form[pl.ds(1, 120, stride=2), :] = jnp.where(low, turned[2], turned[3])
        form[pl.ds(240, 120, stride=2), :] = line[1]
        form[pl.ds(241, 120, stride=2), :] = jnp.where(low, turned[3], turned[4])
        mid[pl.ds(0, 120, stride=2), :] = line[2]
        mid[pl.ds(1, 120, stride=2), :] = turned[4]
        low = lane_low(80)
        form[480:560, :] = jnp.where(low, mid[0:80, :], pltpu.roll(mid[160:240, :], 64, 1))
        form[560:640, :] = jnp.where(low, mid[80:160, :], 0.0)

    form[GAIN_LINE : GAIN_LINE + 1, :] = jnp.where(
        lane_low(1), form[GAIN_LINE : GAIN_LINE + 1, :], gains_ref[...]
    )
    a_ref[...] = form[0:240, :].astype(bf16)
    b_ref[...] = form[240:480, :].astype(bf16)
    c_ref[...] = form[480:640, :].astype(bf16)


SMEM_SPEC = pl.BlockSpec(memory_space=pltpu.SMEM)
ANY_SPEC = pl.BlockSpec(memory_space=pl.ANY)


def form_attention(wide, lines, gains):
    return pl.pallas_call(
        form_attention_kernel,
        in_specs=[SMEM_SPEC, pl.BlockSpec((LINES, 128)), pl.BlockSpec((1, 128))],
        out_shape=[jax.ShapeDtypeStruct((n, 128), bf16) for n in PIECES],
        scratch_shapes=[pltpu.VMEM((240, 128), f32), pltpu.VMEM((FORM, 128), f32)],
        name="form_attention",
    )(wide, lines, gains)


def unform_attention_kernel(wide_ref, *refs):
    pieces, (lines_ref, gains_ref, mid, form) = refs[:6], refs[6:]
    base = 0
    for n, keep, got in zip(PIECES, pieces[0::2], pieces[1::2]):
        form[base : base + n, :] = keep[...].astype(f32) + got[...].astype(f32)
        base += n
    gains_ref[...] = form[GAIN_LINE : GAIN_LINE + 1, :]

    @pl.when(wide_ref[0] == 1)
    def _():
        rows_to_lines_960(lambda c: form[80 * c : 80 * c + 80, :], lines_ref, 0, 80, mid)

    @pl.when(wide_ref[0] == 0)
    def _():
        low = lane_low(120)
        mid[0:80, :] = form[480:560, :]
        mid[80:160, :] = form[560:640, :]
        mid[160:240, :] = pltpu.roll(form[480:560, :], 64, 1)
        even = [form[pl.ds(0, 120, stride=2), :], form[pl.ds(240, 120, stride=2), :]]
        odd = [form[pl.ds(1, 120, stride=2), :], form[pl.ds(241, 120, stride=2), :]]
        even.append(mid[pl.ds(0, 120, stride=2), :])
        odd.append(mid[pl.ds(1, 120, stride=2), :])
        odd = [pltpu.roll(value, 64, 1) for value in odd]
        lines_ref[pl.ds(0, 120, stride=5), :] = even[0]
        lines_ref[pl.ds(1, 120, stride=5), :] = even[1]
        lines_ref[pl.ds(2, 120, stride=5), :] = jnp.where(low, even[2], odd[0])
        lines_ref[pl.ds(3, 120, stride=5), :] = jnp.where(low, odd[0], odd[1])
        lines_ref[pl.ds(4, 120, stride=5), :] = jnp.where(low, odd[1], odd[2])


def unform_attention(wide, addends):
    return pl.pallas_call(
        unform_attention_kernel,
        in_specs=[SMEM_SPEC] + [pl.BlockSpec((n, 128)) for n in PIECES for _ in range(2)],
        out_shape=[jax.ShapeDtypeStruct((LINES, 128), f32), jax.ShapeDtypeStruct((1, 128), f32)],
        scratch_shapes=[pltpu.VMEM((240, 128), f32), pltpu.VMEM((FORM, 128), f32)],
        name="unform_attention",
    )(wide, *addends)


def wide_pieces(c):
    return [((80 * c + 16 * m) // 32, (80 * c + 16 * m) % 32, 16 * m) for m in range(5)]


def form_feedforward_kernel(narrow_ref, lines_ref, out, mid):
    for s in range(SLOTS):

        @pl.when(narrow_ref[s] == 1)
        def _():
            mid[30:32, :] = jnp.zeros((2, 128), f32)
            for c in range(20):
                mid[0:30, :] = lines_ref[pl.ds(LINES * s + c, 30, stride=20), :]
                out[s, c] = mid[0:32, :].astype(bf16)

        @pl.when(narrow_ref[s] == 0)
        def _():
            def store(c, value):
                if c == 7:
                    value = jnp.where(lane_low(80), value, 0.0)
                for k, r, m in wide_pieces(c):
                    out[s, k, r : r + 16, :] = value[m : m + 16].astype(bf16)

            lines_to_rows_960(lines_ref, LINES * s, 80, mid, store)


def form_feedforward(narrow, lines):
    return pl.pallas_call(
        form_feedforward_kernel,
        in_specs=[SMEM_SPEC, pl.BlockSpec((SLOTS * LINES, 128))],
        out_shape=jax.ShapeDtypeStruct((SLOTS, 20, 32, 128), bf16),
        scratch_shapes=[pltpu.VMEM((80, 128), f32)],
        name="form_feedforward",
    )(narrow, lines)


def unform_feedforward_kernel(narrow_ref, *refs):
    pieces, (lines_ref, mid) = refs[: 2 * SLOTS], refs[2 * SLOTS :]
    for s in range(SLOTS):
        keep, got = pieces[2 * s], pieces[2 * s + 1]

        @pl.when(narrow_ref[s] == 1)
        def _():
            for c in range(20):
                mid[0:32, :] = keep[c].astype(f32) + got[c].astype(f32)
                lines_ref[pl.ds(LINES * s + c, 30, stride=20), :] = mid[0:30, :]

        @pl.when(narrow_ref[s] == 0)
        def _():
            def load(c):
                return jnp.concatenate(
                    [
                        keep[k, r : r + 16, :].astype(f32) + got[k, r : r + 16, :].astype(f32)
                        for k, r, m in wide_pieces(c)
                    ],
                    axis=0,
                )

            rows_to_lines_960(load, lines_ref, LINES * s, 80, mid)


def unform_feedforward(narrow, addends):
    return pl.pallas_call(
        unform_feedforward_kernel,
        in_specs=[SMEM_SPEC] + [pl.BlockSpec((20, 32, 128))] * (2 * SLOTS),
        out_shape=jax.ShapeDtypeStruct((SLOTS * LINES, 128), f32),
        scratch_shapes=[pltpu.VMEM((80, 128), f32)],
        name="unform_feedforward",
    )(narrow, *addends)


def place_attention_kernel(table_ref, *refs):
    halves = [refs[2 * k : 2 * k + 2] for k in range(SLOTS)]
    query_ref, kv_ref, out_ref, gains_ref, units, sem = refs[2 * SLOTS :]

    def start(d, carry):
        base = 0
        for k, n in enumerate(PIECES):
            copy_from(halves[k], table_ref[UNITS * k + d], units.at[d, base : base + n, :], sem)
            base += n
        return carry

    lax.fori_loop(0, UNITS, start, 0)
    wait_for(units, sem)

    def wide(out, first):
        def body(u, carry):
            rows = pl.ds(pl.multiple_of(80 * u, 16), 80)
            for c in range(7):
                out[rows, 128 * c : 128 * c + 128] = units[first + u, 80 * c : 80 * c + 80, :]
            out[rows, 896:960] = units[first + u, 560:640, :64]
            return carry

        lax.fori_loop(0, 12, body, 0)

    def keyed(j, carry):
        low = lane_low(240)
        chunks = []
        for first in (12, 16):
            unit = units[first + j].astype(f32)
            last = jnp.concatenate(
                [unit[480:640], pltpu.roll(unit[480:560], 64, 1)], axis=0
            )
            lines = (unit[0:240], unit[240:480], last)
            chunks.append([(lines[h // 2], h % 2) for h in range(KEY_VALUE_HEADS)])
        rows = pl.ds(pl.multiple_of(240 * j, 16), 240)
        for h in range(KEY_VALUE_HEADS):
            kv_ref[rows, 128 * h : 128 * h + 128] = jnp.where(
                low, placed(chunks[0][h], 0), placed(chunks[1][h], 1)
            ).astype(bf16)
        return carry

    lax.fori_loop(0, 4, keyed, 0)
    wide(query_ref, 0)
    wide(out_ref, 20)
    for u in range(UNITS):
        gains_ref[u : u + 1, :] = units[u, GAIN_LINE : GAIN_LINE + 1, :].astype(f32)


def place_attention(table, gathered):
    return pl.pallas_call(
        place_attention_kernel,
        in_specs=[SMEM_SPEC] + [ANY_SPEC] * (2 * SLOTS),
        out_shape=[
            jax.ShapeDtypeStruct((MODEL_WIDTH, MODEL_WIDTH), bf16),
            jax.ShapeDtypeStruct((MODEL_WIDTH, 2 * KV_WIDTH), bf16),
            jax.ShapeDtypeStruct((MODEL_WIDTH, MODEL_WIDTH), bf16),
            jax.ShapeDtypeStruct((UNITS, 128), f32),
        ],
        scratch_shapes=[pltpu.VMEM((UNITS, FORM, 128), bf16), pltpu.SemaphoreType.DMA],
        name="place_attention",
    )(table, *gathered)


def split_attention_kernel(table_ref, query_ref, kv_ref, out_ref, gains_ref, *refs):
    *keeps, sent, units, sem = refs

    def send(d):
        row = lax.broadcasted_iota(jnp.int32, (16, 128), 0)
        lane = lax.broadcasted_iota(jnp.int32, (16, 128), 1)
        block = units[d, GAIN_LINE : GAIN_LINE + 16, :].astype(f32)
        units[d, GAIN_LINE : GAIN_LINE + 16, :] = jnp.where(
            jnp.logical_and(row == 0, lane >= 64), gains_ref[pl.ds(d, 1), :], block
        ).astype(bf16)
        base = 0
        for k, n in enumerate(PIECES):
            copy_to(
                units.at[d, base : base + n, :],
                lambda p: keeps[k].at[p],
                lambda p: sent.at[p, base : base + n, :],
                table_ref[UNITS * k + d],
                sem,
            )
            base += n

    def wide(source, first):
        def body(u, carry):
            rows = pl.ds(pl.multiple_of(80 * u, 16), 80)
            for c in range(7):
                units[first + u, 80 * c : 80 * c + 80, :] = source[rows, 128 * c : 128 * c + 128]
            tail = source[rows, 896:960]
            units[first + u, 560:640, :] = jnp.concatenate([tail, jnp.zeros_like(tail)], axis=1)
            send(first + u)
            return carry

        lax.fori_loop(0, 12, body, 0)

    def keyed(j, carry):
        low = lane_low(240)
        rows = pl.ds(pl.multiple_of(240 * j, 16), 240)
        for upper, first in ((0, 12), (1, 16)):
            heads = [
                (kv_ref[rows, 128 * h : 128 * h + 128].astype(f32), upper)
                for h in range(KEY_VALUE_HEADS)
            ]
            for c in range(2):
                units[first + j, 240 * c : 240 * c + 240, :] = jnp.where(
                    low, placed(heads[2 * c], 0), placed(heads[2 * c + 1], 1)
                ).astype(bf16)
            last = placed(heads[4], 0)
            turned = placed(heads[4], 1)
            units[first + j, 480:560, :] = jnp.where(
                lane_low(80), last[0:80], turned[160:240]
            ).astype(bf16)
            units[first + j, 560:640, :] = jnp.where(lane_low(80), last[80:160], 0.0).astype(bf16)
            send(first + j)
        return carry

    lax.fori_loop(0, 4, keyed, 0)
    wide(query_ref, 0)
    wide(out_ref, 20)
    wait_for(units, sem)


def split_attention(table, d_query, d_kv, d_out, gains):
    return pl.pallas_call(
        split_attention_kernel,
        in_specs=[
            SMEM_SPEC,
            pl.BlockSpec((MODEL_WIDTH, MODEL_WIDTH)),
            pl.BlockSpec((MODEL_WIDTH, 2 * KV_WIDTH)),
            pl.BlockSpec((MODEL_WIDTH, MODEL_WIDTH)),
            pl.BlockSpec((UNITS, 128)),
        ],
        out_specs=[ANY_SPEC] * (SLOTS + 1),
        out_shape=[jax.ShapeDtypeStruct((16, n, 128), bf16) for n in PIECES + (FORM,)],
        scratch_shapes=[pltpu.VMEM((UNITS, FORM, 128), bf16), pltpu.SemaphoreType.DMA],
        name="split_attention",
    )(table, d_query, d_kv, d_out, gains)


def feedforward_kernel(
    table_ref,
    hidden_ref,
    turned_ref,
    grad_ref,
    gate_ref,
    up_ref,
    down_ref,
    out_ref,
    d_hidden_ref,
    *refs,
):
    keeps, sent = refs[:SLOTS], refs[SLOTS]
    down, inner_rows, inner_turned, d_both, both_out, down_out, sems = refs[SLOTS + 1 :]
    q = pl.program_id(0)
    chunks = pl.num_programs(0)
    slot = lax.rem(q, 2)

    def send_terms():
        for u in range(2 * UNITS):
            device, s = divmod(u, SLOTS)
            copy_to(
                both_out.at[slot, u // UNITS, u % UNITS],
                lambda p: keeps[s].at[p, pl.ds(5 * q, 5)],
                lambda p: sent.at[s, p, pl.ds(5 * q, 5)],
                table_ref[UNITS * s + device],
                sems.at[slot, 0],
            )
        for v in range(8):
            unit = 2 * UNITS + 8 * q + v
            device = unit // SLOTS
            for s in range(SLOTS):

                @pl.when(unit - SLOTS * device == s)
                def _():
                    copy_to(
                        down_out.at[slot, v],
                        lambda p: keeps[s].at[p],
                        lambda p: sent.at[s, p],
                        table_ref[UNITS * s + device],
                        sems.at[slot, 1],
                    )

    def wait_terms(side):
        wait_for(both_out.at[side], sems.at[side, 0])
        wait_for(down_out.at[side], sems.at[side, 1])

    for v in range(8):
        for c in range(8):
            for k, r, m in wide_pieces(c):
                down[80 * v + m : 80 * v + m + 16, 128 * c : 128 * c + 128] = down_ref[
                    v, k, r : r + 16, :
                ]

    @pl.when(q == 0)
    def _():
        out_ref[...] = jnp.zeros(out_ref.shape, f32)
        d_hidden_ref[...] = jnp.zeros(d_hidden_ref.shape, f32)

    def rows_step(i, carry):
        rows = pl.ds(pl.multiple_of(256 * i, 256), 256)
        weights = jnp.concatenate(
            [ref[:, c].reshape(PAD_WIDTH, 128) for ref in (gate_ref, up_ref) for c in range(5)],
            axis=1,
        )
        both = jnp.dot(hidden_ref[rows, :], weights, preferred_element_type=f32)
        gate, upper = both[:, :CHUNK], both[:, CHUNK:]
        sigmoid_gate = jax.nn.sigmoid(gate)
        activated = gate * sigmoid_gate
        inner = (activated * upper).astype(bf16)
        inner_rows[rows, :] = inner
        out_ref[rows, :] += jnp.dot(inner, down[...], preferred_element_type=f32)
        d_inner = dot_of(grad_ref[rows, :], down[...], 1, 1)
        d_gate = d_inner * upper * sigmoid_gate * (1.0 + gate * (1.0 - sigmoid_gate))
        d_upper = d_inner * activated
        d_pair = jnp.concatenate([d_gate, d_upper], axis=1).astype(bf16)
        d_both[rows, :] = d_pair
        d_hidden_ref[rows, :] += dot_of(d_pair, weights, 1, 1)
        return carry

    lax.fori_loop(0, 2, rows_step, 0)
    inner_turned[...] = inner_rows[...].T

    @pl.when(q >= 2)
    def _():
        wait_terms(slot)

    def both_step(i, carry):
        rows = pl.ds(pl.multiple_of(256 * i, 256), 256)
        terms = jnp.dot(turned_ref[rows, :], d_both[...], preferred_element_type=f32).astype(bf16)
        units = pl.ds(8 * i, 8)
        for c in range(10):
            both_out[slot, c // 5, units, c % 5] = terms[:, 128 * c : 128 * c + 128].reshape(
                8, 32, 128
            )
        return carry

    lax.fori_loop(0, 4, both_step, 0)

    def down_step(i, carry):
        rows = pl.ds(pl.multiple_of(320 * i, 16), 320)
        terms = jnp.dot(
            inner_turned[rows, :], grad_ref[...], preferred_element_type=f32
        ).astype(bf16)
        for v in range(4):
            for c in range(8):
                for k, r, m in wide_pieces(c):
                    down_out[slot, 4 * i + v, k, r : r + 16, :] = terms[
                        80 * v + m : 80 * v + m + 16, 128 * c : 128 * c + 128
                    ]
        return carry

    lax.fori_loop(0, 2, down_step, 0)
    send_terms()

    @pl.when(q == chunks - 1)
    def _():
        for side in range(2):
            wait_terms(side)


def feedforward(table, hidden, turned, grad, weights):
    block = jax.ShapeDtypeStruct((16, 20, 32, 128), bf16)
    full = lambda shape: pl.BlockSpec(shape, lambda q: (0, 0))
    return pl.pallas_call(
        feedforward_kernel,
        grid=(FF // CHUNK,),
        in_specs=[
            SMEM_SPEC,
            full((TOK_DEV, PAD_WIDTH)),
            full((PAD_WIDTH, TOK_DEV)),
            full((TOK_DEV, PAD_WIDTH)),
            pl.BlockSpec((32, 5, 32, 128), lambda q: (0, q, 0, 0)),
            pl.BlockSpec((32, 5, 32, 128), lambda q: (1, q, 0, 0)),
            pl.BlockSpec((8, 20, 32, 128), lambda q: (8 + q, 0, 0, 0)),
        ],
        out_specs=[full((TOK_DEV, PAD_WIDTH))] * 2 + [ANY_SPEC] * (SLOTS + 1),
        out_shape=[jax.ShapeDtypeStruct((TOK_DEV, PAD_WIDTH), f32)] * 2
        + [block] * SLOTS
        + [jax.ShapeDtypeStruct((SLOTS,) + block.shape, bf16)],
        scratch_shapes=[
            pltpu.VMEM((CHUNK, PAD_WIDTH), bf16),
            pltpu.VMEM((TOK_DEV, CHUNK), bf16),
            pltpu.VMEM((CHUNK, TOK_DEV), bf16),
            pltpu.VMEM((TOK_DEV, 2 * CHUNK), bf16),
            pltpu.VMEM((2, 2, 32, 5, 32, 128), bf16),
            pltpu.VMEM((2, 8, 20, 32, 128), bf16),
            pltpu.SemaphoreType.DMA((2, 2)),
        ],
        compiler_params=pltpu.CompilerParams(vmem_limit_bytes=60 * 2**20),
        name="feedforward",
    )(table, hidden, turned, grad, weights, weights, weights)


def spread_matrix():
    column = jnp.arange(PAD_WIDTH, dtype=jnp.int32)
    entry = jnp.where(column % 32 < 30, 30 * (column // 32) + column % 32, -1)
    return (jnp.arange(MODEL_WIDTH, dtype=jnp.int32)[:, None] == entry[None, :]).astype(bf16)


def rope_tables(positions):
    steps = jnp.arange(HEAD_SIZE // 2, dtype=f32) * (2.0 / HEAD_SIZE)
    inverse = jnp.exp(-math.log(10000.0) * steps)
    angles = inverse[:, None] * positions.astype(f32)[None, :]
    return (jnp.cos(angles), jnp.sin(angles))


def norm_scale(field):
    return lax.rsqrt(jnp.mean(field * field, axis=1, keepdims=True) + epsilon)


def norm_back(upstream, normed, scale, gain):
    scaled = upstream * gain[None, :]
    return scale * (scaled - normed * jnp.mean(scaled * normed, axis=1, keepdims=True))


def adam_step(grad, moment, second, master):
    moment_new = 0.9 * moment + 0.1 * grad
    second_new = 0.999 * second + 0.001 * grad * grad
    corrected = moment_new / (1.0 - 0.9**ADAM_STEP)
    scaled = second_new / (1.0 - 0.999**ADAM_STEP)
    update = -learning_rate * (corrected / (jnp.sqrt(scaled) + 1e-08) + weight_decay * master)
    return (moment_new, second_new, update)


def gather_lines(block):
    return lax.all_gather(block, ALL_AXES, axis=0, tiled=True)


def scatter_lines(lines):
    return lax.psum_scatter(lines, ALL_AXES, scatter_dimension=0, tiled=True)


def local(
    layer_input,
    cotangent,
    master_attention,
    master_feedforward,
    master_gains,
    first_attention,
    second_attention,
    first_feedforward,
    second_feedforward,
    first_gains,
    second_gains,
    block_start,
    block_fill,
):
    devices = lax.axis_size(ALL_AXES)
    attention_lines = master_attention.shape[0] // 128
    feedforward_lines = master_feedforward.shape[0] // 128
    gain_count = master_gains.shape[0]
    padded = (attention_lines // 16 + 1) * 16

    in_units = devices == UNITS
    if in_units:
        table = positions()
        device = (
            lax.axis_index("dp") * lax.axis_size("shard") + lax.axis_index("shard")
        ).astype(jnp.int32)
        wide = jnp.logical_or(device < 12, device >= 20).astype(jnp.int32)[None]
        narrow = (SLOTS * device + jnp.arange(SLOTS, dtype=jnp.int32) < 2 * UNITS).astype(jnp.int32)
        gain_row = jnp.pad(
            master_gains.reshape(1, gain_count), ((0, 0), (64, 64 - gain_count))
        )
        pieces = form_attention(wide, master_attention.reshape(LINES, 128), gain_row)
        gathered = [half for k in range(SLOTS) for half in gather_colour(pieces[k], k)]
        forms = form_feedforward(narrow, master_feedforward.reshape(SLOTS * LINES, 128))
        feedforward_all = gather_lines(forms.reshape(SLOTS * FORM, 128))
        query_weight, kv_weight, out_weight, gain_rows = place_attention(table, gathered)
        gains_all = gain_rows[:, 64 : 64 + gain_count].reshape(-1)
    else:
        gain_lines = jnp.pad(
            master_gains.astype(bf16).reshape(1, gain_count),
            ((0, padded - attention_lines - 1), (0, 128 - gain_count)),
        )
        attention_block = jnp.concatenate(
            [master_attention.astype(bf16).reshape(attention_lines, 128), gain_lines], axis=0
        )
        by_device = gather_lines(attention_block).reshape(devices, padded, 128)
        feedforward_all = gather_lines(
            master_feedforward.astype(bf16).reshape(feedforward_lines, 128)
        )
        gains_all = by_device[:, attention_lines, :gain_count].reshape(-1).astype(f32)
        units = by_device[:, :attention_lines].reshape(UNITS, LINES, 128)
        query_weight = unpack_wide(units, 0)
        kv_weight = unpack_kv(units)
        out_weight = unpack_wide(units, 20)
    gain_one, gain_two = gains_all[:MODEL_WIDTH], gains_all[MODEL_WIDTH:]

    shard = lax.axis_index("shard").astype(jnp.int32)
    place = shard[None]
    first_row = shard * TOK_DEV
    first_block = shard * (TOK_DEV // BLK)
    local_slots = first_row + jnp.arange(TOK_DEV, dtype=jnp.int32)
    local_starts = lax.dynamic_slice_in_dim(block_start, first_block, TOK_DEV // BLK)
    local_fills = lax.dynamic_slice_in_dim(block_fill, first_block, TOK_DEV // BLK)
    live_rows = local_slots % BLK < jnp.repeat(local_fills, BLK)
    cosine_table, sine_table = rope_tables(local_slots - jnp.repeat(local_starts, BLK) * BLK)

    def rotate(field, scale):
        heads = field.shape[0]
        front = field[:, : HEAD_SIZE // 2]
        back = field[:, HEAD_SIZE // 2 :]
        return (
            jnp.concatenate(
                [
                    front * cosine_table[None] - back * sine_table[None],
                    back * cosine_table[None] + front * sine_table[None],
                ],
                axis=1,
            ).astype(bf16)
            * bf16(scale)
        ).reshape(heads * HEAD_SIZE, TOK_DEV)

    inputs = layer_input.astype(f32)
    scale_one = norm_scale(inputs)
    normed_one = inputs * scale_one
    first_hidden = (normed_one * gain_one[None, :]).astype(bf16)
    kv_turned = dot_of(kv_weight, first_hidden, 0, 1).reshape(
        KEY_VALUE_HEADS, 2, HEAD_SIZE, TOK_DEV
    )
    keys = rotate(kv_turned[:, 0], 1.0).reshape(KEY_VALUE_HEADS, 1, HEAD_SIZE, TOK_DEV)
    values = kv_turned[:, 1:].astype(bf16)
    kv_rows = jnp.concatenate([keys, values], axis=1).reshape(2 * KV_WIDTH, TOK_DEV).T
    if in_units:
        across = swap(kv_rows, ROW_BIT)
        kv_all = [kv_rows, swap(kv_rows, CORE_BIT), across, swap(across, CORE_BIT)]
    else:
        kv_all = [lax.all_gather(kv_rows, "shard", axis=0, tiled=True)]
    query_turned = rotate(
        dot_of(query_weight, first_hidden, 0, 1).reshape(QUERY_HEADS, HEAD_SIZE, TOK_DEV),
        score_scale,
    )
    mixed_turned, logs = attention_forward(block_start, block_fill, place, query_turned, kv_all)
    middle = inputs + dot_of(mixed_turned, out_weight, 0, 0)
    scale_two = norm_scale(middle)
    normed_two = middle * scale_two
    hidden_two = (normed_two * gain_two[None, :]).astype(bf16)

    grad_out = cotangent.astype(f32) * live_rows[:, None].astype(f32)
    grad_low = grad_out.astype(bf16)
    if in_units:
        spread = spread_matrix()
        outcome, d_spread, *ff_keeps, ff_sent = feedforward(
            table,
            dot_of(hidden_two, spread, 1, 0).astype(bf16),
            dot_of(spread, hidden_two, 0, 1).astype(bf16),
            jnp.pad(grad_low, ((0, 0), (0, PAD_WIDTH - MODEL_WIDTH))),
            feedforward_all.reshape(3 * UNITS, 20, 32, 128),
        )
        layer_output = middle + outcome[:, :MODEL_WIDTH]
        d_coarse = lax.reduce_precision(d_spread, 8, 7)
        d_hidden_two = dot_of(d_coarse.astype(bf16), spread, 1, 1) + dot_of(
            (d_spread - d_coarse).astype(bf16), spread, 1, 1
        )
        ff_sent = swap(ff_sent, CORE_BIT)
    else:
        gate_weight, up_weight, down_weight = unpack_ff(feedforward_all)
        gate = dot_of(hidden_two, gate_weight, 1, 0)
        upper = dot_of(hidden_two, up_weight, 1, 0)
        sigmoid_gate = jax.nn.sigmoid(gate)
        activated = gate * sigmoid_gate
        inner = (activated * upper).astype(bf16)
        layer_output = middle + dot_of(inner, down_weight, 1, 0)
        d_down_weight = dot_of(inner, grad_low, 0, 0).astype(bf16)
        d_inner = dot_of(grad_low, down_weight, 1, 1)
        d_gate = (
            d_inner * upper * sigmoid_gate * (1.0 + gate * (1.0 - sigmoid_gate))
        ).astype(bf16)
        d_upper = (d_inner * activated).astype(bf16)
        d_gate_weight = dot_of(hidden_two, d_gate, 0, 0).astype(bf16)
        d_up_weight = dot_of(hidden_two, d_upper, 0, 0).astype(bf16)
        d_hidden_two = dot_of(d_gate, gate_weight, 1, 1) + dot_of(d_upper, up_weight, 1, 1)
        feedforward_gradient = (
            scatter_lines(pack_ff(d_gate_weight, d_up_weight, d_down_weight))
            .astype(f32)
            .reshape(-1)
        )

    d_gain_two = jnp.sum(d_hidden_two * normed_two, axis=0)
    d_middle = grad_out + norm_back(d_hidden_two, normed_two, scale_two, gain_two)

    d_branch = d_middle.astype(bf16)
    d_out_weight = dot_of(mixed_turned, d_branch, 1, 0).astype(bf16)
    d_mixed = dot_of(out_weight, d_branch, 1, 1).astype(bf16)
    if in_units:
        ff_sent, d_mixed = lax.optimization_barrier((ff_sent, d_mixed))
        ff_held = scatter_stage([([keep], None) for keep in ff_keeps], 0, list(ff_sent))
    backward_of = lambda first, count, after: attention_backward(
        first,
        count,
        block_start,
        block_fill,
        place,
        query_turned,
        d_mixed,
        mixed_turned,
        logs,
        cosine_table,
        sine_table,
        kv_all,
        after,
    )
    if in_units:
        d_query, d_kv_rows = [], []
        for number, (first, count) in enumerate(BACKWARD_CALLS):
            d_query_part, *d_kv = backward_of(first, count, [send for _, send in ff_held])
            arrived = [
                swap(send, stages(colour)[number + 1]) for colour, (_, send) in enumerate(ff_held)
            ]
            d_kv, arrived = lax.optimization_barrier((d_kv, arrived))
            ff_held = scatter_stage(ff_held, number + 1, arrived)
            across = d_kv[2] + swap(d_kv[3], CORE_BIT)
            d_query.append(d_query_part)
            d_kv_rows.append(d_kv[0] + swap(d_kv[1], CORE_BIT) + swap(across, ROW_BIT))
        d_query = jnp.concatenate(d_query, axis=0)
        d_kv_rows = jnp.concatenate(d_kv_rows, axis=1)
        arrived = [swap(send, stages(colour)[2]) for colour, (_, send) in enumerate(ff_held)]
    else:
        d_query, d_kv = backward_of(0, KEY_VALUE_HEADS, ())
        d_kv_rows = lax.psum_scatter(d_kv, "shard", scatter_dimension=0, tiled=True)
    d_kv_turned = d_kv_rows.T.reshape(KEY_VALUE_HEADS, 2, HEAD_SIZE, TOK_DEV)
    d_front = d_kv_turned[:, 0, : HEAD_SIZE // 2].astype(f32)
    d_back = d_kv_turned[:, 0, HEAD_SIZE // 2 :].astype(f32)
    d_keys = jnp.concatenate(
        [
            d_front * cosine_table[None] + d_back * sine_table[None],
            d_back * cosine_table[None] - d_front * sine_table[None],
        ],
        axis=1,
    ).astype(bf16)
    d_kv_lin = jnp.concatenate([d_keys[:, None], d_kv_turned[:, 1:]], axis=1).reshape(
        2 * KV_WIDTH, TOK_DEV
    )
    d_query_weight = dot_of(first_hidden, d_query, 0, 1).astype(bf16)
    d_kv_weight = dot_of(first_hidden, d_kv_lin, 0, 1).astype(bf16)
    d_hidden_one = dot_of(d_query, query_weight, 0, 1) + dot_of(d_kv_lin, kv_weight, 0, 1)
    d_gain_one = jnp.sum(d_hidden_one * normed_one, axis=0)
    input_gradient = d_middle + norm_back(d_hidden_one, normed_one, scale_one, gain_one)

    gain_terms = jnp.concatenate([d_gain_one, d_gain_two])
    if in_units:
        gain_rows = jnp.pad(
            gain_terms.reshape(UNITS, gain_count), ((0, 0), (64, 64 - gain_count))
        )
        arrived, d_query_weight = lax.optimization_barrier((arrived, d_query_weight))
        ff_held = scatter_stage(ff_held, 2, arrived)
        for number in range(3, len(stages(0))):
            ff_held = scatter_stage(ff_held, number)
        ff_addends = [addend for pair in ff_held for addend in pair]
        feedforward_gradient = unform_feedforward(narrow, ff_addends).reshape(-1)
        *keeps, sent = split_attention(table, d_query_weight, d_kv_weight, d_out_weight, gain_rows)
        sent = swap(sent, CORE_BIT)
        arrived = [sent[:, sum(PIECES[:k]) : sum(PIECES[: k + 1])] for k in range(SLOTS)]
        held = scatter_stage([([keep], None) for keep in keeps], 0, arrived)
        for number in range(1, len(stages(0))):
            held = scatter_stage(held, number)
        addends = [addend for pair in held for addend in pair]
        attention_sum, gain_sum = unform_attention(wide, addends)
        attention_gradient = attention_sum.reshape(-1)
        gains_gradient = gain_sum[0, 64 : 64 + gain_count]
    else:
        no_gains = jnp.zeros((UNITS, GAIN_LINES, 128), bf16)
        terms = pack_attention(d_query_weight, d_kv_weight, d_out_weight, no_gains)
        terms = jnp.concatenate(
            [
                terms[:, :LINES].reshape(devices, attention_lines, 128),
                jnp.pad(
                    gain_terms.astype(bf16).reshape(devices, 1, gain_count),
                    ((0, 0), (0, padded - attention_lines - 1), (0, 128 - gain_count)),
                ),
            ],
            axis=1,
        )
        summed = scatter_lines(terms.reshape(devices * padded, 128)).astype(f32)
        attention_gradient = summed[:attention_lines].reshape(-1)
        gains_gradient = summed[attention_lines, :gain_count]

    attention_first, attention_second, attention_update = adam_step(
        attention_gradient, first_attention, second_attention, master_attention
    )
    feedforward_first, feedforward_second, feedforward_update = adam_step(
        feedforward_gradient, first_feedforward, second_feedforward, master_feedforward
    )
    gains_first, gains_second, gains_update = adam_step(
        gains_gradient, first_gains, second_gains, master_gains
    )
    return (
        layer_output,
        input_gradient,
        attention_gradient,
        feedforward_gradient,
        gains_gradient,
        attention_first,
        attention_second,
        feedforward_first,
        feedforward_second,
        gains_first,
        gains_second,
        attention_update,
        feedforward_update,
        gains_update,
    )


def solution(mesh):
    rows = P(ALL_AXES, None)
    flat = P(ALL_AXES)
    return jax.shard_map(
        local,
        mesh=mesh,
        in_specs=(rows, rows) + (flat,) * 9 + (P("dp"), P("dp")),
        out_specs=(rows, rows) + (flat,) * 12,
        check_vma=False,
    )
```

```python
import functools
import math

import jax
import jax.numpy as jnp
from jax import lax
from jax.experimental import pallas as pl
from jax.experimental.pallas import tpu as pltpu
from jax.sharding import PartitionSpec as P

MODEL_WIDTH = 960
QUERY_HEADS = 15
KEY_VALUE_HEADS = 5
GROUPED = QUERY_HEADS // KEY_VALUE_HEADS
HEAD_SIZE = 64
FF = 2560
BLK = 128
ADAM_STEP = 10
TOK_DEV = 512
KV_WIDTH = KEY_VALUE_HEADS * HEAD_SIZE
TILE = 256
WIDE = GROUPED * BLK
UNITS = 32
LINES = 600
GAIN_LINES = 8
ALL_AXES = ("dp", "shard")

epsilon = 1e-05
masked_value = -1e30
learning_rate = 0.03
weight_decay = 0.1
score_scale = 1.0 / math.sqrt(HEAD_SIZE)
f32 = jnp.float32
bf16 = jnp.bfloat16


def lines_to_rows_2560(scratch, base, rows, store):
    for c in range(20):
        store(c, scratch[pl.ds(base + c, rows, stride=20), :])


def rows_to_lines_2560(load, scratch, base, rows):
    for c in range(20):
        scratch[pl.ds(base + c, rows, stride=20), :] = load(c)


def lane_low(rows):
    return lax.broadcasted_iota(jnp.int32, (rows, 128), 1) < 64


def lines_to_rows_960(scratch, base, rows, mid, store):
    half = rows // 2
    low = lane_low(half)
    line = [scratch[pl.ds(base + k, half, stride=15), :] for k in range(15)]
    turned = [None] * 7 + [pltpu.roll(line[k], 64, 1) for k in range(7, 15)]
    for c in range(8):
        mid[pl.ds(0, half, stride=2), :] = line[c]
        odd = jnp.where(low, turned[7 + c], turned[8 + c]) if c < 7 else turned[14]
        mid[pl.ds(1, half, stride=2), :] = odd
        store(c, mid[pl.ds(0, rows), :])


def rows_to_lines_960(load, scratch, base, rows, mid):
    half = rows // 2
    low = lane_low(half)
    odds = []
    for c in range(8):
        mid[pl.ds(0, rows), :] = load(c)
        even = mid[pl.ds(0, half, stride=2), :]
        odd = pltpu.roll(mid[pl.ds(1, half, stride=2), :], 64, 1)
        odds.append(odd)
        if c < 7:
            scratch[pl.ds(base + c, half, stride=15), :] = even
        else:
            scratch[pl.ds(base + 7, half, stride=15), :] = jnp.where(low, even, odds[0])
        if c > 0:
            scratch[pl.ds(base + 7 + c, half, stride=15), :] = jnp.where(low, odds[c - 1], odd)


def half_chunks(lines):
    even = [(lines[0], 0), (lines[0], 1), (lines[1], 0), (lines[1], 1), (lines[2], 0)]
    odd = [(lines[2], 1), (lines[3], 0), (lines[3], 1), (lines[4], 0), (lines[4], 1)]
    return even, odd


def placed(chunk, upper):
    line, side = chunk
    return line if side == upper else pltpu.roll(line, 64, 1)


def unpack_ff_kernel(lines_ref, gate_ref, up_ref, down_ref, scratch, mid):
    phase = pl.program_id(0)
    scratch[...] = lines_ref[...].astype(f32)
    for number, out in ((0, gate_ref), (1, up_ref)):

        @pl.when(phase == number)
        def _():
            def store(c, value):
                out[:, 128 * c : 128 * c + 128] = value.astype(bf16)

            lines_to_rows_2560(scratch, 0, 96, store)

    @pl.when(phase == 2)
    def _():
        def store(c, value):
            if c < 7:
                down_ref[:, 128 * c : 128 * c + 128] = value.astype(bf16)
            else:
                down_ref[:, 896:960] = value[:, :64].astype(bf16)

        lines_to_rows_960(scratch, 0, 256, mid, store)


def pinned(phase):
    def index(p, j):
        return (jnp.where(p == phase, j, jnp.where(p < phase, 0, 9)), 0)

    return index


def unpack_ff(lines):
    return pl.pallas_call(
        unpack_ff_kernel,
        grid=(3, 10),
        in_specs=[pl.BlockSpec((1920, 128), lambda p, j: (p * 10 + j, 0))],
        out_specs=[
            pl.BlockSpec((96, FF), pinned(0)),
            pl.BlockSpec((96, FF), pinned(1)),
            pl.BlockSpec((256, MODEL_WIDTH), pinned(2)),
        ],
        out_shape=[
            jax.ShapeDtypeStruct((MODEL_WIDTH, FF), bf16),
            jax.ShapeDtypeStruct((MODEL_WIDTH, FF), bf16),
            jax.ShapeDtypeStruct((FF, MODEL_WIDTH), bf16),
        ],
        scratch_shapes=[pltpu.VMEM((1920, 128), f32), pltpu.VMEM((256, 128), f32)],
        name="unpack_feedforward",
    )(lines)


def pack_ff_kernel(gate_ref, up_ref, down_ref, lines_ref, scratch, mid):
    phase = pl.program_id(0)
    for number, source in ((0, gate_ref), (1, up_ref)):

        @pl.when(phase == number)
        def _():
            rows_to_lines_2560(
                lambda c: source[:, 128 * c : 128 * c + 128].astype(f32), scratch, 0, 96
            )

    @pl.when(phase == 2)
    def _():
        def load(c):
            if c < 7:
                return down_ref[:, 128 * c : 128 * c + 128].astype(f32)
            tail = down_ref[:, 896:960].astype(f32)
            return jnp.concatenate([tail, tail], axis=1)

        rows_to_lines_960(load, scratch, 0, 256, mid)

    lines_ref[...] = scratch[...].astype(bf16)


def pack_ff(gate, up, down):
    return pl.pallas_call(
        pack_ff_kernel,
        grid=(3, 10),
        in_specs=[
            pl.BlockSpec((96, FF), pinned(0)),
            pl.BlockSpec((96, FF), pinned(1)),
            pl.BlockSpec((256, MODEL_WIDTH), pinned(2)),
        ],
        out_specs=pl.BlockSpec((1920, 128), lambda p, j: (p * 10 + j, 0)),
        out_shape=jax.ShapeDtypeStruct((3 * 19200, 128), bf16),
        scratch_shapes=[pltpu.VMEM((1920, 128), f32), pltpu.VMEM((256, 128), f32)],
        name="pack_feedforward",
    )(gate, up, down)


def unpack_wide_kernel(lines_ref, out_ref, scratch, mid):
    for u in range(4):
        scratch[...] = lines_ref[u].astype(f32)
        base = u * 80

        def store(c, value):
            if c < 7:
                out_ref[base : base + 80, 128 * c : 128 * c + 128] = value.astype(bf16)
            else:
                out_ref[base : base + 80, 896:960] = value[:, :64].astype(bf16)

        lines_to_rows_960(scratch, 0, 80, mid, store)


def unpack_wide(lines, first):
    depth = lines.shape[1]
    return pl.pallas_call(
        unpack_wide_kernel,
        grid=(3,),
        in_specs=[pl.BlockSpec((4, depth, 128), lambda j: (first // 4 + j, 0, 0))],
        out_specs=pl.BlockSpec((320, MODEL_WIDTH), lambda j: (j, 0)),
        out_shape=jax.ShapeDtypeStruct((MODEL_WIDTH, MODEL_WIDTH), bf16),
        scratch_shapes=[pltpu.VMEM((depth, 128), f32), pltpu.VMEM((80, 128), f32)],
        name="unpack_attention",
    )(lines)


def unpack_kv_kernel(key_ref, value_ref, out_ref, key_lines, value_lines, mid):
    low = lane_low(120)
    key_lines[...] = key_ref[0].astype(f32)
    value_lines[...] = value_ref[0].astype(f32)
    keys = half_chunks([key_lines[pl.ds(k, 120, stride=5), :] for k in range(5)])
    values = half_chunks([value_lines[pl.ds(k, 120, stride=5), :] for k in range(5)])
    for h in range(KEY_VALUE_HEADS):
        for parity in range(2):
            mid[pl.ds(parity, 120, stride=2), :] = jnp.where(
                low, placed(keys[parity][h], 0), placed(values[parity][h], 1)
            )
        out_ref[:, 128 * h : 128 * h + 128] = mid[...].astype(bf16)


def unpack_kv(lines):
    depth = lines.shape[1]
    return pl.pallas_call(
        unpack_kv_kernel,
        grid=(4,),
        in_specs=[
            pl.BlockSpec((1, depth, 128), lambda j: (12 + j, 0, 0)),
            pl.BlockSpec((1, depth, 128), lambda j: (16 + j, 0, 0)),
        ],
        out_specs=pl.BlockSpec((240, 2 * KV_WIDTH), lambda j: (j, 0)),
        out_shape=jax.ShapeDtypeStruct((MODEL_WIDTH, 2 * KV_WIDTH), bf16),
        scratch_shapes=[
            pltpu.VMEM((depth, 128), f32),
            pltpu.VMEM((depth, 128), f32),
            pltpu.VMEM((240, 128), f32),
        ],
        name="unpack_key_value",
    )(lines, lines)


def pack_attention_kernel(query_ref, kv_ref, out_weight_ref, gains_ref, lines_ref, scratch, mid):
    step = pl.program_id(0)

    def wide(source):
        for u in range(4):
            base = u * 80

            def load(c):
                if c < 7:
                    return source[base : base + 80, 128 * c : 128 * c + 128].astype(f32)
                tail = source[base : base + 80, 896:960].astype(f32)
                return jnp.concatenate([tail, tail], axis=1)

            rows_to_lines_960(load, scratch, 0, 80, mid)
            lines_ref[u, :LINES, :] = scratch[...].astype(bf16)

    @pl.when(step < 3)
    def _():
        wide(query_ref)

    @pl.when(step >= 5)
    def _():
        wide(out_weight_ref)

    for number, upper in ((3, 0), (4, 1)):

        @pl.when(step == number)
        def _():
            low = lane_low(120)
            for u in range(4):
                evens, odds = [], []
                for h in range(KEY_VALUE_HEADS):
                    mid[...] = kv_ref[
                        240 * u : 240 * u + 240, 128 * h : 128 * h + 128
                    ].astype(f32)
                    evens.append((mid[pl.ds(0, 120, stride=2), :], upper))
                    odds.append((mid[pl.ds(1, 120, stride=2), :], upper))
                run = evens + odds
                for k in range(5):
                    scratch[pl.ds(k, 120, stride=5), :] = jnp.where(
                        low, placed(run[2 * k], 0), placed(run[2 * k + 1], 1)
                    )
                lines_ref[u, :LINES, :] = scratch[...].astype(bf16)

    for u in range(4):
        lines_ref[u, LINES:, :] = gains_ref[u]


def pack_attention(d_query, d_kv, d_out, gains):
    return pl.pallas_call(
        pack_attention_kernel,
        grid=(8,),
        in_specs=[
            pl.BlockSpec((320, MODEL_WIDTH), lambda s: (jnp.minimum(s, 2), 0)),
            pl.BlockSpec((MODEL_WIDTH, 2 * KV_WIDTH), lambda s: (0, 0)),
            pl.BlockSpec((320, MODEL_WIDTH), lambda s: (jnp.maximum(s - 5, 0), 0)),
            pl.BlockSpec((4, GAIN_LINES, 128), lambda s: (s, 0, 0)),
        ],
        out_specs=pl.BlockSpec((4, LINES + GAIN_LINES, 128), lambda s: (s, 0, 0)),
        out_shape=jax.ShapeDtypeStruct((UNITS, LINES + GAIN_LINES, 128), bf16),
        scratch_shapes=[pltpu.VMEM((LINES, 128), f32), pltpu.VMEM((240, 128), f32)],
        name="pack_attention",
    )(d_query, d_kv, d_out, gains)


def tile_range(starts_ref, fills_ref, block):
    first_slot = starts_ref[block] * BLK
    last_slot = block * BLK + fills_ref[block]
    tile_first = first_slot // TILE
    tile_last = (block * BLK) // TILE
    ragged_first = jnp.logical_and(first_slot % TILE != 0, tile_first < tile_last)
    return first_slot, last_slot, tile_first, tile_last, ragged_first.astype(jnp.int32)


def allowed_pairs(tile, block, first_slot, last_slot):
    key_slot = tile * TILE + lax.broadcasted_iota(jnp.int32, (TILE, WIDE), 0)
    lane = lax.broadcasted_iota(jnp.int32, (TILE, WIDE), 1)
    query_slot = block * BLK + lax.rem(lane, BLK)
    return jnp.logical_and(
        jnp.logical_and(key_slot >= first_slot, key_slot <= query_slot),
        jnp.logical_or(key_slot < last_slot, key_slot == query_slot),
    )


def over_tiles(span, block, step):
    first_slot, last_slot, tile_first, tile_last, ragged = span

    def masked(tile):
        step(tile, allowed_pairs(tile, block, first_slot, last_slot))

    def edge(k, carry):
        masked(jnp.where(k == ragged, tile_last, tile_first))
        return carry

    lax.fori_loop(0, 1 + ragged, edge, 0)

    def inner(tile, carry):
        step(tile, None)
        return carry

    lax.fori_loop(tile_first + ragged, tile_last, inner, 0)


def transpose_kv(kv_ref, turned, tiles):
    def body(t, carry):
        rows = pl.ds(pl.multiple_of(t * TILE, TILE), TILE)
        for h in range(KEY_VALUE_HEADS):
            turned[t, 128 * h : 128 * h + 128, :] = kv_ref[rows, 128 * h : 128 * h + 128].T
        return carry

    lax.fori_loop(0, tiles, body, 0)


def lay_out_kv(blocks, kv_ref, place):
    size = blocks[0].shape[0]
    for apart, block in enumerate(blocks):
        spot = apart if len(blocks) == 1 else place ^ apart
        kv_ref[pl.ds(pl.multiple_of(spot * size, TILE), size), :] = block[...]


def heads_beside(ref, h):
    return jnp.concatenate(
        [
            ref[HEAD_SIZE * (GROUPED * h + g) : HEAD_SIZE * (GROUPED * h + g + 1), :]
            for g in range(GROUPED)
        ],
        axis=1,
    )


def attention_forward_kernel(
    starts_ref, fills_ref, place_ref, query_ref, *refs
):
    kv_blocks = refs[:-8]
    mixed_ref, log_ref, kv_ref, turned, pairs, tops, totals, sums = refs[-8:]
    i = pl.program_id(0)
    block = place_ref[0] * (TOK_DEV // BLK) + i

    @pl.when(i == 0)
    def _():
        lay_out_kv(kv_blocks, kv_ref, place_ref[0])
        transpose_kv(kv_ref, turned, kv_ref.shape[0] // TILE)

    for h in range(KEY_VALUE_HEADS):
        pairs[h, :HEAD_SIZE, :] = heads_beside(query_ref, h)
        pairs[h, HEAD_SIZE:, :] = jnp.zeros((HEAD_SIZE, WIDE), bf16)
    tops[...] = jnp.full(tops.shape, masked_value, f32)
    totals[...] = jnp.zeros(totals.shape, f32)
    sums[...] = jnp.zeros(sums.shape, f32)

    def step(tile, allowed):
        rows = pl.ds(pl.multiple_of(tile * TILE, TILE), TILE)

        def score(h):
            return jnp.dot(
                kv_ref[rows, 128 * h : 128 * h + 128], pairs[h], preferred_element_type=f32
            )

        def weigh(h, scores):
            if allowed is not None:
                scores = jnp.where(allowed, scores, masked_value)
            top_old = tops[h]
            top = jnp.maximum(top_old, jnp.max(scores, axis=0, keepdims=True))
            weights = jnp.exp(scores - top)
            shrink = jnp.exp(top_old - top)
            tops[h] = top
            totals[h] = totals[h] * shrink + jnp.sum(weights, axis=0, keepdims=True)
            return weights.astype(bf16), shrink

        def gather(h, weights, shrink):
            sums[h] = sums[h] * shrink + jnp.dot(
                turned[tile, 128 * h + HEAD_SIZE : 128 * h + 128, :],
                weights,
                preferred_element_type=f32,
            )

        scores = [score(h) for h in range(KEY_VALUE_HEADS)]
        held = None
        for h in range(KEY_VALUE_HEADS):
            weighed = weigh(h, scores[h])
            if held is not None:
                gather(h - 1, *held)
            held = weighed
        gather(KEY_VALUE_HEADS - 1, *held)

    over_tiles(tile_range(starts_ref, fills_ref, block), block, step)
    for h in range(KEY_VALUE_HEADS):
        outcome = (sums[h] / totals[h]).astype(bf16)
        log_total = tops[h] + jnp.log(totals[h])
        for g in range(GROUPED):
            head = GROUPED * h + g
            mixed_ref[HEAD_SIZE * head : HEAD_SIZE * (head + 1), :] = outcome[:, BLK * g : BLK * (g + 1)]
            log_ref[head : head + 1, :] = log_total[:, BLK * g : BLK * (g + 1)]
    log_ref[QUERY_HEADS:, :] = jnp.zeros((1, BLK), f32)


def token_block(rows):
    return pl.BlockSpec((rows, BLK), lambda i, *_: (0, i))


def whole(shape):
    return pl.BlockSpec(shape, lambda i, *_: (0,) * len(shape))


def attention_forward(starts, fills, place, query, kv):
    group = sum(block.shape[0] for block in kv)
    return pl.pallas_call(
        attention_forward_kernel,
        grid_spec=pltpu.PrefetchScalarGridSpec(
            num_scalar_prefetch=3,
            grid=(TOK_DEV // BLK,),
            in_specs=[token_block(MODEL_WIDTH)] + [whole(block.shape) for block in kv],
            out_specs=[token_block(MODEL_WIDTH), token_block(16)],
            scratch_shapes=[
                pltpu.VMEM((group, 2 * KV_WIDTH), bf16),
                pltpu.VMEM((group // TILE, 2 * KV_WIDTH, TILE), bf16),
                pltpu.VMEM((KEY_VALUE_HEADS, 2 * HEAD_SIZE, WIDE), bf16),
                pltpu.VMEM((KEY_VALUE_HEADS, 1, WIDE), f32),
                pltpu.VMEM((KEY_VALUE_HEADS, 1, WIDE), f32),
                pltpu.VMEM((KEY_VALUE_HEADS, HEAD_SIZE, WIDE), f32),
            ],
        ),
        out_shape=[
            jax.ShapeDtypeStruct((MODEL_WIDTH, TOK_DEV), bf16),
            jax.ShapeDtypeStruct((16, TOK_DEV), f32),
        ],
        name="attention_forward",
    )(starts, fills, place, query, *kv)


def attention_backward_kernel(
    first,
    blocks,
    starts_ref,
    fills_ref,
    place_ref,
    query_ref,
    upstream_ref,
    mixed_ref,
    log_ref,
    cosine_ref,
    sine_ref,
    *refs,
):
    kv_blocks, refs = refs[:blocks], refs[-(blocks + 10) :]
    d_query_ref, d_kv_blocks = refs[0], refs[1 : blocks + 1]
    kv_ref, turned, pairs, query_rows, upstream_rows, deltas, logs, sums, kv_sums = refs[blocks + 1 :]
    count = kv_sums.shape[0]
    i = pl.program_id(0)
    block = place_ref[0] * (TOK_DEV // BLK) + i
    tiles = kv_ref.shape[0] // TILE

    @pl.when(i == 0)
    def _():
        for apart, source in enumerate(kv_blocks):
            size = source.shape[0]
            spot = apart if blocks == 1 else place_ref[0] ^ apart
            kv_ref[pl.ds(pl.multiple_of(spot * size, TILE), size), :] = source[
                :, 128 * first : 128 * (first + count)
            ]

        def prepare(t, carry):
            rows = pl.ds(pl.multiple_of(t * TILE, TILE), TILE)
            for h in range(count):
                turned[t, HEAD_SIZE * h : HEAD_SIZE * (h + 1), :] = kv_ref[
                    rows, 128 * h : 128 * h + 128
                ].T[:HEAD_SIZE]
            kv_sums[:, rows, :] = jnp.zeros((count, TILE, 128), f32)
            return carry

        lax.fori_loop(0, tiles, prepare, 0)

    blank = jnp.zeros((HEAD_SIZE, WIDE), bf16)
    for h in range(count):
        query = heads_beside(query_ref, first + h)
        upstream = heads_beside(upstream_ref, first + h)
        pairs[h, :HEAD_SIZE, :WIDE] = query
        pairs[h, HEAD_SIZE:, :WIDE] = blank
        pairs[h, :HEAD_SIZE, WIDE:] = blank
        pairs[h, HEAD_SIZE:, WIDE:] = upstream
        query_rows[h] = pairs[h, :, :WIDE].T
        upstream_rows[h] = pairs[h, :, WIDE:].T
        deltas[h] = jnp.sum(
            upstream.astype(f32) * heads_beside(mixed_ref, first + h).astype(f32),
            axis=0,
            keepdims=True,
        )
        line = GROUPED * (first + h)
        logs[h] = jnp.concatenate(
            [log_ref[line + g : line + g + 1, :] for g in range(GROUPED)], axis=1
        )
    sums[...] = jnp.zeros(sums.shape, f32)

    def step(tile, allowed):
        rows = pl.ds(pl.multiple_of(tile * TILE, TILE), TILE)

        def score(h):
            return jnp.dot(
                kv_ref[rows, 128 * h : 128 * h + 128], pairs[h], preferred_element_type=f32
            )

        def weigh(h, both):
            scores = both[:, :WIDE]
            if allowed is not None:
                scores = jnp.where(allowed, scores, masked_value)
            probs = jnp.exp(scores - logs[h])
            d_scores = (probs * (both[:, WIDE:] - deltas[h])).astype(bf16)
            return probs.astype(bf16), d_scores

        def gather(h, probs, d_scores):
            kv_sums[h, rows, :] += jnp.dot(
                d_scores, query_rows[h], preferred_element_type=f32
            ) + jnp.dot(probs, upstream_rows[h], preferred_element_type=f32)
            sums[h] += jnp.dot(
                turned[tile, HEAD_SIZE * h : HEAD_SIZE * (h + 1), :],
                d_scores,
                preferred_element_type=f32,
            )

        following = score(0)
        held = None
        for h in range(count):
            both = following
            if h + 1 < count:
                following = score(h + 1)
            weighed = weigh(h, both)
            if held is not None:
                gather(h - 1, *held)
            held = weighed
        gather(count - 1, *held)

    over_tiles(tile_range(starts_ref, fills_ref, block), block, step)
    cosine = cosine_ref[...]
    sine = sine_ref[...]
    half = HEAD_SIZE // 2
    for h in range(count):
        for g in range(GROUPED):
            head = GROUPED * h + g
            front = sums[h, :half, BLK * g : BLK * (g + 1)] * score_scale
            back = sums[h, half:, BLK * g : BLK * (g + 1)] * score_scale
            d_query_ref[HEAD_SIZE * head : HEAD_SIZE * head + half, :] = (
                front * cosine + back * sine
            ).astype(bf16)
            d_query_ref[HEAD_SIZE * head + half : HEAD_SIZE * (head + 1), :] = (
                back * cosine - front * sine
            ).astype(bf16)

    @pl.when(i == pl.num_programs(0) - 1)
    def _():
        size = kv_blocks[0].shape[0]
        for apart, out in enumerate(d_kv_blocks):
            spot = apart if blocks == 1 else place_ref[0] ^ apart

            def emit(t, carry):
                rows = pl.ds(pl.multiple_of(spot * size + t * TILE, TILE), TILE)
                for h in range(count):
                    out[pl.ds(pl.multiple_of(t * TILE, TILE), TILE), 128 * h : 128 * h + 128] = (
                        kv_sums[h, rows, :].astype(bf16)
                    )
                return carry

            lax.fori_loop(0, size // TILE, emit, 0)


def attention_backward(
    first, count, starts, fills, place, query, upstream, mixed, logs, cosine, sine, kv, after=()
):
    group = sum(block.shape[0] for block in kv)
    half = HEAD_SIZE // 2
    outs = [(block.shape[0], 128 * count) for block in kv]
    return pl.pallas_call(
        functools.partial(attention_backward_kernel, first, len(kv)),
        grid_spec=pltpu.PrefetchScalarGridSpec(
            num_scalar_prefetch=3,
            grid=(TOK_DEV // BLK,),
            in_specs=[
                token_block(MODEL_WIDTH),
                token_block(MODEL_WIDTH),
                token_block(MODEL_WIDTH),
                token_block(16),
                token_block(half),
                token_block(half),
            ]
            + [whole(block.shape) for block in kv]
            + [pl.BlockSpec(memory_space=pl.ANY)] * len(after),
            out_specs=[token_block(GROUPED * HEAD_SIZE * count)] + [whole(shape) for shape in outs],
            scratch_shapes=[
                pltpu.VMEM((group, 128 * count), bf16),
                pltpu.VMEM((group // TILE, HEAD_SIZE * count, TILE), bf16),
                pltpu.VMEM((count, 2 * HEAD_SIZE, 2 * WIDE), bf16),
                pltpu.VMEM((count, WIDE, 128), bf16),
                pltpu.VMEM((count, WIDE, 128), bf16),
                pltpu.VMEM((count, 1, WIDE), f32),
                pltpu.VMEM((count, 1, WIDE), f32),
                pltpu.VMEM((count, HEAD_SIZE, WIDE), f32),
                pltpu.VMEM((count, group, 128), f32),
            ],
        ),
        out_shape=[jax.ShapeDtypeStruct((GROUPED * HEAD_SIZE * count, TOK_DEV), bf16)]
        + [jax.ShapeDtypeStruct(shape, bf16) for shape in outs],
        name="attention_backward",
    )(starts, fills, place, query, upstream, mixed, logs, cosine, sine, *kv, *after)


def dot_of(left, right, left_dim, right_dim):
    return lax.dot_general(
        left, right, (((left_dim,), (right_dim,)), ((), ())), preferred_element_type=f32
    )


SLOTS = 3
FORM = 640
PIECES = (240, 240, 160)
GAIN_LINE = 560
PAD_WIDTH = 1024
CHUNK = 640
CORE_BIT = ("shard", 1)
ROW_BIT = ("shard", 2)
NEAR_BITS = (ROW_BIT, ("dp", 1), ("dp", 2))
FAR_BITS = (("dp", 4),)
BACKWARD_CALLS = ((0, 5),)


def stages(colour):
    return (CORE_BIT,) + NEAR_BITS[colour:] + NEAR_BITS[:colour] + FAR_BITS


def swap(value, bit):
    axis, mask = bit
    size = lax.axis_size(axis)
    return lax.ppermute(value, axis, [(i, i ^ mask) for i in range(size)])


def gather_colour(own, colour):
    held = own[None]
    for bit in reversed(stages(colour)[1:]):
        held = jnp.concatenate([held, swap(held, bit)], axis=0)
    return held, swap(held, CORE_BIT)


def scatter_stage(held, number, arrived=None):
    outcome = []
    total = lambda parts: sum(part.astype(f32) for part in parts)
    bits = [stages(colour)[number] for colour in range(len(held))]
    if arrived is None and len(set(bits)) == 1:
        flat = [send.reshape(-1, 128) for _, send in held]
        merged = swap(jnp.concatenate(flat, axis=0), bits[0])
        arrived, base = [], 0
        for (_, send), lines in zip(held, flat):
            arrived.append(merged[base : base + lines.shape[0]].reshape(send.shape))
            base += lines.shape[0]
    if arrived is None:
        arrived = [swap(send, bit) for (_, send), bit in zip(held, bits)]
    for (parts, _), got in zip(held, arrived):
        half = got.shape[0] // 2
        if half == 0:
            outcome.append((total(parts)[0].astype(bf16), got[0]))
        else:
            parts = parts + [got]
            outcome.append(
                ([part[:half] for part in parts], total([part[half:] for part in parts]).astype(bf16))
            )
    return outcome


def positions():
    device = jnp.arange(UNITS, dtype=jnp.int32)
    width = lax.axis_size("shard")
    apart = {
        "dp": (device // width) ^ lax.axis_index("dp").astype(jnp.int32),
        "shard": (device % width) ^ lax.axis_index("shard").astype(jnp.int32),
    }
    tables = []
    for colour in range(SLOTS):
        place = jnp.zeros((UNITS,), jnp.int32)
        for axis, mask in stages(colour):
            place = 2 * place + (apart[axis] & mask) // mask
        tables.append(place)
    return jnp.concatenate(tables)


def copy_from(halves, place, dst, sem, pick=lambda ref: ref):
    for number, ref in enumerate(halves):

        @pl.when(place // 16 == number)
        def _():
            pltpu.make_async_copy(pick(ref.at[lax.rem(place, 16)]), dst, sem).start()


def copy_to(src, keep, send, place, sem):
    for number, pick in enumerate((keep, send)):

        @pl.when(place // 16 == number)
        def _():
            pltpu.make_async_copy(src, pick(lax.rem(place, 16)), sem).start()


def wait_for(ref, sem):
    pltpu.make_async_copy(ref, ref, sem).wait()


def form_attention_kernel(wide_ref, lines_ref, gains_ref, a_ref, b_ref, c_ref, mid, form):
    @pl.when(wide_ref[0] == 1)
    def _():
        def store(c, value):
            if c == 7:
                value = jnp.where(lane_low(80), value, 0.0)
            form[80 * c : 80 * c + 80, :] = value

        lines_to_rows_960(lines_ref, 0, 80, mid, store)

    @pl.when(wide_ref[0] == 0)
    def _():
        low = lane_low(120)
        line = [lines_ref[pl.ds(k, 120, stride=5), :] for k in range(5)]
        turned = [None, None] + [pltpu.roll(line[k], 64, 1) for k in range(2, 5)]
        form[pl.ds(0, 120, stride=2), :] = line[0]
        form[pl.ds(1, 120, stride=2), :] = jnp.where(low, turned[2], turned[3])
        form[pl.ds(240, 120, stride=2), :] = line[1]
        form[pl.ds(241, 120, stride=2), :] = jnp.where(low, turned[3], turned[4])
        mid[pl.ds(0, 120, stride=2), :] = line[2]
        mid[pl.ds(1, 120, stride=2), :] = turned[4]
        low = lane_low(80)
        form[480:560, :] = jnp.where(low, mid[0:80, :], pltpu.roll(mid[160:240, :], 64, 1))
        form[560:640, :] = jnp.where(low, mid[80:160, :], 0.0)

    form[GAIN_LINE : GAIN_LINE + 1, :] = jnp.where(
        lane_low(1), form[GAIN_LINE : GAIN_LINE + 1, :], gains_ref[...]
    )
    a_ref[...] = form[0:240, :].astype(bf16)
    b_ref[...] = form[240:480, :].astype(bf16)
    c_ref[...] = form[480:640, :].astype(bf16)


SMEM_SPEC = pl.BlockSpec(memory_space=pltpu.SMEM)
ANY_SPEC = pl.BlockSpec(memory_space=pl.ANY)


def form_attention(wide, lines, gains):
    return pl.pallas_call(
        form_attention_kernel,
        in_specs=[SMEM_SPEC, pl.BlockSpec((LINES, 128)), pl.BlockSpec((1, 128))],
        out_shape=[jax.ShapeDtypeStruct((n, 128), bf16) for n in PIECES],
        scratch_shapes=[pltpu.VMEM((240, 128), f32), pltpu.VMEM((FORM, 128), f32)],
        name="form_attention",
    )(wide, lines, gains)


def unform_attention_kernel(wide_ref, *refs):
    pieces, (lines_ref, gains_ref, mid, form) = refs[:6], refs[6:]
    base = 0
    for n, keep, got in zip(PIECES, pieces[0::2], pieces[1::2]):
        form[base : base + n, :] = keep[...].astype(f32) + got[...].astype(f32)
        base += n
    gains_ref[...] = form[GAIN_LINE : GAIN_LINE + 1, :]

    @pl.when(wide_ref[0] == 1)
    def _():
        rows_to_lines_960(lambda c: form[80 * c : 80 * c + 80, :], lines_ref, 0, 80, mid)

    @pl.when(wide_ref[0] == 0)
    def _():
        low = lane_low(120)
        mid[0:80, :] = form[480:560, :]
        mid[80:160, :] = form[560:640, :]
        mid[160:240, :] = pltpu.roll(form[480:560, :], 64, 1)
        even = [form[pl.ds(0, 120, stride=2), :], form[pl.ds(240, 120, stride=2), :]]
        odd = [form[pl.ds(1, 120, stride=2), :], form[pl.ds(241, 120, stride=2), :]]
        even.append(mid[pl.ds(0, 120, stride=2), :])
        odd.append(mid[pl.ds(1, 120, stride=2), :])
        odd = [pltpu.roll(value, 64, 1) for value in odd]
        lines_ref[pl.ds(0, 120, stride=5), :] = even[0]
        lines_ref[pl.ds(1, 120, stride=5), :] = even[1]
        lines_ref[pl.ds(2, 120, stride=5), :] = jnp.where(low, even[2], odd[0])
        lines_ref[pl.ds(3, 120, stride=5), :] = jnp.where(low, odd[0], odd[1])
        lines_ref[pl.ds(4, 120, stride=5), :] = jnp.where(low, odd[1], odd[2])


def unform_attention(wide, addends):
    return pl.pallas_call(
        unform_attention_kernel,
        in_specs=[SMEM_SPEC] + [pl.BlockSpec((n, 128)) for n in PIECES for _ in range(2)],
        out_shape=[jax.ShapeDtypeStruct((LINES, 128), f32), jax.ShapeDtypeStruct((1, 128), f32)],
        scratch_shapes=[pltpu.VMEM((240, 128), f32), pltpu.VMEM((FORM, 128), f32)],
        name="unform_attention",
    )(wide, *addends)


def wide_pieces(c):
    return [((80 * c + 16 * m) // 32, (80 * c + 16 * m) % 32, 16 * m) for m in range(5)]


def form_feedforward_kernel(narrow_ref, lines_ref, out, mid):
    for s in range(SLOTS):

        @pl.when(narrow_ref[s] == 1)
        def _():
            mid[30:32, :] = jnp.zeros((2, 128), f32)
            for c in range(20):
                mid[0:30, :] = lines_ref[pl.ds(LINES * s + c, 30, stride=20), :]
                out[s, c] = mid[0:32, :].astype(bf16)

        @pl.when(narrow_ref[s] == 0)
        def _():
            def store(c, value):
                if c == 7:
                    value = jnp.where(lane_low(80), value, 0.0)
                for k, r, m in wide_pieces(c):
                    out[s, k, r : r + 16, :] = value[m : m + 16].astype(bf16)

            lines_to_rows_960(lines_ref, LINES * s, 80, mid, store)


def form_feedforward(narrow, lines):
    return pl.pallas_call(
        form_feedforward_kernel,
        in_specs=[SMEM_SPEC, pl.BlockSpec((SLOTS * LINES, 128))],
        out_shape=jax.ShapeDtypeStruct((SLOTS, 20, 32, 128), bf16),
        scratch_shapes=[pltpu.VMEM((80, 128), f32)],
        name="form_feedforward",
    )(narrow, lines)


def unform_feedforward_kernel(narrow_ref, *refs):
    pieces, (lines_ref, mid) = refs[: 2 * SLOTS], refs[2 * SLOTS :]
    for s in range(SLOTS):
        keep, got = pieces[2 * s], pieces[2 * s + 1]

        @pl.when(narrow_ref[s] == 1)
        def _():
            for c in range(20):
                mid[0:32, :] = keep[c].astype(f32) + got[c].astype(f32)
                lines_ref[pl.ds(LINES * s + c, 30, stride=20), :] = mid[0:30, :]

        @pl.when(narrow_ref[s] == 0)
        def _():
            def load(c):
                return jnp.concatenate(
                    [
                        keep[k, r : r + 16, :].astype(f32) + got[k, r : r + 16, :].astype(f32)
                        for k, r, m in wide_pieces(c)
                    ],
                    axis=0,
                )

            rows_to_lines_960(load, lines_ref, LINES * s, 80, mid)


def unform_feedforward(narrow, addends):
    return pl.pallas_call(
        unform_feedforward_kernel,
        in_specs=[SMEM_SPEC] + [pl.BlockSpec((20, 32, 128))] * (2 * SLOTS),
        out_shape=jax.ShapeDtypeStruct((SLOTS * LINES, 128), f32),
        scratch_shapes=[pltpu.VMEM((80, 128), f32)],
        name="unform_feedforward",
    )(narrow, *addends)


def place_attention_kernel(table_ref, *refs):
    halves = [refs[2 * k : 2 * k + 2] for k in range(SLOTS)]
    query_ref, kv_ref, out_ref, gains_ref, units, sem = refs[2 * SLOTS :]

    def start(d, carry):
        base = 0
        for k, n in enumerate(PIECES):
            copy_from(halves[k], table_ref[UNITS * k + d], units.at[d, base : base + n, :], sem)
            base += n
        return carry

    lax.fori_loop(0, UNITS, start, 0)
    wait_for(units, sem)

    def wide(out, first):
        def body(u, carry):
            rows = pl.ds(pl.multiple_of(80 * u, 16), 80)
            for c in range(7):
                out[rows, 128 * c : 128 * c + 128] = units[first + u, 80 * c : 80 * c + 80, :]
            out[rows, 896:960] = units[first + u, 560:640, :64]
            return carry

        lax.fori_loop(0, 12, body, 0)

    def keyed(j, carry):
        low = lane_low(240)
        chunks = []
        for first in (12, 16):
            unit = units[first + j].astype(f32)
            last = jnp.concatenate(
                [unit[480:640], pltpu.roll(unit[480:560], 64, 1)], axis=0
            )
            lines = (unit[0:240], unit[240:480], last)
            chunks.append([(lines[h // 2], h % 2) for h in range(KEY_VALUE_HEADS)])
        rows = pl.ds(pl.multiple_of(240 * j, 16), 240)
        for h in range(KEY_VALUE_HEADS):
            kv_ref[rows, 128 * h : 128 * h + 128] = jnp.where(
                low, placed(chunks[0][h], 0), placed(chunks[1][h], 1)
            ).astype(bf16)
        return carry

    lax.fori_loop(0, 4, keyed, 0)
    wide(query_ref, 0)
    wide(out_ref, 20)
    for u in range(UNITS):
        gains_ref[u : u + 1, :] = units[u, GAIN_LINE : GAIN_LINE + 1, :].astype(f32)


def place_attention(table, gathered):
    return pl.pallas_call(
        place_attention_kernel,
        in_specs=[SMEM_SPEC] + [ANY_SPEC] * (2 * SLOTS),
        out_shape=[
            jax.ShapeDtypeStruct((MODEL_WIDTH, MODEL_WIDTH), bf16),
            jax.ShapeDtypeStruct((MODEL_WIDTH, 2 * KV_WIDTH), bf16),
            jax.ShapeDtypeStruct((MODEL_WIDTH, MODEL_WIDTH), bf16),
            jax.ShapeDtypeStruct((UNITS, 128), f32),
        ],
        scratch_shapes=[pltpu.VMEM((UNITS, FORM, 128), bf16), pltpu.SemaphoreType.DMA],
        name="place_attention",
    )(table, *gathered)


def split_attention_kernel(table_ref, query_ref, kv_ref, out_ref, gains_ref, *refs):
    *keeps, sent, units, sem = refs

    def send(d):
        row = lax.broadcasted_iota(jnp.int32, (16, 128), 0)
        lane = lax.broadcasted_iota(jnp.int32, (16, 128), 1)
        block = units[d, GAIN_LINE : GAIN_LINE + 16, :].astype(f32)
        units[d, GAIN_LINE : GAIN_LINE + 16, :] = jnp.where(
            jnp.logical_and(row == 0, lane >= 64), gains_ref[pl.ds(d, 1), :], block
        ).astype(bf16)
        base = 0
        for k, n in enumerate(PIECES):
            copy_to(
                units.at[d, base : base + n, :],
                lambda p: keeps[k].at[p],
                lambda p: sent.at[p, base : base + n, :],
                table_ref[UNITS * k + d],
                sem,
            )
            base += n

    def wide(source, first):
        def body(u, carry):
            rows = pl.ds(pl.multiple_of(80 * u, 16), 80)
            for c in range(7):
                units[first + u, 80 * c : 80 * c + 80, :] = source[rows, 128 * c : 128 * c + 128]
            tail = source[rows, 896:960]
            units[first + u, 560:640, :] = jnp.concatenate([tail, jnp.zeros_like(tail)], axis=1)
            send(first + u)
            return carry

        lax.fori_loop(0, 12, body, 0)

    def keyed(j, carry):
        low = lane_low(240)
        rows = pl.ds(pl.multiple_of(240 * j, 16), 240)
        for upper, first in ((0, 12), (1, 16)):
            heads = [
                (kv_ref[rows, 128 * h : 128 * h + 128].astype(f32), upper)
                for h in range(KEY_VALUE_HEADS)
            ]
            for c in range(2):
                units[first + j, 240 * c : 240 * c + 240, :] = jnp.where(
                    low, placed(heads[2 * c], 0), placed(heads[2 * c + 1], 1)
                ).astype(bf16)
            last = placed(heads[4], 0)
            turned = placed(heads[4], 1)
            units[first + j, 480:560, :] = jnp.where(
                lane_low(80), last[0:80], turned[160:240]
            ).astype(bf16)
            units[first + j, 560:640, :] = jnp.where(lane_low(80), last[80:160], 0.0).astype(bf16)
            send(first + j)
        return carry

    lax.fori_loop(0, 4, keyed, 0)
    wide(query_ref, 0)
    wide(out_ref, 20)
    wait_for(units, sem)


def split_attention(table, d_query, d_kv, d_out, gains):
    return pl.pallas_call(
        split_attention_kernel,
        in_specs=[
            SMEM_SPEC,
            pl.BlockSpec((MODEL_WIDTH, MODEL_WIDTH)),
            pl.BlockSpec((MODEL_WIDTH, 2 * KV_WIDTH)),
            pl.BlockSpec((MODEL_WIDTH, MODEL_WIDTH)),
            pl.BlockSpec((UNITS, 128)),
        ],
        out_specs=[ANY_SPEC] * (SLOTS + 1),
        out_shape=[jax.ShapeDtypeStruct((16, n, 128), bf16) for n in PIECES + (FORM,)],
        scratch_shapes=[pltpu.VMEM((UNITS, FORM, 128), bf16), pltpu.SemaphoreType.DMA],
        name="split_attention",
    )(table, d_query, d_kv, d_out, gains)


def feedforward_kernel(
    table_ref,
    hidden_ref,
    turned_ref,
    grad_ref,
    gate_ref,
    up_ref,
    down_ref,
    out_ref,
    d_hidden_ref,
    *refs,
):
    keeps, sent = refs[:SLOTS], refs[SLOTS]
    down, inner_rows, inner_turned, d_both, both_out, down_out, sems = refs[SLOTS + 1 :]
    q = pl.program_id(0)
    chunks = pl.num_programs(0)
    slot = lax.rem(q, 2)

    def send_terms():
        for u in range(2 * UNITS):
            device, s = divmod(u, SLOTS)
            copy_to(
                both_out.at[slot, u // UNITS, u % UNITS],
                lambda p: keeps[s].at[p, pl.ds(5 * q, 5)],
                lambda p: sent.at[s, p, pl.ds(5 * q, 5)],
                table_ref[UNITS * s + device],
                sems.at[slot, 0],
            )
        for v in range(8):
            unit = 2 * UNITS + 8 * q + v
            device = unit // SLOTS
            for s in range(SLOTS):

                @pl.when(unit - SLOTS * device == s)
                def _():
                    copy_to(
                        down_out.at[slot, v],
                        lambda p: keeps[s].at[p],
                        lambda p: sent.at[s, p],
                        table_ref[UNITS * s + device],
                        sems.at[slot, 1],
                    )

    def wait_terms(side):
        wait_for(both_out.at[side], sems.at[side, 0])
        wait_for(down_out.at[side], sems.at[side, 1])

    for v in range(8):
        for c in range(8):
            for k, r, m in wide_pieces(c):
                down[80 * v + m : 80 * v + m + 16, 128 * c : 128 * c + 128] = down_ref[
                    v, k, r : r + 16, :
                ]

    @pl.when(q == 0)
    def _():
        out_ref[...] = jnp.zeros(out_ref.shape, f32)
        d_hidden_ref[...] = jnp.zeros(d_hidden_ref.shape, f32)

    def rows_step(i, carry):
        rows = pl.ds(pl.multiple_of(256 * i, 256), 256)
        weights = jnp.concatenate(
            [ref[:, c].reshape(PAD_WIDTH, 128) for ref in (gate_ref, up_ref) for c in range(5)],
            axis=1,
        )
        both = jnp.dot(hidden_ref[rows, :], weights, preferred_element_type=f32)
        gate, upper = both[:, :CHUNK], both[:, CHUNK:]
        sigmoid_gate = jax.nn.sigmoid(gate)
        activated = gate * sigmoid_gate
        inner = (activated * upper).astype(bf16)
        inner_rows[rows, :] = inner
        out_ref[rows, :] += jnp.dot(inner, down[...], preferred_element_type=f32)
        d_inner = dot_of(grad_ref[rows, :], down[...], 1, 1)
        d_gate = d_inner * upper * sigmoid_gate * (1.0 + gate * (1.0 - sigmoid_gate))
        d_upper = d_inner * activated
        d_pair = jnp.concatenate([d_gate, d_upper], axis=1).astype(bf16)
        d_both[rows, :] = d_pair
        d_hidden_ref[rows, :] += dot_of(d_pair, weights, 1, 1)
        return carry

    lax.fori_loop(0, 2, rows_step, 0)
    inner_turned[...] = inner_rows[...].T

    @pl.when(q >= 2)
    def _():
        wait_terms(slot)

    def both_step(i, carry):
        rows = pl.ds(pl.multiple_of(256 * i, 256), 256)
        terms = jnp.dot(turned_ref[rows, :], d_both[...], preferred_element_type=f32).astype(bf16)
        units = pl.ds(8 * i, 8)
        for c in range(10):
            both_out[slot, c // 5, units, c % 5] = terms[:, 128 * c : 128 * c + 128].reshape(
                8, 32, 128
            )
        return carry

    lax.fori_loop(0, 4, both_step, 0)

    def down_step(i, carry):
        rows = pl.ds(pl.multiple_of(320 * i, 16), 320)
        terms = jnp.dot(
            inner_turned[rows, :], grad_ref[...], preferred_element_type=f32
        ).astype(bf16)
        for v in range(4):
            for c in range(8):
                for k, r, m in wide_pieces(c):
                    down_out[slot, 4 * i + v, k, r : r + 16, :] = terms[
                        80 * v + m : 80 * v + m + 16, 128 * c : 128 * c + 128
                    ]
        return carry

    lax.fori_loop(0, 2, down_step, 0)
    send_terms()

    @pl.when(q == chunks - 1)
    def _():
        for side in range(2):
            wait_terms(side)


def feedforward(table, hidden, turned, grad, weights):
    block = jax.ShapeDtypeStruct((16, 20, 32, 128), bf16)
    full = lambda shape: pl.BlockSpec(shape, lambda q: (0, 0))
    return pl.pallas_call(
        feedforward_kernel,
        grid=(FF // CHUNK,),
        in_specs=[
            SMEM_SPEC,
            full((TOK_DEV, PAD_WIDTH)),
            full((PAD_WIDTH, TOK_DEV)),
            full((TOK_DEV, PAD_WIDTH)),
            pl.BlockSpec((32, 5, 32, 128), lambda q: (0, q, 0, 0)),
            pl.BlockSpec((32, 5, 32, 128), lambda q: (1, q, 0, 0)),
            pl.BlockSpec((8, 20, 32, 128), lambda q: (8 + q, 0, 0, 0)),
        ],
        out_specs=[full((TOK_DEV, PAD_WIDTH))] * 2 + [ANY_SPEC] * (SLOTS + 1),
        out_shape=[jax.ShapeDtypeStruct((TOK_DEV, PAD_WIDTH), f32)] * 2
        + [block] * SLOTS
        + [jax.ShapeDtypeStruct((SLOTS,) + block.shape, bf16)],
        scratch_shapes=[
            pltpu.VMEM((CHUNK, PAD_WIDTH), bf16),
            pltpu.VMEM((TOK_DEV, CHUNK), bf16),
            pltpu.VMEM((CHUNK, TOK_DEV), bf16),
            pltpu.VMEM((TOK_DEV, 2 * CHUNK), bf16),
            pltpu.VMEM((2, 2, 32, 5, 32, 128), bf16),
            pltpu.VMEM((2, 8, 20, 32, 128), bf16),
            pltpu.SemaphoreType.DMA((2, 2)),
        ],
        compiler_params=pltpu.CompilerParams(vmem_limit_bytes=60 * 2**20),
        name="feedforward",
    )(table, hidden, turned, grad, weights, weights, weights)


def spread_matrix():
    column = jnp.arange(PAD_WIDTH, dtype=jnp.int32)
    entry = jnp.where(column % 32 < 30, 30 * (column // 32) + column % 32, -1)
    return (jnp.arange(MODEL_WIDTH, dtype=jnp.int32)[:, None] == entry[None, :]).astype(bf16)


def rope_tables(positions):
    steps = jnp.arange(HEAD_SIZE // 2, dtype=f32) * (2.0 / HEAD_SIZE)
    inverse = jnp.exp(-math.log(10000.0) * steps)
    angles = inverse[:, None] * positions.astype(f32)[None, :]
    return (jnp.cos(angles), jnp.sin(angles))


def norm_scale(field):
    return lax.rsqrt(jnp.mean(field * field, axis=1, keepdims=True) + epsilon)


def norm_back(upstream, normed, scale, gain):
    scaled = upstream * gain[None, :]
    return scale * (scaled - normed * jnp.mean(scaled * normed, axis=1, keepdims=True))


def adam_step(grad, moment, second, master):
    moment_new = 0.9 * moment + 0.1 * grad
    second_new = 0.999 * second + 0.001 * grad * grad
    corrected = moment_new / (1.0 - 0.9**ADAM_STEP)
    scaled = second_new / (1.0 - 0.999**ADAM_STEP)
    update = -learning_rate * (corrected / (jnp.sqrt(scaled) + 1e-08) + weight_decay * master)
    return (moment_new, second_new, update)


def gather_lines(block):
    return lax.all_gather(block, ALL_AXES, axis=0, tiled=True)


def scatter_lines(lines):
    return lax.psum_scatter(lines, ALL_AXES, scatter_dimension=0, tiled=True)


def local(
    layer_input,
    cotangent,
    master_attention,
    master_feedforward,
    master_gains,
    first_attention,
    second_attention,
    first_feedforward,
    second_feedforward,
    first_gains,
    second_gains,
    block_start,
    block_fill,
):
    devices = lax.axis_size(ALL_AXES)
    attention_lines = master_attention.shape[0] // 128
    feedforward_lines = master_feedforward.shape[0] // 128
    gain_count = master_gains.shape[0]
    padded = (attention_lines // 16 + 1) * 16

    in_units = devices == UNITS
    if in_units:
        table = positions()
        device = (
            lax.axis_index("dp") * lax.axis_size("shard") + lax.axis_index("shard")
        ).astype(jnp.int32)
        wide = jnp.logical_or(device < 12, device >= 20).astype(jnp.int32)[None]
        narrow = (SLOTS * device + jnp.arange(SLOTS, dtype=jnp.int32) < 2 * UNITS).astype(jnp.int32)
        gain_row = jnp.pad(
            master_gains.reshape(1, gain_count), ((0, 0), (64, 64 - gain_count))
        )
        pieces = form_attention(wide, master_attention.reshape(LINES, 128), gain_row)
        gathered = [half for k in range(SLOTS) for half in gather_colour(pieces[k], k)]
        forms = form_feedforward(narrow, master_feedforward.reshape(SLOTS * LINES, 128))
        feedforward_all = gather_lines(forms.reshape(SLOTS * FORM, 128))
        query_weight, kv_weight, out_weight, gain_rows = place_attention(table, gathered)
        gains_all = gain_rows[:, 64 : 64 + gain_count].reshape(-1)
    else:
        gain_lines = jnp.pad(
            master_gains.astype(bf16).reshape(1, gain_count),
            ((0, padded - attention_lines - 1), (0, 128 - gain_count)),
        )
        attention_block = jnp.concatenate(
            [master_attention.astype(bf16).reshape(attention_lines, 128), gain_lines], axis=0
        )
        by_device = gather_lines(attention_block).reshape(devices, padded, 128)
        feedforward_all = gather_lines(
            master_feedforward.astype(bf16).reshape(feedforward_lines, 128)
        )
        gains_all = by_device[:, attention_lines, :gain_count].reshape(-1).astype(f32)
        units = by_device[:, :attention_lines].reshape(UNITS, LINES, 128)
        query_weight = unpack_wide(units, 0)
        kv_weight = unpack_kv(units)
        out_weight = unpack_wide(units, 20)
    gain_one, gain_two = gains_all[:MODEL_WIDTH], gains_all[MODEL_WIDTH:]

    shard = lax.axis_index("shard").astype(jnp.int32)
    place = shard[None]
    first_row = shard * TOK_DEV
    first_block = shard * (TOK_DEV // BLK)
    local_slots = first_row + jnp.arange(TOK_DEV, dtype=jnp.int32)
    local_starts = lax.dynamic_slice_in_dim(block_start, first_block, TOK_DEV // BLK)
    local_fills = lax.dynamic_slice_in_dim(block_fill, first_block, TOK_DEV // BLK)
    live_rows = local_slots % BLK < jnp.repeat(local_fills, BLK)
    cosine_table, sine_table = rope_tables(local_slots - jnp.repeat(local_starts, BLK) * BLK)

    def rotate(field, scale):
        heads = field.shape[0]
        front = field[:, : HEAD_SIZE // 2]
        back = field[:, HEAD_SIZE // 2 :]
        return (
            jnp.concatenate(
                [
                    front * cosine_table[None] - back * sine_table[None],
                    back * cosine_table[None] + front * sine_table[None],
                ],
                axis=1,
            ).astype(bf16)
            * bf16(scale)
        ).reshape(heads * HEAD_SIZE, TOK_DEV)

    inputs = layer_input.astype(f32)
    scale_one = norm_scale(inputs)
    normed_one = inputs * scale_one
    first_hidden = (normed_one * gain_one[None, :]).astype(bf16)
    kv_turned = dot_of(kv_weight, first_hidden, 0, 1).reshape(
        KEY_VALUE_HEADS, 2, HEAD_SIZE, TOK_DEV
    )
    keys = rotate(kv_turned[:, 0], 1.0).reshape(KEY_VALUE_HEADS, 1, HEAD_SIZE, TOK_DEV)
    values = kv_turned[:, 1:].astype(bf16)
    kv_rows = jnp.concatenate([keys, values], axis=1).reshape(2 * KV_WIDTH, TOK_DEV).T
    if in_units:
        across = swap(kv_rows, ROW_BIT)
        kv_all = [kv_rows, swap(kv_rows, CORE_BIT), across, swap(across, CORE_BIT)]
    else:
        kv_all = [lax.all_gather(kv_rows, "shard", axis=0, tiled=True)]
    query_turned = rotate(
        dot_of(query_weight, first_hidden, 0, 1).reshape(QUERY_HEADS, HEAD_SIZE, TOK_DEV),
        score_scale,
    )
    mixed_turned, logs = attention_forward(block_start, block_fill, place, query_turned, kv_all)
    middle = inputs + dot_of(mixed_turned, out_weight, 0, 0)
    scale_two = norm_scale(middle)
    normed_two = middle * scale_two
    hidden_two = (normed_two * gain_two[None, :]).astype(bf16)

    grad_out = cotangent.astype(f32) * live_rows[:, None].astype(f32)
    grad_low = grad_out.astype(bf16)
    if in_units:
        spread = spread_matrix()
        outcome, d_spread, *ff_keeps, ff_sent = feedforward(
            table,
            dot_of(hidden_two, spread, 1, 0).astype(bf16),
            dot_of(spread, hidden_two, 0, 1).astype(bf16),
            jnp.pad(grad_low, ((0, 0), (0, PAD_WIDTH - MODEL_WIDTH))),
            feedforward_all.reshape(3 * UNITS, 20, 32, 128),
        )
        layer_output = middle + outcome[:, :MODEL_WIDTH]
        d_coarse = lax.reduce_precision(d_spread, 8, 7)
        d_hidden_two = dot_of(d_coarse.astype(bf16), spread, 1, 1) + dot_of(
            (d_spread - d_coarse).astype(bf16), spread, 1, 1
        )
        ff_sent = swap(ff_sent, CORE_BIT)
    else:
        gate_weight, up_weight, down_weight = unpack_ff(feedforward_all)
        gate = dot_of(hidden_two, gate_weight, 1, 0)
        upper = dot_of(hidden_two, up_weight, 1, 0)
        sigmoid_gate = jax.nn.sigmoid(gate)
        activated = gate * sigmoid_gate
        inner = (activated * upper).astype(bf16)
        layer_output = middle + dot_of(inner, down_weight, 1, 0)
        d_down_weight = dot_of(inner, grad_low, 0, 0).astype(bf16)
        d_inner = dot_of(grad_low, down_weight, 1, 1)
        d_gate = (
            d_inner * upper * sigmoid_gate * (1.0 + gate * (1.0 - sigmoid_gate))
        ).astype(bf16)
        d_upper = (d_inner * activated).astype(bf16)
        d_gate_weight = dot_of(hidden_two, d_gate, 0, 0).astype(bf16)
        d_up_weight = dot_of(hidden_two, d_upper, 0, 0).astype(bf16)
        d_hidden_two = dot_of(d_gate, gate_weight, 1, 1) + dot_of(d_upper, up_weight, 1, 1)
        feedforward_gradient = (
            scatter_lines(pack_ff(d_gate_weight, d_up_weight, d_down_weight))
            .astype(f32)
            .reshape(-1)
        )

    d_gain_two = jnp.sum(d_hidden_two * normed_two, axis=0)
    d_middle = grad_out + norm_back(d_hidden_two, normed_two, scale_two, gain_two)

    d_branch = d_middle.astype(bf16)
    d_out_weight = dot_of(mixed_turned, d_branch, 1, 0).astype(bf16)
    d_mixed = dot_of(out_weight, d_branch, 1, 1).astype(bf16)
    if in_units:
        ff_sent, d_mixed = lax.optimization_barrier((ff_sent, d_mixed))
        ff_held = scatter_stage([([keep], None) for keep in ff_keeps], 0, list(ff_sent))
    backward_of = lambda first, count, after: attention_backward(
        first,
        count,
        block_start,
        block_fill,
        place,
        query_turned,
        d_mixed,
        mixed_turned,
        logs,
        cosine_table,
        sine_table,
        kv_all,
        after,
    )
    if in_units:
        d_query, d_kv_rows = [], []
        for number, (first, count) in enumerate(BACKWARD_CALLS):
            d_query_part, *d_kv = backward_of(first, count, [send for _, send in ff_held])
            arrived = [
                swap(send, stages(colour)[number + 1]) for colour, (_, send) in enumerate(ff_held)
            ]
            d_kv, arrived = lax.optimization_barrier((d_kv, arrived))
            ff_held = scatter_stage(ff_held, number + 1, arrived)
            across = swap(d_kv[2] + swap(d_kv[3], CORE_BIT), ROW_BIT)
            arrived = [swap(send, stages(colour)[2]) for colour, (_, send) in enumerate(ff_held)]
            ff_held = scatter_stage(ff_held, 2, arrived)
            across, sums = lax.optimization_barrier((across, [send for _, send in ff_held]))
            ff_held = [(parts, send) for (parts, _), send in zip(ff_held, sums)]
            d_query.append(d_query_part)
            d_kv_rows.append(d_kv[0] + swap(d_kv[1], CORE_BIT) + across)
        d_query = jnp.concatenate(d_query, axis=0)
        d_kv_rows = jnp.concatenate(d_kv_rows, axis=1)
        arrived = [swap(send, stages(colour)[3]) for colour, (_, send) in enumerate(ff_held)]
    else:
        d_query, d_kv = backward_of(0, KEY_VALUE_HEADS, ())
        d_kv_rows = lax.psum_scatter(d_kv, "shard", scatter_dimension=0, tiled=True)
    d_kv_turned = d_kv_rows.T.reshape(KEY_VALUE_HEADS, 2, HEAD_SIZE, TOK_DEV)
    d_front = d_kv_turned[:, 0, : HEAD_SIZE // 2].astype(f32)
    d_back = d_kv_turned[:, 0, HEAD_SIZE // 2 :].astype(f32)
    d_keys = jnp.concatenate(
        [
            d_front * cosine_table[None] + d_back * sine_table[None],
            d_back * cosine_table[None] - d_front * sine_table[None],
        ],
        axis=1,
    ).astype(bf16)
    d_kv_lin = jnp.concatenate([d_keys[:, None], d_kv_turned[:, 1:]], axis=1).reshape(
        2 * KV_WIDTH, TOK_DEV
    )
    d_query_weight = dot_of(first_hidden, d_query, 0, 1).astype(bf16)
    d_kv_weight = dot_of(first_hidden, d_kv_lin, 0, 1).astype(bf16)
    d_hidden_one = dot_of(d_query, query_weight, 0, 1) + dot_of(d_kv_lin, kv_weight, 0, 1)
    d_gain_one = jnp.sum(d_hidden_one * normed_one, axis=0)
    input_gradient = d_middle + norm_back(d_hidden_one, normed_one, scale_one, gain_one)

    gain_terms = jnp.concatenate([d_gain_one, d_gain_two])
    if in_units:
        gain_rows = jnp.pad(
            gain_terms.reshape(UNITS, gain_count), ((0, 0), (64, 64 - gain_count))
        )
        arrived, d_query_weight = lax.optimization_barrier((arrived, d_query_weight))
        ff_held = scatter_stage(ff_held, 3, arrived)
        for number in range(4, len(stages(0))):
            ff_held = scatter_stage(ff_held, number)
        ff_addends = [addend for pair in ff_held for addend in pair]
        feedforward_gradient = unform_feedforward(narrow, ff_addends).reshape(-1)
        *keeps, sent = split_attention(table, d_query_weight, d_kv_weight, d_out_weight, gain_rows)
        sent = swap(sent, CORE_BIT)
        arrived = [sent[:, sum(PIECES[:k]) : sum(PIECES[: k + 1])] for k in range(SLOTS)]
        held = scatter_stage([([keep], None) for keep in keeps], 0, arrived)
        for number in range(1, len(stages(0))):
            held = scatter_stage(held, number)
        addends = [addend for pair in held for addend in pair]
        attention_sum, gain_sum = unform_attention(wide, addends)
        attention_gradient = attention_sum.reshape(-1)
        gains_gradient = gain_sum[0, 64 : 64 + gain_count]
    else:
        no_gains = jnp.zeros((UNITS, GAIN_LINES, 128), bf16)
        terms = pack_attention(d_query_weight, d_kv_weight, d_out_weight, no_gains)
        terms = jnp.concatenate(
            [
                terms[:, :LINES].reshape(devices, attention_lines, 128),
                jnp.pad(
                    gain_terms.astype(bf16).reshape(devices, 1, gain_count),
                    ((0, 0), (0, padded - attention_lines - 1), (0, 128 - gain_count)),
                ),
            ],
            axis=1,
        )
        summed = scatter_lines(terms.reshape(devices * padded, 128)).astype(f32)
        attention_gradient = summed[:attention_lines].reshape(-1)
        gains_gradient = summed[attention_lines, :gain_count]

    attention_first, attention_second, attention_update = adam_step(
        attention_gradient, first_attention, second_attention, master_attention
    )
    feedforward_first, feedforward_second, feedforward_update = adam_step(
        feedforward_gradient, first_feedforward, second_feedforward, master_feedforward
    )
    gains_first, gains_second, gains_update = adam_step(
        gains_gradient, first_gains, second_gains, master_gains
    )
    return (
        layer_output,
        input_gradient,
        attention_gradient,
        feedforward_gradient,
        gains_gradient,
        attention_first,
        attention_second,
        feedforward_first,
        feedforward_second,
        gains_first,
        gains_second,
        attention_update,
        feedforward_update,
        gains_update,
    )


def solution(mesh):
    rows = P(ALL_AXES, None)
    flat = P(ALL_AXES)
    return jax.shard_map(
        local,
        mesh=mesh,
        in_specs=(rows, rows) + (flat,) * 9 + (P("dp"), P("dp")),
        out_specs=(rows, rows) + (flat,) * 12,
        check_vma=False,
    )
```
